32 devices in a mesh: dp: 4 (over y, core), seq: 8 (over z, x).
Axes of the slice: x: 2, y: 2, z: 4, core: 2. Of those that a mesh axis runs over, the one named last changes fastest.
Arguments:
- tokens: bfloat16 [8192, 1024], P(('dp', 'seq')), may hold values from -6 to 6
- lengths: int32 [4, 4], P('dp'), may hold values from 1 to 1024, 2048 in all within a row
- cotangent: bfloat16 [8192, 1024], P(('dp', 'seq')), may hold values from -6 to 6
- mixer_gain: bfloat16 [1024], P(('dp', 'seq')), may hold values from 0.5 to 1.5
- query_weight: bfloat16 [1024, 512], P(('dp', 'seq')), may hold values from -0.1875 to 0.1875
- keyval_weight: bfloat16 [1024, 256], P(('dp', 'seq')), may hold values from -0.1875 to 0.1875
- inner_weight: bfloat16 [1024, 3352], P(('dp', 'seq')), may hold values from -0.1875 to 0.1875
- conv_weight: bfloat16 [1792, 4], P(('dp', 'seq')), may hold values from -3 to 3
- conv_bias: bfloat16 [1792], P(('dp', 'seq')), may hold values from -1.5 to 1.5
- ssm_gain: bfloat16 [1536], P(('dp', 'seq')), may hold values from 0.5 to 1.5
- attn_out_weight: bfloat16 [512, 1024], P(('dp', 'seq')), may hold values from -2 to 2
- ssm_out_weight: bfloat16 [1536, 1024], P(('dp', 'seq')), may hold values from -0.15625 to 0.15625
- ffn_gain: bfloat16 [1024], P(('dp', 'seq')), may hold values from 0.5 to 1.5
- gate_up_weight: bfloat16 [1024, 4096], P(('dp', 'seq')), may hold values from -0.1875 to 0.1875
- down_weight: bfloat16 [2048, 1024], P(('dp', 'seq')), may hold values from -0.125 to 0.125
- decay_log: float32 [24], replicated, may hold values from -6 to 0
- step_bias: float32 [24], replicated, may hold values from -4 to -1
- skip_gain: float32 [24], replicated, may hold values from 0.5 to 1.5
Outputs:
- output: bfloat16 [8192, 1024], P(('dp', 'seq'))
- tokens_grad: float32 [8192, 1024], P(('dp', 'seq'))
- mixer_gain_grad: float32 [1024], P(('dp', 'seq'))
- query_weight_grad: float32 [1024, 512], P(('dp', 'seq'))
- keyval_weight_grad: float32 [1024, 256], P(('dp', 'seq'))
- inner_weight_grad: float32 [1024, 3352], P(('dp', 'seq'))
- conv_weight_grad: float32 [1792, 4], P(('dp', 'seq'))
- conv_bias_grad: float32 [1792], P(('dp', 'seq'))
- ssm_gain_grad: float32 [1536], P(('dp', 'seq'))
- attn_out_grad: float32 [512, 1024], P(('dp', 'seq'))
- ssm_out_grad: float32 [1536, 1024], P(('dp', 'seq'))
- ffn_gain_grad: float32 [1024], P(('dp', 'seq'))
- gate_up_grad: float32 [1024, 4096], P(('dp', 'seq'))
- down_grad: float32 [2048, 1024], P(('dp', 'seq'))
- decay_log_grad: float32 [24], replicated
- step_bias_grad: float32 [24], replicated
- skip_gain_grad: float32 [24], replicated
The draws below stay inside these ranges and needn't reach their ends.
Inputs may be any that keep to these rules, and one draw needn't show every extreme that they name: Each row holds one data group's 4 sequence lengths in stream order; a row sums to 2048 and its largest entry is exactly 1024.
All inputs are finite; a program needn't handle non-finite values.
Results may differ from the reference program's by a relative error of at most 0.014.
Values may be sent and summed in bfloat16 or wider, within the bound.
No kernel may reach another device: no remote copies, remote signals or barrier semaphores. Data moves between devices by JAX's collectives and lax.ppermute only.
A program may use at most 256 MiB of HBM per device.

```python
import functools
import math
import jax
import jax.numpy as jnp
import numpy as np
from jax import lax

D = 1024
HEADS = 8
KV_HEADS = 2
HEAD_DIM = 64
SSM_HEADS = 24
SSM_DIM = 64
STATE = 128
CONV = 4
FF = 2048
TOK_DEV = 256
SEQS = 4
GROUP_TOK = 2048
TOKENS = 8192
MOST_LEN = 1024
DS = 1536
CONV_CH = 1792
IN_COLS = 3352
N_DP = 4


def steps_of(key, extent, cuts, smallest, largest):
    loudness, own = 1.0, jax.random.fold_in(key, 6)
    for axis_at, blocks in cuts:
        draws = jnp.exp(jax.random.uniform(jax.random.fold_in(own, axis_at), (blocks,), jnp.float32, smallest / len(cuts), largest / len(cuts)))
        loudness = loudness * jnp.repeat(draws, extent[axis_at] // blocks).reshape([-1 if axis == axis_at else 1 for axis in range(len(extent))])
    return loudness


def profile(number_of, total, limit, skew):
    portions = [(1 << 20) // math.isqrt(rank ** skew) + 1 for rank in range(2, number_of + 1)]
    surplus, holding = total - limit - (number_of - 1), [1] * (number_of - 1)
    while surplus > 0:
        candidates = [i for i in range(number_of - 1) if holding[i] < limit]
        mass, budget = sum([portions[i] for i in candidates]), surplus
        for i in candidates:
            more = min(limit - holding[i], max(1, budget * portions[i] // mass), surplus)
            holding[i] = holding[i] + more
            surplus = surplus - more
    return np.array([limit] + holding)


def ragged(rng, amount, total, bound, lean):
    if amount == 2:
        one = jax.random.randint(rng, (), max(1, total - bound), min(bound, total - 1) + 1)
        return jnp.stack([one, total - one])
    tallies = jnp.asarray(profile(amount, total, bound, lean), jnp.int32)
    twos = (amount - 1) // 2
    giver, taker = tallies[1:1 + 2 * twos:2], tallies[2:2 + 2 * twos:2]
    room = jnp.minimum(giver - 1, bound - taker)
    passed = jax.random.randint(jax.random.fold_in(rng, 1), (twos,), 0, 1 << 20) % (room + 1)
    tallies = tallies.at[1:1 + 2 * twos:2].set(giver - passed).at[2:2 + 2 * twos:2].set(taker + passed)
    return tallies[jax.random.permutation(jax.random.fold_in(rng, 2), amount)]


def bell_draw(key, extent, spread, most, cuts=(), dtype=jnp.bfloat16):
    values = spread * jax.random.normal(key, extent, jnp.float32)
    if cuts:
        values = values * steps_of(key, extent, cuts, -0.22, 0.18)
    return jnp.clip(values, -most, most).astype(dtype)


def setup_inputs(seed: int = 0) -> dict:
    splits = jax.random.split(jax.random.key(seed), 19)
    return {
        "tokens": bell_draw(splits[0], (TOKENS, D), 1.0, 6.0, ((0, 32),)),
        "lengths": jax.vmap(lambda own: ragged(own, SEQS, GROUP_TOK, MOST_LEN, 2))(jax.random.split(splits[1], N_DP)).reshape((N_DP, SEQS)).astype(jnp.int32),
        "cotangent": bell_draw(splits[2], (TOKENS, D), 1.0, 6.0, ((0, 32),)),
        "mixer_gain": jnp.clip(1.0 + 0.1 * jax.random.normal(splits[3], (D,), jnp.float32), 0.5, 1.5).astype(jnp.bfloat16),
        "query_weight": bell_draw(splits[4], (D, HEADS * HEAD_DIM), D ** -0.5, 0.1875, ((0, 32),)),
        "keyval_weight": bell_draw(splits[5], (D, 2 * KV_HEADS * HEAD_DIM), D ** -0.5, 0.1875, ((0, 32),)),
        "inner_weight": bell_draw(splits[6], (D, IN_COLS), D ** -0.5, 0.1875, ((0, 32),)),
        "conv_weight": bell_draw(splits[7], (CONV_CH, CONV), CONV ** -0.5, 3.0, ((0, 32),)),
        "conv_bias": bell_draw(splits[8], (CONV_CH,), 0.3, 1.5, ((0, 32),)),
        "ssm_gain": jnp.clip(1.0 + 0.1 * jax.random.normal(splits[9], (DS,), jnp.float32), 0.5, 1.5).astype(jnp.bfloat16),
        "attn_out_weight": bell_draw(splits[10], (HEADS * HEAD_DIM, D), (HEADS * HEAD_DIM // 64) ** -0.5, 2.0, ((0, 32),)),
        "ssm_out_weight": bell_draw(splits[11], (DS, D), DS ** -0.5, 0.15625, ((0, 32),)),
        "ffn_gain": jnp.clip(1.0 + 0.1 * jax.random.normal(splits[12], (D,), jnp.float32), 0.5, 1.5).astype(jnp.bfloat16),
        "gate_up_weight": bell_draw(splits[13], (D, 2 * FF), D ** -0.5, 0.1875, ((0, 32),)),
        "down_weight": bell_draw(splits[14], (FF, D), FF ** -0.5, 0.125, ((0, 32),)),
        "decay_log": jnp.clip(jax.random.uniform(splits[15], (SSM_HEADS,), jnp.float32, -6.0, 0.0), -6.0, 0.0),
        "step_bias": jnp.clip(jax.random.uniform(splits[16], (SSM_HEADS,), jnp.float32, -4.0, -1.0), -4.0, -1.0),
        "skip_gain": jnp.clip(jax.random.uniform(splits[17], (SSM_HEADS,), jnp.float32, 0.5, 1.5), 0.5, 1.5),
    }


eps_norm = 1e-06
rope_base = 10000.0

@jax.custom_vjp
def low(v):
    return lax.optimization_barrier(v.astype(jnp.bfloat16)).astype(jnp.float32)

@jax.custom_vjp
def low_back(v):
    return v

def low_keep(v):
    return (low(v), None)

def low_pass(kept, grad):
    return (grad,)

def back_keep(v):
    return (v, None)

def back_low(kept, grad):
    return (low(grad),)
low.defvjp(low_keep, low_pass)
low_back.defvjp(back_keep, back_low)

def matmul(left, right):
    return jnp.dot(left, right, precision=lax.Precision.HIGHEST)

def seq_layout(places, seq_lengths):
    ends = jnp.cumsum(seq_lengths).astype(jnp.int32)
    before = (ends[None, :] <= places[:, None]).astype(jnp.int32)
    segments = lax.optimization_barrier(jnp.sum(before, axis=1)).astype(jnp.int32)
    offset = (places - lax.optimization_barrier(jnp.sum(before * seq_lengths[None, :], axis=1))).astype(jnp.int32)
    return (segments, offset)

def rotate(values, offset):
    half = values.shape[-1] // 2
    freq = rope_base ** (-jnp.arange(half).astype(jnp.float32) / half)
    angle = offset.astype(jnp.float32)[:, None] * freq[None, :]
    cosine = jnp.cos(angle)[:, None, :]
    sine = jnp.sin(angle)[:, None, :]
    first_half = values[..., :half]
    second_half = values[..., half:]
    return jnp.concatenate([first_half * cosine - second_half * sine, second_half * cosine + first_half * sine], axis=-1)

def attend_block(product, query, query_place, query_seg, keys, values, key_place, key_seg):
    raw = low_back(product(query, keys.T))
    scores = raw * query.shape[-1] ** (-0.5)
    allowed = (key_seg[None, :] == query_seg[:, None]) & (key_place[None, :] <= query_place[:, None])
    scores = jnp.where(allowed, scores, -1e+30)
    total = jax.nn.logsumexp(scores, axis=1, keepdims=True)
    weights = low(jnp.exp(scores - total))
    return product(weights, values)

def attention(product, queries, keyvals, query_place, query_seg, key_place, key_seg, block):
    rows = queries.shape[0]
    per_head = queries.reshape(rows // block, block, HEADS, HEAD_DIM).transpose(2, 0, 1, 3)
    pairs = keyvals.reshape(-1, 2, KV_HEADS, HEAD_DIM)
    keys_all = pairs[:, 0].transpose(1, 0, 2)
    values_all = pairs[:, 1].transpose(1, 0, 2)
    owner = (jnp.arange(HEADS) // (HEADS // KV_HEADS)).astype(jnp.int32)
    place_blocks = query_place.reshape(-1, block)
    seg_blocks = query_seg.reshape(-1, block)
    step_fn = jax.checkpoint(functools.partial(attend_block, product))

    def one_head(item):
        head_queries, which = item
        keys = keys_all[which]
        values = values_all[which]

        def one_block(part):
            return step_fn(part[0], part[1], part[2], keys, values, key_place, key_seg)
        return lax.map(one_block, (head_queries, place_blocks, seg_blocks))
    outputs = lax.map(one_head, (per_head, owner))
    merged = outputs.transpose(1, 2, 0, 3).reshape(rows, HEADS * HEAD_DIM)
    return low(low_back(merged))

def front(product, stream, gain_one, w_query, w_keyval, w_inner, offset):
    rows = stream.shape[0]
    normed = low(stream * lax.rsqrt(lax.optimization_barrier(jnp.mean(stream * stream, axis=1, keepdims=True)) + eps_norm) * gain_one[None, :])
    queries = low_back(product(normed, w_query))
    keyvals = low_back(product(normed, w_keyval))
    inner = low(low_back(product(normed, w_inner)))
    queries = low(rotate(queries.reshape(rows, HEADS, HEAD_DIM), offset).reshape(rows, HEADS * HEAD_DIM))
    pairs = keyvals.reshape(rows, 2, KV_HEADS, HEAD_DIM)
    keys = rotate(pairs[:, 0], offset)
    keyvals = low(jnp.stack([keys, pairs[:, 1]], axis=1).reshape(rows, 2 * KV_HEADS * HEAD_DIM))
    return (queries, keyvals, inner)

def mixer_inputs(inner, rim, w_conv, b_conv, step_bias, decay_log, ext_seg, own_seg):
    rows = inner.shape[0]
    channels = inner[:, DS:DS + CONV_CH]
    extended = jnp.concatenate([rim, channels], axis=0)
    mixed = jnp.zeros_like(channels) + b_conv[None, :]
    for tap in range(CONV):
        same = (ext_seg[tap:tap + rows] == own_seg).astype(jnp.float32)
        mixed = mixed + extended[tap:tap + rows] * w_conv[:, tap][None, :] * same[:, None]
    active = jax.nn.silu(mixed)
    signal = active[:, :DS].reshape(rows, SSM_HEADS, SSM_DIM)
    inputs_b = active[:, DS:DS + STATE]
    inputs_c = active[:, DS + STATE:]
    step = jax.nn.softplus(inner[:, DS + CONV_CH:] + step_bias[None, :])
    log_decay = -step * jnp.exp(decay_log)[None, :]
    return (signal, inputs_b, inputs_c, step, log_decay)

def ssd_block(state, signal, inputs_b, inputs_c, step, log_decay, segments, seg_prev):
    size = signal.shape[0]
    cum = jnp.cumsum(log_decay, axis=0)
    diff = cum[:, None, :] - cum[None, :, :]
    order = jnp.arange(size)
    keep = (order[:, None] >= order[None, :]) & (segments[:, None] == segments[None, :])
    decay = jnp.exp(jnp.where(keep[:, :, None], diff, -1e+30))
    scores = jnp.dot(inputs_c, inputs_b.T, precision=lax.Precision.HIGHEST)
    weighted = signal * step[:, :, None]
    result = jnp.einsum('tsh,ts,shp->thp', decay, scores, weighted, precision=lax.Precision.HIGHEST)
    carry = (segments == seg_prev).astype(jnp.float32)
    entering = jnp.einsum('tn,hpn->thp', inputs_c, state, precision=lax.Precision.HIGHEST)
    result = result + entering * (jnp.exp(cum) * carry[:, None])[:, :, None]
    tail = jnp.exp(cum[-1][None, :] - cum) * (segments == segments[-1]).astype(jnp.float32)[:, None]
    added = jnp.einsum('sh,shp,sn->hpn', tail, weighted, inputs_b, precision=lax.Precision.HIGHEST)
    new_state = state * (jnp.exp(cum[-1]) * carry[-1])[:, None, None] + added
    return (new_state, result)

def ssd_run(signal, inputs_b, inputs_c, step, log_decay, skip_gain, segments, seg_first, block):
    rows = signal.shape[0]
    count = rows // block
    before = jnp.concatenate([jnp.reshape(seg_first, (1,)).astype(jnp.int32), segments[:-1]])
    starts = before.reshape(count, block)[:, 0]

    def advance(state, item):
        return ssd_block(state, *item)
    initial = jnp.zeros((SSM_HEADS, SSM_DIM, STATE), jnp.float32)
    final, pieces = lax.scan(jax.checkpoint(advance), initial, (signal.reshape(count, block, SSM_HEADS, SSM_DIM), inputs_b.reshape(count, block, STATE), inputs_c.reshape(count, block, STATE), step.reshape(count, block, SSM_HEADS), log_decay.reshape(count, block, SSM_HEADS), segments.reshape(count, block), starts))
    output = pieces.reshape(rows, SSM_HEADS, SSM_DIM) + skip_gain[None, :, None] * signal
    return (output.reshape(rows, DS), final)

def post(product, stream, attended, ssd_out, gate_in, w_attn_out, w_ssm_out, gain_ssm, gain_two, w_gate_up, w_down):
    gated = ssd_out * jax.nn.silu(gate_in)
    normed = gated * lax.rsqrt(lax.optimization_barrier(jnp.mean(gated * gated, axis=1, keepdims=True)) + eps_norm) * gain_ssm[None, :]
    mixed_out = low(normed)
    branch = low_back(product(attended, w_attn_out) + product(mixed_out, w_ssm_out))
    middle = stream + branch
    normed_two = low(middle * lax.rsqrt(lax.optimization_barrier(jnp.mean(middle * middle, axis=1, keepdims=True)) + eps_norm) * gain_two[None, :])
    gate_up = low_back(product(normed_two, w_gate_up))
    width = w_down.shape[0]
    hidden = low(jax.nn.silu(gate_up[:, :width]) * gate_up[:, width:])
    return middle + low_back(product(hidden, w_down))

def layer_group(stream, seq_lengths, params):
    gain_one, w_query, w_keyval, w_inner, w_conv, b_conv, gain_ssm, w_attn_out, w_ssm_out, gain_two, w_gate_up, w_down, decay_log, step_bias, skip_gain = params
    rows = stream.shape[0]
    places = jnp.arange(rows).astype(jnp.int32)
    segments, offset = seq_layout(places, seq_lengths)
    queries, keyvals, inner = front(matmul, stream, gain_one, w_query, w_keyval, w_inner, offset)
    attended = attention(matmul, queries, keyvals, places, segments, places, segments, min(512, TOK_DEV))
    rim = jnp.zeros((CONV - 1, CONV_CH), jnp.float32)
    ext_seg = jnp.concatenate([jnp.full((CONV - 1,), -1, jnp.int32), segments])
    signal, inputs_b, inputs_c, step, log_decay = mixer_inputs(inner, rim, w_conv, b_conv, step_bias, decay_log, ext_seg, segments)
    ssd_out, final = ssd_run(signal, inputs_b, inputs_c, step, log_decay, skip_gain, segments, jnp.array(-1, jnp.int32), min(128, TOK_DEV))
    return post(matmul, stream, attended, ssd_out, inner[:, :DS], w_attn_out, w_ssm_out, gain_ssm, gain_two, w_gate_up, w_down)

def reference(tokens, lengths, cotangent, mixer_gain, query_weight, keyval_weight, inner_weight, conv_weight, conv_bias, ssm_gain, attn_out_weight, ssm_out_weight, ffn_gain, gate_up_weight, down_weight, decay_log, step_bias, skip_gain):
    params = tuple((item.astype(jnp.float32) for item in (mixer_gain, query_weight, keyval_weight, inner_weight, conv_weight, conv_bias, ssm_gain, attn_out_weight, ssm_out_weight, ffn_gain, gate_up_weight, down_weight, decay_log, step_bias, skip_gain)))
    stream = tokens.astype(jnp.float32).reshape(N_DP, GROUP_TOK, D)

    def forward(stream, params):

        def one_group(item):
            return layer_group(item[0], item[1], params)
        return lax.map(one_group, (stream, lengths))
    result, backward = jax.vjp(forward, stream, params)
    grad_stream, grads = backward(cotangent.astype(jnp.float32).reshape(N_DP, GROUP_TOK, D))
    return (result.reshape(TOKENS, D).astype(jnp.bfloat16), grad_stream.reshape(TOKENS, D), grads[0], grads[1], grads[2], grads[3], grads[4], grads[5], grads[6], grads[7], grads[8], grads[9], grads[10], grads[11], grads[12], grads[13], grads[14])
```

```python
import functools

import jax
import jax.numpy as jnp
from jax import lax
from jax.experimental import pallas as pl
from jax.experimental.pallas import tpu as pltpu
from jax.sharding import PartitionSpec as P

HEADS = 8
KV_HEADS = 2
HEAD_DIM = 64
SSM_HEADS = 24
SSM_DIM = 64
STATE = 128
CONV = 4
DS = 1536
CONV_CH = 1792
RIM = 16
LANES = 128
A_COLS = 2 * KV_HEADS * HEAD_DIM + HEADS * HEAD_DIM + 2 * STATE + LANES
EPS = 1e-6
BASE = 10000.0
NEG = -1e30
AXES = ("dp", "seq")

f32 = jnp.float32
bf16 = jnp.bfloat16


def nn(a, b):
    return lax.dot_general(a, b, (((1,), (0,)), ((), ())), preferred_element_type=f32)


def tn(a, b):
    return lax.dot_general(a, b, (((0,), (0,)), ((), ())), preferred_element_type=f32)


def nt(a, b):
    return lax.dot_general(a, b, (((1,), (1,)), ((), ())), preferred_element_type=f32)


def nn_full(a, b):
    return lax.dot_general(
        a, b, (((1,), (0,)), ((), ())), precision=lax.Precision.HIGHEST, preferred_element_type=f32
    )


def iota(shape, dim):
    return lax.broadcasted_iota(jnp.int32, shape, dim)


def head_spread():
    row = iota((LANES, DS), 0)
    return (iota((LANES, DS), 1) // SSM_DIM == row).astype(f32)


def head_sum_matrix():
    col = iota((DS, LANES), 1)
    return (iota((DS, LANES), 0) // SSM_DIM == col).astype(f32)


def extents():
    across, along = lax.axis_size("dp"), lax.axis_size("seq")
    return {
        "x": (1, 2),
        "z": (2, along // 2),
        "core": (along, 2),
        "y": (2 * along, across // 2),
    }


def my_index():
    return lax.axis_index("dp") * lax.axis_size("seq") + lax.axis_index("seq")


def place_on(group):
    unit, size = extents()[group]
    return (my_index() // unit) % size


def swap(array, mask):
    count = lax.axis_size("dp") * lax.axis_size("seq")
    return lax.ppermute(array, AXES, [(i, i ^ mask) for i in range(count)])


def in_order(pieces, place):
    pieces = list(pieces)
    bit = 1
    while bit < len(pieces):
        flag = (place // bit) % 2 == 1
        pieces = [jnp.where(flag, pieces[j ^ bit], pieces[j]) for j in range(len(pieces))]
        bit *= 2
    return pieces


def collect(array, group, axis):
    unit, size = extents()[group]
    pieces = [array] + [swap(array, k * unit) for k in range(1, size)]
    return jnp.stack(in_order(pieces, place_on(group)), axis)


def gather_pair(shard, first):
    full = collect(shard, "z", 0)
    if first == "y":
        full = collect(collect(full, "y", 0), "x", 2)
    else:
        full = collect(collect(full, "x", 1), "y", 0)
    other = swap(full, extents()["core"][0])
    shape = (full.shape[0], full.shape[1] * full.shape[2] * full.shape[3], full.shape[4])
    return full.reshape(shape), other.reshape(shape)


def fold(total, group, axis):
    unit, size = extents()[group]
    place = place_on(group)
    result = lax.dynamic_index_in_dim(total, place, axis, False).astype(f32)
    for k in range(1, size):
        part = lax.dynamic_index_in_dim(total, place ^ k, axis, False).astype(bf16)
        result = result + swap(part, k * unit).astype(f32)
    return result


def reduce_pair(own, received, rows, first):
    table = extents()
    shape = (table["y"][1], table["z"][1], table["x"][1], rows, own.shape[-1])
    total = own.reshape(shape).astype(f32) + received.reshape(shape).astype(f32)
    if first == "x":
        total = fold(fold(total, "x", 2), "y", 0)
    else:
        total = fold(fold(total, "y", 0), "x", 1)
    return fold(total, "z", 0)


def gather_small(vector):
    full = collect(collect(collect(vector, "z", 0), "x", 1), "core", 0)
    return collect(full, "y", 0).reshape(-1, vector.shape[-1])


def sum_small(array):
    mask = 1
    while mask < lax.axis_size("dp") * lax.axis_size("seq"):
        array = array + swap(array, mask)
        mask *= 2
    return array


def shifted(array, by):
    count = lax.axis_size("seq")
    pairs = [(i, i + by) for i in range(count) if 0 <= i + by < count]
    return lax.ppermute(array, "seq", pairs)


def link(earlier, later):
    carry = later[1]
    wide = jnp.repeat(carry[0, :SSM_HEADS], SSM_DIM)[:, None]
    return (later[0] + wide * earlier[0], carry * earlier[1])


def carried(state, carry, back, sign):
    def moved(pair, by):
        packed = jnp.concatenate([pair[0], jnp.pad(pair[1], ((0, RIM - 1), (0, 0)))], 0)
        got = shifted(packed.astype(bf16), sign * by).astype(f32)
        return (got[:DS], got[DS : DS + 1])

    pair = (state, carry)
    by = 1
    while by < back:
        pair = link(moved(pair, by), pair)
        by *= 2
    return moved(pair, 1)[0]


def halves(block, core):
    width = block.shape[1] // 2
    low, high = block[:, :width], block[:, width:]
    return jnp.where(core == 0, low, high), jnp.where(core == 0, high, low)


def put(ref, y, own, other, core):
    width = own.shape[1]
    base = y * 2 * width
    ref[:, base : base + width] = jnp.where(core == 0, own, other).astype(ref.dtype)
    ref[:, base + width : base + 2 * width] = jnp.where(core == 0, other, own).astype(ref.dtype)


def sides(ref, core, count):
    width = ref.shape[-1] // count
    return [halves(ref[:, y * width : (y + 1) * width], core) for y in range(count)]


def cross_half(value):
    lane = iota(value.shape, 1) % HEAD_DIM
    up = pltpu.roll(value, LANES - HEAD_DIM // 2, 1)
    down = pltpu.roll(value, HEAD_DIM // 2, 1)
    return jnp.where(lane < HEAD_DIM // 2, up, down)


def turned(value, cos, sin):
    return value * cos + cross_half(value) * sin


def turned_back(value, cos, sin):
    return value * cos - cross_half(value) * sin


def split_heads(pair, which, lane):
    flipped = pltpu.roll(pair, HEAD_DIM, 1)
    if which == 0:
        return jnp.where(lane < HEAD_DIM, pair, 0.0), jnp.where(lane < HEAD_DIM, flipped, 0.0)
    return jnp.where(lane >= HEAD_DIM, flipped, 0.0), jnp.where(lane >= HEAD_DIM, pair, 0.0)


def join_heads(even, odd, which, lane):
    if which == 0:
        return jnp.where(lane < HEAD_DIM, even, pltpu.roll(odd, HEAD_DIM, 1))
    return jnp.where(lane < HEAD_DIM, pltpu.roll(even, HEAD_DIM, 1), odd)


def conv_taps(chan_ref, cols, off):
    ext = chan_ref[:, cols].astype(f32)
    taps = []
    for i in range(CONV):
        back = CONV - 1 - i
        rows = pltpu.roll(ext, back, 0)[RIM:] if back else ext[RIM:]
        taps.append(rows * (off >= back).astype(f32))
    return taps


def sigmoid(v):
    return 1.0 / (1.0 + jnp.exp(-v))


def softplus(v):
    return jnp.maximum(v, 0.0) + jnp.log1p(jnp.exp(-jnp.abs(v)))


def tail_of(cum, off):
    rows = cum.shape[0]
    last_off = off[rows - 1 :, :]
    keep = iota((rows, 1), 0) >= rows - 1 - last_off
    return jnp.exp(cum[rows - 1 :, :] - cum) * keep.astype(f32)


def fade_of(cum, off):
    keep = off > iota((cum.shape[0], 1), 0)
    return jnp.exp(cum) * keep.astype(f32)


def carry_of(cum, off):
    rows = cum.shape[0]
    return jnp.exp(cum[rows - 1 :, :]) * (off[rows - 1 :, :] >= rows).astype(f32)


def front_kernel(
    core_ref, tok_ref, gain_ref, wa_own, wa_oth, wb_own, wb_oth, cos_ref, sin_ref, off_ref,
    cw_ref, cb_ref, sb_ref, dec_ref,
    q8_ref, kv_ref, normed_ref, chan_ref, x_ref, bc_ref, step_ref, cum_ref, cumt_ref, z_ref,
    state_ref, carry_ref,
    n_ref, xt_ref,
):
    core = core_ref[0]
    rows = cos_ref.shape[0]
    tok = tok_ref[...].astype(f32)
    rms = lax.rsqrt(jnp.mean(tok * tok, axis=1, keepdims=True) + EPS)
    n_ref[...] = (tok * rms * gain_ref[...]).astype(bf16)
    normed_ref[...] = n_ref[RIM:, :]
    count = wa_own.shape[0]
    blocks = sides(n_ref, core, count)

    def project(own_ref, oth_ref, cols):
        total = 0.0
        for y, (own, oth) in enumerate(blocks):
            total = total + nn(own, own_ref[y, :, cols]) + nn(oth, oth_ref[y, :, cols])
        return total

    lane = iota((rows, LANES), 1)
    cos, sin, off = cos_ref[...], sin_ref[...], off_ref[...]
    kv = project(wa_own, wa_oth, pl.ds(0, 256))[RIM:]
    kv_ref[:, :LANES] = turned(kv[:, :LANES], cos, sin).astype(bf16)
    kv_ref[:, LANES:] = kv[:, LANES:].astype(bf16)
    queries = project(wa_own, wa_oth, pl.ds(256, 512))[RIM:]
    for j in range(HEADS // 2):
        pair = turned(queries[:, j * LANES : (j + 1) * LANES], cos, sin)
        even, odd = split_heads(pair, j // 2, lane)
        q8_ref[2 * j] = even.astype(bf16)
        q8_ref[2 * j + 1] = odd.astype(bf16)
    rest = project(wa_own, wa_oth, pl.ds(768, 384))
    chan_ref[:, DS:] = rest[:, : 2 * STATE].astype(bf16)
    z = rest[RIM:, 2 * STATE :].astype(bf16).astype(f32) + sb_ref[...]
    for j in range(DS // 512):
        cols = slice(j * 512, (j + 1) * 512)
        chan_ref[:, cols] = project(wb_own, wb_oth, pl.ds(j * 512, 512)).astype(bf16)
    z_ref[...] = z
    step = softplus(z)
    step_ref[...] = step
    tri = (iota((rows, rows), 0) >= iota((rows, rows), 1)).astype(f32)
    cum = nn_full(tri, -step * dec_ref[...])
    cum_ref[...] = cum
    cumt_ref[...] = cum.T
    carry_ref[...] = carry_of(cum, off)
    weight = nn_full(step * tail_of(cum, off), head_spread())
    for j in range(CONV_CH // 256):
        cols = slice(j * 256, (j + 1) * 256)
        mixed = cb_ref[:, cols]
        for i, tap in enumerate(conv_taps(chan_ref, cols, off)):
            mixed = mixed + tap * cw_ref[i : i + 1, cols]
        active = mixed * sigmoid(mixed)
        if j < DS // 256:
            x_ref[:, cols] = active
            xt_ref[:, cols] = (active * weight[:, cols]).astype(bf16)
        else:
            bc_ref[...] = active
    state_ref[...] = tn(xt_ref[...], bc_ref[:, :STATE].astype(bf16))


def scan_masks(off, rows):
    t, s = iota((rows, rows), 0), iota((rows, rows), 1)
    return (s <= t) & (s >= t - off)


def scan_kernel(x_ref, bc_ref, step_ref, cum_ref, cumt_ref, off_ref, y_ref, xw_ref, ce_ref):
    rows = x_ref.shape[0]
    spread = head_spread()
    xw_ref[...] = (x_ref[...] * nn_full(step_ref[...], spread)).astype(bf16)
    ce_ref[...] = nn_full(cum_ref[...], spread)
    keys, reads = bc_ref[:, :STATE].astype(bf16), bc_ref[:, STATE:].astype(bf16)
    scores = jnp.where(scan_masks(off_ref[...], rows), nt(reads, keys), 0.0)
    lane = iota((rows, LANES), 1)

    def pair(j, unused):
        cols = pl.ds(pl.multiple_of(j * LANES, LANES), LANES)
        wide = ce_ref[:, cols]
        xw = xw_ref[:, cols]
        outs = []
        for k in range(2):
            late = wide[:, k * SSM_DIM : k * SSM_DIM + 1]
            early = cumt_ref[pl.ds(2 * j + k, 1), :]
            decay = jnp.exp(jnp.minimum(late - early, 0.0))
            outs.append(nn((decay * scores).astype(bf16), xw))
        y_ref[:, cols] = jnp.where(lane < SSM_DIM, outs[0], outs[1])
        return unused

    lax.fori_loop(0, SSM_HEADS // 2, pair, 0)


def attend_bias(off, rows, window):
    query = iota((rows, window), 0) + (window - rows)
    key = iota((rows, window), 1)
    return jnp.where((key <= query) & (key >= query - off), 0.0, NEG)


def attend_kernel(count, q8_ref, *refs):
    pieces, (off_ref, att_ref, lse_ref, k_ref, v_ref, bias_ref, o_ref) = refs[:count], refs[count:]
    rows = off_ref.shape[0]
    window = count * rows
    for i, piece in enumerate(pieces):
        k_ref[i * rows : (i + 1) * rows, :] = piece[:, :LANES]
        v_ref[i * rows : (i + 1) * rows, :] = piece[:, LANES:]
    bias_ref[...] = attend_bias(off_ref[...], rows, window)
    lane = iota((rows, LANES), 1)

    def head(h, lses):
        scores = nt(q8_ref[h], k_ref[...]) * HEAD_DIM**-0.5 + bias_ref[...]
        top = jnp.max(scores, axis=1, keepdims=True)
        probs = jnp.exp(scores - top)
        total = jnp.sum(probs, axis=1, keepdims=True)
        o_ref[h] = nn((probs * (1.0 / total)).astype(bf16), v_ref[...])
        return jnp.where(lane == h, top + jnp.log(total), lses)

    lse_ref[...] = lax.fori_loop(0, HEADS, head, jnp.zeros((rows, LANES), f32))
    for j in range(HEADS // 2):
        pair = join_heads(o_ref[2 * j], o_ref[2 * j + 1], j // 2, lane)
        att_ref[:, j * LANES : (j + 1) * LANES] = pair.astype(bf16)


def attend_back_kernel(count, q8_ref, *refs):
    pieces, rest = refs[:count], refs[count:]
    off_ref, lse_ref, datt_ref, cos_ref, sin_ref, dq_ref, dkv_ref = rest[:7]
    k_ref, v_ref, bias_ref, do_ref, dq8_ref = rest[7:]
    rows = off_ref.shape[0]
    window = count * rows
    for i, piece in enumerate(pieces):
        k_ref[i * rows : (i + 1) * rows, :] = piece[:, :LANES]
        v_ref[i * rows : (i + 1) * rows, :] = piece[:, LANES:]
    bias_ref[...] = attend_bias(off_ref[...], rows, window)
    lane = iota((rows, LANES), 1)
    for j in range(HEADS // 2):
        pair = datt_ref[:, j * LANES : (j + 1) * LANES].astype(f32)
        even, odd = split_heads(pair, j // 2, lane)
        do_ref[2 * j] = even.astype(bf16)
        do_ref[2 * j + 1] = odd.astype(bf16)
    dkv_ref[...] = jnp.zeros(dkv_ref.shape, f32)

    def head(h, unused):
        query, grad = q8_ref[h], do_ref[h]
        total = jnp.sum(jnp.where(lane == h, lse_ref[...], 0.0), axis=1, keepdims=True)
        scores = nt(query, k_ref[...]) * HEAD_DIM**-0.5 + bias_ref[...]
        probs = jnp.exp(scores - total)
        dprobs = nt(grad, v_ref[...])
        mean = jnp.sum(probs * dprobs, axis=1, keepdims=True)
        draw = (probs * (dprobs - mean) * HEAD_DIM**-0.5).astype(bf16)
        dq8_ref[h] = nn(draw, k_ref[...])
        dkv_ref[:, :LANES] += tn(draw, query)
        dkv_ref[:, LANES:] += tn(probs.astype(bf16), grad)
        return unused

    lax.fori_loop(0, HEADS, head, 0)
    for j in range(HEADS // 2):
        pair = join_heads(dq8_ref[2 * j], dq8_ref[2 * j + 1], j // 2, lane)
        back = turned_back(pair, cos_ref[...], sin_ref[...])
        dq_ref[:, j * LANES : (j + 1) * LANES] = back.astype(bf16)


def post_kernel(
    core_ref, tok_ref, cot_ref, att_ref, yl_ref, x_ref, bc_ref, cum_ref, off_ref, entry_ref,
    skip_ref, normed_ref, gssm_ref, gffn_ref,
    gate_own, gate_oth, ao_own, ao_oth, so_own, so_oth, gu_own, gu_oth, down_own, down_oth,
    out_ref, dmid_ref, datt_ref, dssd_ref, ycore_ref, dentry_ref, n2_ref, hid_ref, mixed_ref,
    dbr_ref, dgu_ref, dgate_ref, dng_ref, dgssm_ref, dgffn_ref,
    gi_ref, gd_ref, mid_ref, gu_ref, dn_ref, dmx_ref, fd_ref,
):
    core = core_ref[0]
    rows, width = tok_ref.shape
    ff = hid_ref.shape[1]
    count = gate_own.shape[0]
    ys = range(count)
    reads = bc_ref[:, STATE:].astype(bf16)
    blocks = sides(normed_ref, core, count)
    spread = head_spread()
    fade = nn_full(fade_of(cum_ref[...], off_ref[...]), spread)
    entered = nt(reads, entry_ref[...].astype(bf16))
    square = 0.0
    for j in range(DS // 512):
        cols = slice(j * 512, (j + 1) * 512)
        gate = 0.0
        for y, (own, oth) in enumerate(blocks):
            gate = gate + nn(own, gate_own[y, :, cols]) + nn(oth, gate_oth[y, :, cols])
        gate = gate.astype(bf16).astype(f32)
        gi_ref[:, cols] = gate
        ycore = yl_ref[:, cols] + fade[:, cols] * entered[:, cols]
        ycore_ref[:, cols] = ycore
        ssd = ycore + skip_ref[:, cols] * x_ref[:, cols]
        gated = ssd * gate * sigmoid(gate)
        gd_ref[:, cols] = gated
        square = square + jnp.sum(gated * gated, axis=1, keepdims=True)
    rms_gate = lax.rsqrt(square / DS + EPS)
    mixed_ref[...] = (gd_ref[...] * rms_gate * gssm_ref[...]).astype(bf16)
    att_blocks = sides(att_ref, core, count)
    mix_blocks = sides(mixed_ref, core, count)
    square = 0.0
    for j in range(width // 512):
        cols = slice(j * 512, (j + 1) * 512)
        branch = 0.0
        for y in ys:
            branch = branch + nn(att_blocks[y][0], ao_own[y, :, cols])
            branch = branch + nn(att_blocks[y][1], ao_oth[y, :, cols])
            branch = branch + nn(mix_blocks[y][0], so_own[y, :, cols])
            branch = branch + nn(mix_blocks[y][1], so_oth[y, :, cols])
        middle = tok_ref[:, cols].astype(f32) + branch
        mid_ref[:, cols] = middle
        square = square + jnp.sum(middle * middle, axis=1, keepdims=True)
    rms = lax.rsqrt(square / width + EPS)
    n2_ref[...] = (mid_ref[...] * rms * gffn_ref[...]).astype(bf16)
    blocks = sides(n2_ref, core, count)

    def up(j, unused):
        cols = pl.ds(pl.multiple_of(j * 512, 512), 512)
        total = 0.0
        for y, (own, oth) in enumerate(blocks):
            total = total + nn(own, gu_own[y, :, cols]) + nn(oth, gu_oth[y, :, cols])
        gu_ref[:, cols] = total
        return unused

    lax.fori_loop(0, 2 * ff // 512, up, 0)
    for j in range(ff // 512):
        gate = gu_ref[:, j * 512 : (j + 1) * 512]
        lift = gu_ref[:, ff + j * 512 : ff + (j + 1) * 512]
        hid_ref[:, j * 512 : (j + 1) * 512] = (gate * sigmoid(gate) * lift).astype(bf16)
    blocks = sides(hid_ref, core, count)
    for j in range(width // 512):
        cols = slice(j * 512, (j + 1) * 512)
        total = mid_ref[:, cols]
        for y, (own, oth) in enumerate(blocks):
            total = total + nn(own, down_own[y, :, cols]) + nn(oth, down_oth[y, :, cols])
        out_ref[:, cols] = total.astype(bf16)
    cot = cot_ref[...]
    wide = ff // count // 2
    for y in ys:
        own, oth = nt(cot, down_own[y]), nt(cot, down_oth[y])
        for k in range(2):
            dhid = jnp.where(core == k, own, oth)
            base = (2 * y + k) * wide
            gate = gu_ref[:, base : base + wide]
            lift = gu_ref[:, ff + base : ff + base + wide]
            sg = sigmoid(gate)
            dgate = dhid * lift * (sg * (1.0 + gate * (1.0 - sg)))
            dgu_ref[:, base : base + wide] = dgate.astype(bf16)
            dgu_ref[:, ff + base : ff + base + wide] = (dhid * gate * sg).astype(bf16)
    for y in ys:
        put(dn_ref, y, nt(dgu_ref[...], gu_own[y]), nt(dgu_ref[...], gu_oth[y]), core)
    unit = mid_ref[...] * rms
    dn = dn_ref[...]
    dgffn_ref[...] = jnp.sum(dn * unit, axis=0, keepdims=True)
    dn = dn * gffn_ref[...]
    dmid = cot.astype(f32) + rms * (dn - unit * jnp.mean(dn * unit, axis=1, keepdims=True))
    dmid_ref[...] = dmid
    dbr_ref[...] = dmid.astype(bf16)
    for y in ys:
        put(datt_ref, y, nt(dbr_ref[...], ao_own[y]), nt(dbr_ref[...], ao_oth[y]), core)
        put(dmx_ref, y, nt(dbr_ref[...], so_own[y]), nt(dbr_ref[...], so_oth[y]), core)
    mean = 0.0
    for j in range(DS // 512):
        cols = slice(j * 512, (j + 1) * 512)
        unit = gd_ref[:, cols] * rms_gate
        dmx = dmx_ref[:, cols]
        dgssm_ref[:, cols] = jnp.sum(dmx * unit, axis=0, keepdims=True)
        mean = mean + jnp.sum(dmx * gssm_ref[:, cols] * unit, axis=1, keepdims=True)
    mean = mean / DS
    for j in range(DS // 512):
        cols = slice(j * 512, (j + 1) * 512)
        unit = gd_ref[:, cols] * rms_gate
        dgated = rms_gate * (dmx_ref[:, cols] * gssm_ref[:, cols] - unit * mean)
        gate = gi_ref[:, cols]
        sg = sigmoid(gate)
        ssd = ycore_ref[:, cols] + skip_ref[:, cols] * x_ref[:, cols]
        dssd = dgated * gate * sg
        dssd_ref[:, cols] = dssd
        dgate_ref[:, cols] = (dgated * ssd * (sg * (1.0 + gate * (1.0 - sg)))).astype(bf16)
        fd_ref[:, cols] = (dssd * fade[:, cols]).astype(bf16)
    dentry_ref[...] = tn(fd_ref[...], reads)
    for y in ys:
        put(dng_ref, y, nt(dgate_ref[...], gate_own[y]), nt(dgate_ref[...], gate_oth[y]), core)


def picked(ref, y, count, side):
    width = ref.shape[1] // count
    half = width // 2
    base = y * width
    low, high = ref[:, base : base + half], ref[:, base + half : base + width]
    return jnp.where(side == 0, low, high)


def products_kernel(pairs, side_ref, *refs):
    side = side_ref[0]
    names = max(max(p) for p in pairs) + 1
    ins, outs = refs[:names], refs[names:]
    for (a, g), out in zip(pairs, outs):
        count = out.shape[0]
        for y in range(count):
            left = picked(ins[a], y, count, side)
            for j in range(0, out.shape[2], 512):
                stop = min(j + 512, out.shape[2])
                out[y, :, j:stop] = tn(left, ins[g][:, j:stop]).astype(bf16)


def scan_back_kernel(
    dy_ref, ycore_ref, x_ref, bc_ref, step_ref, cum_ref, cumt_ref, z_ref, off_ref, entry_ref,
    down_ref, skip_ref, dec_ref, chan_ref, cw_ref, cb_ref,
    dext_ref, dz_ref, dcw_ref, dcb_ref, heads_ref,
    xw_ref, ce_ref, dyb_ref, dxw_ref, dg_ref, dact_ref,
):
    rows = x_ref.shape[0]
    spread, gather = head_spread(), head_sum_matrix()
    off, cum = off_ref[...], cum_ref[...]
    step_wide = nn_full(step_ref[...], spread)
    xw_ref[...] = (x_ref[...] * step_wide).astype(bf16)
    dyb_ref[...] = dy_ref[...].astype(bf16)
    ce_ref[...] = nn_full(cum, spread)
    keys, reads = bc_ref[:, :STATE].astype(bf16), bc_ref[:, STATE:].astype(bf16)
    keep = scan_masks(off, rows)
    scores = jnp.where(keep, nt(reads, keys), 0.0)
    lane = iota((rows, LANES), 1)
    dg_ref[...] = jnp.zeros((rows, rows), f32)

    def pair(j, unused):
        cols = pl.ds(pl.multiple_of(j * LANES, LANES), LANES)
        wide = ce_ref[:, cols]
        xw, dy = xw_ref[:, cols], dyb_ref[:, cols]
        outs = []
        for k in range(2):
            late = wide[:, k * SSM_DIM : k * SSM_DIM + 1]
            early = cumt_ref[pl.ds(2 * j + k, 1), :]
            decay = jnp.exp(jnp.minimum(late - early, 0.0))
            outs.append(tn((decay * scores).astype(bf16), dy))
            own = (lane < SSM_DIM) if k == 0 else (lane >= SSM_DIM)
            dm = nt(jnp.where(own, dy.astype(f32), 0.0).astype(bf16), xw)
            dg_ref[...] += dm * decay
        dxw_ref[:, cols] = jnp.where(lane < SSM_DIM, outs[0], outs[1])
        return unused

    lax.fori_loop(0, SSM_HEADS // 2, pair, 0)
    dscores = jnp.where(keep, dg_ref[...], 0.0).astype(bf16)
    down = down_ref[...].astype(bf16)
    tail = nn_full(tail_of(cum, off), spread)
    fade = nn_full(fade_of(cum, off), spread)
    bd = nt(keys, down) * tail
    xw = xw_ref[...].astype(f32)
    dxw = dxw_ref[...] + bd
    dact_ref[:, DS : DS + STATE] = tn(dscores, reads) + nn((tail * xw).astype(bf16), down)
    dact_ref[:, DS + STATE :] = nn(dscores, keys) + nn(
        (fade * dy_ref[...]).astype(bf16), entry_ref[...].astype(bf16)
    )
    through = jnp.sum(nn_full(xw * bd, gather), axis=0, keepdims=True)
    product = nt(jnp.ones((8, STATE), f32), down_ref[...] * entry_ref[...])
    kept = nn_full(product, gather)[:1] * carry_of(cum, off)
    last = (iota((rows, 1), 0) == rows - 1).astype(f32)
    dyb = dyb_ref[...].astype(f32)
    dcum = nn_full(dyb * ycore_ref[...] - xw * dxw, gather) + last * (through + kept)
    tri = (iota((rows, rows), 0) <= iota((rows, rows), 1)).astype(f32)
    dlog = nn_full(tri, dcum)
    x = x_ref[...]
    step, dec = step_ref[...], dec_ref[...]
    dstep = nn_full(dxw * x, gather) - dlog * dec
    dz = dstep * sigmoid(z_ref[...])
    dz_ref[...] = dz
    heads_ref[...] = jnp.zeros(heads_ref.shape, f32)
    heads_ref[0:1, :] = jnp.sum(dlog * (-step * dec), axis=0, keepdims=True)
    heads_ref[1:2, :] = jnp.sum(dz, axis=0, keepdims=True)
    heads_ref[2:3, :] = jnp.sum(nn_full(dy_ref[...] * x, gather), axis=0, keepdims=True)
    dact_ref[:, :DS] = dxw * step_wide + skip_ref[...] * dy_ref[...]
    dcw_ref[...] = jnp.zeros(dcw_ref.shape, f32)
    for j in range(CONV_CH // 256):
        cols = slice(j * 256, (j + 1) * 256)
        taps = conv_taps(chan_ref, cols, off)
        mixed = cb_ref[:, cols]
        for i, tap in enumerate(taps):
            mixed = mixed + tap * cw_ref[i : i + 1, cols]
        sg = sigmoid(mixed)
        dmix = dact_ref[:, cols] * (sg * (1.0 + mixed * (1.0 - sg)))
        dcb_ref[:, cols] = jnp.sum(dmix, axis=0, keepdims=True)
        total = 0.0
        for i, tap in enumerate(taps):
            back = CONV - 1 - i
            dcw_ref[i : i + 1, cols] = jnp.sum(dmix * tap, axis=0, keepdims=True)
            part = dmix * ((off >= back).astype(f32) * cw_ref[i : i + 1, cols])
            part = jnp.concatenate([jnp.zeros((RIM, 256), f32), part], axis=0)
            total = total + (pltpu.roll(part, rows + RIM - back, 0) if back else part)
        dext_ref[:, cols] = total


def back_grads_kernel(count, dq_ref, own_ref, *refs):
    parts, rest = refs[:count], refs[count:]
    dext_ref, ret_ref, dz_ref, cos_ref, sin_ref, ga_ref, gb_ref = rest
    rows = dq_ref.shape[0]
    dkv = own_ref[...]
    for part in parts:
        dkv = dkv + part[...].astype(f32)
    ga_ref[:, :LANES] = turned_back(dkv[:, :LANES], cos_ref[...], sin_ref[...]).astype(bf16)
    ga_ref[:, LANES:256] = dkv[:, LANES:].astype(bf16)
    ga_ref[:, 256:768] = dq_ref[...]
    ga_ref[: rows - RIM, 768:1024] = dext_ref[RIM:rows, DS:].astype(bf16)
    ga_ref[rows - RIM :, 768:1024] = (dext_ref[rows:, DS:] + ret_ref[:, DS:]).astype(bf16)
    ga_ref[:, 1024:] = dz_ref[...].astype(bf16)
    gb_ref[: rows - RIM, :] = dext_ref[RIM:rows, :DS].astype(bf16)
    gb_ref[rows - RIM :, :] = (dext_ref[rows:, :DS] + ret_ref[:, :DS]).astype(bf16)


def back_kernel(
    core_ref, ga_ref, gb_ref, wa_own, wa_oth, wb_own, wb_oth, tok_ref, dmid_ref, dng_ref, gain_ref,
    dtok_ref, dgain_ref, dn_ref,
):
    core = core_ref[0]
    for y in range(wa_own.shape[0]):
        own = nt(ga_ref[...], wa_own[y]) + nt(gb_ref[...], wb_own[y])
        oth = nt(ga_ref[...], wa_oth[y]) + nt(gb_ref[...], wb_oth[y])
        put(dn_ref, y, own, oth, core)
    dn = dn_ref[...] + dng_ref[...]
    tok = tok_ref[...].astype(f32)
    rms = lax.rsqrt(jnp.mean(tok * tok, axis=1, keepdims=True) + EPS)
    unit = tok * rms
    dgain_ref[...] = jnp.sum(dn * unit, axis=0, keepdims=True)
    dn = dn * gain_ref[...]
    dtok_ref[...] = dmid_ref[...] + rms * (dn - unit * jnp.mean(dn * unit, axis=1, keepdims=True))


def run(kernel, name, outs, args, scalars=0, scratch=(), flops=0):
    moved = sum(a.size * a.dtype.itemsize for a in args)
    shapes = [jax.ShapeDtypeStruct(shape, kind) for shape, kind in outs]
    moved += sum(s.size * s.dtype.itemsize for s in shapes)
    specs = [pl.BlockSpec(memory_space=pltpu.SMEM)] * scalars
    specs += [pl.BlockSpec(memory_space=pltpu.VMEM)] * (len(args) - scalars)
    return pl.pallas_call(
        kernel,
        name=name,
        out_shape=shapes,
        in_specs=specs,
        out_specs=[pl.BlockSpec(memory_space=pltpu.VMEM)] * len(shapes),
        scratch_shapes=[pltpu.VMEM(shape, kind) for shape, kind in scratch],
        compiler_params=pltpu.CompilerParams(vmem_limit_bytes=60 * 2**20),
        cost_estimate=pl.CostEstimate(flops=flops, bytes_accessed=moved, transcendentals=0),
    )(*args)


def padded(vector, width):
    return jnp.pad(vector.astype(f32), (0, width - vector.shape[0]))[None, :]


def local(
    tokens, lengths, cotangent, mixer_gain, query_weight, keyval_weight, inner_weight, conv_weight,
    conv_bias, ssm_gain, attn_out_weight, ssm_out_weight, ffn_gain, gate_up_weight, down_weight,
    decay_log, step_bias, skip_gain,
):
    rows, width = tokens.shape
    seq_count, seq_rank = lax.axis_size("seq"), lax.axis_index("seq")
    side = place_on("core").reshape(1)
    back = (rows * seq_count // 2) // rows
    part = query_weight.shape[0]
    heads_width, ff = HEADS * HEAD_DIM, gate_up_weight.shape[1] // 2
    a_rows, s_rows, f_rows = attn_out_weight.shape[0], ssm_out_weight.shape[0], down_weight.shape[0]
    ys = lax.axis_size("dp") // 2

    rim = shifted(tokens[rows - RIM :], 1)
    small = jnp.concatenate(
        [mixer_gain, conv_weight.reshape(-1), conv_bias, ssm_gain, ffn_gain]
    ).astype(f32)
    counts = [mixer_gain.size, conv_weight.size, conv_bias.size, ssm_gain.size, ffn_gain.size]
    slots = -(-small.size // LANES) * LANES
    small = gather_small(jnp.pad(small, (0, slots - small.size)))
    inner_tail = inner_weight[:, DS + CONV_CH :]
    front_a = jnp.concatenate(
        [
            keyval_weight,
            query_weight,
            inner_weight[:, 2 * DS : DS + CONV_CH],
            jnp.pad(inner_tail, ((0, 0), (0, LANES - SSM_HEADS))),
        ],
        1,
    )
    wa_own, wa_oth = gather_pair(front_a, "y")
    wb_own, wb_oth = gather_pair(inner_weight[:, DS : 2 * DS], "x")
    gate_own, gate_oth = gather_pair(inner_weight[:, :DS], "y")
    gu_own, gu_oth = gather_pair(gate_up_weight, "y")
    middle = jnp.concatenate([down_weight, attn_out_weight, ssm_out_weight], 0)
    mids = gather_pair(middle, "x")

    def unpacked(full, start, size):
        full = full.reshape(ys, -1, middle.shape[0], width)[:, :, start : start + size]
        return full.reshape(ys, -1, width)

    down_own, down_oth = (unpacked(m, 0, f_rows) for m in mids)
    ao_own, ao_oth = (unpacked(m, f_rows, a_rows) for m in mids)
    so_own, so_oth = (unpacked(m, f_rows + a_rows, s_rows) for m in mids)

    starts = [sum(counts[:i]) for i in range(len(counts))]
    gain_one, w_conv, b_conv, gain_ssm, gain_two = (
        small[:, s : s + c].reshape(-1) for s, c in zip(starts, counts)
    )
    w_conv = jnp.pad(w_conv.reshape(CONV_CH, CONV).T, ((0, 8 - CONV), (0, 0)))
    gain_one, b_conv, gain_ssm, gain_two = (
        v[None, :] for v in (gain_one, b_conv, gain_ssm, gain_two)
    )
    places = seq_rank * rows + jnp.arange(rows)
    begin = jnp.zeros_like(places)
    end = jnp.int32(0)
    for i in range(lengths.shape[1]):
        end = end + lengths[0, i]
        begin = jnp.where(end <= places, end, begin)
    offset = (places - begin).astype(jnp.int32)
    half = HEAD_DIM // 2
    freq = BASE ** (-jnp.arange(half).astype(f32) / half)
    angle = offset.astype(f32)[:, None] * freq[None, :]
    cos = jnp.tile(jnp.cos(angle), (1, 4))
    sin = jnp.sin(angle)
    sin = jnp.tile(jnp.concatenate([-sin, sin], 1), (1, 2))
    off = offset[:, None]
    step_bias_row, decay_row = padded(step_bias, LANES), padded(jnp.exp(decay_log), LANES)
    skip = jnp.repeat(skip_gain, SSM_DIM)[None, :]

    (q8, kv, normed, chan, x, bc, step, cum, cumt, z, state, carry) = run(
        front_kernel,
        "front",
        [
            ((HEADS, rows, LANES), bf16),
            ((rows, 256), bf16),
            ((rows, width), bf16),
            ((rows + RIM, CONV_CH), bf16),
            ((rows, DS), f32),
            ((rows, 2 * STATE), f32),
            ((rows, LANES), f32),
            ((rows, LANES), f32),
            ((LANES, rows), f32),
            ((rows, LANES), f32),
            ((DS, STATE), f32),
            ((1, LANES), f32),
        ],
        (
            side, jnp.concatenate([rim, tokens], 0), gain_one, wa_own, wa_oth, wb_own, wb_oth,
            cos, sin, off, w_conv, b_conv, step_bias_row, decay_row,
        ),
        scalars=1,
        scratch=[((rows + RIM, width), bf16), ((rows, DS), bf16)],
        flops=2 * rows * width * (A_COLS + DS),
    )
    pieces = [shifted(kv, back - i) for i in range(back)] + [kv]
    entry = carried(state, carry, back, 1)
    window = (back + 1) * rows
    y_local = run(
        scan_kernel, "scan", [((rows, DS), f32)], (x, bc, step, cum, cumt, off),
        scratch=[((rows, DS), bf16), ((rows, DS), f32)], flops=2 * SSM_HEADS * rows * rows * 128,
    )[0]
    attended, lse = run(
        functools.partial(attend_kernel, back + 1),
        "attend",
        [((rows, heads_width), bf16), ((rows, LANES), f32)],
        (q8, *pieces, off),
        scratch=[
            ((window, LANES), bf16),
            ((window, LANES), bf16),
            ((rows, window), f32),
            ((HEADS, rows, LANES), f32),
        ],
        flops=4 * HEADS * rows * window * LANES,
    )
    (
        output, dmid, datt, dssd, ycore, dentry, n2, hidden, mixed, dbr, dgu, dgate, dng,
        g_ssm, g_ffn,
    ) = run(
        post_kernel,
        "post",
        [
            ((rows, width), bf16),
            ((rows, width), f32),
            ((rows, heads_width), bf16),
            ((rows, DS), f32),
            ((rows, DS), f32),
            ((DS, STATE), f32),
            ((rows, width), bf16),
            ((rows, ff), bf16),
            ((rows, DS), bf16),
            ((rows, width), bf16),
            ((rows, 2 * ff), bf16),
            ((rows, DS), bf16),
            ((rows, width), f32),
            ((1, DS), f32),
            ((1, width), f32),
        ],
        (
            side, tokens, cotangent, attended, y_local, x, bc, cum, off, entry, skip, normed,
            gain_ssm, gain_two, gate_own, gate_oth, ao_own, ao_oth, so_own, so_oth, gu_own, gu_oth,
            down_own, down_oth,
        ),
        scalars=1,
        scratch=[
            ((rows, DS), f32),
            ((rows, DS), f32),
            ((rows, width), f32),
            ((rows, 2 * ff), f32),
            ((rows, width), f32),
            ((rows, DS), f32),
            ((rows, DS), bf16),
        ],
        flops=4 * rows * width * (3 * ff + DS + DS + heads_width),
    )

    def weight_grads(which):
        pairs = [(0, 1), (2, 3), (4, 5), (6, 5), (7, 8)]
        made = run(
            functools.partial(products_kernel, pairs),
            "weights",
            [
                ((ys, width // 2 // ys, 2 * ff), bf16),
                ((ys, ff // 2 // ys, width), bf16),
                ((ys, heads_width // 2 // ys, width), bf16),
                ((ys, DS // 2 // ys, width), bf16),
                ((ys, width // 2 // ys, DS), bf16),
            ],
            (which, n2, dgu, hidden, cotangent, attended, dbr, mixed, normed, dgate),
            scalars=1,
            flops=rows * width * (3 * ff + DS + DS + heads_width),
        )
        packed = jnp.concatenate(
            [
                m.reshape(ys, -1, r, width)
                for m, r in zip(made[1:4], (f_rows, a_rows, s_rows))
            ],
            2,
        )
        return made[0], packed, made[4]

    core_unit = extents()["core"][0]
    downstream = carried(dentry, carry, back, -1)
    others = weight_grads(1 - side)
    got = [swap(a, core_unit) for a in others]
    owns = weight_grads(side)
    r_gu = reduce_pair(owns[0], got[0], part, "x")
    r_mid = reduce_pair(owns[1], got[1], middle.shape[0], "y")
    r_gate = reduce_pair(owns[2], got[2], part, "x")
    dq, dkv = run(
        functools.partial(attend_back_kernel, back + 1),
        "attend_back",
        [((rows, heads_width), bf16), ((window, 256), f32)],
        (q8, *pieces, off, lse, datt, cos, sin),
        scratch=[
            ((window, LANES), bf16),
            ((window, LANES), bf16),
            ((rows, window), f32),
            ((HEADS, rows, LANES), bf16),
            ((HEADS, rows, LANES), f32),
        ],
        flops=10 * HEADS * rows * window * LANES,
    )
    dkv = dkv.reshape(back + 1, rows, 256)
    returned_kv = [shifted(dkv[i].astype(bf16), i - back) for i in range(back)]
    dext, dz, g_conv, g_conv_bias, heads = run(
        scan_back_kernel,
        "scan_back",
        [
            ((rows + RIM, CONV_CH), f32),
            ((rows, LANES), f32),
            ((8, CONV_CH), f32),
            ((1, CONV_CH), f32),
            ((8, LANES), f32),
        ],
        (
            dssd, ycore, x, bc, step, cum, cumt, z, off, entry, downstream, skip, decay_row, chan,
            w_conv, b_conv,
        ),
        scratch=[
            ((rows, DS), bf16),
            ((rows, DS), f32),
            ((rows, DS), bf16),
            ((rows, DS), f32),
            ((rows, rows), f32),
            ((rows, CONV_CH), f32),
        ],
        flops=4 * SSM_HEADS * rows * rows * 128,
    )
    ret = shifted(dext[:RIM], -1)
    ga, gb = run(
        functools.partial(back_grads_kernel, back),
        "back_grads",
        [((rows, A_COLS), bf16), ((rows, DS), bf16)],
        (dq, dkv[back], *returned_kv, dext, ret, dz, cos, sin),
    )

    def front_grads(which):
        return run(
            functools.partial(products_kernel, [(0, 1), (0, 2)]),
            "front_weights",
            [((ys, width // 2 // ys, A_COLS), bf16), ((ys, width // 2 // ys, DS), bf16)],
            (which, normed, ga, gb),
            scalars=1,
            flops=rows * width * (A_COLS + DS),
        )

    others = front_grads(1 - side)
    got = [swap(a, core_unit) for a in others]
    owns = front_grads(side)
    r_a = reduce_pair(owns[0], got[0], part, "x")
    r_b = reduce_pair(owns[1], got[1], part, "y")
    grad_tokens, g_mixer = run(
        back_kernel,
        "back",
        [((rows, width), f32), ((1, width), f32)],
        (side, ga, gb, wa_own, wa_oth, wb_own, wb_oth, tokens, dmid, dng, gain_one),
        scalars=1,
        scratch=[((rows, width), f32)],
        flops=2 * rows * width * (A_COLS + DS),
    )
    vector = jnp.concatenate(
        [
            g_mixer.reshape(-1), g_conv[:CONV].T.reshape(-1), g_conv_bias.reshape(-1),
            g_ssm.reshape(-1), g_ffn.reshape(-1), heads[:3].reshape(-1),
        ]
    )
    vector = sum_small(vector.reshape(-1, LANES)).reshape(-1)
    me = my_index()
    small_out = []
    start = 0
    count = lax.axis_size("dp") * lax.axis_size("seq")
    for size in counts:
        small_out.append(lax.dynamic_slice_in_dim(vector, start + me * size, size, 0))
        start += count * size
    heads = vector[start:].reshape(3, LANES)[:, :SSM_HEADS]
    g_inner = jnp.concatenate([r_gate, r_b, r_a[:, 768 : 1024 + SSM_HEADS]], 1)
    return (
        output,
        grad_tokens,
        small_out[0],
        r_a[:, 256:768],
        r_a[:, :256],
        g_inner,
        small_out[1].reshape(-1, CONV),
        small_out[2],
        small_out[3],
        r_mid[f_rows : f_rows + a_rows],
        r_mid[f_rows + a_rows :],
        small_out[4],
        r_gu,
        r_mid[:f_rows],
        heads[0],
        heads[1],
        heads[2],
    )


def solution(mesh):
    lead, flat, rep = P(AXES, None), P(AXES), P()
    return jax.shard_map(
        local,
        mesh=mesh,
        in_specs=(
            lead, P("dp", None), lead, flat, lead, lead, lead, lead, flat, flat, lead, lead, flat,
            lead, lead, rep, rep, rep,
        ),
        out_specs=(
            lead, lead, flat, lead, lead, lead, lead, flat, flat, lead, lead, flat, lead, lead,
            rep, rep, rep,
        ),
        check_vma=False,
    )
```

```python
import functools

import jax
import jax.numpy as jnp
from jax import lax
from jax.experimental import pallas as pl
from jax.experimental.pallas import tpu as pltpu
from jax.sharding import PartitionSpec as P

HEADS = 8
KV_HEADS = 2
HEAD_DIM = 64
SSM_HEADS = 24
SSM_DIM = 64
STATE = 128
CONV = 4
DS = 1536
CONV_CH = 1792
RIM = 16
LANES = 128
A_COLS = 2 * KV_HEADS * HEAD_DIM + HEADS * HEAD_DIM + 2 * STATE + LANES
EPS = 1e-6
BASE = 10000.0
NEG = -1e30
AXES = ("y", "core", "z", "x")
SEQ = AXES[2:]

f32 = jnp.float32
bf16 = jnp.bfloat16


def nn(a, b):
    return lax.dot_general(a, b, (((1,), (0,)), ((), ())), preferred_element_type=f32)


def tn(a, b):
    return lax.dot_general(a, b, (((0,), (0,)), ((), ())), preferred_element_type=f32)


def nt(a, b):
    return lax.dot_general(a, b, (((1,), (1,)), ((), ())), preferred_element_type=f32)


def terms(value, count):
    parts = []
    for unused in range(count):
        parts.append(value.astype(bf16))
        value = value - parts[-1].astype(f32)
    return parts


def nn_left(value, ones, count):
    return sum(nn(part, ones) for part in terms(value, count))


def nn_right(ones, value, count):
    return sum(nn(ones, part) for part in terms(value, count))


def iota(shape, dim):
    return lax.broadcasted_iota(jnp.int32, shape, dim)


def head_spread():
    row = iota((LANES, DS), 0)
    return (iota((LANES, DS), 1) // SSM_DIM == row).astype(f32).astype(bf16)


def head_sum_matrix():
    col = iota((DS, LANES), 1)
    return (iota((DS, LANES), 0) // SSM_DIM == col).astype(f32).astype(bf16)


def extents():
    along = lax.axis_size(SEQ)
    return {
        "x": (1, 2),
        "z": (2, along // 2),
        "core": (along, 2),
        "y": (2 * along, lax.axis_size("y")),
    }


def my_index():
    return lax.axis_index(AXES)


def place_on(group):
    unit, size = extents()[group]
    return (my_index() // unit) % size


def swap(array, mask):
    count = lax.axis_size(AXES)
    return lax.ppermute(array, AXES, [(i, i ^ mask) for i in range(count)])


def in_order(pieces, place):
    pieces = list(pieces)
    bit = 1
    while bit < len(pieces):
        flag = (place // bit) % 2 == 1
        pieces = [jnp.where(flag, pieces[j ^ bit], pieces[j]) for j in range(len(pieces))]
        bit *= 2
    return pieces


def collect(array, group, axis):
    unit, size = extents()[group]
    pieces = [array] + [swap(array, k * unit) for k in range(1, size)]
    return jnp.stack(in_order(pieces, place_on(group)), axis)


def gather_pair(full, first):
    if first == "y":
        full = collect(collect(full, "y", 0), "x", 2)
    else:
        full = collect(collect(full, "x", 1), "y", 0)
    other = swap(full, extents()["core"][0])
    shape = (full.shape[0], full.shape[1] * full.shape[2] * full.shape[3], full.shape[4])
    return full.reshape(shape), other.reshape(shape)


def cut(total, group, axis):
    size = extents()[group][1]
    place = place_on(group)
    keep = lax.dynamic_index_in_dim(total, place, axis, False)
    parts = [lax.dynamic_index_in_dim(total, place ^ k, axis, False) for k in range(1, size)]
    return keep, [p.astype(bf16) for p in parts]


def crossed(parts, group):
    unit = extents()[group][0]
    return [swap(part, (k + 1) * unit) for k, part in enumerate(parts)]


def joined(keep, received):
    total = keep.astype(f32)
    for part in received:
        total = total + part.astype(f32)
    return total


class Reduction:
    def __init__(self, total, rows, first):
        table = extents()
        self.total = total.reshape(
            table["y"][1], table["z"][1], table["x"][1], rows, total.shape[-1]
        )
        order = [("x", 2), ("y", 0)] if first == "x" else [("y", 0), ("x", 1)]
        self.stages = order + [("z", 0)]

    def send(self):
        (group, axis), self.stages = self.stages[0], self.stages[1:]
        self.keep, self.parts = cut(self.total, group, axis)
        self.received = crossed(self.parts, group)
        return self.parts

    def receive(self, *others):
        self.received = after(self.received, *others)
        self.total = joined(self.keep, self.received)
        return self.total


def after(value, *others):
    return lax.optimization_barrier((value, others))[0]


def gather_small(vector):
    full = collect(collect(collect(vector, "z", 0), "x", 1), "core", 0)
    return collect(full, "y", 0).reshape(-1, vector.shape[-1])


def dealt(array, axes):
    return lax.all_to_all(array, axes, 0, 0, tiled=True)


def shared(array, axes):
    return dealt(jnp.broadcast_to(array[None], (lax.axis_size(axes), *array.shape)), axes)


def shifted(array, by):
    count = lax.axis_size(SEQ)
    pairs = [(i, i + by) for i in range(count) if 0 <= i + by < count]
    return lax.ppermute(array, SEQ, pairs)


def link(earlier, later):
    carry = later[1]
    wide = jnp.repeat(carry[0, :SSM_HEADS], SSM_DIM)[:, None]
    return (later[0] + wide * earlier[0], carry * earlier[1])


class Carrying:
    def __init__(self, state, carry, back, sign):
        self.pair, self.back, self.sign, self.by = (state, carry), back, sign, 0

    def send(self):
        packed = jnp.concatenate(
            [self.pair[0], jnp.pad(self.pair[1], ((0, RIM - 1), (0, 0)))], 0
        ).astype(bf16)
        steps = [self.by] if self.by else [1] + [2] * (self.back > 1)
        self.got = [shifted(packed, self.sign * by) for by in steps]
        return packed

    def receive(self, *others):
        pairs = []
        for got in after(self.got, *others):
            got = got.astype(f32)
            pairs.append((got[:DS], got[DS : DS + 1]))
        self.by = 2 * self.by if self.by else min(self.back, 2)
        if len(pairs) == 2:
            self.pair = link(pairs[1], pairs[0])
        else:
            self.pair = link(pairs[0], self.pair) if self.by > 2 else pairs[0]
        return self.pair[0] if self.by >= self.back else None


def halves(block, core):
    width = block.shape[1] // 2
    low, high = block[:, :width], block[:, width:]
    return jnp.where(core == 0, low, high), jnp.where(core == 0, high, low)


def put(ref, y, own, other, core):
    width = own.shape[1]
    base = y * 2 * width
    ref[:, base : base + width] = jnp.where(core == 0, own, other).astype(ref.dtype)
    ref[:, base + width : base + 2 * width] = jnp.where(core == 0, other, own).astype(ref.dtype)


def sides(ref, core, count):
    width = ref.shape[-1] // count
    return [halves(ref[:, y * width : (y + 1) * width], core) for y in range(count)]


def cross_half(value):
    lane = iota(value.shape, 1) % HEAD_DIM
    up = pltpu.roll(value, LANES - HEAD_DIM // 2, 1)
    down = pltpu.roll(value, HEAD_DIM // 2, 1)
    return jnp.where(lane < HEAD_DIM // 2, up, down)


def turned(value, cos, sin):
    return value * cos + cross_half(value) * sin


def turned_back(value, cos, sin):
    return value * cos - cross_half(value) * sin


def split_heads(pair, which, lane):
    flipped = pltpu.roll(pair, HEAD_DIM, 1)
    if which == 0:
        return jnp.where(lane < HEAD_DIM, pair, 0.0), jnp.where(lane < HEAD_DIM, flipped, 0.0)
    return jnp.where(lane >= HEAD_DIM, flipped, 0.0), jnp.where(lane >= HEAD_DIM, pair, 0.0)


def join_heads(even, odd, which, lane):
    if which == 0:
        return jnp.where(lane < HEAD_DIM, even, pltpu.roll(odd, HEAD_DIM, 1))
    return jnp.where(lane < HEAD_DIM, pltpu.roll(even, HEAD_DIM, 1), odd)


def conv_taps(chan_ref, cols, off):
    ext = chan_ref[:, cols].astype(f32)
    taps = []
    for i in range(CONV):
        back = CONV - 1 - i
        rows = pltpu.roll(ext, back, 0)[RIM:] if back else ext[RIM:]
        taps.append(rows * (off >= back).astype(f32))
    return taps


def sigmoid(v):
    return 1.0 / (1.0 + jnp.exp(-v))


def softplus(v):
    return jnp.maximum(v, 0.0) + jnp.log1p(jnp.exp(-jnp.abs(v)))


def tail_of(cum, off):
    rows = cum.shape[0]
    last_off = off[rows - 1 :, :]
    keep = iota((rows, 1), 0) >= rows - 1 - last_off
    return jnp.exp(cum[rows - 1 :, :] - cum) * keep.astype(f32)


def fade_of(cum, off):
    keep = off > iota((cum.shape[0], 1), 0)
    return jnp.exp(cum) * keep.astype(f32)


def carry_of(cum, off):
    rows = cum.shape[0]
    return jnp.exp(cum[rows - 1 :, :]) * (off[rows - 1 :, :] >= rows).astype(f32)


def front_kernel(
    core_ref, tok_ref, gain_ref, wa_own, wa_oth, wb_own, wb_oth, cos_ref, sin_ref, off_ref,
    cw_ref, cb_ref, sb_ref, dec_ref,
    q8_ref, kv_ref, normed_ref, nrim_ref, chan_ref, x_ref, bc_ref, step_ref, cum_ref, cumt_ref, z_ref,
    state_ref, carry_ref,
    n_ref, xt_ref,
):
    core = core_ref[0]
    rows = cos_ref.shape[0]
    tok = tok_ref[...].astype(f32)
    rms = lax.rsqrt(jnp.mean(tok * tok, axis=1, keepdims=True) + EPS)
    n_ref[...] = (tok * rms * gain_ref[...]).astype(bf16)
    normed_ref[...] = n_ref[RIM:, :]
    nrim_ref[...] = n_ref[:RIM, :]
    count = wa_own.shape[0]
    blocks = sides(n_ref, core, count)

    def project(own_ref, oth_ref, cols):
        total = 0.0
        for y, (own, oth) in enumerate(blocks):
            total = total + nn(own, own_ref[y, :, cols]) + nn(oth, oth_ref[y, :, cols])
        return total

    lane = iota((rows, LANES), 1)
    cos, sin, off = cos_ref[...], sin_ref[...], off_ref[...]
    kv = project(wa_own, wa_oth, pl.ds(0, 256))[RIM:]
    kv_ref[:, :LANES] = turned(kv[:, :LANES], cos, sin).astype(bf16)
    kv_ref[:, LANES:] = kv[:, LANES:].astype(bf16)
    queries = project(wa_own, wa_oth, pl.ds(256, 512))[RIM:]
    for j in range(HEADS // 2):
        pair = turned(queries[:, j * LANES : (j + 1) * LANES], cos, sin)
        even, odd = split_heads(pair, j // 2, lane)
        q8_ref[2 * j] = even.astype(bf16)
        q8_ref[2 * j + 1] = odd.astype(bf16)
    rest = project(wa_own, wa_oth, pl.ds(768, 384))
    chan_ref[:, DS:] = rest[:, : 2 * STATE].astype(bf16)
    z = rest[RIM:, 2 * STATE :].astype(bf16).astype(f32) + sb_ref[...]
    for j in range(DS // 512):
        cols = slice(j * 512, (j + 1) * 512)
        chan_ref[:, cols] = project(wb_own, wb_oth, pl.ds(j * 512, 512)).astype(bf16)
    z_ref[...] = z
    step = softplus(z)
    step_ref[...] = step
    tri = (iota((rows, rows), 0) >= iota((rows, rows), 1)).astype(f32).astype(bf16)
    cum = nn_right(tri, -step * dec_ref[...], 3)
    cum_ref[...] = cum
    cumt_ref[...] = cum.T
    carry_ref[...] = carry_of(cum, off)
    weight = nn_left(step * tail_of(cum, off), head_spread(), 2)
    for j in range(CONV_CH // 256):
        cols = slice(j * 256, (j + 1) * 256)
        mixed = cb_ref[:, cols]
        for i, tap in enumerate(conv_taps(chan_ref, cols, off)):
            mixed = mixed + tap * cw_ref[i : i + 1, cols]
        active = mixed * sigmoid(mixed)
        if j < DS // 256:
            x_ref[:, cols] = active
            xt_ref[:, cols] = (active * weight[:, cols]).astype(bf16)
        else:
            bc_ref[...] = active
    state_ref[...] = tn(xt_ref[...], bc_ref[:, :STATE].astype(bf16))


def scan_masks(off, rows):
    t, s = iota((rows, rows), 0), iota((rows, rows), 1)
    return (s <= t) & (s >= t - off)


def scan_kernel(x_ref, bc_ref, step_ref, cum_ref, cumt_ref, off_ref, y_ref, xw_ref, ce_ref):
    rows = x_ref.shape[0]
    spread = head_spread()
    xw_ref[...] = (x_ref[...] * nn_left(step_ref[...], spread, 2)).astype(bf16)
    ce_ref[...] = nn_left(cum_ref[...], spread, 3)
    keys, reads = bc_ref[:, :STATE].astype(bf16), bc_ref[:, STATE:].astype(bf16)
    scores = jnp.where(scan_masks(off_ref[...], rows), nt(reads, keys), 0.0)
    lane = iota((rows, LANES), 1)

    def pair(j, unused):
        cols = pl.ds(pl.multiple_of(j * LANES, LANES), LANES)
        wide = ce_ref[:, cols]
        xw = xw_ref[:, cols]
        outs = []
        for k in range(2):
            late = wide[:, k * SSM_DIM : k * SSM_DIM + 1]
            early = cumt_ref[pl.ds(2 * j + k, 1), :]
            decay = jnp.exp(jnp.minimum(late - early, 0.0))
            outs.append(nn((decay * scores).astype(bf16), xw))
        y_ref[:, cols] = jnp.where(lane < SSM_DIM, outs[0], outs[1])
        return unused

    lax.fori_loop(0, SSM_HEADS // 2, pair, 0)


def attend_bias(off, rows, window):
    query = iota((rows, window), 0) + (window - rows)
    key = iota((rows, window), 1)
    return jnp.where((key <= query) & (key >= query - off), 0.0, NEG)


def window_of(count, rank, kv_ref, k_ref, v_ref):
    rows = kv_ref.shape[1]
    for i in range(count):
        piece = jnp.maximum(rank - (count - 1 - i), 0)
        k_ref[i * rows : (i + 1) * rows, :] = kv_ref[piece, :, :LANES]
        v_ref[i * rows : (i + 1) * rows, :] = kv_ref[piece, :, LANES:]


def attend_kernel(
    count, rank_ref, q8_ref, kv_ref, off_ref, att_ref, lse_ref, k_ref, v_ref, bias_ref, o_ref
):
    rows = off_ref.shape[0]
    window = count * rows
    window_of(count, rank_ref[0], kv_ref, k_ref, v_ref)
    bias_ref[...] = attend_bias(off_ref[...], rows, window)
    lane = iota((rows, LANES), 1)

    def head(h, lses):
        scores = nt(q8_ref[h], k_ref[...]) * HEAD_DIM**-0.5 + bias_ref[...]
        top = jnp.max(scores, axis=1, keepdims=True)
        probs = jnp.exp(scores - top)
        total = jnp.sum(probs, axis=1, keepdims=True)
        o_ref[h] = nn((probs * (1.0 / total)).astype(bf16), v_ref[...])
        return jnp.where(lane == h, top + jnp.log(total), lses)

    lse_ref[...] = lax.fori_loop(0, HEADS, head, jnp.zeros((rows, LANES), f32)).T
    for j in range(HEADS // 2):
        pair = join_heads(o_ref[2 * j], o_ref[2 * j + 1], j // 2, lane)
        att_ref[:, j * LANES : (j + 1) * LANES] = pair.astype(bf16)


def attend_back_kernel(
    count, rank_ref, q8_ref, kv_ref, off_ref, lse_ref, datt_ref, cos_ref, sin_ref,
    dq_ref, out_ref, k_ref, v_ref, bias_ref, do_ref, dq8_ref, dkv_ref,
):
    rows = off_ref.shape[1]
    window = count * rows
    rank = rank_ref[0]
    window_of(count, rank, kv_ref, k_ref, v_ref)
    query = iota((window, rows), 1) + (window - rows)
    key = iota((window, rows), 0)
    bias_ref[...] = jnp.where((key <= query) & (key >= query - off_ref[...]), 0.0, NEG)
    lane = iota((rows, LANES), 1)
    for j in range(HEADS // 2):
        pair = datt_ref[:, j * LANES : (j + 1) * LANES].astype(f32)
        even, odd = split_heads(pair, j // 2, lane)
        do_ref[2 * j] = even.astype(bf16)
        do_ref[2 * j + 1] = odd.astype(bf16)
    dkv_ref[...] = jnp.zeros(dkv_ref.shape, f32)

    def head(h, unused):
        query, grad = q8_ref[h], do_ref[h]
        scores = nt(k_ref[...], query) * HEAD_DIM**-0.5 + bias_ref[...]
        probs = jnp.exp(scores - lse_ref[pl.ds(h, 1), :])
        dprobs = nt(v_ref[...], grad)
        mean = jnp.sum(probs * dprobs, axis=0, keepdims=True)
        draw = (probs * (dprobs - mean) * HEAD_DIM**-0.5).astype(bf16)
        dkv_ref[:, :LANES] += nn(draw, query)
        dkv_ref[:, LANES:] += nn(probs.astype(bf16), grad)
        dq8_ref[h] = tn(draw, k_ref[...])
        return unused

    lax.fori_loop(0, HEADS, head, 0)
    out_ref[...] = jnp.zeros(out_ref.shape, bf16)
    for i in range(count):
        piece = rank - (count - 1 - i)

        @pl.when(piece >= 0)
        def unused():
            out_ref[piece] = dkv_ref[i * rows : (i + 1) * rows, :].astype(bf16)

    for j in range(HEADS // 2):
        pair = join_heads(dq8_ref[2 * j], dq8_ref[2 * j + 1], j // 2, lane)
        back = turned_back(pair, cos_ref[...], sin_ref[...])
        dq_ref[:, j * LANES : (j + 1) * LANES] = back.astype(bf16)


class PackedWeights:
    def __init__(self, sources, held, sems, parts):
        self.held = held
        part, a_part, s_part, f_part = self.parts = parts
        self.so_at = 2 * part
        self.gu_at = self.so_at + s_part
        self.down_at = self.gu_at + 4 * part
        ends = [0, self.so_at, self.gu_at, self.down_at + f_part]
        self.copies = []
        for k in range(3):
            rows = pl.ds(ends[k], ends[k + 1] - ends[k])
            self.copies.append(
                [
                    pltpu.make_async_copy(
                        sources[i].at[:, :, rows], held.at[i, :, :, rows], sems.at[k, i]
                    )
                    for i in range(2)
                ]
            )
        for pair in self.copies:
            for copy in pair:
                copy.start()

    def wait(self, k):
        for copy in self.copies[k]:
            copy.wait()

    def block(self, i, y, start, size, cols):
        got = self.held[i, y, :, start : start + size, cols]
        return got.reshape(got.shape[0] * size, got.shape[2])

    def gate(self, i, y, j):
        part = self.parts[0]
        return self.block(i, y, j // 2 * part, part, slice(j % 2 * 512, j % 2 * 512 + 512))

    def ao(self, i, y, j):
        part, a_part = self.parts[:2]
        return self.block(i, y, part + j * a_part, a_part, slice(512, 1024))

    def so(self, i, y, j):
        return self.block(i, y, self.so_at, self.parts[2], slice(j * 512, j * 512 + 512))

    def down(self, i, y, j):
        return self.block(i, y, self.down_at, self.parts[3], slice(j * 512, j * 512 + 512))

    def gu(self, i, y, j):
        part = self.parts[0]
        start = pl.multiple_of(self.gu_at + j // 2 * part, 16)
        cols = pl.multiple_of(j % 2 * 512, 512)
        got = self.held[i, y, :, pl.ds(start, part), pl.ds(cols, 512)]
        return got.reshape(got.shape[0] * part, 512)


class PlainWeights:
    def __init__(self, refs):
        self.refs = refs

    def wait(self, k):
        pass

    def block(self, name, i, y, j):
        return self.refs[2 * name + i][y, :, j * 512 : j * 512 + 512]

    def gate(self, i, y, j):
        return self.block(0, i, y, j)

    def ao(self, i, y, j):
        return self.block(1, i, y, j)

    def so(self, i, y, j):
        return self.block(2, i, y, j)

    def down(self, i, y, j):
        return self.block(3, i, y, j)

    def gu(self, i, y, j):
        return self.refs[8 + i][y, :, pl.ds(pl.multiple_of(j * 512, 512), 512)]


def post_kernel(
    parts, ys, core_ref, tok_ref, cot_ref, att_ref, yl_ref, x_ref, bc_ref, cum_ref, off_ref,
    entry_ref, skip_ref, normed_ref, gssm_ref, gffn_ref, *refs,
):
    if parts:
        weights = PackedWeights(refs[:2], refs[-2], refs[-1], parts)
        refs = refs[2:-2]
    else:
        weights, refs = PlainWeights(refs[:10]), refs[10:]
    pairs = [(i, y) for y in range(ys) for i in range(2)]

    def through(ref, weight, j):
        blocks = sides(ref, core, ys)
        return sum(nn(blocks[y][i], weight(i, y, j)) for i, y in pairs)

    def back_through(ref, grad, weight, count):
        for y in range(ys):
            both = []
            for i in range(2):
                both.append(
                    sum(nt(grad[:, j * 512 : j * 512 + 512], weight(i, y, j)) for j in range(count))
                )
            put(ref, y, both[0], both[1], core)

    (
        out_ref, dmid_ref, datt_ref, dssd_ref, ycore_ref, dentry_ref, send_ref, keep_ref, dng_ref,
        gi_ref, gd_ref, mid_ref, gu_ref, dn_ref, dmx_ref, fd_ref, n2_ref, hid_ref, mixed_ref, dh_ref,
    ) = refs
    core = core_ref[0]
    rows, width = tok_ref.shape
    heads_width = att_ref.shape[1]
    ff = hid_ref.shape[1]
    half = keep_ref.shape[1]
    cot_at, dbr_at, dgate_at, sel_at = 2 * ff, 2 * ff + width, 2 * ff + 2 * width, 2 * ff + 2 * width + DS
    reads = bc_ref[:, STATE:].astype(bf16)
    spread = head_spread()
    fade = nn_left(fade_of(cum_ref[...], off_ref[...]), spread, 2)
    entered = nt(reads, entry_ref[...].astype(bf16))
    square = 0.0
    weights.wait(0)
    for j in range(DS // 512):
        cols = slice(j * 512, (j + 1) * 512)
        gate = through(normed_ref, weights.gate, j).astype(bf16).astype(f32)
        gi_ref[:, cols] = gate
        ycore = yl_ref[:, cols] + fade[:, cols] * entered[:, cols]
        ycore_ref[:, cols] = ycore
        ssd = ycore + skip_ref[:, cols] * x_ref[:, cols]
        gated = ssd * gate * sigmoid(gate)
        gd_ref[:, cols] = gated
        square = square + jnp.sum(gated * gated, axis=1, keepdims=True)
    rms_gate = lax.rsqrt(square / DS + EPS)
    mixed_ref[...] = (gd_ref[...] * rms_gate * gssm_ref[...]).astype(bf16)
    square = 0.0
    weights.wait(1)
    for j in range(width // 512):
        cols = slice(j * 512, (j + 1) * 512)
        branch = through(att_ref, weights.ao, j) + through(mixed_ref, weights.so, j)
        middle = tok_ref[:, cols].astype(f32) + branch
        mid_ref[:, cols] = middle
        square = square + jnp.sum(middle * middle, axis=1, keepdims=True)
    rms = lax.rsqrt(square / width + EPS)
    n2_ref[...] = (mid_ref[...] * rms * gffn_ref[...]).astype(bf16)
    weights.wait(2)
    blocks = sides(n2_ref, core, ys)

    def up(j, unused):
        cols = pl.ds(pl.multiple_of(j * 512, 512), 512)
        gu_ref[:, cols] = sum(nn(blocks[y][i], weights.gu(i, y, j)) for i, y in pairs)
        return unused

    lax.fori_loop(0, 2 * ff // 512, up, 0)
    for j in range(ff // 512):
        gate = gu_ref[:, j * 512 : (j + 1) * 512]
        lift = gu_ref[:, ff + j * 512 : ff + (j + 1) * 512]
        hid_ref[:, j * 512 : (j + 1) * 512] = (gate * sigmoid(gate) * lift).astype(bf16)
    for j in range(width // 512):
        cols = slice(j * 512, (j + 1) * 512)
        out_ref[:, cols] = (mid_ref[:, cols] + through(hid_ref, weights.down, j)).astype(bf16)
    cot = cot_ref[...]
    back_through(dh_ref, cot, weights.down, 2)
    for j in range(ff // 512):
        cols = slice(j * 512, (j + 1) * 512)
        gate = gu_ref[:, cols]
        lift = gu_ref[:, ff + j * 512 : ff + (j + 1) * 512]
        sg = sigmoid(gate)
        dhid = dh_ref[:, cols]
        dgate = dhid * lift * (sg * (1.0 + gate * (1.0 - sg)))
        send_ref[:, cols] = dgate.astype(bf16)
        send_ref[:, ff + j * 512 : ff + (j + 1) * 512] = (dhid * gate * sg).astype(bf16)
    send_ref[:, cot_at:dbr_at] = cot
    wide = width // ys // 2

    def down(j, totals):
        grad = send_ref[:, pl.ds(pl.multiple_of(j * 512, 512), 512)]
        return [t + nt(grad, weights.gu(i, y, j)) for t, (i, y) in zip(totals, pairs)]

    zero = [jnp.zeros((rows, wide), f32)] * len(pairs)
    totals = lax.fori_loop(0, 2 * ff // 512, down, zero)
    for y in range(ys):
        put(dn_ref, y, totals[2 * y], totals[2 * y + 1], core)
    unit = mid_ref[...] * rms
    dn = dn_ref[...]
    dn = dn * gffn_ref[...]
    dmid = cot.astype(f32) + rms * (dn - unit * jnp.mean(dn * unit, axis=1, keepdims=True))
    dmid_ref[...] = dmid
    dbr = dmid.astype(bf16)
    send_ref[:, dbr_at:dgate_at] = dbr
    back_through(datt_ref, dbr, weights.ao, 2)
    back_through(dmx_ref, dbr, weights.so, 2)
    mean = 0.0
    for j in range(DS // 512):
        cols = slice(j * 512, (j + 1) * 512)
        unit = gd_ref[:, cols] * rms_gate
        dmx = dmx_ref[:, cols]
        mean = mean + jnp.sum(dmx * gssm_ref[:, cols] * unit, axis=1, keepdims=True)
    mean = mean / DS
    for j in range(DS // 512):
        cols = slice(j * 512, (j + 1) * 512)
        unit = gd_ref[:, cols] * rms_gate
        dgated = rms_gate * (dmx_ref[:, cols] * gssm_ref[:, cols] - unit * mean)
        gate = gi_ref[:, cols]
        sg = sigmoid(gate)
        ssd = ycore_ref[:, cols] + skip_ref[:, cols] * x_ref[:, cols]
        dssd = dgated * gate * sg
        dssd_ref[:, cols] = dssd
        dgate = (dgated * ssd * (sg * (1.0 + gate * (1.0 - sg)))).astype(bf16)
        send_ref[:, dgate_at + j * 512 : dgate_at + (j + 1) * 512] = dgate
        fd_ref[:, cols] = (dssd * fade[:, cols]).astype(bf16)
    back_through(dng_ref, send_ref[:, dgate_at:sel_at], weights.gate, 3)
    dentry_ref[...] = tn(fd_ref[...], reads)
    at = 0
    for ref in (n2_ref, hid_ref, att_ref, mixed_ref, normed_ref):
        count = ys
        wide = ref.shape[1] // count
        for y in range(count):
            own, oth = halves(ref[:, y * wide : (y + 1) * wide], core)
            keep_ref[:, at : at + wide // 2] = own
            send_ref[:, sel_at + at : sel_at + at + wide // 2] = oth
            at += wide // 2


def products_kernel(plan, extra, keep_ref, own_ref, act_ref, *refs):
    got_ref, outs = act_ref, refs
    if extra:
        (extra_ref, *outs) = refs
    for which, a_at, act_at, size, g_at in plan:
        out = outs[which]
        for y in range(out.shape[0]):
            left = keep_ref[:, a_at + y * size : a_at + (y + 1) * size]
            right = act_ref[:, act_at + y * size : act_at + (y + 1) * size]
            for j in range(0, out.shape[-1], 512):
                stop = min(j + 512, out.shape[-1])
                total = tn(left, own_ref[:, g_at + j : g_at + stop])
                total = total + tn(right, got_ref[:, g_at + j : g_at + stop])
                if extra and which == 0 and stop == out.shape[-1]:
                    total = total + extra_ref[y]
                out[y, :, j:stop] = total.astype(bf16)


def split_products_kernel(plan, extra, y_ref, x_ref, keep_ref, own_ref, act_ref, *refs):
    got_ref, outs = act_ref, refs
    if extra:
        (extra_ref, *outs) = refs
    xkeep_ref, xsend_ref, ykeep_ref, ysend_ref = outs
    my_y, my_x = y_ref[0], x_ref[0]
    for kind, place, a_at, act_at, size, g_at, wide in plan:
        for k in range(2):
            y = k if kind == "x" else lax.rem(my_y + k, 2)
            left = keep_ref[:, pl.ds(pl.multiple_of(a_at + y * size, LANES), size)]
            right = act_ref[:, pl.ds(pl.multiple_of(act_at + y * size, LANES), size)]
            keep, send = (xkeep_ref, xsend_ref) if kind == "x" else (ykeep_ref, ysend_ref)
            for j in range(0, wide, 512):
                stop = min(j + 512, wide)
                total = tn(left, own_ref[:, g_at + j : g_at + stop])
                total = total + tn(right, got_ref[:, g_at + j : g_at + stop])
                if kind == "x":
                    zs, each = keep.shape[1], keep.shape[2]
                    if extra and stop == wide:
                        total = total + extra_ref[k]
                    cols = slice(place + j, place + stop)
                    total = total.reshape(zs, 2, each, stop - j)
                    low, high = total[:, 0], total[:, 1]
                    keep[k, :, :, cols] = jnp.where(my_x == 0, low, high).astype(bf16)
                    send[k, :, :, cols] = jnp.where(my_x == 0, high, low).astype(bf16)
                else:
                    count = keep.shape[0]
                    each = size // count
                    total = total.reshape(count, each, stop - j).astype(bf16)
                    (send if k else keep)[:, place : place + each, j:stop] = total


def fold_one_kernel(
    y_ref, x_ref, xkeep_ref, xgot_ref, ykeep_ref, ygot_ref,
    xkeep_out, xsend_out, ykeep_out, ysend_out,
):
    my_y, my_x = y_ref[0], x_ref[0]
    xkeep_out[...] = xkeep_ref[my_y].astype(f32) + xgot_ref[my_y].astype(f32)
    other = 1 - my_y
    xsend_out[...] = (xkeep_ref[other].astype(f32) + xgot_ref[other].astype(f32)).astype(bf16)
    for z in range(ykeep_out.shape[0]):
        at = 2 * z + my_x
        ykeep_out[z] = ykeep_ref[at].astype(f32) + ygot_ref[at].astype(f32)
        at = 2 * z + 1 - my_x
        ysend_out[z] = (ykeep_ref[at].astype(f32) + ygot_ref[at].astype(f32)).astype(bf16)


def laid(refs, width):
    at = 0
    for ref in refs:
        each = ref.shape[-2]
        for j in range(ref.shape[-1] // width):
            yield ref, at, j * width
            at += each


def fold_two_kernel(xkeep_ref, xgot_ref, ykeep_ref, ygot_ref, out_ref):
    width = out_ref.shape[2]
    keeps = laid((xkeep_ref, ykeep_ref), width)
    gots = laid((xgot_ref, ygot_ref), width)
    for (keep, at, col), (got, *unused) in zip(keeps, gots):
        each = keep.shape[-2]
        value = keep[:, :, col : col + width] + got[:, :, col : col + width].astype(f32)
        out_ref[:, at : at + each, :] = value.astype(bf16)


def fold_three_kernel(got_ref, *outs):
    width = got_ref.shape[2]
    for out, at, col in laid(outs, width):
        rows = slice(at, at + out.shape[0])
        total = got_ref[0, rows, :].astype(f32)
        for z in range(1, got_ref.shape[0]):
            total = total + got_ref[z, rows, :].astype(f32)
        out[:, col : col + width] = total


class PairReduction:
    def __init__(self, pieces, width):
        self.places = tuple(place_on(g).reshape(1).astype(jnp.int32) for g in ("y", "x"))
        self.xkeep, xsend, self.ykeep, ysend = pieces
        self.width = width
        self.send(xsend, ysend, "x", "y")

    def send(self, xsend, ysend, first, second):
        self.sent = (xsend, ysend)
        self.gots = (
            swap(xsend, extents()[first][0]), swap(ysend, extents()[second][0])
        )

    def fold_one(self, *others):
        gots = after(self.gots, *others)
        x, y = self.xkeep.shape, self.ykeep.shape
        x, y = x[1:], (y[0] // 2, *y[1:])
        self.xkeep, xsend, self.ykeep, ysend = run(
            fold_one_kernel, "fold_one", [(x, f32), (x, bf16), (y, f32), (y, bf16)],
            (*self.places, self.xkeep, gots[0], self.ykeep, gots[1]),
            scalars=2,
        )
        self.send(xsend, ysend, "y", "x")

    def fold_two(self, *others):
        gots = after(self.gots, *others)
        self.shapes = [self.xkeep.shape[1:], self.ykeep.shape[1:]]
        rows = sum(r * c // self.width for r, c in self.shapes)
        zs = self.xkeep.shape[0]
        self.sent = run(
            fold_two_kernel, "fold_two", [((zs, rows, self.width), bf16)],
            (self.xkeep, gots[0], self.ykeep, gots[1]),
        )[0]
        self.gots = dealt(self.sent, "z")

    def fold_three(self, *others):
        gots = after(self.gots, *others)
        self.sent = run(
            fold_three_kernel, "fold_three", [(shape, f32) for shape in self.shapes], (gots,),
        )
        return self.sent


class PlainReduction:
    def __init__(self, pieces, rows):
        self.parts = [Reduction(pieces[0], rows[0], "x"), Reduction(pieces[1], rows[1], "y")]
        self.sent = [part.send() for part in self.parts]

    def fold_one(self, *others):
        for part in self.parts:
            part.receive(*others)
        self.sent = [part.send() for part in self.parts]

    fold_two = fold_one

    def fold_three(self, *others):
        self.sent = [part.receive(*others) for part in self.parts]
        return self.sent


def scan_back_kernel(
    dy_ref, x_ref, bc_ref, step_ref, cum_ref, cumt_ref, off_ref, dxw_ref, ds_ref,
    xw_ref, ce_ref, dyb_ref, dg_ref,
):
    rows = x_ref.shape[0]
    spread = head_spread()
    xw_ref[...] = (x_ref[...] * nn_left(step_ref[...], spread, 2)).astype(bf16)
    dyb_ref[...] = dy_ref[...].astype(bf16)
    ce_ref[...] = nn_left(cum_ref[...], spread, 3)
    keys, reads = bc_ref[:, :STATE].astype(bf16), bc_ref[:, STATE:].astype(bf16)
    early, late = iota((rows, rows), 0), iota((rows, rows), 1)
    keep = (early <= late) & (early >= late - off_ref[...])
    scores = jnp.where(keep, nt(keys, reads), 0.0)
    lane = iota((rows, LANES), 1)
    dg_ref[...] = jnp.zeros((rows, rows), f32)

    def pair(j, unused):
        cols = pl.ds(pl.multiple_of(j * LANES, LANES), LANES)
        wide = ce_ref[:, cols]
        xw, dy = xw_ref[:, cols], dyb_ref[:, cols]
        outs = []
        change = 0.0
        for k in range(2):
            first = wide[:, k * SSM_DIM : k * SSM_DIM + 1]
            second = cumt_ref[pl.ds(2 * j + k, 1), :]
            decay = jnp.exp(jnp.minimum(second - first, 0.0))
            outs.append(nn((decay * scores).astype(bf16), dy))
            mine = (lane < SSM_DIM) if k == 0 else (lane >= SSM_DIM)
            change = change + nt(xw * mine.astype(bf16), dy) * decay
        dg_ref[...] += change
        dxw_ref[:, cols] = jnp.where(lane < SSM_DIM, outs[0], outs[1])
        return unused

    lax.fori_loop(0, SSM_HEADS // 2, pair, 0)
    ds_ref[...] = jnp.where(keep, dg_ref[...], 0.0).astype(bf16)


def mixer_back_kernel(
    dy_ref, ycore_ref, x_ref, bc_ref, step_ref, cum_ref, z_ref, off_ref, entry_ref,
    down_ref, skip_ref, dec_ref, chan_ref, cw_ref, cb_ref, dxwl_ref, ds_ref,
    dext_ref, dz_ref, small_ref,
    dact_ref,
):
    rows = x_ref.shape[0]
    spread, gather = head_spread(), head_sum_matrix()
    off, cum = off_ref[...], cum_ref[...]
    step_wide = nn_left(step_ref[...], spread, 2)
    keys, reads = bc_ref[:, :STATE].astype(bf16), bc_ref[:, STATE:].astype(bf16)
    dscores = ds_ref[...]
    down = down_ref[...].astype(bf16)
    tail = nn_left(tail_of(cum, off), spread, 2)
    fade = nn_left(fade_of(cum, off), spread, 2)
    bd = nt(keys, down) * tail
    xw = (x_ref[...] * step_wide).astype(bf16).astype(f32)
    dxw = dxwl_ref[...] + bd
    dact_ref[:, DS : DS + STATE] = nn(dscores, reads) + nn((tail * xw).astype(bf16), down)
    dact_ref[:, DS + STATE :] = tn(dscores, keys) + nn(
        (fade * dy_ref[...]).astype(bf16), entry_ref[...].astype(bf16)
    )
    ones = jnp.ones((8, STATE), bf16)
    product = sum(nt(ones, part) for part in terms(down_ref[...] * entry_ref[...], 3))
    through = jnp.sum(xw * bd, axis=0, keepdims=True)
    direct = jnp.sum(dy_ref[...] * x_ref[...], axis=0, keepdims=True)
    row = iota((8, DS), 0)
    sums = jnp.where(row == 0, product, jnp.where(row == 1, through, direct))
    sums = nn_left(sums, gather, 3)
    through, kept = sums[1:2], sums[0:1] * carry_of(cum, off)
    last = (iota((rows, 1), 0) == rows - 1).astype(f32)
    dyb = dy_ref[...].astype(bf16).astype(f32)
    dcum = nn_left(dyb * ycore_ref[...] - xw * dxw, gather, 2) + last * (through + kept)
    tri = (iota((rows, rows), 0) <= iota((rows, rows), 1)).astype(f32).astype(bf16)
    dlog = nn_right(tri, dcum, 3)
    x = x_ref[...]
    step, dec = step_ref[...], dec_ref[...]
    dstep = nn_left(dxw * x, gather, 2) - dlog * dec
    dz = dstep * sigmoid(z_ref[...])
    dz_ref[...] = dz
    small_ref[...] = jnp.zeros(small_ref.shape, f32)
    small_ref[CONV + 1 : CONV + 2, :LANES] = jnp.sum(dlog * (-step * dec), axis=0, keepdims=True)
    small_ref[CONV + 1 : CONV + 2, LANES : 2 * LANES] = jnp.sum(dz, axis=0, keepdims=True)
    small_ref[CONV + 1 : CONV + 2, 2 * LANES : 3 * LANES] = sums[2:3]
    dact_ref[:, :DS] = dxw * step_wide + skip_ref[...] * dy_ref[...]
    for j in range(CONV_CH // 256):
        cols = slice(j * 256, (j + 1) * 256)
        taps = conv_taps(chan_ref, cols, off)
        mixed = cb_ref[:, cols]
        for i, tap in enumerate(taps):
            mixed = mixed + tap * cw_ref[i : i + 1, cols]
        sg = sigmoid(mixed)
        dmix = dact_ref[:, cols] * (sg * (1.0 + mixed * (1.0 - sg)))
        small_ref[CONV : CONV + 1, cols] = jnp.sum(dmix, axis=0, keepdims=True)
        total = 0.0
        for i, tap in enumerate(taps):
            back = CONV - 1 - i
            small_ref[i : i + 1, cols] = jnp.sum(dmix * tap, axis=0, keepdims=True)
            part = dmix * ((off >= back).astype(f32) * cw_ref[i : i + 1, cols])
            part = jnp.concatenate([jnp.zeros((RIM, 256), f32), part], axis=0)
            total = total + (pltpu.roll(part, rows + RIM - back, 0) if back else part)
        dext_ref[:, cols] = total


def back_grads_kernel(
    ys, core_ref, dq_ref, dkv_ref, dext_ref, dz_ref, cos_ref, sin_ref, normed_ref, nrim_ref,
    ga_ref, keep_ref,
):
    core = core_ref[0]
    dkv = dkv_ref[0].astype(f32)
    for i in range(1, dkv_ref.shape[0]):
        dkv = dkv + dkv_ref[i].astype(f32)
    ga_ref[:RIM, :768] = jnp.zeros((RIM, 768), bf16)
    ga_ref[:RIM, 1024:A_COLS] = jnp.zeros((RIM, LANES), bf16)
    ga_ref[RIM:, :LANES] = turned_back(dkv[:, :LANES], cos_ref[...], sin_ref[...]).astype(bf16)
    ga_ref[RIM:, LANES:256] = dkv[:, LANES:].astype(bf16)
    ga_ref[RIM:, 256:768] = dq_ref[...]
    ga_ref[:, 768:1024] = dext_ref[:, DS:].astype(bf16)
    ga_ref[RIM:, 1024:A_COLS] = dz_ref[...].astype(bf16)
    ga_ref[:, A_COLS : A_COLS + DS] = dext_ref[:, :DS].astype(bf16)
    wide = normed_ref.shape[1] // ys
    at, to = 0, A_COLS + DS
    for y in range(ys):
        cols = slice(y * wide, (y + 1) * wide)
        for ref, rows in ((nrim_ref, slice(0, RIM)), (normed_ref, slice(RIM, None))):
            own, oth = halves(ref[:, cols], core)
            keep_ref[rows, at : at + wide // 2] = own
            ga_ref[rows, to + at : to + at + wide // 2] = oth
        at += wide // 2


def back_kernel(
    core_ref, gab_ref, wa_own, wa_oth, wb_own, wb_oth, tok_ref, dmid_ref, dng_ref, gain_ref,
    dtok_ref, drim_ref, dn_ref,
):
    core = core_ref[0]
    for y in range(wa_own.shape[0]):
        ga, gb = gab_ref[:, :A_COLS], gab_ref[:, A_COLS : A_COLS + DS]
        own = nt(ga, wa_own[y]) + nt(gb, wb_own[y])
        oth = nt(ga, wa_oth[y]) + nt(gb, wb_oth[y])
        put(dn_ref, y, own, oth, core)

    def through_norm(dn, tok):
        tok = tok.astype(f32)
        rms = lax.rsqrt(jnp.mean(tok * tok, axis=1, keepdims=True) + EPS)
        unit = tok * rms
        dn = dn * gain_ref[...]
        return rms * (dn - unit * jnp.mean(dn * unit, axis=1, keepdims=True))

    drim_ref[...] = through_norm(dn_ref[:RIM, :], tok_ref[:RIM, :])
    dtok_ref[...] = dmid_ref[...] + through_norm(dn_ref[RIM:, :] + dng_ref[...], tok_ref[RIM:, :])


def gain_kernel(pairs, count, *refs):
    gains, refs = refs[:count], refs[count:]
    outs = refs[-count:]
    for k, out in enumerate(outs):
        total = 0.0
        for group, w, g in pairs:
            if group == k:
                total = total + jnp.sum(
                    refs[w][...].astype(f32) * refs[g][...], axis=1, keepdims=True
                )
        out[...] = total / gains[k][...].astype(f32)


def run(kernel, name, outs, args, scalars=0, scratch=(), flops=0, left=0, sems=()):
    moved = sum(a.size * a.dtype.itemsize for a in args)
    shapes = [jax.ShapeDtypeStruct(shape, kind) for shape, kind in outs]
    moved += sum(s.size * s.dtype.itemsize for s in shapes)
    specs = [pl.BlockSpec(memory_space=pltpu.SMEM)] * scalars
    specs += [pl.BlockSpec(memory_space=pltpu.VMEM)] * (len(args) - scalars - left)
    specs += [pl.BlockSpec(memory_space=pl.ANY)] * left
    return pl.pallas_call(
        kernel,
        name=name,
        out_shape=shapes,
        in_specs=specs,
        out_specs=[pl.BlockSpec(memory_space=pltpu.VMEM)] * len(shapes),
        scratch_shapes=[pltpu.VMEM(shape, kind) for shape, kind in scratch]
        + [pltpu.SemaphoreType.DMA(shape) for shape in sems],
        compiler_params=pltpu.CompilerParams(vmem_limit_bytes=62 * 2**20),
        cost_estimate=pl.CostEstimate(
            flops=flops, bytes_accessed=moved, transcendentals=0
        ),
    )(*args)


def padded(vector, width):
    return jnp.pad(vector.astype(f32), (0, width - vector.shape[0]))[None, :]


def local(
    tokens, lengths, cotangent, mixer_gain, query_weight, keyval_weight, inner_weight, conv_weight,
    conv_bias, ssm_gain, attn_out_weight, ssm_out_weight, ffn_gain, gate_up_weight, down_weight,
    decay_log, step_bias, skip_gain,
):
    rows, width = tokens.shape
    seq_count, seq_rank = lax.axis_size(SEQ), lax.axis_index(SEQ)
    side = place_on("core").reshape(1)
    back = (rows * seq_count // 2) // rows
    part = query_weight.shape[0]
    heads_width, ff = HEADS * HEAD_DIM, gate_up_weight.shape[1] // 2
    a_rows, s_rows, f_rows = attn_out_weight.shape[0], ssm_out_weight.shape[0], down_weight.shape[0]
    ys = lax.axis_size("y")

    rim = shifted(tokens[rows - RIM :], 1)
    small = jnp.concatenate(
        [mixer_gain, conv_weight.reshape(-1), conv_bias, ssm_gain, ffn_gain]
    ).astype(f32)
    counts = [mixer_gain.size, conv_weight.size, conv_bias.size, ssm_gain.size, ffn_gain.size]
    slots = -(-small.size // LANES) * LANES
    small = gather_small(jnp.pad(small, (0, slots - small.size)))
    inner_tail = inner_weight[:, DS + CONV_CH :]
    front_a = jnp.concatenate(
        [
            keyval_weight,
            query_weight,
            inner_weight[:, 2 * DS : DS + CONV_CH],
            jnp.pad(inner_tail, ((0, 0), (0, LANES - SSM_HEADS))),
        ],
        1,
    )
    front = shared(jnp.concatenate([front_a, inner_weight[:, DS : 2 * DS]], 1), "z")
    wa_own, wa_oth = gather_pair(front[:, :, :A_COLS], "y")
    wb_own, wb_oth = gather_pair(front[:, :, A_COLS:], "x")
    others = lax.axis_size(SEQ)
    aligned = ys == 2 and others == 8 and all(r % 16 == 0 for r in (part, a_rows, s_rows, f_rows))
    core_unit = extents()["core"][0]
    packed = jnp.concatenate(
        [
            inner_weight[:, :width],
            jnp.concatenate(
                [
                    inner_weight[:, width:DS],
                    jnp.concatenate([attn_out_weight[:, :512], attn_out_weight[:, 512:]], 0),
                ],
                1,
            ),
            ssm_out_weight,
        ]
        + [gate_up_weight[:, k * width : (k + 1) * width] for k in range(2 * ff // width)]
        + [down_weight],
        0,
    )
    packed = lax.all_gather(packed, ("y", "z", "x"), axis=0)
    packed = packed.reshape(ys, others, *packed.shape[1:])
    starts = [sum(counts[:i]) for i in range(len(counts))]
    gain_one, w_conv, b_conv, gain_ssm, gain_two = (
        small[:, s : s + c].reshape(-1) for s, c in zip(starts, counts)
    )
    w_conv = jnp.pad(w_conv.reshape(CONV_CH, CONV).T, ((0, 8 - CONV), (0, 0)))
    gain_one, b_conv, gain_ssm, gain_two = (
        v[None, :] for v in (gain_one, b_conv, gain_ssm, gain_two)
    )
    tokens_rim = jnp.concatenate([rim, tokens], 0)
    places = seq_rank * rows + jnp.arange(rows)
    begin = jnp.zeros_like(places)
    end = jnp.int32(0)
    for i in range(lengths.shape[1]):
        end = end + lengths[0, i]
        begin = jnp.where(end <= places, end, begin)
    offset = (places - begin).astype(jnp.int32)
    half = HEAD_DIM // 2
    freq = BASE ** (-jnp.arange(half).astype(f32) / half)
    angle = offset.astype(f32)[:, None] * freq[None, :]
    cos = jnp.tile(jnp.cos(angle), (1, 4))
    sin = jnp.sin(angle)
    sin = jnp.tile(jnp.concatenate([-sin, sin], 1), (1, 2))
    off = offset[:, None]
    step_bias_row, decay_row = padded(step_bias, LANES), padded(jnp.exp(decay_log), LANES)
    skip = jnp.repeat(skip_gain, SSM_DIM)[None, :]

    (q8, kv, normed, nrim, chan, x, bc, step, cum, cumt, z, state, carry) = run(
        front_kernel,
        "front",
        [
            ((HEADS, rows, LANES), bf16),
            ((rows, 256), bf16),
            ((rows, width), bf16),
            ((RIM, width), bf16),
            ((rows + RIM, CONV_CH), bf16),
            ((rows, DS), f32),
            ((rows, 2 * STATE), f32),
            ((rows, LANES), f32),
            ((rows, LANES), f32),
            ((LANES, rows), f32),
            ((rows, LANES), f32),
            ((DS, STATE), f32),
            ((1, LANES), f32),
        ],
        (
            side, tokens_rim, gain_one, wa_own, wa_oth, wb_own, wb_oth,
            cos, sin, off, w_conv, b_conv, step_bias_row, decay_row,
        ),
        scalars=1,
        scratch=[((rows + RIM, width), bf16), ((rows, DS), bf16)],
        flops=2 * rows * width * (A_COLS + DS),
    )
    carrying = Carrying(state, carry, back, 1)
    sent_state = carrying.send()
    rank = seq_rank.reshape(1).astype(jnp.int32)
    kv_all = shared(kv, SEQ)
    window = (back + 1) * rows
    y_local = run(
        scan_kernel, "scan", [((rows, DS), f32)],
        after((x, bc, step, cum, cumt, off), sent_state),
        scratch=[((rows, DS), bf16), ((rows, DS), f32)], flops=2 * SSM_HEADS * rows * rows * 128,
    )[0]
    order = y_local
    entry = None
    while entry is None:
        entry = carrying.receive(order)
        if entry is None:
            sent_state = carrying.send()
    packed = after(packed, order, sent_state)
    packed = (packed, swap(packed, core_unit))
    post_scratch, post_sems = [], []
    if aligned:
        parts, post_weights = (part, a_rows, s_rows, f_rows), packed
        post_scratch, post_sems = [((2, *packed[0].shape), bf16)], [(3, 2)]
    else:
        parts = ()
        gu_at = 2 * part + s_rows

        def taken(full, start, size, low, high):
            return full[:, :, start : start + size, low:high].reshape(ys, -1, high - low)

        def joined_columns(blocks):
            return [jnp.concatenate([taken(f, *block) for block in blocks], 2) for f in packed]

        post_weights = (
            *joined_columns([(0, part, 0, width), (part, part, 0, DS - width)]),
            *joined_columns([(part + k * a_rows, a_rows, 512, 1024) for k in range(2)]),
            *joined_columns([(2 * part, s_rows, 0, width)]),
            *joined_columns([(gu_at + 4 * part, f_rows, 0, width)]),
            *joined_columns([(gu_at + k * part, part, 0, width) for k in range(2 * ff // width)]),
        )

    attended, lse = run(
        functools.partial(attend_kernel, back + 1),
        "attend",
        [((rows, heads_width), bf16), ((LANES, rows), f32)],
        after((rank, q8, kv_all, off), packed[0]),
        scalars=1,
        scratch=[
            ((window, LANES), bf16),
            ((window, LANES), bf16),
            ((rows, window), f32),
            ((HEADS, rows, LANES), f32),
        ],
        flops=4 * HEADS * rows * window * LANES,
    )
    half = (2 * width + ff + heads_width + DS) // 2
    sent = 2 * ff + 2 * width + DS
    output, dmid, datt, dssd, ycore, dentry, send, keep, dng = run(
        functools.partial(post_kernel, parts, ys),
        "post",
        [
            ((rows, width), bf16),
            ((rows, width), f32),
            ((rows, heads_width), bf16),
            ((rows, DS), f32),
            ((rows, DS), f32),
            ((DS, STATE), f32),
            ((rows, sent + half), bf16),
            ((rows, half), bf16),
            ((rows, width), f32),
        ],
        (
            side, tokens, cotangent, attended, y_local, x, bc, cum, off, entry, skip, normed,
            gain_ssm, gain_two, *post_weights,
        ),
        scalars=1,
        left=2 if aligned else 0,
        sems=post_sems,
        scratch=[
            ((rows, DS), f32),
            ((rows, DS), f32),
            ((rows, width), f32),
            ((rows, 2 * ff), f32),
            ((rows, width), f32),
            ((rows, DS), f32),
            ((rows, DS), bf16),
            ((rows, width), bf16),
            ((rows, ff), bf16),
            ((rows, DS), bf16),
            ((rows, ff), f32),
        ]
        + post_scratch,
        flops=4 * rows * width * (3 * ff + DS + DS + heads_width),
    )
    got = swap(send, core_unit)
    carrying = Carrying(dentry, carry, back, -1)
    sent_state = carrying.send()
    off_row = offset[None, :]
    sizes = [width // 2, ff // 2, heads_width // 2, DS // 2, width // 2]
    ats = [sum(sizes[:i]) for i in range(5)]
    sizes = [size // ys for size in sizes]
    n2_at, hid_at, att_at, mix_at, norm_at = ats
    cot_at, dbr_at, dgate_at = 2 * ff, 2 * ff + width, 2 * ff + 2 * width
    places = tuple(place_on(g).reshape(1).astype(jnp.int32) for g in ("y", "x"))

    def weight_sums(name, x_parts, y_parts, keep, own, got, extra=()):
        flops = sum(4 * rows * p[2] * p[4] * ys for p in x_parts + y_parts)
        plan, at, tall = [], 0, y_parts[0][4]
        for p in x_parts:
            plan.append(("x", at, *p))
            at += p[4]
        wide, at = at, 0
        for p in y_parts:
            plan.append(("y", at, *p))
            at += p[2] // others
        if aligned:
            xs = (ys, others // 2, x_parts[0][2] // others, wide)
            made = run(
                functools.partial(split_products_kernel, plan, len(extra)),
                name,
                [(xs, bf16), (xs, bf16), ((others, at, tall), bf16), ((others, at, tall), bf16)],
                (*places, keep, own, got, *extra),
                scalars=2,
                flops=flops,
            )
            return PairReduction(made, 512 if wide % 512 == 0 else 384)
        parts = x_parts + y_parts
        made = run(
            functools.partial(
                products_kernel, [(i, *p[:4]) for i, p in enumerate(parts)], len(extra)
            ),
            name,
            [((ys, p[2], p[4]), bf16) for p in parts],
            (keep, own, got, *extra),
            flops=flops,
        )
        heads = made[: len(x_parts)]
        tails = [m.reshape(ys, others, -1, tall) for m in made[len(x_parts) :]]
        rows_of = (x_parts[0][2] // others, at)
        return PlainReduction((jnp.concatenate(heads, 2), jnp.concatenate(tails, 2)), rows_of)

    dq, dkv = run(
        functools.partial(attend_back_kernel, back + 1),
        "attend_back",
        [((rows, heads_width), bf16), ((seq_count, rows, 256), bf16)],
        after((rank, q8, kv_all, off_row, lse, datt, cos, sin), sent_state),
        scalars=1,
        scratch=[
            ((window, LANES), bf16),
            ((window, LANES), bf16),
            ((window, rows), f32),
            ((HEADS, rows, LANES), bf16),
            ((HEADS, rows, LANES), f32),
            ((window, 256), f32),
        ],
        flops=10 * HEADS * rows * window * LANES,
    )
    dkv_got = dealt(dkv, SEQ)
    downstream = carrying.receive(dq)
    if downstream is None:
        sent_state = carrying.send()
    keep, send, got = after((keep, send, got), dq, sent_state)
    red_one = weight_sums(
        "weights_one",
        [(n2_at, sent + n2_at, sizes[0], 0, ff)],
        [(hid_at, sent + hid_at, sizes[1], cot_at, width)],
        keep,
        send,
        got,
    )
    while downstream is None:
        downstream = carrying.receive(red_one.sent)
        if downstream is None:
            carrying.send()
    keep, send, got = after((keep, send, got), red_one.sent, downstream)
    red_two = weight_sums(
        "weights_two",
        [
            (n2_at, sent + n2_at, sizes[0], ff, ff),
            (norm_at, sent + norm_at, sizes[4], dgate_at, DS),
        ],
        [
            (att_at, sent + att_at, sizes[2], dbr_at, width),
            (mix_at, sent + mix_at, sizes[3], dbr_at, width),
        ],
        keep,
        send,
        got,
    )
    dxw, dscores = run(
        scan_back_kernel,
        "scan_back",
        [((rows, DS), f32), ((rows, rows), bf16)],
        after((dssd, x, bc, step, cum, cumt, off_row), red_two.sent),
        scratch=[
            ((rows, DS), bf16),
            ((rows, DS), f32),
            ((rows, DS), bf16),
            ((rows, rows), f32),
        ],
        flops=4 * SSM_HEADS * rows * rows * 128,
    )

    red_one.fold_one(dxw)
    dext, dz, small = run(
        mixer_back_kernel,
        "mixer_back",
        [
            ((rows + RIM, CONV_CH), f32),
            ((rows, LANES), f32),
            ((8, CONV_CH), f32),
        ],
        after(
            (
                dssd, ycore, x, bc, step, cum, z, off, entry, downstream, skip, decay_row, chan,
                w_conv, b_conv, dxw, dscores,
            ),
            red_one.sent,
        ),
        scratch=[((rows, CONV_CH), f32)],
        flops=8 * rows * DS * 128,
    )
    count = lax.axis_size(AXES)
    small_got = swap(small, core_unit)
    gab, norm_keep = run(
        functools.partial(back_grads_kernel, ys),
        "back_grads",
        [((rows + RIM, A_COLS + DS + width // 2), bf16), ((rows + RIM, width // 2), bf16)],
        (side, dq, dkv_got, dext, dz, cos, sin, normed, nrim),
        scalars=1,
    )
    gab_got = swap(gab, core_unit)
    red_two.fold_one(gab)
    small = small + after(small_got, gab)
    per_device = jnp.concatenate(
        [
            small[: CONV + 1].reshape(CONV + 1, count, -1).transpose(1, 0, 2).reshape(count, -1),
            jnp.broadcast_to(
                small[CONV + 1, : 3 * LANES].reshape(3, LANES)[:, :SSM_HEADS].reshape(1, -1),
                (count, 3 * SSM_HEADS),
            ),
        ],
        1,
    )
    slots = per_device.shape[1]
    free = LANES - SSM_HEADS
    per_device = lax.dynamic_index_in_dim(
        per_device.reshape(ys, 2, others, slots), place_on("core"), 1, False
    )
    extra = jnp.pad(per_device, ((0, 0), (0, 0), (0, part * free - slots)))
    extra = extra.reshape(ys, others * part, free)
    aside = 512 if A_COLS % 512 == 0 else A_COLS % 512
    extra = jnp.pad(extra, ((0, 0), (0, 0), (aside - free, 0)))
    grad_tokens, grad_rim = run(
        back_kernel,
        "back",
        [((rows, width), f32), ((RIM, width), f32)],
        (
            side, after(gab, red_two.sent), wa_own, wa_oth, wb_own, wb_oth, tokens_rim, dmid, dng,
            gain_one,
        ),
        scalars=1,
        scratch=[((rows + RIM, width), f32)],
        flops=2 * rows * width * (A_COLS + DS),
    )
    rim_got = shifted(grad_rim, -1)
    norm_keep, gab, gab_got, extra = after((norm_keep, gab, gab_got, extra), grad_tokens)
    red_three = weight_sums(
        "front_weights",
        [(0, A_COLS + DS, sizes[4], 0, A_COLS)],
        [(0, A_COLS + DS, sizes[4], A_COLS, DS)],
        norm_keep,
        gab,
        gab_got,
        (extra,),
    )
    red_one.fold_two(red_three.sent)
    red_two.fold_two(red_one.sent)
    red_three.fold_one(red_two.sent)
    r_one, r_down = red_one.fold_three(red_three.sent)
    red_three.fold_two(r_one)
    r_two, r_out = red_two.fold_three(red_three.sent)
    rim_got = after(rim_got, r_two)
    grad_tokens = grad_tokens.at[rows - RIM :].add(rim_got)
    r_e, r_f = red_three.fold_three(grad_tokens)
    r_gu = jnp.concatenate([r_one, r_two[:, :ff]], 1)
    small = r_e[:, A_COLS - free :].reshape(-1)[:slots]
    conv = small[: (CONV + 1) * conv_bias.size].reshape(CONV + 1, -1)
    heads = small[(CONV + 1) * conv_bias.size :].reshape(3, SSM_HEADS)
    g_inner = jnp.concatenate([r_two[:, ff:], r_f, r_e[:, 768 : 1024 + SSM_HEADS]], 1)
    g_mixer, g_ssm, g_ffn = run(
        functools.partial(
            gain_kernel, [(0, 0, 1), (0, 2, 3), (0, 4, 5), (1, 6, 7), (2, 8, 9)], 3
        ),
        "gains",
        [((part, 1), f32), ((s_rows, 1), f32), ((part, 1), f32)],
        (
            mixer_gain[:, None], ssm_gain[:, None], ffn_gain[:, None],
            keyval_weight, r_e[:, :256], query_weight, r_e[:, 256:768], inner_weight, g_inner,
            ssm_out_weight, r_out[a_rows:], gate_up_weight, r_gu,
        ),
    )
    return (
        output,
        grad_tokens,
        g_mixer[:, 0],
        r_e[:, 256:768],
        r_e[:, :256],
        g_inner,
        conv[:CONV].T,
        conv[CONV],
        g_ssm[:, 0],
        r_out[:a_rows],
        r_out[a_rows:],
        g_ffn[:, 0],
        r_gu,
        r_down,
        heads[0],
        heads[1],
        heads[2],
    )


def solution(mesh):
    across, along = mesh.shape["dp"], mesh.shape["seq"]
    mesh = jax.sharding.Mesh(mesh.devices.reshape(across // 2, 2, along // 2, 2), AXES)
    lead, flat, rep = P(AXES, None), P(AXES), P()
    return jax.shard_map(
        local,
        mesh=mesh,
        in_specs=(
            lead, P(AXES[:2], None), lead, flat, lead, lead, lead, lead, flat, flat, lead, lead, flat,
            lead, lead, rep, rep, rep,
        ),
        out_specs=(
            lead, lead, flat, lead, lead, lead, lead, flat, flat, lead, lead, flat, lead, lead,
            rep, rep, rep,
        ),
        check_vma=False,
    )
```

```python
import functools

import jax
import jax.numpy as jnp
from jax import lax
from jax.experimental import pallas as pl
from jax.experimental.pallas import tpu as pltpu
from jax.sharding import PartitionSpec as P

HEADS = 8
KV_HEADS = 2
HEAD_DIM = 64
SSM_HEADS = 24
SSM_DIM = 64
STATE = 128
CONV = 4
DS = 1536
CONV_CH = 1792
RIM = 16
LANES = 128
A_COLS = 2 * KV_HEADS * HEAD_DIM + HEADS * HEAD_DIM + 2 * STATE + LANES
EPS = 1e-6
BASE = 10000.0
NEG = -1e30
SCALE = 6_600_000_000
AXES = ("y", "core", "z", "x")
SEQ = AXES[2:]

f32 = jnp.float32
bf16 = jnp.bfloat16


def nn(a, b):
    return lax.dot_general(a, b, (((1,), (0,)), ((), ())), preferred_element_type=f32)


def tn(a, b):
    return lax.dot_general(a, b, (((0,), (0,)), ((), ())), preferred_element_type=f32)


def nt(a, b):
    return lax.dot_general(a, b, (((1,), (1,)), ((), ())), preferred_element_type=f32)


def terms(value, count):
    parts = []
    for unused in range(count):
        parts.append(value.astype(bf16))
        value = value - parts[-1].astype(f32)
    return parts


def nn_left(value, ones, count):
    return sum(nn(part, ones) for part in terms(value, count))


def nn_right(ones, value, count):
    return sum(nn(ones, part) for part in terms(value, count))


def iota(shape, dim):
    return lax.broadcasted_iota(jnp.int32, shape, dim)


def head_spread():
    row = iota((LANES, DS), 0)
    return (iota((LANES, DS), 1) // SSM_DIM == row).astype(f32).astype(bf16)


def head_sum_matrix():
    col = iota((DS, LANES), 1)
    return (iota((DS, LANES), 0) // SSM_DIM == col).astype(f32).astype(bf16)


def extents():
    along = lax.axis_size(SEQ)
    return {
        "x": (1, 2),
        "z": (2, along // 2),
        "core": (along, 2),
        "y": (2 * along, lax.axis_size("y")),
    }


def my_index():
    return lax.axis_index(AXES)


def place_on(group):
    unit, size = extents()[group]
    return (my_index() // unit) % size


def swap(array, mask):
    count = lax.axis_size(AXES)
    return lax.ppermute(array, AXES, [(i, i ^ mask) for i in range(count)])


def in_order(pieces, place):
    pieces = list(pieces)
    bit = 1
    while bit < len(pieces):
        flag = (place // bit) % 2 == 1
        pieces = [jnp.where(flag, pieces[j ^ bit], pieces[j]) for j in range(len(pieces))]
        bit *= 2
    return pieces


def collect(array, group, axis):
    unit, size = extents()[group]
    pieces = [array] + [swap(array, k * unit) for k in range(1, size)]
    return jnp.stack(in_order(pieces, place_on(group)), axis)


def gather_pair(full, first):
    if first == "y":
        full = collect(collect(full, "y", 0), "x", 2)
    else:
        full = collect(collect(full, "x", 1), "y", 0)
    other = swap(full, extents()["core"][0])
    shape = (full.shape[0], full.shape[1] * full.shape[2] * full.shape[3], full.shape[4])
    return full.reshape(shape), other.reshape(shape)


def cut(total, group, axis):
    size = extents()[group][1]
    place = place_on(group)
    keep = lax.dynamic_index_in_dim(total, place, axis, False)
    parts = [lax.dynamic_index_in_dim(total, place ^ k, axis, False) for k in range(1, size)]
    return keep, [p.astype(bf16) for p in parts]


def crossed(parts, group):
    unit = extents()[group][0]
    return [swap(part, (k + 1) * unit) for k, part in enumerate(parts)]


def joined(keep, received):
    total = keep.astype(f32)
    for part in received:
        total = total + part.astype(f32)
    return total


class Reduction:
    def __init__(self, total, rows, first):
        table = extents()
        self.total = total.reshape(
            table["y"][1], table["z"][1], table["x"][1], rows, total.shape[-1]
        )
        order = [("x", 2), ("y", 0)] if first == "x" else [("y", 0), ("x", 1)]
        self.stages = order + [("z", 0)]

    def send(self):
        (group, axis), self.stages = self.stages[0], self.stages[1:]
        self.keep, self.parts = cut(self.total, group, axis)
        self.received = crossed(self.parts, group)
        return self.parts

    def receive(self, *others):
        self.received = after(self.received, *others)
        self.total = joined(self.keep, self.received)
        return self.total


def after(value, *others):
    return lax.optimization_barrier((value, others))[0]


def gather_small(vector):
    full = collect(collect(collect(vector, "z", 0), "x", 1), "core", 0)
    return collect(full, "y", 0).reshape(-1, vector.shape[-1])


def dealt(array, axes):
    return lax.all_to_all(array, axes, 0, 0, tiled=True)


def shared(array, axes):
    return dealt(jnp.broadcast_to(array[None], (lax.axis_size(axes), *array.shape)), axes)


def shifted(array, by):
    count = lax.axis_size(SEQ)
    pairs = [(i, i + by) for i in range(count) if 0 <= i + by < count]
    return lax.ppermute(array, SEQ, pairs)


def link(earlier, later):
    carry = later[1]
    wide = jnp.repeat(carry[0, :SSM_HEADS], SSM_DIM)[:, None]
    return (later[0] + wide * earlier[0], carry * earlier[1])


class Carrying:
    def __init__(self, state, carry, back, sign):
        self.pair, self.back, self.sign, self.by = (state, carry), back, sign, 0

    def send(self):
        packed = jnp.concatenate(
            [self.pair[0], jnp.pad(self.pair[1], ((0, RIM - 1), (0, 0)))], 0
        ).astype(bf16)
        steps = [self.by] if self.by else [1] + [2] * (self.back > 1)
        self.got = [shifted(packed, self.sign * by) for by in steps]
        return packed

    def receive(self, *others):
        pairs = []
        for got in after(self.got, *others):
            got = got.astype(f32)
            pairs.append((got[:DS], got[DS : DS + 1]))
        self.by = 2 * self.by if self.by else min(self.back, 2)
        if len(pairs) == 2:
            self.pair = link(pairs[1], pairs[0])
        else:
            self.pair = link(pairs[0], self.pair) if self.by > 2 else pairs[0]
        return self.pair[0] if self.by >= self.back else None


def halves(block, core):
    width = block.shape[1] // 2
    low, high = block[:, :width], block[:, width:]
    return jnp.where(core == 0, low, high), jnp.where(core == 0, high, low)


def put(ref, y, own, other, core):
    width = own.shape[1]
    base = y * 2 * width
    ref[:, base : base + width] = jnp.where(core == 0, own, other).astype(ref.dtype)
    ref[:, base + width : base + 2 * width] = jnp.where(core == 0, other, own).astype(ref.dtype)


def sides(ref, core, count):
    width = ref.shape[-1] // count
    return [halves(ref[:, y * width : (y + 1) * width], core) for y in range(count)]


def cross_half(value):
    lane = iota(value.shape, 1) % HEAD_DIM
    up = pltpu.roll(value, LANES - HEAD_DIM // 2, 1)
    down = pltpu.roll(value, HEAD_DIM // 2, 1)
    return jnp.where(lane < HEAD_DIM // 2, up, down)


def turned(value, cos, sin):
    return value * cos + cross_half(value) * sin


def turned_back(value, cos, sin):
    return value * cos - cross_half(value) * sin


def split_heads(pair, which, lane):
    flipped = pltpu.roll(pair, HEAD_DIM, 1)
    if which == 0:
        return jnp.where(lane < HEAD_DIM, pair, 0.0), jnp.where(lane < HEAD_DIM, flipped, 0.0)
    return jnp.where(lane >= HEAD_DIM, flipped, 0.0), jnp.where(lane >= HEAD_DIM, pair, 0.0)


def join_heads(even, odd, which, lane):
    if which == 0:
        return jnp.where(lane < HEAD_DIM, even, pltpu.roll(odd, HEAD_DIM, 1))
    return jnp.where(lane < HEAD_DIM, pltpu.roll(even, HEAD_DIM, 1), odd)


def conv_taps(chan_ref, cols, off):
    ext = chan_ref[:, cols].astype(f32)
    taps = []
    for i in range(CONV):
        back = CONV - 1 - i
        rows = pltpu.roll(ext, back, 0)[RIM:] if back else ext[RIM:]
        taps.append(rows * (off >= back).astype(f32))
    return taps


def sigmoid(v):
    return 1.0 / (1.0 + jnp.exp(-v))


def softplus(v):
    return jnp.maximum(v, 0.0) + jnp.log1p(jnp.exp(-jnp.abs(v)))


def tail_of(cum, off):
    rows = cum.shape[0]
    last_off = off[rows - 1 :, :]
    keep = iota((rows, 1), 0) >= rows - 1 - last_off
    return jnp.exp(cum[rows - 1 :, :] - cum) * keep.astype(f32)


def fade_of(cum, off):
    keep = off > iota((cum.shape[0], 1), 0)
    return jnp.exp(cum) * keep.astype(f32)


def carry_of(cum, off):
    rows = cum.shape[0]
    return jnp.exp(cum[rows - 1 :, :]) * (off[rows - 1 :, :] >= rows).astype(f32)


def pack_kernel(
    gu_ref, inner_ref, ao_ref, so_ref, down_ref, kv_ref, q_ref, post_ref, front_ref
):
    part, width = gu_ref.shape[0], down_ref.shape[1]
    a_rows = ao_ref.shape[0]
    post_ref[:part, :] = inner_ref[:, :width]
    post_ref[part : 2 * part, : DS - width] = inner_ref[:, width:DS]
    for k in range(2):
        rows = slice(part + k * a_rows, part + (k + 1) * a_rows)
        post_ref[rows, DS - width :] = ao_ref[:, k * 512 : (k + 1) * 512]
    at = 2 * part
    post_ref[at : at + so_ref.shape[0], :] = so_ref[...]
    at += so_ref.shape[0]
    for k in range(gu_ref.shape[1] // width):
        post_ref[at : at + part, :] = gu_ref[:, k * width : (k + 1) * width]
        at += part
    post_ref[at:, :] = down_ref[...]
    front_ref[:, :256] = kv_ref[...]
    front_ref[:, 256:768] = q_ref[...]
    front_ref[:, 768:1024] = inner_ref[:, 2 * DS : DS + CONV_CH]
    front_ref[:, 1024:A_COLS] = jnp.zeros((part, LANES), bf16)
    front_ref[:, 1024 : 1024 + SSM_HEADS] = inner_ref[:, DS + CONV_CH :]
    front_ref[:, A_COLS:] = inner_ref[:, DS : 2 * DS]


def front_kernel(
    core_ref, tok_ref, gain_ref, wa_own, wa_oth, wb_own, wb_oth, cos_ref, sin_ref, off_ref,
    cw_ref, cb_ref, sb_ref, dec_ref,
    q8_ref, kv_ref, normed_ref, nrim_ref, chan_ref, x_ref, bc_ref, step_ref, cum_ref, cumt_ref, z_ref,
    state_ref, carry_ref,
    n_ref, xt_ref,
):
    core = core_ref[0]
    rows = cos_ref.shape[0]
    tok = tok_ref[...].astype(f32)
    rms = lax.rsqrt(jnp.mean(tok * tok, axis=1, keepdims=True) + EPS)
    n_ref[...] = (tok * rms * gain_ref[...]).astype(bf16)
    normed_ref[...] = n_ref[RIM:, :]
    nrim_ref[...] = n_ref[:RIM, :]
    count = wa_own.shape[0]
    blocks = sides(n_ref, core, count)

    def project(own_ref, oth_ref, cols):
        total = 0.0
        for y, (own, oth) in enumerate(blocks):
            total = total + nn(own, own_ref[y, :, cols]) + nn(oth, oth_ref[y, :, cols])
        return total

    lane = iota((rows, LANES), 1)
    cos, sin, off = cos_ref[...], sin_ref[...], off_ref[...]
    kv = project(wa_own, wa_oth, pl.ds(0, 256))[RIM:]
    kv_ref[:, :LANES] = turned(kv[:, :LANES], cos, sin).astype(bf16)
    kv_ref[:, LANES:] = kv[:, LANES:].astype(bf16)
    queries = project(wa_own, wa_oth, pl.ds(256, 512))[RIM:]
    for j in range(HEADS // 2):
        pair = turned(queries[:, j * LANES : (j + 1) * LANES], cos, sin)
        even, odd = split_heads(pair, j // 2, lane)
        q8_ref[2 * j] = even.astype(bf16)
        q8_ref[2 * j + 1] = odd.astype(bf16)
    rest = project(wa_own, wa_oth, pl.ds(768, 384))
    chan_ref[:, DS:] = rest[:, : 2 * STATE].astype(bf16)
    z = rest[RIM:, 2 * STATE :].astype(bf16).astype(f32) + sb_ref[...]
    for j in range(DS // 512):
        cols = slice(j * 512, (j + 1) * 512)
        chan_ref[:, cols] = project(wb_own, wb_oth, pl.ds(j * 512, 512)).astype(bf16)
    z_ref[...] = z
    step = softplus(z)
    step_ref[...] = step
    tri = (iota((rows, rows), 0) >= iota((rows, rows), 1)).astype(f32).astype(bf16)
    cum = nn_right(tri, -step * dec_ref[...], 3)
    cum_ref[...] = cum
    cumt_ref[...] = cum.T
    carry_ref[...] = carry_of(cum, off)
    weight = nn_left(step * tail_of(cum, off), head_spread(), 2)
    for j in range(CONV_CH // 256):
        cols = slice(j * 256, (j + 1) * 256)
        mixed = cb_ref[:, cols]
        for i, tap in enumerate(conv_taps(chan_ref, cols, off)):
            mixed = mixed + tap * cw_ref[i : i + 1, cols]
        active = mixed * sigmoid(mixed)
        if j < DS // 256:
            x_ref[:, cols] = active
            xt_ref[:, cols] = (active * weight[:, cols]).astype(bf16)
        else:
            bc_ref[...] = active
    state_ref[...] = tn(xt_ref[...], bc_ref[:, :STATE].astype(bf16))


def scan_masks(off, rows):
    t, s = iota((rows, rows), 0), iota((rows, rows), 1)
    return (s <= t) & (s >= t - off)


def scan_kernel(x_ref, bc_ref, step_ref, cum_ref, cumt_ref, off_ref, y_ref, xw_ref, ce_ref):
    rows = x_ref.shape[0]
    spread = head_spread()
    xw_ref[...] = (x_ref[...] * nn_left(step_ref[...], spread, 2)).astype(bf16)
    ce_ref[...] = nn_left(cum_ref[...], spread, 3)
    keys, reads = bc_ref[:, :STATE].astype(bf16), bc_ref[:, STATE:].astype(bf16)
    scores = jnp.where(scan_masks(off_ref[...], rows), nt(reads, keys), 0.0)
    lane = iota((rows, LANES), 1)

    def pair(j, unused):
        cols = pl.ds(pl.multiple_of(j * LANES, LANES), LANES)
        wide = ce_ref[:, cols]
        xw = xw_ref[:, cols]
        outs = []
        for k in range(2):
            late = wide[:, k * SSM_DIM : k * SSM_DIM + 1]
            early = cumt_ref[pl.ds(2 * j + k, 1), :]
            decay = jnp.exp(jnp.minimum(late - early, 0.0))
            outs.append(nn((decay * scores).astype(bf16), xw))
        y_ref[:, cols] = jnp.where(lane < SSM_DIM, outs[0], outs[1])
        return unused

    lax.fori_loop(0, SSM_HEADS // 2, pair, 0)


def attend_bias(off, rows, window):
    query = iota((rows, window), 0) + (window - rows)
    key = iota((rows, window), 1)
    return jnp.where((key <= query) & (key >= query - off), 0.0, NEG)


def window_of(count, rank, kv_ref, k_ref, v_ref):
    rows = kv_ref.shape[1]
    for i in range(count):
        piece = jnp.maximum(rank - (count - 1 - i), 0)
        k_ref[i * rows : (i + 1) * rows, :] = kv_ref[piece, :, :LANES]
        v_ref[i * rows : (i + 1) * rows, :] = kv_ref[piece, :, LANES:]


def attend_kernel(
    count, rank_ref, q8_ref, kv_ref, off_ref, att_ref, lse_ref, k_ref, v_ref, bias_ref, o_ref
):
    rows = off_ref.shape[0]
    window = count * rows
    window_of(count, rank_ref[0], kv_ref, k_ref, v_ref)
    bias_ref[...] = attend_bias(off_ref[...], rows, window)
    lane = iota((rows, LANES), 1)

    def head(h, lses):
        scores = nt(q8_ref[h], k_ref[...]) * HEAD_DIM**-0.5 + bias_ref[...]
        top = jnp.max(scores, axis=1, keepdims=True)
        probs = jnp.exp(scores - top)
        total = jnp.sum(probs, axis=1, keepdims=True)
        o_ref[h] = nn((probs * (1.0 / total)).astype(bf16), v_ref[...])
        return jnp.where(lane == h, top + jnp.log(total), lses)

    lse_ref[...] = lax.fori_loop(0, HEADS, head, jnp.zeros((rows, LANES), f32)).T
    for j in range(HEADS // 2):
        pair = join_heads(o_ref[2 * j], o_ref[2 * j + 1], j // 2, lane)
        att_ref[:, j * LANES : (j + 1) * LANES] = pair.astype(bf16)


def attend_back_kernel(
    count, rank_ref, q8_ref, kv_ref, off_ref, lse_ref, datt_ref, cos_ref, sin_ref,
    dq_ref, out_ref, k_ref, v_ref, bias_ref, do_ref, dq8_ref, dkv_ref,
):
    rows = off_ref.shape[1]
    window = count * rows
    rank = rank_ref[0]
    window_of(count, rank, kv_ref, k_ref, v_ref)
    query = iota((window, rows), 1) + (window - rows)
    key = iota((window, rows), 0)
    bias_ref[...] = jnp.where((key <= query) & (key >= query - off_ref[...]), 0.0, NEG)
    lane = iota((rows, LANES), 1)
    for j in range(HEADS // 2):
        pair = datt_ref[:, j * LANES : (j + 1) * LANES].astype(f32)
        even, odd = split_heads(pair, j // 2, lane)
        do_ref[2 * j] = even.astype(bf16)
        do_ref[2 * j + 1] = odd.astype(bf16)
    dkv_ref[...] = jnp.zeros(dkv_ref.shape, f32)

    def head(h, unused):
        query, grad = q8_ref[h], do_ref[h]
        scores = nt(k_ref[...], query) * HEAD_DIM**-0.5 + bias_ref[...]
        probs = jnp.exp(scores - lse_ref[pl.ds(h, 1), :])
        dprobs = nt(v_ref[...], grad)
        mean = jnp.sum(probs * dprobs, axis=0, keepdims=True)
        draw = (probs * (dprobs - mean) * HEAD_DIM**-0.5).astype(bf16)
        dkv_ref[:, :LANES] += nn(draw, query)
        dkv_ref[:, LANES:] += nn(probs.astype(bf16), grad)
        dq8_ref[h] = tn(draw, k_ref[...])
        return unused

    lax.fori_loop(0, HEADS, head, 0)
    out_ref[...] = jnp.zeros(out_ref.shape, bf16)
    for i in range(count):
        piece = rank - (count - 1 - i)

        @pl.when(piece >= 0)
        def unused():
            out_ref[piece] = dkv_ref[i * rows : (i + 1) * rows, :].astype(bf16)

    for j in range(HEADS // 2):
        pair = join_heads(dq8_ref[2 * j], dq8_ref[2 * j + 1], j // 2, lane)
        back = turned_back(pair, cos_ref[...], sin_ref[...])
        dq_ref[:, j * LANES : (j + 1) * LANES] = back.astype(bf16)


class PackedWeights:
    def __init__(self, source, core, held, sems, parts):
        self.held = held
        part, a_part, s_part, f_part = self.parts = parts
        self.so_at = 2 * part
        self.gu_at = self.so_at + s_part
        self.down_at = self.gu_at + 4 * part
        ends = [0, self.so_at, self.gu_at, self.down_at + f_part]
        self.copies = []
        for k in range(3):
            rows = pl.ds(ends[k], ends[k + 1] - ends[k])
            self.copies.append(
                [
                    pltpu.make_async_copy(
                        source.at[:, lax.rem(core + i, 2), :, rows],
                        held.at[i, :, :, rows],
                        sems.at[k, i],
                    )
                    for i in range(2)
                ]
            )
        for pair in self.copies:
            for copy in pair:
                copy.start()

    def wait(self, k):
        for copy in self.copies[k]:
            copy.wait()

    def block(self, i, y, start, size, col):
        rows, cols = pl.ds(pl.multiple_of(start, 16), size), pl.ds(pl.multiple_of(col, 512), 512)
        got = self.held[i, y, :, rows, cols]
        return got.reshape(got.shape[0] * size, 512)

    def gate(self, i, y, j):
        part = self.parts[0]
        return self.block(i, y, j // 2 * part, part, j % 2 * 512)

    def ao(self, i, y, j):
        part, a_part = self.parts[:2]
        return self.block(i, y, part + j * a_part, a_part, 512)

    def so(self, i, y, j):
        return self.block(i, y, self.so_at, self.parts[2], j * 512)

    def down(self, i, y, j):
        return self.block(i, y, self.down_at, self.parts[3], j * 512)

    def gu(self, i, y, j):
        part = self.parts[0]
        return self.block(i, y, self.gu_at + j // 2 * part, part, j % 2 * 512)


class PlainWeights:
    def __init__(self, refs):
        self.refs = refs

    def wait(self, k):
        pass

    def block(self, name, i, y, j):
        return self.refs[2 * name + i][y, :, pl.ds(pl.multiple_of(j * 512, 512), 512)]

    def gate(self, i, y, j):
        return self.block(0, i, y, j)

    def ao(self, i, y, j):
        return self.block(1, i, y, j)

    def so(self, i, y, j):
        return self.block(2, i, y, j)

    def down(self, i, y, j):
        return self.block(3, i, y, j)

    def gu(self, i, y, j):
        return self.refs[8 + i][y, :, pl.ds(pl.multiple_of(j * 512, 512), 512)]


def post_kernel(
    parts, ys, core_ref, tok_ref, cot_ref, att_ref, yl_ref, x_ref, bc_ref, cum_ref, off_ref,
    entry_ref, skip_ref, normed_ref, gssm_ref, gffn_ref, *refs,
):
    if parts:
        weights = PackedWeights(refs[0], core_ref[0], refs[-2], refs[-1], parts)
        refs = refs[1:-2]
    else:
        weights, refs = PlainWeights(refs[:10]), refs[10:]
    pairs = [(i, y) for y in range(ys) for i in range(2)]

    def through(blocks, weight, j):
        return sum(nn(blocks[y][i], weight(i, y, j)) for i, y in pairs)

    def back_through(ref, grad, weight, count):
        for y in range(ys):
            both = []
            for i in range(2):
                both.append(
                    sum(nt(grad[:, j * 512 : j * 512 + 512], weight(i, y, j)) for j in range(count))
                )
            put(ref, y, both[0], both[1], core)

    (
        out_ref, dmid_ref, datt_ref, dssd_ref, ycore_ref, dentry_ref, send_ref, keep_ref, dng_ref,
        gi_ref, gd_ref, mid_ref, gu_ref, dn_ref, dmx_ref, fd_ref, n2_ref, hid_ref, mixed_ref, dh_ref, fade_ref, ent_ref,
    ) = refs
    core = core_ref[0]
    rows, width = tok_ref.shape
    heads_width = att_ref.shape[1]
    ff = hid_ref.shape[1]
    half = keep_ref.shape[1]
    cot_at, dbr_at, dgate_at, sel_at = 2 * ff, 2 * ff + width, 2 * ff + 2 * width, 2 * ff + 2 * width + DS
    reads = bc_ref[:, STATE:].astype(bf16)
    spread = head_spread()
    fade_ref[...] = nn_left(fade_of(cum_ref[...], off_ref[...]), spread, 2)
    ent_ref[...] = nt(reads, entry_ref[...].astype(bf16))
    none = jnp.zeros((rows, 1), f32)

    def at(j, first=0):
        return pl.ds(pl.multiple_of(first + j * 512, 512), 512)

    weights.wait(0)
    blocks = sides(normed_ref, core, ys)

    def gates(j, square):
        cols = at(j)
        gate = through(blocks, weights.gate, j).astype(bf16).astype(f32)
        gi_ref[:, cols] = gate
        ycore = yl_ref[:, cols] + fade_ref[:, cols] * ent_ref[:, cols]
        ycore_ref[:, cols] = ycore
        ssd = ycore + skip_ref[:, cols] * x_ref[:, cols]
        gated = ssd * gate * sigmoid(gate)
        gd_ref[:, cols] = gated
        return square + jnp.sum(gated * gated, axis=1, keepdims=True)

    square = lax.fori_loop(0, DS // 512, gates, none, unroll=True)
    rms_gate = lax.rsqrt(square / DS + EPS)
    mixed_ref[...] = (gd_ref[...] * rms_gate * gssm_ref[...]).astype(bf16)
    weights.wait(1)
    att_blocks, mix_blocks = sides(att_ref, core, ys), sides(mixed_ref, core, ys)

    def branches(j, square):
        branch = through(att_blocks, weights.ao, j) + through(mix_blocks, weights.so, j)
        middle = tok_ref[:, at(j)].astype(f32) + branch
        mid_ref[:, at(j)] = middle
        return square + jnp.sum(middle * middle, axis=1, keepdims=True)

    square = lax.fori_loop(0, width // 512, branches, none, unroll=True)
    rms = lax.rsqrt(square / width + EPS)
    n2_ref[...] = (mid_ref[...] * rms * gffn_ref[...]).astype(bf16)
    weights.wait(2)
    ups = sides(n2_ref, core, ys)

    def up(j, unused):
        gu_ref[:, at(j)] = through(ups, weights.gu, j)
        return unused

    lax.fori_loop(0, 2 * ff // 512, up, 0)

    def hide(j, unused):
        gate = gu_ref[:, at(j)]
        hid_ref[:, at(j)] = (gate * sigmoid(gate) * gu_ref[:, at(j, ff)]).astype(bf16)
        return unused

    lax.fori_loop(0, ff // 512, hide, 0)
    hids = sides(hid_ref, core, ys)

    def finals(j, unused):
        out_ref[:, at(j)] = (mid_ref[:, at(j)] + through(hids, weights.down, j)).astype(bf16)
        return unused

    lax.fori_loop(0, width // 512, finals, 0, unroll=True)
    cot = cot_ref[...]
    back_through(dh_ref, cot, weights.down, 2)

    def unhide(j, unused):
        gate, lift, dhid = gu_ref[:, at(j)], gu_ref[:, at(j, ff)], dh_ref[:, at(j)]
        sg = sigmoid(gate)
        dgate = dhid * lift * (sg * (1.0 + gate * (1.0 - sg)))
        send_ref[:, at(j)] = dgate.astype(bf16)
        send_ref[:, at(j, ff)] = (dhid * gate * sg).astype(bf16)
        return unused

    lax.fori_loop(0, ff // 512, unhide, 0)
    send_ref[:, cot_at:dbr_at] = cot
    wide = width // ys // 2

    def down(j, totals):
        grad = send_ref[:, pl.ds(pl.multiple_of(j * 512, 512), 512)]
        return [t + nt(grad, weights.gu(i, y, j)) for t, (i, y) in zip(totals, pairs)]

    zero = [jnp.zeros((rows, wide), f32)] * len(pairs)
    totals = lax.fori_loop(0, 2 * ff // 512, down, zero)
    for y in range(ys):
        put(dn_ref, y, totals[2 * y], totals[2 * y + 1], core)
    unit = mid_ref[...] * rms
    dn = dn_ref[...]
    dn = dn * gffn_ref[...]
    dmid = cot.astype(f32) + rms * (dn - unit * jnp.mean(dn * unit, axis=1, keepdims=True))
    dmid_ref[...] = dmid
    dbr = dmid.astype(bf16)
    send_ref[:, dbr_at:dgate_at] = dbr
    back_through(datt_ref, dbr, weights.ao, 2)
    back_through(dmx_ref, dbr, weights.so, 2)

    def means(j, mean):
        unit = gd_ref[:, at(j)] * rms_gate
        return mean + jnp.sum(dmx_ref[:, at(j)] * gssm_ref[:, at(j)] * unit, axis=1, keepdims=True)

    mean = lax.fori_loop(0, DS // 512, means, none) / DS

    def ungate(j, unused):
        cols = at(j)
        unit = gd_ref[:, cols] * rms_gate
        dgated = rms_gate * (dmx_ref[:, cols] * gssm_ref[:, cols] - unit * mean)
        gate = gi_ref[:, cols]
        sg = sigmoid(gate)
        ssd = ycore_ref[:, cols] + skip_ref[:, cols] * x_ref[:, cols]
        dssd = dgated * gate * sg
        dssd_ref[:, cols] = dssd
        dgate = (dgated * ssd * (sg * (1.0 + gate * (1.0 - sg)))).astype(bf16)
        send_ref[:, at(j, dgate_at)] = dgate
        fd_ref[:, cols] = (dssd * fade_ref[:, cols]).astype(bf16)
        return unused

    lax.fori_loop(0, DS // 512, ungate, 0)
    back_through(dng_ref, send_ref[:, dgate_at:sel_at], weights.gate, 3)
    dentry_ref[...] = tn(fd_ref[...], reads)
    to = 0
    for ref in (n2_ref, hid_ref, att_ref, mixed_ref, normed_ref):
        count = ys
        wide = ref.shape[1] // count
        for y in range(count):
            own, oth = halves(ref[:, y * wide : (y + 1) * wide], core)
            keep_ref[:, to : to + wide // 2] = own
            send_ref[:, sel_at + to : sel_at + to + wide // 2] = oth
            to += wide // 2


def products_kernel(plan, extra, keep_ref, own_ref, act_ref, *refs):
    got_ref, outs = act_ref, refs
    if extra:
        (extra_ref, *outs) = refs
    for which, a_at, act_at, size, g_at in plan:
        out = outs[which]
        for y in range(out.shape[0]):
            left = keep_ref[:, a_at + y * size : a_at + (y + 1) * size]
            right = act_ref[:, act_at + y * size : act_at + (y + 1) * size]
            for j in range(0, out.shape[-1], 512):
                stop = min(j + 512, out.shape[-1])
                total = tn(left, own_ref[:, g_at + j : g_at + stop])
                total = total + tn(right, got_ref[:, g_at + j : g_at + stop])
                if extra and which == 0 and stop == out.shape[-1]:
                    total = total + extra_ref[y]
                out[y, :, j:stop] = total.astype(bf16)


def split_products_kernel(plan, extra, y_ref, x_ref, keep_ref, own_ref, act_ref, *refs):
    got_ref, outs = act_ref, refs
    if extra:
        (extra_ref, *outs) = refs
    xkeep_ref, xsend_ref, ykeep_ref, ysend_ref = outs
    my_y, my_x = y_ref[0], x_ref[0]
    for kind, place, a_at, act_at, size, g_at, wide in plan:
        for k in range(2):
            y = k if kind == "x" else lax.rem(my_y + k, 2)
            left = keep_ref[:, pl.ds(pl.multiple_of(a_at + y * size, LANES), size)]
            right = act_ref[:, pl.ds(pl.multiple_of(act_at + y * size, LANES), size)]
            keep, send = (xkeep_ref, xsend_ref) if kind == "x" else (ykeep_ref, ysend_ref)
            block = 512 if wide % 512 == 0 else 384

            def columns(j, unused):
                at = pl.ds(pl.multiple_of(g_at + j * block, LANES), block)
                total = tn(left, own_ref[:, at]) + tn(right, got_ref[:, at])
                if kind == "x":
                    zs, each = keep.shape[1], keep.shape[2]
                    if extra:
                        total = total + extra_ref[k] * (j == wide // block - 1).astype(f32)
                    cols = pl.ds(pl.multiple_of(place + j * block, LANES), block)
                    total = total.reshape(zs, 2, each, block)
                    low, high = total[:, 0], total[:, 1]
                    keep[k, :, :, cols] = jnp.where(my_x == 0, low, high).astype(bf16)
                    send[k, :, :, cols] = jnp.where(my_x == 0, high, low).astype(bf16)
                else:
                    count = keep.shape[0]
                    each = size // count
                    cols = pl.ds(pl.multiple_of(j * block, LANES), block)
                    total = total.reshape(count, each, block).astype(bf16)
                    (send if k else keep)[:, place : place + each, cols] = total
                return unused

            lax.fori_loop(0, wide // block, columns, 0, unroll=True)


def fold_one_kernel(
    y_ref, x_ref, xkeep_ref, xgot_ref, ykeep_ref, ygot_ref,
    xkeep_out, xsend_out, ykeep_out, ysend_out,
):
    my_y, my_x = y_ref[0], x_ref[0]
    xkeep_out[...] = xkeep_ref[my_y].astype(f32) + xgot_ref[my_y].astype(f32)
    other = 1 - my_y
    xsend_out[...] = (xkeep_ref[other].astype(f32) + xgot_ref[other].astype(f32)).astype(bf16)
    for z in range(ykeep_out.shape[0]):
        at = 2 * z + my_x
        ykeep_out[z] = ykeep_ref[at].astype(f32) + ygot_ref[at].astype(f32)
        at = 2 * z + 1 - my_x
        ysend_out[z] = (ykeep_ref[at].astype(f32) + ygot_ref[at].astype(f32)).astype(bf16)


def laid(refs, width):
    at = 0
    for ref in refs:
        each = ref.shape[-2]
        for j in range(ref.shape[-1] // width):
            yield ref, at, j * width
            at += each


def fold_two_kernel(xkeep_ref, xgot_ref, ykeep_ref, ygot_ref, out_ref):
    width = out_ref.shape[2]
    keeps = laid((xkeep_ref, ykeep_ref), width)
    gots = laid((xgot_ref, ygot_ref), width)
    for (keep, at, col), (got, *unused) in zip(keeps, gots):
        each = keep.shape[-2]
        value = keep[:, :, col : col + width] + got[:, :, col : col + width].astype(f32)
        out_ref[:, at : at + each, :] = value.astype(bf16)


def fold_three_kernel(got_ref, *outs):
    width = got_ref.shape[2]
    for out, at, col in laid(outs, width):
        rows = slice(at, at + out.shape[0])
        total = got_ref[0, rows, :].astype(f32)
        for z in range(1, got_ref.shape[0]):
            total = total + got_ref[z, rows, :].astype(f32)
        out[:, col : col + width] = total


def row_sums(value):
    ones = jnp.ones((8, value.shape[1]), bf16)
    return sum(nt(ones, part) for part in terms(value, 3))[:1]


def summed(got_ref, rows):
    total = got_ref[0, rows, :].astype(f32)
    for z in range(1, got_ref.shape[0]):
        total = total + got_ref[z, rows, :].astype(f32)
    return total


def finish_post_kernel(
    got_ref, one_ref, guw_ref, sow_ref, gffn_ref, gssm_ref,
    gu_ref, gate_ref, ao_ref, so_ref, dffn_ref, dssm_ref,
):
    part, ups = one_ref.shape
    wide = got_ref.shape[2]
    gu_ref[:, :ups] = one_ref[...]
    at = 0
    for out, start in ((gu_ref, ups), (gate_ref, 0)):
        for col in range(start, out.shape[1], wide):
            out[:, col : col + wide] = summed(got_ref, slice(at, at + part))
            at += part
    for col in range(0, ao_ref.shape[1], wide):
        for out in (ao_ref, so_ref):
            out[:, col : col + wide] = summed(got_ref, slice(at, at + out.shape[0]))
            at += out.shape[0]
    dffn_ref[...] = row_sums(guw_ref[...].astype(f32) * gu_ref[...]) / gffn_ref[...]
    dssm_ref[...] = row_sums(sow_ref[...].astype(f32) * so_ref[...]) / gssm_ref[...]


def finish_front_kernel(
    got_ref, gate_ref, kvw_ref, qw_ref, iw_ref, gain_ref,
    kv_ref, q_ref, inner_ref, conv_ref, bias_ref, log_ref, step_ref, skip_ref, dgain_ref,
):
    part, wide = kv_ref.shape[0], got_ref.shape[2]
    count = A_COLS // wide
    blocks = [summed(got_ref, slice(k * part, (k + 1) * part)) for k in range(count)]
    first = jnp.concatenate(blocks, axis=1)
    kv_ref[...] = first[:, :256]
    q_ref[...] = first[:, 256:768]
    inner_ref[:, :DS] = gate_ref[...]
    for k in range(DS // wide):
        rows = slice((count + k) * part, (count + k + 1) * part)
        inner_ref[:, DS + k * wide : DS + (k + 1) * wide] = summed(got_ref, rows)
    last = first[:, 1024:]
    inner_ref[:, 2 * DS : 2 * DS + 2 * STATE] = first[:, 768:1024]
    inner_ref[:, DS + CONV_CH :] = last[:, :SSM_HEADS]
    turned_last = last.T
    own = bias_ref.shape[1]
    conv_ref[...] = turned_last[SSM_HEADS : SSM_HEADS + own, :CONV]
    bias_ref[...] = last[CONV : CONV + 1, SSM_HEADS : SSM_HEADS + own]
    for k, out in enumerate((log_ref, step_ref, skip_ref)):
        out[...] = last[CONV + 1 + k : CONV + 2 + k, SSM_HEADS : 2 * SSM_HEADS]
    total = row_sums(kvw_ref[...].astype(f32) * kv_ref[...])
    total = total + row_sums(qw_ref[...].astype(f32) * q_ref[...])
    total = total + row_sums(iw_ref[...].astype(f32) * inner_ref[...])
    dgain_ref[...] = total / gain_ref[...]


class PairReduction:
    def __init__(self, pieces, width):
        self.places = tuple(place_on(g).reshape(1).astype(jnp.int32) for g in ("y", "x"))
        self.xkeep, xsend, self.ykeep, ysend = pieces
        self.width = width
        self.send(xsend, ysend, "x", "y")

    def send(self, xsend, ysend, first, second):
        self.sent = (xsend, ysend)
        self.gots = (
            swap(xsend, extents()[first][0]), swap(ysend, extents()[second][0])
        )

    def fold_one(self, *others):
        gots = after(self.gots, *others)
        x, y = self.xkeep.shape, self.ykeep.shape
        x, y = x[1:], (y[0] // 2, *y[1:])
        self.xkeep, xsend, self.ykeep, ysend = run(
            fold_one_kernel, "fold_one", [(x, f32), (x, bf16), (y, f32), (y, bf16)],
            (*self.places, self.xkeep, gots[0], self.ykeep, gots[1]),
            scalars=2,
        )
        self.send(xsend, ysend, "y", "x")

    def fold_two(self, *others):
        gots = after(self.gots, *others)
        self.shapes = [self.xkeep.shape[1:], self.ykeep.shape[1:]]
        rows = sum(r * c // self.width for r, c in self.shapes)
        zs = self.xkeep.shape[0]
        self.sent = run(
            fold_two_kernel, "fold_two", [((zs, rows, self.width), bf16)],
            (self.xkeep, gots[0], self.ykeep, gots[1]),
        )[0]
        self.gots = dealt(self.sent, "z")

    def fold_three(self, *others):
        gots = after(self.gots, *others)
        self.sent = run(
            fold_three_kernel, "fold_three", [(shape, f32) for shape in self.shapes], (gots,),
        )
        return self.sent


class PlainReduction:
    def __init__(self, pieces, rows):
        self.parts = [Reduction(pieces[0], rows[0], "x"), Reduction(pieces[1], rows[1], "y")]
        self.sent = [part.send() for part in self.parts]

    def fold_one(self, *others):
        for part in self.parts:
            part.receive(*others)
        self.sent = [part.send() for part in self.parts]

    fold_two = fold_one

    def fold_three(self, *others):
        self.sent = [part.receive(*others) for part in self.parts]
        return self.sent


def scan_back_kernel(
    dy_ref, x_ref, bc_ref, step_ref, cum_ref, cumt_ref, off_ref, dxw_ref, ds_ref,
    xw_ref, ce_ref, dyb_ref, dg_ref,
):
    rows = x_ref.shape[0]
    spread = head_spread()
    xw_ref[...] = (x_ref[...] * nn_left(step_ref[...], spread, 2)).astype(bf16)
    dyb_ref[...] = dy_ref[...].astype(bf16)
    ce_ref[...] = nn_left(cum_ref[...], spread, 3)
    keys, reads = bc_ref[:, :STATE].astype(bf16), bc_ref[:, STATE:].astype(bf16)
    early, late = iota((rows, rows), 0), iota((rows, rows), 1)
    keep = (early <= late) & (early >= late - off_ref[...])
    scores = jnp.where(keep, nt(keys, reads), 0.0)
    lane = iota((rows, LANES), 1)
    dg_ref[...] = jnp.zeros((rows, rows), f32)

    def pair(j, unused):
        cols = pl.ds(pl.multiple_of(j * LANES, LANES), LANES)
        wide = ce_ref[:, cols]
        xw, dy = xw_ref[:, cols], dyb_ref[:, cols]
        outs = []
        change = 0.0
        for k in range(2):
            first = wide[:, k * SSM_DIM : k * SSM_DIM + 1]
            second = cumt_ref[pl.ds(2 * j + k, 1), :]
            decay = jnp.exp(jnp.minimum(second - first, 0.0))
            outs.append(nn((decay * scores).astype(bf16), dy))
            mine = (lane < SSM_DIM) if k == 0 else (lane >= SSM_DIM)
            change = change + nt(xw * mine.astype(bf16), dy) * decay
        dg_ref[...] += change
        dxw_ref[:, cols] = jnp.where(lane < SSM_DIM, outs[0], outs[1])
        return unused

    lax.fori_loop(0, SSM_HEADS // 2, pair, 0)
    ds_ref[...] = jnp.where(keep, dg_ref[...], 0.0).astype(bf16)


def mixer_back_kernel(
    dy_ref, ycore_ref, x_ref, bc_ref, step_ref, cum_ref, z_ref, off_ref, entry_ref,
    down_ref, skip_ref, dec_ref, chan_ref, cw_ref, cb_ref, dxwl_ref, ds_ref,
    dext_ref, dz_ref, small_ref,
    dact_ref,
):
    rows = x_ref.shape[0]
    spread, gather = head_spread(), head_sum_matrix()
    off, cum = off_ref[...], cum_ref[...]
    step_wide = nn_left(step_ref[...], spread, 2)
    keys, reads = bc_ref[:, :STATE].astype(bf16), bc_ref[:, STATE:].astype(bf16)
    dscores = ds_ref[...]
    down = down_ref[...].astype(bf16)
    tail = nn_left(tail_of(cum, off), spread, 2)
    fade = nn_left(fade_of(cum, off), spread, 2)
    bd = nt(keys, down) * tail
    xw = (x_ref[...] * step_wide).astype(bf16).astype(f32)
    dxw = dxwl_ref[...] + bd
    dact_ref[:, DS : DS + STATE] = nn(dscores, reads) + nn((tail * xw).astype(bf16), down)
    dact_ref[:, DS + STATE :] = tn(dscores, keys) + nn(
        (fade * dy_ref[...]).astype(bf16), entry_ref[...].astype(bf16)
    )
    ones = jnp.ones((8, STATE), bf16)
    product = sum(nt(ones, part) for part in terms(down_ref[...] * entry_ref[...], 3))
    through = jnp.sum(xw * bd, axis=0, keepdims=True)
    direct = jnp.sum(dy_ref[...] * x_ref[...], axis=0, keepdims=True)
    row = iota((8, DS), 0)
    sums = jnp.where(row == 0, product, jnp.where(row == 1, through, direct))
    sums = nn_left(sums, gather, 3)
    through, kept = sums[1:2], sums[0:1] * carry_of(cum, off)
    last = (iota((rows, 1), 0) == rows - 1).astype(f32)
    dyb = dy_ref[...].astype(bf16).astype(f32)
    dcum = nn_left(dyb * ycore_ref[...] - xw * dxw, gather, 2) + last * (through + kept)
    tri = (iota((rows, rows), 0) <= iota((rows, rows), 1)).astype(f32).astype(bf16)
    dlog = nn_right(tri, dcum, 3)
    x = x_ref[...]
    step, dec = step_ref[...], dec_ref[...]
    dstep = nn_left(dxw * x, gather, 2) - dlog * dec
    dz = dstep * sigmoid(z_ref[...])
    dz_ref[...] = dz
    small_ref[...] = jnp.zeros(small_ref.shape, f32)
    small_ref[CONV + 1 : CONV + 2, :LANES] = jnp.sum(dlog * (-step * dec), axis=0, keepdims=True)
    small_ref[CONV + 1 : CONV + 2, LANES : 2 * LANES] = jnp.sum(dz, axis=0, keepdims=True)
    small_ref[CONV + 1 : CONV + 2, 2 * LANES : 3 * LANES] = sums[2:3]
    dact_ref[:, :DS] = dxw * step_wide + skip_ref[...] * dy_ref[...]
    for j in range(CONV_CH // 256):
        cols = slice(j * 256, (j + 1) * 256)
        taps = conv_taps(chan_ref, cols, off)
        mixed = cb_ref[:, cols]
        for i, tap in enumerate(taps):
            mixed = mixed + tap * cw_ref[i : i + 1, cols]
        sg = sigmoid(mixed)
        dmix = dact_ref[:, cols] * (sg * (1.0 + mixed * (1.0 - sg)))
        small_ref[CONV : CONV + 1, cols] = jnp.sum(dmix, axis=0, keepdims=True)
        total = 0.0
        for i, tap in enumerate(taps):
            back = CONV - 1 - i
            small_ref[i : i + 1, cols] = jnp.sum(dmix * tap, axis=0, keepdims=True)
            part = dmix * ((off >= back).astype(f32) * cw_ref[i : i + 1, cols])
            part = jnp.concatenate([jnp.zeros((RIM, 256), f32), part], axis=0)
            total = total + (pltpu.roll(part, rows + RIM - back, 0) if back else part)
        dext_ref[:, cols] = total


def back_grads_kernel(
    ys, core_ref, dq_ref, dkv_ref, dext_ref, dz_ref, cos_ref, sin_ref, normed_ref, nrim_ref,
    ga_ref, keep_ref,
):
    core = core_ref[0]
    dkv = dkv_ref[0].astype(f32)
    for i in range(1, dkv_ref.shape[0]):
        dkv = dkv + dkv_ref[i].astype(f32)
    ga_ref[:RIM, :768] = jnp.zeros((RIM, 768), bf16)
    ga_ref[:RIM, 1024:A_COLS] = jnp.zeros((RIM, LANES), bf16)
    ga_ref[RIM:, :LANES] = turned_back(dkv[:, :LANES], cos_ref[...], sin_ref[...]).astype(bf16)
    ga_ref[RIM:, LANES:256] = dkv[:, LANES:].astype(bf16)
    ga_ref[RIM:, 256:768] = dq_ref[...]
    ga_ref[:, 768:1024] = dext_ref[:, DS:].astype(bf16)
    ga_ref[RIM:, 1024:A_COLS] = dz_ref[...].astype(bf16)
    ga_ref[:, A_COLS : A_COLS + DS] = dext_ref[:, :DS].astype(bf16)
    wide = normed_ref.shape[1] // ys
    at, to = 0, A_COLS + DS
    for y in range(ys):
        cols = slice(y * wide, (y + 1) * wide)
        for ref, rows in ((nrim_ref, slice(0, RIM)), (normed_ref, slice(RIM, None))):
            own, oth = halves(ref[:, cols], core)
            keep_ref[rows, at : at + wide // 2] = own
            ga_ref[rows, to + at : to + at + wide // 2] = oth
        at += wide // 2


def back_kernel(
    core_ref, gab_ref, wa_own, wa_oth, wb_own, wb_oth, tok_ref, dmid_ref, dng_ref, gain_ref,
    dtok_ref, drim_ref, dn_ref,
):
    core = core_ref[0]
    for y in range(wa_own.shape[0]):
        ga, gb = gab_ref[:, :A_COLS], gab_ref[:, A_COLS : A_COLS + DS]
        own = nt(ga, wa_own[y]) + nt(gb, wb_own[y])
        oth = nt(ga, wa_oth[y]) + nt(gb, wb_oth[y])
        put(dn_ref, y, own, oth, core)

    def through_norm(dn, tok):
        tok = tok.astype(f32)
        rms = lax.rsqrt(jnp.mean(tok * tok, axis=1, keepdims=True) + EPS)
        unit = tok * rms
        dn = dn * gain_ref[...]
        return rms * (dn - unit * jnp.mean(dn * unit, axis=1, keepdims=True))

    drim_ref[...] = through_norm(dn_ref[:RIM, :], tok_ref[:RIM, :])
    dtok_ref[...] = dmid_ref[...] + through_norm(dn_ref[RIM:, :] + dng_ref[...], tok_ref[RIM:, :])


def gain_kernel(pairs, count, *refs):
    gains, refs = refs[:count], refs[count:]
    outs = refs[-count:]
    for k, out in enumerate(outs):
        total = 0.0
        for group, w, g in pairs:
            if group == k:
                total = total + jnp.sum(
                    refs[w][...].astype(f32) * refs[g][...], axis=1, keepdims=True
                )
        out[...] = total / gains[k][...].astype(f32)


def run(kernel, name, outs, args, scalars=0, scratch=(), us=3, left=0, sems=()):
    moved = sum(a.size * a.dtype.itemsize for a in args)
    shapes = [jax.ShapeDtypeStruct(shape, kind) for shape, kind in outs]
    moved += sum(s.size * s.dtype.itemsize for s in shapes)
    specs = [pl.BlockSpec(memory_space=pltpu.SMEM)] * scalars
    specs += [pl.BlockSpec(memory_space=pltpu.VMEM)] * (len(args) - scalars - left)
    specs += [pl.BlockSpec(memory_space=pl.ANY)] * left
    return pl.pallas_call(
        kernel,
        name=name,
        out_shape=shapes,
        in_specs=specs,
        out_specs=[pl.BlockSpec(memory_space=pltpu.VMEM)] * len(shapes),
        scratch_shapes=[pltpu.VMEM(shape, kind) for shape, kind in scratch]
        + [pltpu.SemaphoreType.DMA(shape) for shape in sems],
        compiler_params=pltpu.CompilerParams(vmem_limit_bytes=62 * 2**20),
        cost_estimate=pl.CostEstimate(
            flops=us * SCALE, bytes_accessed=moved, transcendentals=0
        ),
    )(*args)


def padded(vector, width):
    return jnp.pad(vector.astype(f32), (0, width - vector.shape[0]))[None, :]


def local(
    tokens, lengths, cotangent, mixer_gain, query_weight, keyval_weight, inner_weight, conv_weight,
    conv_bias, ssm_gain, attn_out_weight, ssm_out_weight, ffn_gain, gate_up_weight, down_weight,
    decay_log, step_bias, skip_gain,
):
    rows, width = tokens.shape
    seq_count, seq_rank = lax.axis_size(SEQ), lax.axis_index(SEQ)
    side = place_on("core").reshape(1)
    back = (rows * seq_count // 2) // rows
    part = query_weight.shape[0]
    heads_width, ff = HEADS * HEAD_DIM, gate_up_weight.shape[1] // 2
    a_rows, s_rows, f_rows = attn_out_weight.shape[0], ssm_out_weight.shape[0], down_weight.shape[0]
    ys = lax.axis_size("y")

    rim = shifted(tokens[rows - RIM :], 1)
    small = jnp.concatenate(
        [mixer_gain, conv_weight.reshape(-1), conv_bias, ssm_gain, ffn_gain]
    ).astype(f32)
    counts = [mixer_gain.size, conv_weight.size, conv_bias.size, ssm_gain.size, ffn_gain.size]
    slots = -(-small.size // LANES) * LANES
    small = gather_small(jnp.pad(small, (0, slots - small.size)))
    others = lax.axis_size(SEQ)
    aligned = ys == 2 and others == 8 and all(r % 16 == 0 for r in (part, a_rows, s_rows, f_rows))
    core_unit = extents()["core"][0]
    pack_rows = 6 * part + s_rows + f_rows
    if aligned:
        packed, front = run(
            pack_kernel,
            "pack",
            [((pack_rows, width), bf16), ((part, A_COLS + DS), bf16)],
            (
                gate_up_weight, inner_weight, attn_out_weight, ssm_out_weight, down_weight,
                keyval_weight, query_weight,
            ),
        )
    else:
        tail = jnp.pad(inner_weight[:, DS + CONV_CH :], ((0, 0), (0, LANES - SSM_HEADS)))
        front = jnp.concatenate(
            [
                keyval_weight, query_weight, inner_weight[:, 2 * DS : DS + CONV_CH], tail,
                inner_weight[:, DS : 2 * DS],
            ],
            1,
        )
        ao = jnp.concatenate([attn_out_weight[:, :512], attn_out_weight[:, 512:]], 0)
        packed = jnp.concatenate(
            [
                inner_weight[:, :width],
                jnp.concatenate([inner_weight[:, width:DS], ao], 1),
                ssm_out_weight,
            ]
            + [gate_up_weight[:, k * width : (k + 1) * width] for k in range(2 * ff // width)]
            + [down_weight],
            0,
        )
    front = shared(front, "z")
    wa_own, wa_oth = gather_pair(front[:, :, :A_COLS], "y")
    wb_own, wb_oth = gather_pair(front[:, :, A_COLS:], "x")
    packed = lax.all_gather(packed, AXES, axis=0)
    packed = packed.reshape(ys, 2, others, *packed.shape[1:])
    starts = [sum(counts[:i]) for i in range(len(counts))]
    gain_one, w_conv, b_conv, gain_ssm, gain_two = (
        small[:, s : s + c].reshape(-1) for s, c in zip(starts, counts)
    )
    w_conv = jnp.pad(w_conv.reshape(CONV_CH, CONV).T, ((0, 8 - CONV), (0, 0)))
    gain_one, b_conv, gain_ssm, gain_two = (
        v[None, :] for v in (gain_one, b_conv, gain_ssm, gain_two)
    )
    tokens_rim = jnp.concatenate([rim, tokens], 0)
    places = seq_rank * rows + jnp.arange(rows)
    begin = jnp.zeros_like(places)
    end = jnp.int32(0)
    for i in range(lengths.shape[1]):
        end = end + lengths[0, i]
        begin = jnp.where(end <= places, end, begin)
    offset = (places - begin).astype(jnp.int32)
    half = HEAD_DIM // 2
    freq = BASE ** (-jnp.arange(half).astype(f32) / half)
    angle = offset.astype(f32)[:, None] * freq[None, :]
    cos = jnp.tile(jnp.cos(angle), (1, 4))
    sin = jnp.sin(angle)
    sin = jnp.tile(jnp.concatenate([-sin, sin], 1), (1, 2))
    off = offset[:, None]
    step_bias_row, decay_row = padded(step_bias, LANES), padded(jnp.exp(decay_log), LANES)
    skip = jnp.repeat(skip_gain, SSM_DIM)[None, :]

    (q8, kv, normed, nrim, chan, x, bc, step, cum, cumt, z, state, carry) = run(
        front_kernel,
        "front",
        [
            ((HEADS, rows, LANES), bf16),
            ((rows, 256), bf16),
            ((rows, width), bf16),
            ((RIM, width), bf16),
            ((rows + RIM, CONV_CH), bf16),
            ((rows, DS), f32),
            ((rows, 2 * STATE), f32),
            ((rows, LANES), f32),
            ((rows, LANES), f32),
            ((LANES, rows), f32),
            ((rows, LANES), f32),
            ((DS, STATE), f32),
            ((1, LANES), f32),
        ],
        (
            side, tokens_rim, gain_one, wa_own, wa_oth, wb_own, wb_oth,
            cos, sin, off, w_conv, b_conv, step_bias_row, decay_row,
        ),
        scalars=1,
        scratch=[((rows + RIM, width), bf16), ((rows, DS), bf16)],
        us=8,
    )
    carrying = Carrying(state, carry, back, 1)
    sent_state = carrying.send()
    rank = seq_rank.reshape(1).astype(jnp.int32)
    kv_slots = jnp.broadcast_to(kv[None], (seq_count, *kv.shape))
    kv_all = dealt(kv_slots, SEQ)
    window = (back + 1) * rows
    y_local = run(
        scan_kernel, "scan", [((rows, DS), f32)],
        after((x, bc, step, cum, cumt, off), sent_state, kv_slots),
        scratch=[((rows, DS), bf16), ((rows, DS), f32)], us=8,
    )[0]
    entry = carrying.receive(y_local)
    if entry is None:
        sent_state = carrying.send()
    attended, lse = run(
        functools.partial(attend_kernel, back + 1),
        "attend",
        [((rows, heads_width), bf16), ((LANES, rows), f32)],
        after((rank, q8, kv_all, off), sent_state),
        scalars=1,
        scratch=[
            ((window, LANES), bf16),
            ((window, LANES), bf16),
            ((rows, window), f32),
            ((HEADS, rows, LANES), f32),
        ],
        us=10,
    )
    while entry is None:
        entry = carrying.receive(attended)
        if entry is None:
            carrying.send()
    packed = after(packed, entry)
    post_scratch, post_sems = [], []
    if aligned:
        parts, post_weights = (part, a_rows, s_rows, f_rows), (packed,)
        post_scratch, post_sems = [((2, ys, others, *packed.shape[3:]), bf16)], [(3, 2)]
    else:
        parts = ()
        gu_at = 2 * part + s_rows
        packed = [
            lax.dynamic_index_in_dim(packed, place_on("core") ^ i, 1, False) for i in range(2)
        ]

        def taken(full, start, size, low, high):
            return full[:, :, start : start + size, low:high].reshape(ys, -1, high - low)

        def joined_columns(blocks):
            return [jnp.concatenate([taken(f, *block) for block in blocks], 2) for f in packed]

        post_weights = (
            *joined_columns([(0, part, 0, width), (part, part, 0, DS - width)]),
            *joined_columns([(part + k * a_rows, a_rows, 512, 1024) for k in range(2)]),
            *joined_columns([(2 * part, s_rows, 0, width)]),
            *joined_columns([(gu_at + 4 * part, f_rows, 0, width)]),
            *joined_columns([(gu_at + k * part, part, 0, width) for k in range(2 * ff // width)]),
        )

    half = (2 * width + ff + heads_width + DS) // 2
    sent = 2 * ff + 2 * width + DS
    output, dmid, datt, dssd, ycore, dentry, send, keep, dng = run(
        functools.partial(post_kernel, parts, ys),
        "post",
        [
            ((rows, width), bf16),
            ((rows, width), f32),
            ((rows, heads_width), bf16),
            ((rows, DS), f32),
            ((rows, DS), f32),
            ((DS, STATE), f32),
            ((rows, sent + half), bf16),
            ((rows, half), bf16),
            ((rows, width), f32),
        ],
        (
            side, tokens, cotangent, attended, y_local, x, bc, cum, off, entry, skip, normed,
            gain_ssm, gain_two, *post_weights,
        ),
        scalars=1,
        left=1 if aligned else 0,
        sems=post_sems,
        scratch=[
            ((rows, DS), f32),
            ((rows, DS), f32),
            ((rows, width), f32),
            ((rows, 2 * ff), f32),
            ((rows, width), f32),
            ((rows, DS), f32),
            ((rows, DS), bf16),
            ((rows, width), bf16),
            ((rows, ff), bf16),
            ((rows, DS), bf16),
            ((rows, ff), f32),
            ((rows, DS), f32),
            ((rows, DS), f32),
        ]
        + post_scratch,
        us=30,
    )
    got = swap(send, core_unit)
    carrying = Carrying(dentry, carry, back, -1)
    sent_state = carrying.send()
    off_row = offset[None, :]
    sizes = [width // 2, ff // 2, heads_width // 2, DS // 2, width // 2]
    ats = [sum(sizes[:i]) for i in range(5)]
    sizes = [size // ys for size in sizes]
    n2_at, hid_at, att_at, mix_at, norm_at = ats
    cot_at, dbr_at, dgate_at = 2 * ff, 2 * ff + width, 2 * ff + 2 * width
    places = tuple(place_on(g).reshape(1).astype(jnp.int32) for g in ("y", "x"))

    def weight_sums(name, x_parts, y_parts, keep, own, got, extra=()):
        plan, at, tall = [], 0, y_parts[0][4]
        for p in x_parts:
            plan.append(("x", at, *p))
            at += p[4]
        wide, at = at, 0
        for p in y_parts:
            plan.append(("y", at, *p))
            at += p[2] // others
        if aligned:
            xs = (ys, others // 2, x_parts[0][2] // others, wide)
            made = run(
                functools.partial(split_products_kernel, plan, len(extra)),
                name,
                [(xs, bf16), (xs, bf16), ((others, at, tall), bf16), ((others, at, tall), bf16)],
                (*places, keep, own, got, *extra),
                scalars=2,
                us=9,
            )
            return PairReduction(made, 512 if wide % 512 == 0 else 384)
        parts = x_parts + y_parts
        made = run(
            functools.partial(
                products_kernel, [(i, *p[:4]) for i, p in enumerate(parts)], len(extra)
            ),
            name,
            [((ys, p[2], p[4]), bf16) for p in parts],
            (keep, own, got, *extra),
            us=9,
        )
        heads = made[: len(x_parts)]
        tails = [m.reshape(ys, others, -1, tall) for m in made[len(x_parts) :]]
        rows_of = (x_parts[0][2] // others, at)
        return PlainReduction((jnp.concatenate(heads, 2), jnp.concatenate(tails, 2)), rows_of)

    dxw, dscores = run(
        scan_back_kernel,
        "scan_back",
        [((rows, DS), f32), ((rows, rows), bf16)],
        after((dssd, x, bc, step, cum, cumt, off_row), sent_state),
        scratch=[
            ((rows, DS), bf16),
            ((rows, DS), f32),
            ((rows, DS), bf16),
            ((rows, rows), f32),
        ],
        us=9,
    )

    downstream = carrying.receive(dxw)
    if downstream is None:
        sent_state = carrying.send()
    keep, send, got = after((keep, send, got), dxw, sent_state)
    red_one = weight_sums(
        "weights_one",
        [(n2_at, sent + n2_at, sizes[0], 0, ff)],
        [(hid_at, sent + hid_at, sizes[1], cot_at, width)],
        keep,
        send,
        got,
    )
    keep, send, got = after((keep, send, got), red_one.sent)
    red_two = weight_sums(
        "weights_two",
        [
            (n2_at, sent + n2_at, sizes[0], ff, ff),
            (norm_at, sent + norm_at, sizes[4], dgate_at, DS),
        ],
        [
            (att_at, sent + att_at, sizes[2], dbr_at, width),
            (mix_at, sent + mix_at, sizes[3], dbr_at, width),
        ],
        keep,
        send,
        got,
    )
    dq, dkv = run(
        functools.partial(attend_back_kernel, back + 1),
        "attend_back",
        [((rows, heads_width), bf16), ((seq_count, rows, 256), bf16)],
        after((rank, q8, kv_all, off_row, lse, datt, cos, sin), red_two.sent),
        scalars=1,
        scratch=[
            ((window, LANES), bf16),
            ((window, LANES), bf16),
            ((window, rows), f32),
            ((HEADS, rows, LANES), bf16),
            ((HEADS, rows, LANES), f32),
            ((window, 256), f32),
        ],
        us=14,
    )
    dkv_got = dealt(dkv, SEQ)
    while downstream is None:
        downstream = carrying.receive(dq)
        if downstream is None:
            carrying.send()
    red_one.fold_one(dq, downstream)
    dext, dz, small = run(
        mixer_back_kernel,
        "mixer_back",
        [
            ((rows + RIM, CONV_CH), f32),
            ((rows, LANES), f32),
            ((8, CONV_CH), f32),
        ],
        after(
            (
                dssd, ycore, x, bc, step, cum, z, off, entry, downstream, skip, decay_row, chan,
                w_conv, b_conv, dxw, dscores,
            ),
            red_one.sent,
        ),
        scratch=[((rows, CONV_CH), f32)],
        us=13,
    )
    count = lax.axis_size(AXES)
    small_got = swap(small, core_unit)
    gab, norm_keep = run(
        functools.partial(back_grads_kernel, ys),
        "back_grads",
        [((rows + RIM, A_COLS + DS + width // 2), bf16), ((rows + RIM, width // 2), bf16)],
        (side, dq, dkv_got, dext, dz, cos, sin, normed, nrim),
        scalars=1,
    )
    gab_got = swap(gab, core_unit)
    red_two.fold_one(gab)
    small = small + after(small_got, gab)
    free = LANES - SSM_HEADS
    convs = small[: CONV + 1].reshape(CONV + 1, count, -1).transpose(1, 0, 2)
    head_sums = small[CONV + 1, : 3 * LANES].reshape(3, LANES)[:, :SSM_HEADS]
    if aligned:
        head_sums = jnp.broadcast_to(head_sums[None], (count, 3, SSM_HEADS))
        per_device = jnp.concatenate(
            [
                jnp.pad(convs, ((0, 0), (0, 0), (0, free - convs.shape[2]))),
                jnp.pad(head_sums, ((0, 0), (0, 0), (0, free - SSM_HEADS))),
            ],
            1,
        )
        slots = CONV + 4
    else:
        head_sums = jnp.broadcast_to(head_sums.reshape(1, -1), (count, 3 * SSM_HEADS))
        per_device = jnp.concatenate([convs.reshape(count, -1), head_sums], 1)
        slots = per_device.shape[1]
        per_device = jnp.pad(per_device, ((0, 0), (0, part * free - slots)))
        per_device = per_device.reshape(count, part, free)
    per_device = lax.dynamic_index_in_dim(
        per_device.reshape(ys, 2, others, -1, free), place_on("core"), 1, False
    )
    aside = 384 if aligned else A_COLS % 512
    extra = jnp.pad(
        per_device, ((0, 0), (0, 0), (0, part - per_device.shape[2]), (aside - free, 0))
    ).reshape(ys, others * part, aside)
    grad_tokens, grad_rim = run(
        back_kernel,
        "back",
        [((rows, width), f32), ((RIM, width), f32)],
        (
            side, after(gab, red_two.sent), wa_own, wa_oth, wb_own, wb_oth, tokens_rim, dmid, dng,
            gain_one,
        ),
        scalars=1,
        scratch=[((rows + RIM, width), f32)],
        us=7,
    )
    red_one.fold_two(grad_tokens)
    norm_keep, gab, gab_got, extra = after((norm_keep, gab, gab_got, extra), red_one.sent)
    red_three = weight_sums(
        "front_weights",
        [(0, A_COLS + DS, sizes[4], 0, A_COLS)],
        [(0, A_COLS + DS, sizes[4], A_COLS, DS)],
        norm_keep,
        gab,
        gab_got,
        (extra,),
    )
    red_two.fold_two(red_three.sent)
    r_one, r_down = red_one.fold_three(red_two.sent)
    red_three.fold_one(r_one)
    rim_got = shifted(after(grad_rim, red_three.sent), -1)
    red_three.fold_two(red_three.sent)
    if aligned:
        r_gu, r_gate, r_ao, r_so, g_ffn, g_ssm = run(
            finish_post_kernel,
            "finish_post",
            [
                ((part, 2 * ff), f32),
                ((part, DS), f32),
                ((a_rows, width), f32),
                ((s_rows, width), f32),
                ((1, part), f32),
                ((1, s_rows), f32),
            ],
            (
                after(red_two.gots, red_three.sent), r_one, gate_up_weight, ssm_out_weight,
                ffn_gain.astype(f32)[None, :], ssm_gain.astype(f32)[None, :],
            ),
        )
        rim_got = after(rim_got, r_gu)
        grad_tokens = grad_tokens.at[rows - RIM :].add(rim_got)
        r_kv, r_q, g_inner, g_conv, g_bias, g_log, g_step, g_skip, g_mixer = run(
            finish_front_kernel,
            "finish_front",
            [
                ((part, 256), f32),
                ((part, heads_width), f32),
                ((part, inner_weight.shape[1]), f32),
                (conv_weight.shape, f32),
                ((1, conv_bias.size), f32),
                ((1, SSM_HEADS), f32),
                ((1, SSM_HEADS), f32),
                ((1, SSM_HEADS), f32),
                ((1, part), f32),
            ],
            (
                after(red_three.gots, grad_tokens), r_gate, keyval_weight, query_weight,
                inner_weight, mixer_gain.astype(f32)[None, :],
            ),
        )
        g_bias, g_mixer, g_ssm, g_ffn = (v[0] for v in (g_bias, g_mixer, g_ssm, g_ffn))
        heads = [v[0] for v in (g_log, g_step, g_skip)]
    else:
        r_two, r_out = red_two.fold_three(red_three.sent)
        rim_got = after(rim_got, r_two)
        grad_tokens = grad_tokens.at[rows - RIM :].add(rim_got)
        r_e, r_f = red_three.fold_three(grad_tokens)
        r_gu = jnp.concatenate([r_one, r_two[:, :ff]], 1)
        small = r_e[:, A_COLS - free :].reshape(-1)[:slots]
        conv = small[: (CONV + 1) * conv_bias.size].reshape(CONV + 1, -1)
        g_conv, g_bias = conv[:CONV].T, conv[CONV]
        heads = small[(CONV + 1) * conv_bias.size :].reshape(3, SSM_HEADS)
        g_inner = jnp.concatenate([r_two[:, ff:], r_f, r_e[:, 768 : 1024 + SSM_HEADS]], 1)
        r_kv, r_q, r_ao, r_so = r_e[:, :256], r_e[:, 256:768], r_out[:a_rows], r_out[a_rows:]
        pairs = [(0, 0, 1), (0, 2, 3), (0, 4, 5), (1, 6, 7), (2, 8, 9)]
        gains = run(
            functools.partial(gain_kernel, pairs, 3),
            "gains",
            [((part, 1), f32), ((s_rows, 1), f32), ((part, 1), f32)],
            (
                mixer_gain[:, None], ssm_gain[:, None], ffn_gain[:, None],
                keyval_weight, r_kv, query_weight, r_q, inner_weight, g_inner,
                ssm_out_weight, r_so, gate_up_weight, r_gu,
            ),
        )
        g_mixer, g_ssm, g_ffn = (v[:, 0] for v in gains)
    return (
        output,
        grad_tokens,
        g_mixer,
        r_q,
        r_kv,
        g_inner,
        g_conv,
        g_bias,
        g_ssm,
        r_ao,
        r_so,
        g_ffn,
        r_gu,
        r_down,
        heads[0],
        heads[1],
        heads[2],
    )


def solution(mesh):
    across, along = mesh.shape["dp"], mesh.shape["seq"]
    mesh = jax.sharding.Mesh(mesh.devices.reshape(across // 2, 2, along // 2, 2), AXES)
    lead, flat, rep = P(AXES, None), P(AXES), P()
    return jax.shard_map(
        local,
        mesh=mesh,
        in_specs=(
            lead, P(AXES[:2], None), lead, flat, lead, lead, lead, lead, flat, flat, lead, lead, flat,
            lead, lead, rep, rep, rep,
        ),
        out_specs=(
            lead, lead, flat, lead, lead, lead, lead, flat, flat, lead, lead, flat, lead, lead,
            rep, rep, rep,
        ),
        check_vma=False,
    )
```

```python
import functools

import jax
import jax.numpy as jnp
from jax import lax
from jax.experimental import pallas as pl
from jax.experimental.pallas import tpu as pltpu
from jax.sharding import PartitionSpec as P

HEADS = 8
KV_HEADS = 2
HEAD_DIM = 64
SSM_HEADS = 24
SSM_DIM = 64
STATE = 128
CONV = 4
DS = 1536
CONV_CH = 1792
RIM = 16
LANES = 128
A_COLS = 2 * KV_HEADS * HEAD_DIM + HEADS * HEAD_DIM + 2 * STATE + LANES
EPS = 1e-6
BASE = 10000.0
NEG = -1e30
SCALE = 6_600_000_000
AXES = ("y", "core", "z", "x")
SEQ = AXES[2:]

f32 = jnp.float32
bf16 = jnp.bfloat16


def nn(a, b):
    return lax.dot_general(a, b, (((1,), (0,)), ((), ())), preferred_element_type=f32)


def tn(a, b):
    return lax.dot_general(a, b, (((0,), (0,)), ((), ())), preferred_element_type=f32)


def nt(a, b):
    return lax.dot_general(a, b, (((1,), (1,)), ((), ())), preferred_element_type=f32)


def terms(value, count):
    parts = []
    for unused in range(count):
        parts.append(value.astype(bf16))
        value = value - parts[-1].astype(f32)
    return parts


def nn_left(value, ones, count):
    return sum(nn(part, ones) for part in terms(value, count))


def nn_right(ones, value, count):
    return sum(nn(ones, part) for part in terms(value, count))


def iota(shape, dim):
    return lax.broadcasted_iota(jnp.int32, shape, dim)


def head_spread():
    row = iota((LANES, DS), 0)
    return (iota((LANES, DS), 1) // SSM_DIM == row).astype(f32).astype(bf16)


def head_sum_matrix():
    col = iota((DS, LANES), 1)
    return (iota((DS, LANES), 0) // SSM_DIM == col).astype(f32).astype(bf16)


def extents():
    along = lax.axis_size(SEQ)
    return {
        "x": (1, 2),
        "z": (2, along // 2),
        "core": (along, 2),
        "y": (2 * along, lax.axis_size("y")),
    }


def my_index():
    return lax.axis_index(AXES)


def place_on(group):
    unit, size = extents()[group]
    return (my_index() // unit) % size


def swap(array, mask):
    count = lax.axis_size(AXES)
    return lax.ppermute(array, AXES, [(i, i ^ mask) for i in range(count)])


def in_order(pieces, place):
    pieces = list(pieces)
    bit = 1
    while bit < len(pieces):
        flag = (place // bit) % 2 == 1
        pieces = [jnp.where(flag, pieces[j ^ bit], pieces[j]) for j in range(len(pieces))]
        bit *= 2
    return pieces


def collect(array, group, axis):
    unit, size = extents()[group]
    pieces = [array] + [swap(array, k * unit) for k in range(1, size)]
    return jnp.stack(in_order(pieces, place_on(group)), axis)


def gather_pair(full, first):
    if first == "y":
        full = collect(collect(full, "y", 0), "x", 2)
    else:
        full = collect(collect(full, "x", 1), "y", 0)
    other = swap(full, extents()["core"][0])
    shape = (full.shape[0], full.shape[1] * full.shape[2] * full.shape[3], full.shape[4])
    return full.reshape(shape), other.reshape(shape)


def cut(total, group, axis):
    size = extents()[group][1]
    place = place_on(group)
    keep = lax.dynamic_index_in_dim(total, place, axis, False)
    parts = [lax.dynamic_index_in_dim(total, place ^ k, axis, False) for k in range(1, size)]
    return keep, [p.astype(bf16) for p in parts]


def crossed(parts, group):
    unit = extents()[group][0]
    return [swap(part, (k + 1) * unit) for k, part in enumerate(parts)]


def joined(keep, received):
    total = keep.astype(f32)
    for part in received:
        total = total + part.astype(f32)
    return total


class Reduction:
    def __init__(self, total, rows, first):
        table = extents()
        self.total = total.reshape(
            table["y"][1], table["z"][1], table["x"][1], rows, total.shape[-1]
        )
        order = [("x", 2), ("y", 0)] if first == "x" else [("y", 0), ("x", 1)]
        self.stages = order + [("z", 0)]

    def send(self):
        (group, axis), self.stages = self.stages[0], self.stages[1:]
        self.keep, self.parts = cut(self.total, group, axis)
        self.received = crossed(self.parts, group)
        return self.parts

    def receive(self, *others):
        self.received = after(self.received, *others)
        self.total = joined(self.keep, self.received)
        return self.total


def after(value, *others):
    return lax.optimization_barrier((value, others))[0]


def gather_small(vector):
    full = collect(collect(collect(vector, "z", 0), "x", 1), "core", 0)
    return collect(full, "y", 0).reshape(-1, vector.shape[-1])


def dealt(array, axes):
    return lax.all_to_all(array, axes, 0, 0, tiled=True)


def shared(array, axes):
    return dealt(jnp.broadcast_to(array[None], (lax.axis_size(axes), *array.shape)), axes)


def shifted(array, by):
    count = lax.axis_size(SEQ)
    pairs = [(i, i + by) for i in range(count) if 0 <= i + by < count]
    return lax.ppermute(array, SEQ, pairs)


def link(earlier, later):
    carry = later[1]
    wide = jnp.repeat(carry[0, :SSM_HEADS], SSM_DIM)[:, None]
    return (later[0] + wide * earlier[0], carry * earlier[1])


class Carrying:
    def __init__(self, state, carry, back, sign):
        self.pair, self.back, self.sign, self.by = (state, carry), back, sign, 0

    def send(self):
        packed = jnp.concatenate(
            [self.pair[0], jnp.pad(self.pair[1], ((0, RIM - 1), (0, 0)))], 0
        ).astype(bf16)
        steps = [self.by] if self.by else [1] + [2] * (self.back > 1)
        self.got = [shifted(packed, self.sign * by) for by in steps]
        return packed

    def receive(self, *others):
        pairs = []
        for got in after(self.got, *others):
            got = got.astype(f32)
            pairs.append((got[:DS], got[DS : DS + 1]))
        self.by = 2 * self.by if self.by else min(self.back, 2)
        if len(pairs) == 2:
            self.pair = link(pairs[1], pairs[0])
        else:
            self.pair = link(pairs[0], self.pair) if self.by > 2 else pairs[0]
        return self.pair[0] if self.by >= self.back else None


def halves(block, core):
    width = block.shape[1] // 2
    low, high = block[:, :width], block[:, width:]
    return jnp.where(core == 0, low, high), jnp.where(core == 0, high, low)


def put(ref, y, own, other, core):
    width = own.shape[1]
    base = y * 2 * width
    ref[:, base : base + width] = jnp.where(core == 0, own, other).astype(ref.dtype)
    ref[:, base + width : base + 2 * width] = jnp.where(core == 0, other, own).astype(ref.dtype)


def sides(ref, core, count):
    width = ref.shape[-1] // count
    return [halves(ref[:, y * width : (y + 1) * width], core) for y in range(count)]


def cross_half(value):
    lane = iota(value.shape, 1) % HEAD_DIM
    up = pltpu.roll(value, LANES - HEAD_DIM // 2, 1)
    down = pltpu.roll(value, HEAD_DIM // 2, 1)
    return jnp.where(lane < HEAD_DIM // 2, up, down)


def turned(value, cos, sin):
    return value * cos + cross_half(value) * sin


def turned_back(value, cos, sin):
    return value * cos - cross_half(value) * sin


def split_heads(pair, which, lane):
    flipped = pltpu.roll(pair, HEAD_DIM, 1)
    if which == 0:
        return jnp.where(lane < HEAD_DIM, pair, 0.0), jnp.where(lane < HEAD_DIM, flipped, 0.0)
    return jnp.where(lane >= HEAD_DIM, flipped, 0.0), jnp.where(lane >= HEAD_DIM, pair, 0.0)


def join_heads(even, odd, which, lane):
    if which == 0:
        return jnp.where(lane < HEAD_DIM, even, pltpu.roll(odd, HEAD_DIM, 1))
    return jnp.where(lane < HEAD_DIM, pltpu.roll(even, HEAD_DIM, 1), odd)


def conv_taps(chan_ref, cols, off):
    ext = chan_ref[:, cols].astype(f32)
    taps = []
    for i in range(CONV):
        back = CONV - 1 - i
        rows = pltpu.roll(ext, back, 0)[RIM:] if back else ext[RIM:]
        taps.append(rows * (off >= back).astype(f32))
    return taps


def sigmoid(v):
    return 1.0 / (1.0 + jnp.exp(-v))


def softplus(v):
    return jnp.maximum(v, 0.0) + jnp.log1p(jnp.exp(-jnp.abs(v)))


def tail_of(cum, off):
    rows = cum.shape[0]
    last_off = off[rows - 1 :, :]
    keep = iota((rows, 1), 0) >= rows - 1 - last_off
    return jnp.exp(cum[rows - 1 :, :] - cum) * keep.astype(f32)


def fade_of(cum, off):
    keep = off > iota((cum.shape[0], 1), 0)
    return jnp.exp(cum) * keep.astype(f32)


def carry_of(cum, off):
    rows = cum.shape[0]
    return jnp.exp(cum[rows - 1 :, :]) * (off[rows - 1 :, :] >= rows).astype(f32)


def pack_kernel(
    gu_ref, inner_ref, ao_ref, so_ref, down_ref, kv_ref, q_ref, post_ref, front_ref
):
    part, width = gu_ref.shape[0], down_ref.shape[1]
    a_rows = ao_ref.shape[0]
    post_ref[:part, :] = inner_ref[:, :width]
    post_ref[part : 2 * part, : DS - width] = inner_ref[:, width:DS]
    for k in range(2):
        rows = slice(part + k * a_rows, part + (k + 1) * a_rows)
        post_ref[rows, DS - width :] = ao_ref[:, k * 512 : (k + 1) * 512]
    at = 2 * part
    post_ref[at : at + so_ref.shape[0], :] = so_ref[...]
    at += so_ref.shape[0]
    for k in range(gu_ref.shape[1] // width):
        post_ref[at : at + part, :] = gu_ref[:, k * width : (k + 1) * width]
        at += part
    post_ref[at:, :] = down_ref[...]
    front_ref[:, :256] = kv_ref[...]
    front_ref[:, 256:768] = q_ref[...]
    front_ref[:, 768:1024] = inner_ref[:, 2 * DS : DS + CONV_CH]
    front_ref[:, 1024:A_COLS] = jnp.zeros((part, LANES), bf16)
    front_ref[:, 1024 : 1024 + SSM_HEADS] = inner_ref[:, DS + CONV_CH :]
    front_ref[:, A_COLS:] = inner_ref[:, DS : 2 * DS]


def front_kernel(
    core_ref, tok_ref, gain_ref, wa_own, wa_oth, wb_own, wb_oth, cos_ref, sin_ref, off_ref,
    cw_ref, cb_ref, sb_ref, dec_ref,
    q8_ref, kv_ref, normed_ref, nrim_ref, chan_ref, x_ref, bc_ref, step_ref, cum_ref, cumt_ref, z_ref,
    state_ref, carry_ref,
    n_ref, xt_ref,
):
    core = core_ref[0]
    rows = cos_ref.shape[0]
    tok = tok_ref[...].astype(f32)
    rms = lax.rsqrt(jnp.mean(tok * tok, axis=1, keepdims=True) + EPS)
    n_ref[...] = (tok * rms * gain_ref[...]).astype(bf16)
    normed_ref[...] = n_ref[RIM:, :]
    nrim_ref[...] = n_ref[:RIM, :]
    count = wa_own.shape[0]
    blocks = sides(n_ref, core, count)

    def project(own_ref, oth_ref, cols):
        total = 0.0
        for y, (own, oth) in enumerate(blocks):
            total = total + nn(own, own_ref[y, :, cols]) + nn(oth, oth_ref[y, :, cols])
        return total

    lane = iota((rows, LANES), 1)
    cos, sin, off = cos_ref[...], sin_ref[...], off_ref[...]
    kv = project(wa_own, wa_oth, pl.ds(0, 256))[RIM:]
    kv_ref[:, :LANES] = turned(kv[:, :LANES], cos, sin).astype(bf16)
    kv_ref[:, LANES:] = kv[:, LANES:].astype(bf16)
    queries = project(wa_own, wa_oth, pl.ds(256, 512))[RIM:]
    for j in range(HEADS // 2):
        pair = turned(queries[:, j * LANES : (j + 1) * LANES], cos, sin)
        even, odd = split_heads(pair, j // 2, lane)
        q8_ref[2 * j] = even.astype(bf16)
        q8_ref[2 * j + 1] = odd.astype(bf16)
    rest = project(wa_own, wa_oth, pl.ds(768, 384))
    chan_ref[:, DS:] = rest[:, : 2 * STATE].astype(bf16)
    z = rest[RIM:, 2 * STATE :].astype(bf16).astype(f32) + sb_ref[...]
    for j in range(DS // 512):
        cols = slice(j * 512, (j + 1) * 512)
        chan_ref[:, cols] = project(wb_own, wb_oth, pl.ds(j * 512, 512)).astype(bf16)
    z_ref[...] = z
    step = softplus(z)
    step_ref[...] = step
    tri = (iota((rows, rows), 0) >= iota((rows, rows), 1)).astype(f32).astype(bf16)
    cum = nn_right(tri, -step * dec_ref[...], 3)
    cum_ref[...] = cum
    cumt_ref[...] = cum.T
    carry_ref[...] = carry_of(cum, off)
    weight = nn_left(step * tail_of(cum, off), head_spread(), 2)
    for j in range(CONV_CH // 256):
        cols = slice(j * 256, (j + 1) * 256)
        mixed = cb_ref[:, cols]
        for i, tap in enumerate(conv_taps(chan_ref, cols, off)):
            mixed = mixed + tap * cw_ref[i : i + 1, cols]
        active = mixed * sigmoid(mixed)
        if j < DS // 256:
            x_ref[:, cols] = active
            xt_ref[:, cols] = (active * weight[:, cols]).astype(bf16)
        else:
            bc_ref[...] = active
    state_ref[...] = tn(xt_ref[...], bc_ref[:, :STATE].astype(bf16))


def scan_masks(off, rows):
    t, s = iota((rows, rows), 0), iota((rows, rows), 1)
    return (s <= t) & (s >= t - off)


def scan_kernel(x_ref, bc_ref, step_ref, cum_ref, cumt_ref, off_ref, y_ref, xw_ref, ce_ref):
    rows = x_ref.shape[0]
    spread = head_spread()
    xw_ref[...] = (x_ref[...] * nn_left(step_ref[...], spread, 2)).astype(bf16)
    ce_ref[...] = nn_left(cum_ref[...], spread, 3)
    keys, reads = bc_ref[:, :STATE].astype(bf16), bc_ref[:, STATE:].astype(bf16)
    scores = jnp.where(scan_masks(off_ref[...], rows), nt(reads, keys), 0.0)
    lane = iota((rows, LANES), 1)

    def pair(j, unused):
        cols = pl.ds(pl.multiple_of(j * LANES, LANES), LANES)
        wide = ce_ref[:, cols]
        xw = xw_ref[:, cols]
        outs = []
        for k in range(2):
            late = wide[:, k * SSM_DIM : k * SSM_DIM + 1]
            early = cumt_ref[pl.ds(2 * j + k, 1), :]
            decay = jnp.exp(jnp.minimum(late - early, 0.0))
            outs.append(nn((decay * scores).astype(bf16), xw))
        y_ref[:, cols] = jnp.where(lane < SSM_DIM, outs[0], outs[1])
        return unused

    lax.fori_loop(0, SSM_HEADS // 2, pair, 0)


def attend_bias(off, rows, window):
    query = iota((rows, window), 0) + (window - rows)
    key = iota((rows, window), 1)
    return jnp.where((key <= query) & (key >= query - off), 0.0, NEG)


def window_of(count, rank, kv_ref, k_ref, v_ref):
    rows = kv_ref.shape[1]
    for i in range(count):
        piece = jnp.maximum(rank - (count - 1 - i), 0)
        k_ref[i * rows : (i + 1) * rows, :] = kv_ref[piece, :, :LANES]
        v_ref[i * rows : (i + 1) * rows, :] = kv_ref[piece, :, LANES:]


def attend_kernel(
    count, rank_ref, q8_ref, kv_ref, off_ref, att_ref, lse_ref, k_ref, v_ref, bias_ref, o_ref
):
    rows = off_ref.shape[0]
    window = count * rows
    window_of(count, rank_ref[0], kv_ref, k_ref, v_ref)
    bias_ref[...] = attend_bias(off_ref[...], rows, window)
    lane = iota((rows, LANES), 1)

    def head(h, lses):
        scores = nt(q8_ref[h], k_ref[...]) * HEAD_DIM**-0.5 + bias_ref[...]
        top = jnp.max(scores, axis=1, keepdims=True)
        probs = jnp.exp(scores - top)
        total = jnp.sum(probs, axis=1, keepdims=True)
        o_ref[h] = nn((probs * (1.0 / total)).astype(bf16), v_ref[...])
        return jnp.where(lane == h, top + jnp.log(total), lses)

    lse_ref[...] = lax.fori_loop(0, HEADS, head, jnp.zeros((rows, LANES), f32)).T
    for j in range(HEADS // 2):
        pair = join_heads(o_ref[2 * j], o_ref[2 * j + 1], j // 2, lane)
        att_ref[:, j * LANES : (j + 1) * LANES] = pair.astype(bf16)


def attend_back_kernel(
    count, rank_ref, q8_ref, kv_ref, off_ref, lse_ref, datt_ref, cos_ref, sin_ref,
    dq_ref, out_ref, k_ref, v_ref, bias_ref, do_ref, dq8_ref, dkv_ref,
):
    rows = off_ref.shape[1]
    window = count * rows
    rank = rank_ref[0]
    window_of(count, rank, kv_ref, k_ref, v_ref)
    query = iota((window, rows), 1) + (window - rows)
    key = iota((window, rows), 0)
    bias_ref[...] = jnp.where((key <= query) & (key >= query - off_ref[...]), 0.0, NEG)
    lane = iota((rows, LANES), 1)
    for j in range(HEADS // 2):
        pair = datt_ref[:, j * LANES : (j + 1) * LANES].astype(f32)
        even, odd = split_heads(pair, j // 2, lane)
        do_ref[2 * j] = even.astype(bf16)
        do_ref[2 * j + 1] = odd.astype(bf16)
    dkv_ref[...] = jnp.zeros(dkv_ref.shape, f32)

    def head(h, unused):
        query, grad = q8_ref[h], do_ref[h]
        scores = nt(k_ref[...], query) * HEAD_DIM**-0.5 + bias_ref[...]
        probs = jnp.exp(scores - lse_ref[pl.ds(h, 1), :])
        dprobs = nt(v_ref[...], grad)
        mean = jnp.sum(probs * dprobs, axis=0, keepdims=True)
        draw = (probs * (dprobs - mean) * HEAD_DIM**-0.5).astype(bf16)
        dkv_ref[:, :LANES] += nn(draw, query)
        dkv_ref[:, LANES:] += nn(probs.astype(bf16), grad)
        dq8_ref[h] = tn(draw, k_ref[...])
        return unused

    lax.fori_loop(0, HEADS, head, 0)
    out_ref[...] = jnp.zeros(out_ref.shape, bf16)
    for i in range(count):
        piece = rank - (count - 1 - i)

        @pl.when(piece >= 0)
        def unused():
            out_ref[piece] = dkv_ref[i * rows : (i + 1) * rows, :].astype(bf16)

    for j in range(HEADS // 2):
        pair = join_heads(dq8_ref[2 * j], dq8_ref[2 * j + 1], j // 2, lane)
        back = turned_back(pair, cos_ref[...], sin_ref[...])
        dq_ref[:, j * LANES : (j + 1) * LANES] = back.astype(bf16)


class PackedWeights:
    def __init__(self, source, core, held, sems, parts):
        self.held = held
        part, a_part, s_part, f_part = self.parts = parts
        self.so_at = 2 * part
        self.gu_at = self.so_at + s_part
        self.down_at = self.gu_at + 4 * part
        ends = [0, self.so_at, self.gu_at, self.down_at + f_part]
        self.copies = []
        for k in range(3):
            rows = pl.ds(ends[k], ends[k + 1] - ends[k])
            self.copies.append(
                [
                    pltpu.make_async_copy(
                        source.at[:, lax.rem(core + i, 2), :, rows],
                        held.at[i, :, :, rows],
                        sems.at[k, i],
                    )
                    for i in range(2)
                ]
            )
        for pair in self.copies:
            for copy in pair:
                copy.start()

    def wait(self, k):
        for copy in self.copies[k]:
            copy.wait()

    def block(self, i, y, start, size, col):
        rows, cols = pl.ds(pl.multiple_of(start, 16), size), pl.ds(pl.multiple_of(col, 512), 512)
        got = self.held[i, y, :, rows, cols]
        return got.reshape(got.shape[0] * size, 512)

    def gate(self, i, y, j):
        part = self.parts[0]
        return self.block(i, y, j // 2 * part, part, j % 2 * 512)

    def ao(self, i, y, j):
        part, a_part = self.parts[:2]
        return self.block(i, y, part + j * a_part, a_part, 512)

    def so(self, i, y, j):
        return self.block(i, y, self.so_at, self.parts[2], j * 512)

    def down(self, i, y, j):
        return self.block(i, y, self.down_at, self.parts[3], j * 512)

    def gu(self, i, y, j):
        part = self.parts[0]
        return self.block(i, y, self.gu_at + j // 2 * part, part, j % 2 * 512)


class PlainWeights:
    def __init__(self, refs):
        self.refs = refs

    def wait(self, k):
        pass

    def block(self, name, i, y, j):
        return self.refs[2 * name + i][y, :, pl.ds(pl.multiple_of(j * 512, 512), 512)]

    def gate(self, i, y, j):
        return self.block(0, i, y, j)

    def ao(self, i, y, j):
        return self.block(1, i, y, j)

    def so(self, i, y, j):
        return self.block(2, i, y, j)

    def down(self, i, y, j):
        return self.block(3, i, y, j)

    def gu(self, i, y, j):
        return self.refs[8 + i][y, :, pl.ds(pl.multiple_of(j * 512, 512), 512)]


def post_kernel(
    parts, ys, core_ref, tok_ref, cot_ref, att_ref, yl_ref, x_ref, bc_ref, cum_ref, off_ref,
    entry_ref, skip_ref, normed_ref, gssm_ref, gffn_ref, *refs,
):
    if parts:
        weights = PackedWeights(refs[0], core_ref[0], refs[-2], refs[-1], parts)
        refs = refs[1:-2]
    else:
        weights, refs = PlainWeights(refs[:10]), refs[10:]
    pairs = [(i, y) for y in range(ys) for i in range(2)]

    def through(blocks, weight, j):
        return sum(nn(blocks[y][i], weight(i, y, j)) for i, y in pairs)

    def back_through(ref, grad, weight, count):
        for y in range(ys):
            both = []
            for i in range(2):
                both.append(
                    sum(nt(grad[:, j * 512 : j * 512 + 512], weight(i, y, j)) for j in range(count))
                )
            put(ref, y, both[0], both[1], core)

    (
        out_ref, dmid_ref, datt_ref, dssd_ref, ycore_ref, dentry_ref, send_ref, keep_ref, dng_ref,
        gi_ref, gd_ref, mid_ref, gu_ref, dn_ref, dmx_ref, fd_ref, n2_ref, hid_ref, mixed_ref, dh_ref, fade_ref, ent_ref,
    ) = refs
    core = core_ref[0]
    rows, width = tok_ref.shape
    heads_width = att_ref.shape[1]
    ff = hid_ref.shape[1]
    half = keep_ref.shape[1]
    cot_at, dbr_at, dgate_at, sel_at = 2 * ff, 2 * ff + width, 2 * ff + 2 * width, 2 * ff + 2 * width + DS
    reads = bc_ref[:, STATE:].astype(bf16)
    spread = head_spread()
    fade_ref[...] = nn_left(fade_of(cum_ref[...], off_ref[...]), spread, 2)
    ent_ref[...] = nt(reads, entry_ref[...].astype(bf16))
    none = jnp.zeros((rows, 1), f32)

    def at(j, first=0):
        return pl.ds(pl.multiple_of(first + j * 512, 512), 512)

    weights.wait(0)
    blocks = sides(normed_ref, core, ys)

    def gates(j, square):
        cols = at(j)
        gate = through(blocks, weights.gate, j).astype(bf16).astype(f32)
        gi_ref[:, cols] = gate
        ycore = yl_ref[:, cols] + fade_ref[:, cols] * ent_ref[:, cols]
        ycore_ref[:, cols] = ycore
        ssd = ycore + skip_ref[:, cols] * x_ref[:, cols]
        gated = ssd * gate * sigmoid(gate)
        gd_ref[:, cols] = gated
        return square + jnp.sum(gated * gated, axis=1, keepdims=True)

    square = lax.fori_loop(0, DS // 512, gates, none, unroll=True)
    rms_gate = lax.rsqrt(square / DS + EPS)
    mixed_ref[...] = (gd_ref[...] * rms_gate * gssm_ref[...]).astype(bf16)
    weights.wait(1)
    att_blocks, mix_blocks = sides(att_ref, core, ys), sides(mixed_ref, core, ys)

    def branches(j, square):
        branch = through(att_blocks, weights.ao, j) + through(mix_blocks, weights.so, j)
        middle = tok_ref[:, at(j)].astype(f32) + branch
        mid_ref[:, at(j)] = middle
        return square + jnp.sum(middle * middle, axis=1, keepdims=True)

    square = lax.fori_loop(0, width // 512, branches, none, unroll=True)
    rms = lax.rsqrt(square / width + EPS)
    n2_ref[...] = (mid_ref[...] * rms * gffn_ref[...]).astype(bf16)
    weights.wait(2)
    ups = sides(n2_ref, core, ys)

    def up(j, unused):
        gu_ref[:, at(j)] = through(ups, weights.gu, j)
        return unused

    lax.fori_loop(0, 2 * ff // 512, up, 0)

    def hide(j, unused):
        gate = gu_ref[:, at(j)]
        hid_ref[:, at(j)] = (gate * sigmoid(gate) * gu_ref[:, at(j, ff)]).astype(bf16)
        return unused

    lax.fori_loop(0, ff // 512, hide, 0)
    hids = sides(hid_ref, core, ys)

    def finals(j, unused):
        out_ref[:, at(j)] = (mid_ref[:, at(j)] + through(hids, weights.down, j)).astype(bf16)
        return unused

    lax.fori_loop(0, width // 512, finals, 0, unroll=True)
    cot = cot_ref[...]
    back_through(dh_ref, cot, weights.down, 2)

    def unhide(j, unused):
        gate, lift, dhid = gu_ref[:, at(j)], gu_ref[:, at(j, ff)], dh_ref[:, at(j)]
        sg = sigmoid(gate)
        dgate = dhid * lift * (sg * (1.0 + gate * (1.0 - sg)))
        send_ref[:, at(j)] = dgate.astype(bf16)
        send_ref[:, at(j, ff)] = (dhid * gate * sg).astype(bf16)
        return unused

    lax.fori_loop(0, ff // 512, unhide, 0)
    send_ref[:, cot_at:dbr_at] = cot
    wide = width // ys // 2

    def down(j, totals):
        grad = send_ref[:, pl.ds(pl.multiple_of(j * 512, 512), 512)]
        return [t + nt(grad, weights.gu(i, y, j)) for t, (i, y) in zip(totals, pairs)]

    zero = [jnp.zeros((rows, wide), f32)] * len(pairs)
    totals = lax.fori_loop(0, 2 * ff // 512, down, zero)
    for y in range(ys):
        put(dn_ref, y, totals[2 * y], totals[2 * y + 1], core)
    unit = mid_ref[...] * rms
    dn = dn_ref[...]
    dn = dn * gffn_ref[...]
    dmid = cot.astype(f32) + rms * (dn - unit * jnp.mean(dn * unit, axis=1, keepdims=True))
    dmid_ref[...] = dmid
    dbr = dmid.astype(bf16)
    send_ref[:, dbr_at:dgate_at] = dbr
    back_through(datt_ref, dbr, weights.ao, 2)
    back_through(dmx_ref, dbr, weights.so, 2)

    def means(j, mean):
        unit = gd_ref[:, at(j)] * rms_gate
        return mean + jnp.sum(dmx_ref[:, at(j)] * gssm_ref[:, at(j)] * unit, axis=1, keepdims=True)

    mean = lax.fori_loop(0, DS // 512, means, none) / DS

    def ungate(j, unused):
        cols = at(j)
        unit = gd_ref[:, cols] * rms_gate
        dgated = rms_gate * (dmx_ref[:, cols] * gssm_ref[:, cols] - unit * mean)
        gate = gi_ref[:, cols]
        sg = sigmoid(gate)
        ssd = ycore_ref[:, cols] + skip_ref[:, cols] * x_ref[:, cols]
        dssd = dgated * gate * sg
        dssd_ref[:, cols] = dssd
        dgate = (dgated * ssd * (sg * (1.0 + gate * (1.0 - sg)))).astype(bf16)
        send_ref[:, at(j, dgate_at)] = dgate
        fd_ref[:, cols] = (dssd * fade_ref[:, cols]).astype(bf16)
        return unused

    lax.fori_loop(0, DS // 512, ungate, 0)
    back_through(dng_ref, send_ref[:, dgate_at:sel_at], weights.gate, 3)
    dentry_ref[...] = tn(fd_ref[...], reads)
    to = 0
    for ref in (n2_ref, hid_ref, att_ref, mixed_ref, normed_ref):
        count = ys
        wide = ref.shape[1] // count
        for y in range(count):
            own, oth = halves(ref[:, y * wide : (y + 1) * wide], core)
            keep_ref[:, to : to + wide // 2] = own
            send_ref[:, sel_at + to : sel_at + to + wide // 2] = oth
            to += wide // 2


def products_kernel(plan, extra, keep_ref, own_ref, act_ref, *refs):
    got_ref, outs = act_ref, refs
    if extra:
        (extra_ref, *outs) = refs
    for which, a_at, act_at, size, g_at in plan:
        out = outs[which]
        for y in range(out.shape[0]):
            left = keep_ref[:, a_at + y * size : a_at + (y + 1) * size]
            right = act_ref[: left.shape[0], act_at + y * size : act_at + (y + 1) * size]
            for j in range(0, out.shape[-1], 512):
                stop = min(j + 512, out.shape[-1])
                total = tn(left, own_ref[: left.shape[0], g_at + j : g_at + stop])
                total = total + tn(right, got_ref[: left.shape[0], g_at + j : g_at + stop])
                if extra and which == 0 and stop == out.shape[-1]:
                    total = total + extra_ref[y]
                out[y, :, j:stop] = total.astype(bf16)


def split_products_kernel(plan, extra, y_ref, x_ref, keep_ref, own_ref, act_ref, *refs):
    got_ref, outs = act_ref, refs
    if extra:
        (extra_ref, *outs) = refs
    xkeep_ref, xsend_ref, ykeep_ref, ysend_ref = outs
    rows = keep_ref.shape[0]
    my_y, my_x = y_ref[0], x_ref[0]
    for kind, place, a_at, act_at, size, g_at, wide in plan:
        for k in range(2):
            y = k if kind == "x" else lax.rem(my_y + k, 2)
            left = keep_ref[:, pl.ds(pl.multiple_of(a_at + y * size, LANES), size)]
            right = act_ref[:rows, pl.ds(pl.multiple_of(act_at + y * size, LANES), size)]
            keep, send = (xkeep_ref, xsend_ref) if kind == "x" else (ykeep_ref, ysend_ref)
            block = 512 if wide % 512 == 0 else 384

            def columns(j, unused):
                at = pl.ds(pl.multiple_of(g_at + j * block, LANES), block)
                total = tn(left, own_ref[:rows, at]) + tn(right, got_ref[:rows, at])
                if kind == "x":
                    zs, each = keep.shape[1], keep.shape[2]
                    if extra:
                        total = total + extra_ref[k] * (j == wide // block - 1).astype(f32)
                    cols = pl.ds(pl.multiple_of(place + j * block, LANES), block)
                    total = total.reshape(zs, 2, each, block)
                    low, high = total[:, 0], total[:, 1]
                    keep[k, :, :, cols] = jnp.where(my_x == 0, low, high).astype(bf16)
                    send[k, :, :, cols] = jnp.where(my_x == 0, high, low).astype(bf16)
                else:
                    count = keep.shape[0]
                    each = size // count
                    cols = pl.ds(pl.multiple_of(j * block, LANES), block)
                    total = total.reshape(count, each, block).astype(bf16)
                    (send if k else keep)[:, place : place + each, cols] = total
                return unused

            lax.fori_loop(0, wide // block, columns, 0, unroll=True)


def fold_one_kernel(
    y_ref, x_ref, xkeep_ref, xgot_ref, ykeep_ref, ygot_ref,
    xkeep_out, xsend_out, ykeep_out, ysend_out,
):
    my_y, my_x = y_ref[0], x_ref[0]
    xkeep_out[...] = xkeep_ref[my_y].astype(f32) + xgot_ref[my_y].astype(f32)
    other = 1 - my_y
    xsend_out[...] = (xkeep_ref[other].astype(f32) + xgot_ref[other].astype(f32)).astype(bf16)
    for z in range(ykeep_out.shape[0]):
        at = 2 * z + my_x
        ykeep_out[z] = ykeep_ref[at].astype(f32) + ygot_ref[at].astype(f32)
        at = 2 * z + 1 - my_x
        ysend_out[z] = (ykeep_ref[at].astype(f32) + ygot_ref[at].astype(f32)).astype(bf16)


def laid(refs, width):
    at = 0
    for ref in refs:
        each = ref.shape[-2]
        for j in range(ref.shape[-1] // width):
            yield ref, at, j * width
            at += each


def fold_two_kernel(z_ref, xkeep_ref, xgot_ref, ykeep_ref, ygot_ref, keep_out, send_out):
    low = lax.rem(z_ref[0], 2)
    width = keep_out.shape[2]
    keeps = laid((xkeep_ref, ykeep_ref), width)
    gots = laid((xgot_ref, ygot_ref), width)
    for (keep, at, col), (got, *unused) in zip(keeps, gots):
        rows, cols = slice(at, at + keep.shape[-2]), slice(col, col + width)
        for high in range(keep_out.shape[0]):
            for out, z in ((keep_out, 2 * high + low), (send_out, 2 * high + 1 - low)):
                value = keep[z, :, cols] + got[z, :, cols].astype(f32)
                out[high, rows, :] = value.astype(out.dtype)


def fold_three_kernel(z_ref, keep_ref, got_ref, keep_out, send_out):
    high = lax.div(z_ref[0], 2)
    keep_out[...] = keep_ref[high] + got_ref[high].astype(f32)
    other = 1 - high
    send_out[...] = (keep_ref[other] + got_ref[other].astype(f32)).astype(bf16)


def summed(refs, rows):
    keep_ref, got_ref = refs
    return keep_ref[rows, :] + got_ref[rows, :].astype(f32)


def fold_four_kernel(keep_ref, got_ref, *outs):
    for out, at, col in laid(outs, keep_ref.shape[1]):
        rows = slice(at, at + out.shape[0])
        out[:, col : col + keep_ref.shape[1]] = summed((keep_ref, got_ref), rows)


def row_sums(value):
    ones = jnp.ones((8, value.shape[1]), bf16)
    return sum(nt(ones, part) for part in terms(value, 3))[:1]


def finish_post_kernel(
    keep_ref, sum_ref, one_ref, guw_ref, sow_ref, gffn_ref, gssm_ref,
    gu_ref, gate_ref, ao_ref, so_ref, dffn_ref, dssm_ref,
):
    both = (keep_ref, sum_ref)
    part, ups = one_ref.shape
    wide = keep_ref.shape[1]
    gu_ref[:, :ups] = one_ref[...]
    at = 0
    for out, start in ((gu_ref, ups), (gate_ref, 0)):
        for col in range(start, out.shape[1], wide):
            out[:, col : col + wide] = summed(both, slice(at, at + part))
            at += part
    for col in range(0, ao_ref.shape[1], wide):
        for out in (ao_ref, so_ref):
            out[:, col : col + wide] = summed(both, slice(at, at + out.shape[0]))
            at += out.shape[0]
    dffn_ref[...] = row_sums(guw_ref[...].astype(f32) * gu_ref[...]) / gffn_ref[...]
    dssm_ref[...] = row_sums(sow_ref[...].astype(f32) * so_ref[...]) / gssm_ref[...]


def finish_front_kernel(
    keep_ref, sum_ref, gate_ref, kvw_ref, qw_ref, iw_ref, gain_ref,
    kv_ref, q_ref, inner_ref, conv_ref, bias_ref, log_ref, step_ref, skip_ref, dgain_ref,
):
    both = (keep_ref, sum_ref)
    part, wide = kv_ref.shape[0], keep_ref.shape[1]
    count = A_COLS // wide
    blocks = [summed(both, slice(k * part, (k + 1) * part)) for k in range(count)]
    first = jnp.concatenate(blocks, axis=1)
    kv_ref[...] = first[:, :256]
    q_ref[...] = first[:, 256:768]
    inner_ref[:, :DS] = gate_ref[...]
    for k in range(DS // wide):
        rows = slice((count + k) * part, (count + k + 1) * part)
        inner_ref[:, DS + k * wide : DS + (k + 1) * wide] = summed(both, rows)
    last = first[:, 1024:]
    inner_ref[:, 2 * DS : 2 * DS + 2 * STATE] = first[:, 768:1024]
    inner_ref[:, DS + CONV_CH :] = last[:, :SSM_HEADS]
    turned_last = last.T
    own = bias_ref.shape[1]
    conv_ref[...] = turned_last[SSM_HEADS : SSM_HEADS + own, :CONV]
    bias_ref[...] = last[CONV : CONV + 1, SSM_HEADS : SSM_HEADS + own]
    for k, out in enumerate((log_ref, step_ref, skip_ref)):
        out[...] = last[CONV + 1 + k : CONV + 2 + k, SSM_HEADS : 2 * SSM_HEADS]
    total = row_sums(kvw_ref[...].astype(f32) * kv_ref[...])
    total = total + row_sums(qw_ref[...].astype(f32) * q_ref[...])
    total = total + row_sums(iw_ref[...].astype(f32) * inner_ref[...])
    dgain_ref[...] = total / gain_ref[...]


class PairReduction:
    def __init__(self, pieces, width):
        self.places = tuple(place_on(g).reshape(1).astype(jnp.int32) for g in ("y", "x", "z"))
        self.xkeep, xsend, self.ykeep, ysend = pieces
        self.width = width
        self.send(xsend, ysend, "x", "y")

    def send(self, xsend, ysend, first, second):
        self.sent = (xsend, ysend)
        self.gots = (
            swap(xsend, extents()[first][0]), swap(ysend, extents()[second][0])
        )

    def fold_one(self, *others):
        gots = after(self.gots, *others)
        x, y = self.xkeep.shape, self.ykeep.shape
        x, y = x[1:], (y[0] // 2, *y[1:])
        self.xkeep, xsend, self.ykeep, ysend = run(
            fold_one_kernel, "fold_one", [(x, f32), (x, bf16), (y, f32), (y, bf16)],
            (*self.places[:2], self.xkeep, gots[0], self.ykeep, gots[1]),
            scalars=2,
        )
        self.send(xsend, ysend, "y", "x")

    def fold_two(self, *others):
        gots = after(self.gots, *others)
        self.shapes = [self.xkeep.shape[1:], self.ykeep.shape[1:]]
        rows = sum(r * c // self.width for r, c in self.shapes)
        half = (self.xkeep.shape[0] // 2, rows, self.width)
        self.keep, self.sent = run(
            fold_two_kernel, "fold_two", [(half, f32), (half, bf16)],
            (self.places[2], self.xkeep, gots[0], self.ykeep, gots[1]),
            scalars=1,
        )
        self.gots = swap(self.sent, extents()["z"][0])

    def fold_three(self, *others):
        whole = self.keep.shape[1:]
        self.keep, self.sent = run(
            fold_three_kernel, "fold_three", [(whole, f32), (whole, bf16)],
            (self.places[2], self.keep, after(self.gots, *others)),
            scalars=1,
        )
        self.gots = swap(self.sent, 2 * extents()["z"][0])

    def fold_four(self, *others):
        return run(
            fold_four_kernel, "fold_four", [(shape, f32) for shape in self.shapes],
            (self.keep, after(self.gots, *others)),
        )


class PlainReduction:
    def __init__(self, pieces, rows):
        self.parts = [Reduction(pieces[0], rows[0], "x"), Reduction(pieces[1], rows[1], "y")]
        self.sent = [part.send() for part in self.parts]

    def fold_one(self, *others):
        for part in self.parts:
            part.receive(*others)
        self.sent = [part.send() for part in self.parts]

    fold_two = fold_one

    def fold_three(self, *others):
        pass

    def fold_four(self, *others):
        return [part.receive(*others) for part in self.parts]


def scan_back_kernel(
    dy_ref, x_ref, bc_ref, step_ref, cum_ref, cumt_ref, off_ref, dxw_ref, ds_ref,
    xw_ref, ce_ref, dyb_ref, dg_ref,
):
    rows = x_ref.shape[0]
    spread = head_spread()
    xw_ref[...] = (x_ref[...] * nn_left(step_ref[...], spread, 2)).astype(bf16)
    dyb_ref[...] = dy_ref[...].astype(bf16)
    ce_ref[...] = nn_left(cum_ref[...], spread, 3)
    keys, reads = bc_ref[:, :STATE].astype(bf16), bc_ref[:, STATE:].astype(bf16)
    early, late = iota((rows, rows), 0), iota((rows, rows), 1)
    keep = (early <= late) & (early >= late - off_ref[...])
    scores = jnp.where(keep, nt(keys, reads), 0.0)
    lane = iota((rows, LANES), 1)
    dg_ref[...] = jnp.zeros((rows, rows), f32)

    def pair(j, unused):
        cols = pl.ds(pl.multiple_of(j * LANES, LANES), LANES)
        wide = ce_ref[:, cols]
        xw, dy = xw_ref[:, cols], dyb_ref[:, cols]
        outs = []
        change = 0.0
        for k in range(2):
            first = wide[:, k * SSM_DIM : k * SSM_DIM + 1]
            second = cumt_ref[pl.ds(2 * j + k, 1), :]
            decay = jnp.exp(jnp.minimum(second - first, 0.0))
            outs.append(nn((decay * scores).astype(bf16), dy))
            mine = (lane < SSM_DIM) if k == 0 else (lane >= SSM_DIM)
            change = change + nt(xw * mine.astype(bf16), dy) * decay
        dg_ref[...] += change
        dxw_ref[:, cols] = jnp.where(lane < SSM_DIM, outs[0], outs[1])
        return unused

    lax.fori_loop(0, SSM_HEADS // 2, pair, 0)
    ds_ref[...] = jnp.where(keep, dg_ref[...], 0.0).astype(bf16)


def mixer_back_kernel(
    dy_ref, ycore_ref, x_ref, bc_ref, step_ref, cum_ref, z_ref, off_ref, entry_ref,
    down_ref, skip_ref, dec_ref, chan_ref, cw_ref, cb_ref, dxwl_ref, ds_ref,
    dext_ref, dz_ref, small_ref,
    dact_ref,
):
    rows = x_ref.shape[0]
    spread, gather = head_spread(), head_sum_matrix()
    off, cum = off_ref[...], cum_ref[...]
    step_wide = nn_left(step_ref[...], spread, 2)
    keys, reads = bc_ref[:, :STATE].astype(bf16), bc_ref[:, STATE:].astype(bf16)
    dscores = ds_ref[...]
    down = down_ref[...].astype(bf16)
    tail = nn_left(tail_of(cum, off), spread, 2)
    fade = nn_left(fade_of(cum, off), spread, 2)
    bd = nt(keys, down) * tail
    xw = (x_ref[...] * step_wide).astype(bf16).astype(f32)
    dxw = dxwl_ref[...] + bd
    dact_ref[:, DS : DS + STATE] = nn(dscores, reads) + nn((tail * xw).astype(bf16), down)
    dact_ref[:, DS + STATE :] = tn(dscores, keys) + nn(
        (fade * dy_ref[...]).astype(bf16), entry_ref[...].astype(bf16)
    )
    ones = jnp.ones((8, STATE), bf16)
    product = sum(nt(ones, part) for part in terms(down_ref[...] * entry_ref[...], 3))
    through = jnp.sum(xw * bd, axis=0, keepdims=True)
    direct = jnp.sum(dy_ref[...] * x_ref[...], axis=0, keepdims=True)
    row = iota((8, DS), 0)
    sums = jnp.where(row == 0, product, jnp.where(row == 1, through, direct))
    sums = nn_left(sums, gather, 3)
    through, kept = sums[1:2], sums[0:1] * carry_of(cum, off)
    last = (iota((rows, 1), 0) == rows - 1).astype(f32)
    dyb = dy_ref[...].astype(bf16).astype(f32)
    dcum = nn_left(dyb * ycore_ref[...] - xw * dxw, gather, 2) + last * (through + kept)
    tri = (iota((rows, rows), 0) <= iota((rows, rows), 1)).astype(f32).astype(bf16)
    dlog = nn_right(tri, dcum, 3)
    x = x_ref[...]
    step, dec = step_ref[...], dec_ref[...]
    dstep = nn_left(dxw * x, gather, 2) - dlog * dec
    dz = dstep * sigmoid(z_ref[...])
    dz_ref[...] = dz
    small_ref[...] = jnp.zeros(small_ref.shape, f32)
    small_ref[CONV + 1 : CONV + 2, :LANES] = jnp.sum(dlog * (-step * dec), axis=0, keepdims=True)
    small_ref[CONV + 1 : CONV + 2, LANES : 2 * LANES] = jnp.sum(dz, axis=0, keepdims=True)
    small_ref[CONV + 1 : CONV + 2, 2 * LANES : 3 * LANES] = sums[2:3]
    dact_ref[:, :DS] = dxw * step_wide + skip_ref[...] * dy_ref[...]
    for j in range(CONV_CH // 256):
        cols = slice(j * 256, (j + 1) * 256)
        taps = conv_taps(chan_ref, cols, off)
        mixed = cb_ref[:, cols]
        for i, tap in enumerate(taps):
            mixed = mixed + tap * cw_ref[i : i + 1, cols]
        sg = sigmoid(mixed)
        dmix = dact_ref[:, cols] * (sg * (1.0 + mixed * (1.0 - sg)))
        small_ref[CONV : CONV + 1, cols] = jnp.sum(dmix, axis=0, keepdims=True)
        total = 0.0
        for i, tap in enumerate(taps):
            back = CONV - 1 - i
            small_ref[i : i + 1, cols] = jnp.sum(dmix * tap, axis=0, keepdims=True)
            part = dmix * ((off >= back).astype(f32) * cw_ref[i : i + 1, cols])
            part = jnp.concatenate([jnp.zeros((RIM, 256), f32), part], axis=0)
            total = total + (pltpu.roll(part, rows + RIM - back, 0) if back else part)
        dext_ref[:, cols] = total


def back_grads_kernel(
    ys, core_ref, dq_ref, dkv_ref, dext_ref, dz_ref, cos_ref, sin_ref, normed_ref, nrim_ref,
    small_ref, ga_ref, keep_ref,
):
    core = core_ref[0]
    count, last = small_ref.shape[0], keep_ref.shape[0]
    ga_ref[last:, :] = jnp.zeros((ga_ref.shape[0] - last, ga_ref.shape[1]), bf16)
    ga_ref[last : last + count, :CONV_CH] = small_ref[...].astype(bf16)
    dkv = dkv_ref[0].astype(f32)
    for i in range(1, dkv_ref.shape[0]):
        dkv = dkv + dkv_ref[i].astype(f32)
    ga_ref[:RIM, :768] = jnp.zeros((RIM, 768), bf16)
    ga_ref[:RIM, 1024:A_COLS] = jnp.zeros((RIM, LANES), bf16)
    ga_ref[RIM:last, :LANES] = turned_back(dkv[:, :LANES], cos_ref[...], sin_ref[...]).astype(bf16)
    ga_ref[RIM:last, LANES:256] = dkv[:, LANES:].astype(bf16)
    ga_ref[RIM:last, 256:768] = dq_ref[...]
    ga_ref[:last, 768:1024] = dext_ref[:, DS:].astype(bf16)
    ga_ref[RIM:last, 1024:A_COLS] = dz_ref[...].astype(bf16)
    ga_ref[:last, A_COLS : A_COLS + DS] = dext_ref[:, :DS].astype(bf16)
    wide = normed_ref.shape[1] // ys
    at, to = 0, A_COLS + DS
    for y in range(ys):
        cols = slice(y * wide, (y + 1) * wide)
        for ref, rows in ((nrim_ref, slice(0, RIM)), (normed_ref, slice(RIM, last))):
            own, oth = halves(ref[:, cols], core)
            keep_ref[rows, at : at + wide // 2] = own
            ga_ref[rows, to + at : to + at + wide // 2] = oth
        at += wide // 2


def back_kernel(
    core_ref, gab_ref, wa_own, wa_oth, wb_own, wb_oth, tok_ref, dmid_ref, dng_ref, gain_ref,
    dtok_ref, drim_ref, dn_ref,
):
    core = core_ref[0]
    for y in range(wa_own.shape[0]):
        last = tok_ref.shape[0]
        ga, gb = gab_ref[:last, :A_COLS], gab_ref[:last, A_COLS : A_COLS + DS]
        own = nt(ga, wa_own[y]) + nt(gb, wb_own[y])
        oth = nt(ga, wa_oth[y]) + nt(gb, wb_oth[y])
        put(dn_ref, y, own, oth, core)

    def through_norm(dn, tok):
        tok = tok.astype(f32)
        rms = lax.rsqrt(jnp.mean(tok * tok, axis=1, keepdims=True) + EPS)
        unit = tok * rms
        dn = dn * gain_ref[...]
        return rms * (dn - unit * jnp.mean(dn * unit, axis=1, keepdims=True))

    drim_ref[...] = through_norm(dn_ref[:RIM, :], tok_ref[:RIM, :])
    dtok_ref[...] = dmid_ref[...] + through_norm(dn_ref[RIM:, :] + dng_ref[...], tok_ref[RIM:, :])


def gain_kernel(pairs, count, *refs):
    gains, refs = refs[:count], refs[count:]
    outs = refs[-count:]
    for k, out in enumerate(outs):
        total = 0.0
        for group, w, g in pairs:
            if group == k:
                total = total + jnp.sum(
                    refs[w][...].astype(f32) * refs[g][...], axis=1, keepdims=True
                )
        out[...] = total / gains[k][...].astype(f32)


def run(kernel, name, outs, args, scalars=0, scratch=(), us=3, left=0, sems=()):
    moved = sum(a.size * a.dtype.itemsize for a in args)
    shapes = [jax.ShapeDtypeStruct(shape, kind) for shape, kind in outs]
    moved += sum(s.size * s.dtype.itemsize for s in shapes)
    specs = [pl.BlockSpec(memory_space=pltpu.SMEM)] * scalars
    specs += [pl.BlockSpec(memory_space=pltpu.VMEM)] * (len(args) - scalars - left)
    specs += [pl.BlockSpec(memory_space=pl.ANY)] * left
    return pl.pallas_call(
        kernel,
        name=name,
        out_shape=shapes,
        in_specs=specs,
        out_specs=[pl.BlockSpec(memory_space=pltpu.VMEM)] * len(shapes),
        scratch_shapes=[pltpu.VMEM(shape, kind) for shape, kind in scratch]
        + [pltpu.SemaphoreType.DMA(shape) for shape in sems],
        compiler_params=pltpu.CompilerParams(vmem_limit_bytes=62 * 2**20),
        cost_estimate=pl.CostEstimate(
            flops=us * SCALE, bytes_accessed=moved, transcendentals=0
        ),
    )(*args)


def padded(vector, width):
    return jnp.pad(vector.astype(f32), (0, width - vector.shape[0]))[None, :]


def local(
    tokens, lengths, cotangent, mixer_gain, query_weight, keyval_weight, inner_weight, conv_weight,
    conv_bias, ssm_gain, attn_out_weight, ssm_out_weight, ffn_gain, gate_up_weight, down_weight,
    decay_log, step_bias, skip_gain,
):
    rows, width = tokens.shape
    seq_count, seq_rank = lax.axis_size(SEQ), lax.axis_index(SEQ)
    side = place_on("core").reshape(1)
    back = (rows * seq_count // 2) // rows
    part = query_weight.shape[0]
    heads_width, ff = HEADS * HEAD_DIM, gate_up_weight.shape[1] // 2
    a_rows, s_rows, f_rows = attn_out_weight.shape[0], ssm_out_weight.shape[0], down_weight.shape[0]
    ys = lax.axis_size("y")

    rim = shifted(tokens[rows - RIM :], 1)
    small = jnp.concatenate(
        [mixer_gain, conv_weight.reshape(-1), conv_bias, ssm_gain, ffn_gain]
    ).astype(f32)
    counts = [mixer_gain.size, conv_weight.size, conv_bias.size, ssm_gain.size, ffn_gain.size]
    slots = -(-small.size // LANES) * LANES
    small = gather_small(jnp.pad(small, (0, slots - small.size)))
    others = lax.axis_size(SEQ)
    aligned = ys == 2 and others == 8 and all(r % 16 == 0 for r in (part, a_rows, s_rows, f_rows))
    core_unit = extents()["core"][0]
    pack_rows = 6 * part + s_rows + f_rows
    if aligned:
        packed, front = run(
            pack_kernel,
            "pack",
            [((pack_rows, width), bf16), ((part, A_COLS + DS), bf16)],
            (
                gate_up_weight, inner_weight, attn_out_weight, ssm_out_weight, down_weight,
                keyval_weight, query_weight,
            ),
        )
    else:
        tail = jnp.pad(inner_weight[:, DS + CONV_CH :], ((0, 0), (0, LANES - SSM_HEADS)))
        front = jnp.concatenate(
            [
                keyval_weight, query_weight, inner_weight[:, 2 * DS : DS + CONV_CH], tail,
                inner_weight[:, DS : 2 * DS],
            ],
            1,
        )
        ao = jnp.concatenate([attn_out_weight[:, :512], attn_out_weight[:, 512:]], 0)
        packed = jnp.concatenate(
            [
                inner_weight[:, :width],
                jnp.concatenate([inner_weight[:, width:DS], ao], 1),
                ssm_out_weight,
            ]
            + [gate_up_weight[:, k * width : (k + 1) * width] for k in range(2 * ff // width)]
            + [down_weight],
            0,
        )
    front = shared(front, "z")
    wa_own, wa_oth = gather_pair(front[:, :, :A_COLS], "y")
    wb_own, wb_oth = gather_pair(front[:, :, A_COLS:], "x")
    packed = lax.all_gather(packed, AXES, axis=0)
    packed = packed.reshape(ys, 2, others, *packed.shape[1:])
    starts = [sum(counts[:i]) for i in range(len(counts))]
    gain_one, w_conv, b_conv, gain_ssm, gain_two = (
        small[:, s : s + c].reshape(-1) for s, c in zip(starts, counts)
    )
    w_conv = jnp.pad(w_conv.reshape(CONV_CH, CONV).T, ((0, 8 - CONV), (0, 0)))
    gain_one, b_conv, gain_ssm, gain_two = (
        v[None, :] for v in (gain_one, b_conv, gain_ssm, gain_two)
    )
    tokens_rim = jnp.concatenate([rim, tokens], 0)
    places = seq_rank * rows + jnp.arange(rows)
    begin = jnp.zeros_like(places)
    end = jnp.int32(0)
    for i in range(lengths.shape[1]):
        end = end + lengths[0, i]
        begin = jnp.where(end <= places, end, begin)
    offset = (places - begin).astype(jnp.int32)
    half = HEAD_DIM // 2
    freq = BASE ** (-jnp.arange(half).astype(f32) / half)
    angle = offset.astype(f32)[:, None] * freq[None, :]
    cos = jnp.tile(jnp.cos(angle), (1, 4))
    sin = jnp.sin(angle)
    sin = jnp.tile(jnp.concatenate([-sin, sin], 1), (1, 2))
    off = offset[:, None]
    step_bias_row, decay_row = padded(step_bias, LANES), padded(jnp.exp(decay_log), LANES)
    skip = jnp.repeat(skip_gain, SSM_DIM)[None, :]

    (q8, kv, normed, nrim, chan, x, bc, step, cum, cumt, z, state, carry) = run(
        front_kernel,
        "front",
        [
            ((HEADS, rows, LANES), bf16),
            ((rows, 256), bf16),
            ((rows, width), bf16),
            ((RIM, width), bf16),
            ((rows + RIM, CONV_CH), bf16),
            ((rows, DS), f32),
            ((rows, 2 * STATE), f32),
            ((rows, LANES), f32),
            ((rows, LANES), f32),
            ((LANES, rows), f32),
            ((rows, LANES), f32),
            ((DS, STATE), f32),
            ((1, LANES), f32),
        ],
        (
            side, tokens_rim, gain_one, wa_own, wa_oth, wb_own, wb_oth,
            cos, sin, off, w_conv, b_conv, step_bias_row, decay_row,
        ),
        scalars=1,
        scratch=[((rows + RIM, width), bf16), ((rows, DS), bf16)],
        us=8,
    )
    carrying = Carrying(state, carry, back, 1)
    sent_state = carrying.send()
    rank = seq_rank.reshape(1).astype(jnp.int32)
    kv_slots = jnp.broadcast_to(kv[None], (seq_count, *kv.shape))
    kv_all = dealt(kv_slots, SEQ)
    window = (back + 1) * rows
    y_local = run(
        scan_kernel, "scan", [((rows, DS), f32)],
        after((x, bc, step, cum, cumt, off), sent_state, kv_slots),
        scratch=[((rows, DS), bf16), ((rows, DS), f32)], us=8,
    )[0]
    entry = carrying.receive(y_local)
    if entry is None:
        sent_state = carrying.send()
    attended, lse = run(
        functools.partial(attend_kernel, back + 1),
        "attend",
        [((rows, heads_width), bf16), ((LANES, rows), f32)],
        after((rank, q8, kv_all, off), sent_state),
        scalars=1,
        scratch=[
            ((window, LANES), bf16),
            ((window, LANES), bf16),
            ((rows, window), f32),
            ((HEADS, rows, LANES), f32),
        ],
        us=10,
    )
    while entry is None:
        entry = carrying.receive(attended)
        if entry is None:
            carrying.send()
    packed = after(packed, entry)
    post_scratch, post_sems = [], []
    if aligned:
        parts, post_weights = (part, a_rows, s_rows, f_rows), (packed,)
        post_scratch, post_sems = [((2, ys, others, *packed.shape[3:]), bf16)], [(3, 2)]
    else:
        parts = ()
        gu_at = 2 * part + s_rows
        packed = [
            lax.dynamic_index_in_dim(packed, place_on("core") ^ i, 1, False) for i in range(2)
        ]

        def taken(full, start, size, low, high):
            return full[:, :, start : start + size, low:high].reshape(ys, -1, high - low)

        def joined_columns(blocks):
            return [jnp.concatenate([taken(f, *block) for block in blocks], 2) for f in packed]

        post_weights = (
            *joined_columns([(0, part, 0, width), (part, part, 0, DS - width)]),
            *joined_columns([(part + k * a_rows, a_rows, 512, 1024) for k in range(2)]),
            *joined_columns([(2 * part, s_rows, 0, width)]),
            *joined_columns([(gu_at + 4 * part, f_rows, 0, width)]),
            *joined_columns([(gu_at + k * part, part, 0, width) for k in range(2 * ff // width)]),
        )

    half = (2 * width + ff + heads_width + DS) // 2
    sent = 2 * ff + 2 * width + DS
    output, dmid, datt, dssd, ycore, dentry, send, keep, dng = run(
        functools.partial(post_kernel, parts, ys),
        "post",
        [
            ((rows, width), bf16),
            ((rows, width), f32),
            ((rows, heads_width), bf16),
            ((rows, DS), f32),
            ((rows, DS), f32),
            ((DS, STATE), f32),
            ((rows, sent + half), bf16),
            ((rows, half), bf16),
            ((rows, width), f32),
        ],
        (
            side, tokens, cotangent, attended, y_local, x, bc, cum, off, entry, skip, normed,
            gain_ssm, gain_two, *post_weights,
        ),
        scalars=1,
        left=1 if aligned else 0,
        sems=post_sems,
        scratch=[
            ((rows, DS), f32),
            ((rows, DS), f32),
            ((rows, width), f32),
            ((rows, 2 * ff), f32),
            ((rows, width), f32),
            ((rows, DS), f32),
            ((rows, DS), bf16),
            ((rows, width), bf16),
            ((rows, ff), bf16),
            ((rows, DS), bf16),
            ((rows, ff), f32),
            ((rows, DS), f32),
            ((rows, DS), f32),
        ]
        + post_scratch,
        us=30,
    )
    got = swap(send, core_unit)
    carrying = Carrying(dentry, carry, back, -1)
    sent_state = carrying.send()
    off_row = offset[None, :]
    sizes = [width // 2, ff // 2, heads_width // 2, DS // 2, width // 2]
    ats = [sum(sizes[:i]) for i in range(5)]
    sizes = [size // ys for size in sizes]
    n2_at, hid_at, att_at, mix_at, norm_at = ats
    cot_at, dbr_at, dgate_at = 2 * ff, 2 * ff + width, 2 * ff + 2 * width
    places = tuple(place_on(g).reshape(1).astype(jnp.int32) for g in ("y", "x"))

    def weight_sums(name, x_parts, y_parts, keep, own, got, extra=()):
        plan, at, tall = [], 0, y_parts[0][4]
        for p in x_parts:
            plan.append(("x", at, *p))
            at += p[4]
        wide, at = at, 0
        for p in y_parts:
            plan.append(("y", at, *p))
            at += p[2] // others
        if aligned:
            xs = (ys, others // 2, x_parts[0][2] // others, wide)
            made = run(
                functools.partial(split_products_kernel, plan, len(extra)),
                name,
                [(xs, bf16), (xs, bf16), ((others, at, tall), bf16), ((others, at, tall), bf16)],
                (*places, keep, own, got, *extra),
                scalars=2,
                us=9,
            )
            return PairReduction(made, 512 if wide % 512 == 0 else 384)
        parts = x_parts + y_parts
        made = run(
            functools.partial(
                products_kernel, [(i, *p[:4]) for i, p in enumerate(parts)], len(extra)
            ),
            name,
            [((ys, p[2], p[4]), bf16) for p in parts],
            (keep, own, got, *extra),
            us=9,
        )
        heads = made[: len(x_parts)]
        tails = [m.reshape(ys, others, -1, tall) for m in made[len(x_parts) :]]
        rows_of = (x_parts[0][2] // others, at)
        return PlainReduction((jnp.concatenate(heads, 2), jnp.concatenate(tails, 2)), rows_of)

    dxw, dscores = run(
        scan_back_kernel,
        "scan_back",
        [((rows, DS), f32), ((rows, rows), bf16)],
        after((dssd, x, bc, step, cum, cumt, off_row), sent_state),
        scratch=[
            ((rows, DS), bf16),
            ((rows, DS), f32),
            ((rows, DS), bf16),
            ((rows, rows), f32),
        ],
        us=9,
    )

    downstream = carrying.receive(dxw)
    if downstream is None:
        sent_state = carrying.send()
    keep, send, got = after((keep, send, got), dxw, sent_state)
    red_one = weight_sums(
        "weights_one",
        [(n2_at, sent + n2_at, sizes[0], 0, ff)],
        [(hid_at, sent + hid_at, sizes[1], cot_at, width)],
        keep,
        send,
        got,
    )
    dq, dkv = run(
        functools.partial(attend_back_kernel, back + 1),
        "attend_back",
        [((rows, heads_width), bf16), ((seq_count, rows, 256), bf16)],
        after((rank, q8, kv_all, off_row, lse, datt, cos, sin), red_one.sent),
        scalars=1,
        scratch=[
            ((window, LANES), bf16),
            ((window, LANES), bf16),
            ((window, rows), f32),
            ((HEADS, rows, LANES), bf16),
            ((HEADS, rows, LANES), f32),
            ((window, 256), f32),
        ],
        us=14,
    )
    dkv_got = dealt(dkv, SEQ)
    keep, send, got = after((keep, send, got), red_one.sent, dq, dkv)
    red_two = weight_sums(
        "weights_two",
        [
            (n2_at, sent + n2_at, sizes[0], ff, ff),
            (norm_at, sent + norm_at, sizes[4], dgate_at, DS),
        ],
        [
            (att_at, sent + att_at, sizes[2], dbr_at, width),
            (mix_at, sent + mix_at, sizes[3], dbr_at, width),
        ],
        keep,
        send,
        got,
    )
    while downstream is None:
        downstream = carrying.receive(red_two.sent)
        if downstream is None:
            carrying.send()
    red_one.fold_one(red_two.sent, downstream)
    dext, dz, small = run(
        mixer_back_kernel,
        "mixer_back",
        [
            ((rows + RIM, CONV_CH), f32),
            ((rows, LANES), f32),
            ((8, CONV_CH), f32),
        ],
        after(
            (
                dssd, ycore, x, bc, step, cum, z, off, entry, downstream, skip, decay_row, chan,
                w_conv, b_conv, dxw, dscores,
            ),
            red_one.sent,
        ),
        scratch=[((rows, CONV_CH), f32)],
        us=13,
    )
    count = lax.axis_size(AXES)
    gab, norm_keep = run(
        functools.partial(back_grads_kernel, ys),
        "back_grads",
        [((rows + 2 * RIM, A_COLS + DS + width // 2), bf16), ((rows + RIM, width // 2), bf16)],
        (side, dq, dkv_got, dext, dz, cos, sin, normed, nrim, small),
        scalars=1,
    )
    gab_got = swap(gab, core_unit)
    small = small + gab_got[rows + RIM : rows + RIM + small.shape[0], :CONV_CH].astype(f32)
    free = LANES - SSM_HEADS
    convs = small[: CONV + 1].reshape(CONV + 1, count, -1).transpose(1, 0, 2)
    head_sums = small[CONV + 1, : 3 * LANES].reshape(3, LANES)[:, :SSM_HEADS]
    if aligned:
        head_sums = jnp.broadcast_to(head_sums[None], (count, 3, SSM_HEADS))
        per_device = jnp.concatenate(
            [
                jnp.pad(convs, ((0, 0), (0, 0), (0, free - convs.shape[2]))),
                jnp.pad(head_sums, ((0, 0), (0, 0), (0, free - SSM_HEADS))),
            ],
            1,
        )
        slots = CONV + 4
    else:
        head_sums = jnp.broadcast_to(head_sums.reshape(1, -1), (count, 3 * SSM_HEADS))
        per_device = jnp.concatenate([convs.reshape(count, -1), head_sums], 1)
        slots = per_device.shape[1]
        per_device = jnp.pad(per_device, ((0, 0), (0, part * free - slots)))
        per_device = per_device.reshape(count, part, free)
    per_device = lax.dynamic_index_in_dim(
        per_device.reshape(ys, 2, others, -1, free), place_on("core"), 1, False
    )
    aside = 384 if aligned else A_COLS % 512
    extra = jnp.pad(
        per_device, ((0, 0), (0, 0), (0, part - per_device.shape[2]), (aside - free, 0))
    ).reshape(ys, others * part, aside)
    grad_tokens, grad_rim = run(
        back_kernel,
        "back",
        [((rows, width), f32), ((RIM, width), f32)],
        (
            side, gab, wa_own, wa_oth, wb_own, wb_oth, tokens_rim, dmid, dng,
            gain_one,
        ),
        scalars=1,
        scratch=[((rows + RIM, width), f32)],
        us=7,
    )
    norm_keep, gab, gab_got, extra = after((norm_keep, gab, gab_got, extra), grad_tokens)
    red_three = weight_sums(
        "front_weights",
        [(0, A_COLS + DS, sizes[4], 0, A_COLS)],
        [(0, A_COLS + DS, sizes[4], A_COLS, DS)],
        norm_keep,
        gab,
        gab_got,
        (extra,),
    )
    red_two.fold_one(red_three.sent)
    red_one.fold_two(red_two.sent)
    red_three.fold_one(red_one.sent)
    red_one.fold_three(red_three.sent)
    red_two.fold_two(red_one.sent)
    red_three.fold_two(red_two.sent)
    red_two.fold_three(red_three.sent)
    rim_got = shifted(after(grad_rim, red_two.sent), -1)
    r_one, r_down = red_one.fold_four(red_two.sent)
    red_three.fold_three(r_one)
    if aligned:
        r_gu, r_gate, r_ao, r_so, g_ffn, g_ssm = run(
            finish_post_kernel,
            "finish_post",
            [
                ((part, 2 * ff), f32),
                ((part, DS), f32),
                ((a_rows, width), f32),
                ((s_rows, width), f32),
                ((1, part), f32),
                ((1, s_rows), f32),
            ],
            (
                red_two.keep, after(red_two.gots, red_three.sent), r_one, gate_up_weight, ssm_out_weight,
                ffn_gain.astype(f32)[None, :], ssm_gain.astype(f32)[None, :],
            ),
        )
        rim_got = after(rim_got, r_gu)
        grad_tokens = grad_tokens.at[rows - RIM :].add(rim_got)
        r_kv, r_q, g_inner, g_conv, g_bias, g_log, g_step, g_skip, g_mixer = run(
            finish_front_kernel,
            "finish_front",
            [
                ((part, 256), f32),
                ((part, heads_width), f32),
                ((part, inner_weight.shape[1]), f32),
                (conv_weight.shape, f32),
                ((1, conv_bias.size), f32),
                ((1, SSM_HEADS), f32),
                ((1, SSM_HEADS), f32),
                ((1, SSM_HEADS), f32),
                ((1, part), f32),
            ],
            (
                red_three.keep, after(red_three.gots, grad_tokens), r_gate, keyval_weight, query_weight,
                inner_weight, mixer_gain.astype(f32)[None, :],
            ),
        )
        g_bias, g_mixer, g_ssm, g_ffn = (v[0] for v in (g_bias, g_mixer, g_ssm, g_ffn))
        heads = [v[0] for v in (g_log, g_step, g_skip)]
    else:
        r_two, r_out = red_two.fold_four(red_three.sent)
        rim_got = after(rim_got, r_two)
        grad_tokens = grad_tokens.at[rows - RIM :].add(rim_got)
        r_e, r_f = red_three.fold_four(grad_tokens)
        r_gu = jnp.concatenate([r_one, r_two[:, :ff]], 1)
        small = r_e[:, A_COLS - free :].reshape(-1)[:slots]
        conv = small[: (CONV + 1) * conv_bias.size].reshape(CONV + 1, -1)
        g_conv, g_bias = conv[:CONV].T, conv[CONV]
        heads = small[(CONV + 1) * conv_bias.size :].reshape(3, SSM_HEADS)
        g_inner = jnp.concatenate([r_two[:, ff:], r_f, r_e[:, 768 : 1024 + SSM_HEADS]], 1)
        r_kv, r_q, r_ao, r_so = r_e[:, :256], r_e[:, 256:768], r_out[:a_rows], r_out[a_rows:]
        pairs = [(0, 0, 1), (0, 2, 3), (0, 4, 5), (1, 6, 7), (2, 8, 9)]
        gains = run(
            functools.partial(gain_kernel, pairs, 3),
            "gains",
            [((part, 1), f32), ((s_rows, 1), f32), ((part, 1), f32)],
            (
                mixer_gain[:, None], ssm_gain[:, None], ffn_gain[:, None],
                keyval_weight, r_kv, query_weight, r_q, inner_weight, g_inner,
                ssm_out_weight, r_so, gate_up_weight, r_gu,
            ),
        )
        g_mixer, g_ssm, g_ffn = (v[:, 0] for v in gains)
    return (
        output,
        grad_tokens,
        g_mixer,
        r_q,
        r_kv,
        g_inner,
        g_conv,
        g_bias,
        g_ssm,
        r_ao,
        r_so,
        g_ffn,
        r_gu,
        r_down,
        heads[0],
        heads[1],
        heads[2],
    )


def solution(mesh):
    across, along = mesh.shape["dp"], mesh.shape["seq"]
    mesh = jax.sharding.Mesh(mesh.devices.reshape(across // 2, 2, along // 2, 2), AXES)
    lead, flat, rep = P(AXES, None), P(AXES), P()
    return jax.shard_map(
        local,
        mesh=mesh,
        in_specs=(
            lead, P(AXES[:2], None), lead, flat, lead, lead, lead, lead, flat, flat, lead, lead, flat,
            lead, lead, rep, rep, rep,
        ),
        out_specs=(
            lead, lead, flat, lead, lead, lead, lead, flat, flat, lead, lead, flat, lead, lead,
            rep, rep, rep,
        ),
        check_vma=False,
    )
```

```python
import functools

import jax
import jax.numpy as jnp
from jax import lax
from jax.experimental import pallas as pl
from jax.experimental.pallas import tpu as pltpu
from jax.sharding import PartitionSpec as P

HEADS = 8
KV_HEADS = 2
HEAD_DIM = 64
SSM_HEADS = 24
SSM_DIM = 64
STATE = 128
CONV = 4
DS = 1536
CONV_CH = 1792
RIM = 16
LANES = 128
A_COLS = 2 * KV_HEADS * HEAD_DIM + HEADS * HEAD_DIM + 2 * STATE + LANES
EPS = 1e-6
BASE = 10000.0
NEG = -1e30
SCALE = 6_600_000_000
AXES = ("y", "core", "z", "x")
SEQ = AXES[2:]

f32 = jnp.float32
bf16 = jnp.bfloat16


def nn(a, b):
    return lax.dot_general(a, b, (((1,), (0,)), ((), ())), preferred_element_type=f32)


def tn(a, b):
    return lax.dot_general(a, b, (((0,), (0,)), ((), ())), preferred_element_type=f32)


def nt(a, b):
    return lax.dot_general(a, b, (((1,), (1,)), ((), ())), preferred_element_type=f32)


def terms(value, count):
    parts = []
    for unused in range(count):
        parts.append(value.astype(bf16))
        value = value - parts[-1].astype(f32)
    return parts


def nn_left(value, ones, count):
    return sum(nn(part, ones) for part in terms(value, count))


def nn_right(ones, value, count):
    return sum(nn(ones, part) for part in terms(value, count))


def iota(shape, dim):
    return lax.broadcasted_iota(jnp.int32, shape, dim)


def head_spread():
    row = iota((LANES, DS), 0)
    return (iota((LANES, DS), 1) // SSM_DIM == row).astype(f32).astype(bf16)


def head_sum_matrix():
    col = iota((DS, LANES), 1)
    return (iota((DS, LANES), 0) // SSM_DIM == col).astype(f32).astype(bf16)


def extents():
    along = lax.axis_size(SEQ)
    return {
        "x": (1, 2),
        "z": (2, along // 2),
        "core": (along, 2),
        "y": (2 * along, lax.axis_size("y")),
    }


def my_index():
    return lax.axis_index(AXES)


def place_on(group):
    unit, size = extents()[group]
    return (my_index() // unit) % size


def swap(array, mask):
    count = lax.axis_size(AXES)
    return lax.ppermute(array, AXES, [(i, i ^ mask) for i in range(count)])


def in_order(pieces, place):
    pieces = list(pieces)
    bit = 1
    while bit < len(pieces):
        flag = (place // bit) % 2 == 1
        pieces = [jnp.where(flag, pieces[j ^ bit], pieces[j]) for j in range(len(pieces))]
        bit *= 2
    return pieces


def collect(array, group, axis):
    unit, size = extents()[group]
    pieces = [array] + [swap(array, k * unit) for k in range(1, size)]
    return jnp.stack(in_order(pieces, place_on(group)), axis)


class Gathering:
    def __init__(self, full, first):
        self.full = full
        self.steps = [("y", 0), ("x", 2)] if first == "y" else [("x", 1), ("y", 0)]
        self.start()

    def start(self):
        unit, size = extents()[self.steps[0][0]]
        self.got = [swap(self.full, k * unit) for k in range(1, size)]

    def finish(self, *others):
        group, axis = self.steps.pop(0)
        pieces = [self.full] + list(after(self.got, *others))
        self.full = jnp.stack(in_order(pieces, place_on(group)), axis)
        if self.steps:
            self.start()
        else:
            self.other = swap(self.full, extents()["core"][0])

    def sides(self, kept):
        shape = (self.full.shape[0], -1, *self.full.shape[5 - kept :])
        return self.full.reshape(shape), self.other.reshape(shape)


def cut(total, group, axis):
    size = extents()[group][1]
    place = place_on(group)
    keep = lax.dynamic_index_in_dim(total, place, axis, False)
    parts = [lax.dynamic_index_in_dim(total, place ^ k, axis, False) for k in range(1, size)]
    return keep, [p.astype(bf16) for p in parts]


def crossed(parts, group):
    unit = extents()[group][0]
    return [swap(part, (k + 1) * unit) for k, part in enumerate(parts)]


def joined(keep, received):
    total = keep.astype(f32)
    for part in received:
        total = total + part.astype(f32)
    return total


class Reduction:
    def __init__(self, total, rows, first):
        table = extents()
        self.total = total.reshape(
            table["y"][1], table["z"][1], table["x"][1], rows, total.shape[-1]
        )
        order = [("x", 2), ("y", 0)] if first == "x" else [("y", 0), ("x", 1)]
        self.stages = order + [("z", 0)]

    def send(self):
        (group, axis), self.stages = self.stages[0], self.stages[1:]
        self.keep, self.parts = cut(self.total, group, axis)
        self.received = crossed(self.parts, group)
        return self.parts

    def receive(self, *others):
        self.received = after(self.received, *others)
        self.total = joined(self.keep, self.received)
        return self.total


def after(value, *others):
    return lax.optimization_barrier((value, others))[0]


def gather_small(vector):
    full = collect(collect(collect(vector, "z", 0), "x", 1), "core", 0)
    return collect(full, "y", 0).reshape(-1, vector.shape[-1])


def dealt(array, axes):
    return lax.all_to_all(array, axes, 0, 0, tiled=True)


def shared(array, axes):
    return dealt(jnp.broadcast_to(array[None], (lax.axis_size(axes), *array.shape)), axes)


def shifted(array, by):
    count = lax.axis_size(SEQ)
    pairs = [(i, i + by) for i in range(count) if 0 <= i + by < count]
    return lax.ppermute(array, SEQ, pairs)


def link(earlier, later):
    carry = later[1]
    wide = jnp.repeat(carry[0, :SSM_HEADS], SSM_DIM)[:, None]
    return (later[0] + wide * earlier[0], carry * earlier[1])


class Carrying:
    def __init__(self, state, carry, back, sign):
        self.pair, self.back, self.sign, self.by = (state, carry), back, sign, 0

    def send(self):
        packed = jnp.concatenate(
            [self.pair[0], jnp.pad(self.pair[1], ((0, RIM - 1), (0, 0)))], 0
        ).astype(bf16)
        steps = [self.by] if self.by else [1] + [2] * (self.back > 1)
        self.got = [shifted(packed, self.sign * by) for by in steps]
        return packed

    def receive(self, *others):
        pairs = []
        for got in after(self.got, *others):
            got = got.astype(f32)
            pairs.append((got[:DS], got[DS : DS + 1]))
        self.by = 2 * self.by if self.by else min(self.back, 2)
        if len(pairs) == 2:
            self.pair = link(pairs[1], pairs[0])
        else:
            self.pair = link(pairs[0], self.pair) if self.by > 2 else pairs[0]
        return self.pair[0] if self.by >= self.back else None


def halves(block, core):
    width = block.shape[1] // 2
    low, high = block[:, :width], block[:, width:]
    return jnp.where(core == 0, low, high), jnp.where(core == 0, high, low)


def put(ref, y, own, other, core):
    width = own.shape[1]
    base = y * 2 * width
    ref[:, base : base + width] = jnp.where(core == 0, own, other).astype(ref.dtype)
    ref[:, base + width : base + 2 * width] = jnp.where(core == 0, other, own).astype(ref.dtype)


def sides(ref, core, count):
    width = ref.shape[-1] // count
    return [halves(ref[:, y * width : (y + 1) * width], core) for y in range(count)]


def cross_half(value):
    lane = iota(value.shape, 1) % HEAD_DIM
    up = pltpu.roll(value, LANES - HEAD_DIM // 2, 1)
    down = pltpu.roll(value, HEAD_DIM // 2, 1)
    return jnp.where(lane < HEAD_DIM // 2, up, down)


def turned(value, cos, sin):
    return value * cos + cross_half(value) * sin


def turned_back(value, cos, sin):
    return value * cos - cross_half(value) * sin


def split_heads(pair, which, lane):
    flipped = pltpu.roll(pair, HEAD_DIM, 1)
    if which == 0:
        return jnp.where(lane < HEAD_DIM, pair, 0.0), jnp.where(lane < HEAD_DIM, flipped, 0.0)
    return jnp.where(lane >= HEAD_DIM, flipped, 0.0), jnp.where(lane >= HEAD_DIM, pair, 0.0)


def join_heads(even, odd, which, lane):
    if which == 0:
        return jnp.where(lane < HEAD_DIM, even, pltpu.roll(odd, HEAD_DIM, 1))
    return jnp.where(lane < HEAD_DIM, pltpu.roll(even, HEAD_DIM, 1), odd)


def conv_taps(chan_ref, cols, off):
    ext = chan_ref[:, cols].astype(f32)
    taps = []
    for i in range(CONV):
        back = CONV - 1 - i
        rows = pltpu.roll(ext, back, 0)[RIM:] if back else ext[RIM:]
        taps.append(rows * (off >= back).astype(f32))
    return taps


def sigmoid(v):
    return 1.0 / (1.0 + jnp.exp(-v))


def softplus(v):
    return jnp.maximum(v, 0.0) + jnp.log1p(jnp.exp(-jnp.abs(v)))


def tail_of(cum, off):
    rows = cum.shape[0]
    last_off = off[rows - 1 :, :]
    keep = iota((rows, 1), 0) >= rows - 1 - last_off
    return jnp.exp(cum[rows - 1 :, :] - cum) * keep.astype(f32)


def fade_of(cum, off):
    keep = off > iota((cum.shape[0], 1), 0)
    return jnp.exp(cum) * keep.astype(f32)


def carry_of(cum, off):
    rows = cum.shape[0]
    return jnp.exp(cum[rows - 1 :, :]) * (off[rows - 1 :, :] >= rows).astype(f32)


def pack_kernel(
    gu_ref, inner_ref, ao_ref, so_ref, kv_ref, q_ref, post_ref, front_ref
):
    part, width = gu_ref.shape[0], post_ref.shape[1]
    a_rows = ao_ref.shape[0]
    post_ref[:part, :] = inner_ref[:, :width]
    post_ref[part : 2 * part, : DS - width] = inner_ref[:, width:DS]
    for k in range(2):
        rows = slice(part + k * a_rows, part + (k + 1) * a_rows)
        post_ref[rows, DS - width :] = ao_ref[:, k * 512 : (k + 1) * 512]
    at = 2 * part
    post_ref[at : at + so_ref.shape[0], :] = so_ref[...]
    at += so_ref.shape[0]
    for k in range(gu_ref.shape[1] // width):
        post_ref[at : at + part, :] = gu_ref[:, k * width : (k + 1) * width]
        at += part
    front_ref[:, :256] = kv_ref[...]
    front_ref[:, 256:768] = q_ref[...]
    front_ref[:, 768:1024] = inner_ref[:, 2 * DS : DS + CONV_CH]
    front_ref[:, 1024:A_COLS] = jnp.zeros((part, LANES), bf16)
    front_ref[:, 1024 : 1024 + SSM_HEADS] = inner_ref[:, DS + CONV_CH :]
    front_ref[:, A_COLS:] = inner_ref[:, DS : 2 * DS]


def front_kernel(
    core_ref, tok_ref, gain_ref, wa_own, wa_oth, wb_own, wb_oth, cos_ref, sin_ref, off_ref,
    cw_ref, cb_ref, sb_ref, dec_ref,
    q8_ref, kv_ref, normed_ref, nrim_ref, chan_ref, x_ref, bc_ref, step_ref, cum_ref, cumt_ref, z_ref,
    state_ref, carry_ref,
    n_ref, xt_ref,
):
    core = core_ref[0]
    rows = cos_ref.shape[0]
    tok = tok_ref[...].astype(f32)
    rms = lax.rsqrt(jnp.mean(tok * tok, axis=1, keepdims=True) + EPS)
    n_ref[...] = (tok * rms * gain_ref[...]).astype(bf16)
    normed_ref[...] = n_ref[RIM:, :]
    nrim_ref[...] = n_ref[:RIM, :]
    count = wa_own.shape[0]
    blocks = sides(n_ref, core, count)

    def project(own_ref, oth_ref, cols):
        total = 0.0
        for y, (own, oth) in enumerate(blocks):
            total = total + nn(own, own_ref[y, :, cols]) + nn(oth, oth_ref[y, :, cols])
        return total

    lane = iota((rows, LANES), 1)
    cos, sin, off = cos_ref[...], sin_ref[...], off_ref[...]
    kv = project(wa_own, wa_oth, pl.ds(0, 256))[RIM:]
    kv_ref[:, :LANES] = turned(kv[:, :LANES], cos, sin).astype(bf16)
    kv_ref[:, LANES:] = kv[:, LANES:].astype(bf16)
    queries = project(wa_own, wa_oth, pl.ds(256, 512))[RIM:]
    for j in range(HEADS // 2):
        pair = turned(queries[:, j * LANES : (j + 1) * LANES], cos, sin)
        even, odd = split_heads(pair, j // 2, lane)
        q8_ref[2 * j] = even.astype(bf16)
        q8_ref[2 * j + 1] = odd.astype(bf16)
    rest = project(wa_own, wa_oth, pl.ds(768, 384))
    chan_ref[:, DS:] = rest[:, : 2 * STATE].astype(bf16)
    z = rest[RIM:, 2 * STATE :].astype(bf16).astype(f32) + sb_ref[...]
    for j in range(DS // 512):
        cols = slice(j * 512, (j + 1) * 512)
        chan_ref[:, cols] = project(wb_own, wb_oth, pl.ds(j * 512, 512)).astype(bf16)
    z_ref[...] = z
    step = softplus(z)
    step_ref[...] = step
    tri = (iota((rows, rows), 0) >= iota((rows, rows), 1)).astype(f32).astype(bf16)
    cum = nn_right(tri, -step * dec_ref[...], 3)
    cum_ref[...] = cum
    cumt_ref[...] = cum.T
    carry_ref[...] = carry_of(cum, off)
    weight = nn_left(step * tail_of(cum, off), head_spread(), 2)
    for j in range(CONV_CH // 256):
        cols = slice(j * 256, (j + 1) * 256)
        mixed = cb_ref[:, cols]
        for i, tap in enumerate(conv_taps(chan_ref, cols, off)):
            mixed = mixed + tap * cw_ref[i : i + 1, cols]
        active = mixed * sigmoid(mixed)
        if j < DS // 256:
            x_ref[:, cols] = active
            xt_ref[:, cols] = (active * weight[:, cols]).astype(bf16)
        else:
            bc_ref[...] = active
    state_ref[...] = tn(xt_ref[...], bc_ref[:, :STATE].astype(bf16))


def scan_masks(off, rows):
    t, s = iota((rows, rows), 0), iota((rows, rows), 1)
    return (s <= t) & (s >= t - off)


def scan_kernel(x_ref, bc_ref, step_ref, cum_ref, cumt_ref, off_ref, y_ref, xw_ref, ce_ref):
    rows = x_ref.shape[0]
    spread = head_spread()
    xw_ref[...] = (x_ref[...] * nn_left(step_ref[...], spread, 2)).astype(bf16)
    ce_ref[...] = nn_left(cum_ref[...], spread, 3)
    keys, reads = bc_ref[:, :STATE].astype(bf16), bc_ref[:, STATE:].astype(bf16)
    scores = jnp.where(scan_masks(off_ref[...], rows), nt(reads, keys), 0.0)
    lane = iota((rows, LANES), 1)

    def pair(j, unused):
        cols = pl.ds(pl.multiple_of(j * LANES, LANES), LANES)
        wide = ce_ref[:, cols]
        xw = xw_ref[:, cols]
        outs = []
        for k in range(2):
            late = wide[:, k * SSM_DIM : k * SSM_DIM + 1]
            early = cumt_ref[pl.ds(2 * j + k, 1), :]
            decay = jnp.exp(jnp.minimum(late - early, 0.0))
            outs.append(nn((decay * scores).astype(bf16), xw))
        y_ref[:, cols] = jnp.where(lane < SSM_DIM, outs[0], outs[1])
        return unused

    lax.fori_loop(0, SSM_HEADS // 2, pair, 0)


def attend_bias(off, rows, window):
    query = iota((rows, window), 0) + (window - rows)
    key = iota((rows, window), 1)
    return jnp.where((key <= query) & (key >= query - off), 0.0, NEG)


def window_of(count, rank, kv_ref, k_ref, v_ref):
    rows = kv_ref.shape[1]
    for i in range(count):
        piece = jnp.maximum(rank - (count - 1 - i), 0)
        k_ref[i * rows : (i + 1) * rows, :] = kv_ref[piece, :, :LANES]
        v_ref[i * rows : (i + 1) * rows, :] = kv_ref[piece, :, LANES:]


def attend_kernel(
    count, rank_ref, q8_ref, kv_ref, off_ref, att_ref, lse_ref, k_ref, v_ref, bias_ref, o_ref
):
    rows = off_ref.shape[0]
    window = count * rows
    window_of(count, rank_ref[0], kv_ref, k_ref, v_ref)
    bias_ref[...] = attend_bias(off_ref[...], rows, window)
    lane = iota((rows, LANES), 1)

    def head(h, lses):
        scores = nt(q8_ref[h], k_ref[...]) * HEAD_DIM**-0.5 + bias_ref[...]
        top = jnp.max(scores, axis=1, keepdims=True)
        probs = jnp.exp(scores - top)
        total = jnp.sum(probs, axis=1, keepdims=True)
        o_ref[h] = nn((probs * (1.0 / total)).astype(bf16), v_ref[...])
        return jnp.where(lane == h, top + jnp.log(total), lses)

    lse_ref[...] = lax.fori_loop(0, HEADS, head, jnp.zeros((rows, LANES), f32)).T
    for j in range(HEADS // 2):
        pair = join_heads(o_ref[2 * j], o_ref[2 * j + 1], j // 2, lane)
        att_ref[:, j * LANES : (j + 1) * LANES] = pair.astype(bf16)


def attend_back_kernel(
    count, rank_ref, q8_ref, kv_ref, off_ref, lse_ref, datt_ref, cos_ref, sin_ref,
    dq_ref, out_ref, k_ref, v_ref, bias_ref, do_ref, dq8_ref, dkv_ref,
):
    rows = off_ref.shape[1]
    window = count * rows
    rank = rank_ref[0]
    window_of(count, rank, kv_ref, k_ref, v_ref)
    query = iota((window, rows), 1) + (window - rows)
    key = iota((window, rows), 0)
    bias_ref[...] = jnp.where((key <= query) & (key >= query - off_ref[...]), 0.0, NEG)
    lane = iota((rows, LANES), 1)
    for j in range(HEADS // 2):
        pair = datt_ref[:, j * LANES : (j + 1) * LANES].astype(f32)
        even, odd = split_heads(pair, j // 2, lane)
        do_ref[2 * j] = even.astype(bf16)
        do_ref[2 * j + 1] = odd.astype(bf16)
    dkv_ref[...] = jnp.zeros(dkv_ref.shape, f32)

    def head(h, unused):
        query, grad = q8_ref[h], do_ref[h]
        scores = nt(k_ref[...], query) * HEAD_DIM**-0.5 + bias_ref[...]
        probs = jnp.exp(scores - lse_ref[pl.ds(h, 1), :])
        dprobs = nt(v_ref[...], grad)
        mean = jnp.sum(probs * dprobs, axis=0, keepdims=True)
        draw = (probs * (dprobs - mean) * HEAD_DIM**-0.5).astype(bf16)
        dkv_ref[:, :LANES] += nn(draw, query)
        dkv_ref[:, LANES:] += nn(probs.astype(bf16), grad)
        dq8_ref[h] = tn(draw, k_ref[...])
        return unused

    lax.fori_loop(0, HEADS, head, 0)
    out_ref[...] = jnp.zeros(out_ref.shape, bf16)
    for i in range(count):
        piece = rank - (count - 1 - i)

        @pl.when(piece >= 0)
        def unused():
            out_ref[piece] = dkv_ref[i * rows : (i + 1) * rows, :].astype(bf16)

    for j in range(HEADS // 2):
        pair = join_heads(dq8_ref[2 * j], dq8_ref[2 * j + 1], j // 2, lane)
        back = turned_back(pair, cos_ref[...], sin_ref[...])
        dq_ref[:, j * LANES : (j + 1) * LANES] = back.astype(bf16)


class PackedWeights:
    def __init__(self, most, downs, core, held, sems, parts):
        self.held = held
        part, a_part, s_part, f_part = self.parts = parts
        self.so_at = 2 * part
        self.gu_at = self.so_at + s_part
        self.down_at = self.gu_at + 4 * part
        places = [
            (0, self.so_at), (self.so_at, s_part), (self.gu_at, 4 * part), (self.down_at, f_part),
        ]
        self.copies = []
        for k, (at, size) in enumerate(places):
            pair = []
            for i in range(2):
                rows = pl.ds(at, size)
                source = most.at[:, lax.rem(core + i, 2), :, rows] if k < 3 else downs[i]
                target = held.at[i, :, :, rows]
                pair.append(pltpu.make_async_copy(source, target, sems.at[k, i]))
            self.copies.append(pair)
        for pair in self.copies:
            for copy in pair:
                copy.start()

    def wait(self, k):
        for copy in self.copies[k]:
            copy.wait()

    def block(self, i, y, start, size, col):
        rows, cols = pl.ds(pl.multiple_of(start, 16), size), pl.ds(pl.multiple_of(col, 512), 512)
        got = self.held[i, y, :, rows, cols]
        return got.reshape(got.shape[0] * size, 512)

    def gate(self, i, y, j):
        part = self.parts[0]
        return self.block(i, y, j // 2 * part, part, j % 2 * 512)

    def ao(self, i, y, j):
        part, a_part = self.parts[:2]
        return self.block(i, y, part + j * a_part, a_part, 512)

    def so(self, i, y, j):
        return self.block(i, y, self.so_at, self.parts[2], j * 512)

    def down(self, i, y, j):
        return self.block(i, y, self.down_at, self.parts[3], j * 512)

    def gu(self, i, y, j):
        part = self.parts[0]
        return self.block(i, y, self.gu_at + j // 2 * part, part, j % 2 * 512)


class PlainWeights:
    def __init__(self, refs):
        self.refs = refs

    def wait(self, k):
        pass

    def block(self, name, i, y, j):
        return self.refs[2 * name + i][y, :, pl.ds(pl.multiple_of(j * 512, 512), 512)]

    def gate(self, i, y, j):
        return self.block(0, i, y, j)

    def ao(self, i, y, j):
        return self.block(1, i, y, j)

    def so(self, i, y, j):
        return self.block(2, i, y, j)

    def down(self, i, y, j):
        return self.block(3, i, y, j)

    def gu(self, i, y, j):
        return self.refs[8 + i][y, :, pl.ds(pl.multiple_of(j * 512, 512), 512)]


def post_kernel(
    parts, ys, core_ref, tok_ref, cot_ref, att_ref, yl_ref, x_ref, bc_ref, cum_ref, off_ref,
    entry_ref, skip_ref, normed_ref, gssm_ref, gffn_ref, *refs,
):
    if parts:
        weights = PackedWeights(refs[0], refs[1:3], core_ref[0], refs[-2], refs[-1], parts)
        refs = refs[3:-2]
    else:
        weights, refs = PlainWeights(refs[:10]), refs[10:]
    pairs = [(i, y) for y in range(ys) for i in range(2)]

    def through(blocks, weight, j):
        return sum(nn(blocks[y][i], weight(i, y, j)) for i, y in pairs)

    def back_through(ref, grad, weight, count):
        for y in range(ys):
            both = []
            for i in range(2):
                both.append(
                    sum(nt(grad[:, j * 512 : j * 512 + 512], weight(i, y, j)) for j in range(count))
                )
            put(ref, y, both[0], both[1], core)

    (
        out_ref, dmid_ref, datt_ref, dssd_ref, ycore_ref, dentry_ref, send_ref, keep_ref, dng_ref,
        gi_ref, gd_ref, mid_ref, gu_ref, dn_ref, dmx_ref, fd_ref, n2_ref, hid_ref, mixed_ref, dh_ref, fade_ref, ent_ref,
    ) = refs
    core = core_ref[0]
    rows, width = tok_ref.shape
    heads_width = att_ref.shape[1]
    ff = hid_ref.shape[1]
    half = keep_ref.shape[1]
    cot_at, dbr_at, dgate_at, sel_at = 2 * ff, 2 * ff + width, 2 * ff + 2 * width, 2 * ff + 2 * width + DS
    reads = bc_ref[:, STATE:].astype(bf16)
    spread = head_spread()
    fade_ref[...] = nn_left(fade_of(cum_ref[...], off_ref[...]), spread, 2)
    ent_ref[...] = nt(reads, entry_ref[...].astype(bf16))
    none = jnp.zeros((rows, 1), f32)

    def at(j, first=0):
        return pl.ds(pl.multiple_of(first + j * 512, 512), 512)

    weights.wait(0)
    blocks = sides(normed_ref, core, ys)

    def gates(j, square):
        cols = at(j)
        gate = through(blocks, weights.gate, j).astype(bf16).astype(f32)
        gi_ref[:, cols] = gate
        ycore = yl_ref[:, cols] + fade_ref[:, cols] * ent_ref[:, cols]
        ycore_ref[:, cols] = ycore
        ssd = ycore + skip_ref[:, cols] * x_ref[:, cols]
        gated = ssd * gate * sigmoid(gate)
        gd_ref[:, cols] = gated
        return square + jnp.sum(gated * gated, axis=1, keepdims=True)

    square = lax.fori_loop(0, DS // 512, gates, none, unroll=True)
    rms_gate = lax.rsqrt(square / DS + EPS)
    mixed_ref[...] = (gd_ref[...] * rms_gate * gssm_ref[...]).astype(bf16)
    weights.wait(1)
    att_blocks, mix_blocks = sides(att_ref, core, ys), sides(mixed_ref, core, ys)

    def branches(j, square):
        branch = through(att_blocks, weights.ao, j) + through(mix_blocks, weights.so, j)
        middle = tok_ref[:, at(j)].astype(f32) + branch
        mid_ref[:, at(j)] = middle
        return square + jnp.sum(middle * middle, axis=1, keepdims=True)

    square = lax.fori_loop(0, width // 512, branches, none, unroll=True)
    rms = lax.rsqrt(square / width + EPS)
    n2_ref[...] = (mid_ref[...] * rms * gffn_ref[...]).astype(bf16)
    weights.wait(2)
    ups = sides(n2_ref, core, ys)

    def up(j, unused):
        gu_ref[:, at(j)] = through(ups, weights.gu, j)
        return unused

    lax.fori_loop(0, 2 * ff // 512, up, 0)

    def hide(j, unused):
        gate = gu_ref[:, at(j)]
        hid_ref[:, at(j)] = (gate * sigmoid(gate) * gu_ref[:, at(j, ff)]).astype(bf16)
        return unused

    lax.fori_loop(0, ff // 512, hide, 0)
    weights.wait(3)
    hids = sides(hid_ref, core, ys)

    def finals(j, unused):
        out_ref[:, at(j)] = (mid_ref[:, at(j)] + through(hids, weights.down, j)).astype(bf16)
        return unused

    lax.fori_loop(0, width // 512, finals, 0, unroll=True)
    cot = cot_ref[...]
    back_through(dh_ref, cot, weights.down, 2)

    def unhide(j, unused):
        gate, lift, dhid = gu_ref[:, at(j)], gu_ref[:, at(j, ff)], dh_ref[:, at(j)]
        sg = sigmoid(gate)
        dgate = dhid * lift * (sg * (1.0 + gate * (1.0 - sg)))
        send_ref[:, at(j)] = dgate.astype(bf16)
        send_ref[:, at(j, ff)] = (dhid * gate * sg).astype(bf16)
        return unused

    lax.fori_loop(0, ff // 512, unhide, 0)
    send_ref[:, cot_at:dbr_at] = cot
    wide = width // ys // 2

    def down(j, totals):
        grad = send_ref[:, pl.ds(pl.multiple_of(j * 512, 512), 512)]
        return [t + nt(grad, weights.gu(i, y, j)) for t, (i, y) in zip(totals, pairs)]

    zero = [jnp.zeros((rows, wide), f32)] * len(pairs)
    totals = lax.fori_loop(0, 2 * ff // 512, down, zero)
    for y in range(ys):
        put(dn_ref, y, totals[2 * y], totals[2 * y + 1], core)
    unit = mid_ref[...] * rms
    dn = dn_ref[...]
    dn = dn * gffn_ref[...]
    dmid = cot.astype(f32) + rms * (dn - unit * jnp.mean(dn * unit, axis=1, keepdims=True))
    dmid_ref[...] = dmid
    dbr = dmid.astype(bf16)
    send_ref[:, dbr_at:dgate_at] = dbr
    back_through(datt_ref, dbr, weights.ao, 2)
    back_through(dmx_ref, dbr, weights.so, 2)

    def means(j, mean):
        unit = gd_ref[:, at(j)] * rms_gate
        return mean + jnp.sum(dmx_ref[:, at(j)] * gssm_ref[:, at(j)] * unit, axis=1, keepdims=True)

    mean = lax.fori_loop(0, DS // 512, means, none) / DS

    def ungate(j, unused):
        cols = at(j)
        unit = gd_ref[:, cols] * rms_gate
        dgated = rms_gate * (dmx_ref[:, cols] * gssm_ref[:, cols] - unit * mean)
        gate = gi_ref[:, cols]
        sg = sigmoid(gate)
        ssd = ycore_ref[:, cols] + skip_ref[:, cols] * x_ref[:, cols]
        dssd = dgated * gate * sg
        dssd_ref[:, cols] = dssd
        dgate = (dgated * ssd * (sg * (1.0 + gate * (1.0 - sg)))).astype(bf16)
        send_ref[:, at(j, dgate_at)] = dgate
        fd_ref[:, cols] = (dssd * fade_ref[:, cols]).astype(bf16)
        return unused

    lax.fori_loop(0, DS // 512, ungate, 0)
    back_through(dng_ref, send_ref[:, dgate_at:sel_at], weights.gate, 3)
    dentry_ref[...] = tn(fd_ref[...], reads)
    to = 0
    for ref in (n2_ref, hid_ref, att_ref, mixed_ref, normed_ref):
        count = ys
        wide = ref.shape[1] // count
        for y in range(count):
            own, oth = halves(ref[:, y * wide : (y + 1) * wide], core)
            keep_ref[:, to : to + wide // 2] = own
            send_ref[:, sel_at + to : sel_at + to + wide // 2] = oth
            to += wide // 2


def products_kernel(plan, extra, keep_ref, own_ref, act_ref, *refs):
    got_ref, outs = act_ref, refs
    if extra:
        (extra_ref, *outs) = refs
    for which, a_at, act_at, size, g_at in plan:
        out = outs[which]
        for y in range(out.shape[0]):
            left = keep_ref[:, a_at + y * size : a_at + (y + 1) * size]
            right = act_ref[: left.shape[0], act_at + y * size : act_at + (y + 1) * size]
            for j in range(0, out.shape[-1], 512):
                stop = min(j + 512, out.shape[-1])
                total = tn(left, own_ref[: left.shape[0], g_at + j : g_at + stop])
                total = total + tn(right, got_ref[: left.shape[0], g_at + j : g_at + stop])
                if extra and which == 0 and stop == out.shape[-1]:
                    total = total + extra_ref[y]
                out[y, :, j:stop] = total.astype(bf16)


def split_products_kernel(plan, extra, y_ref, x_ref, keep_ref, own_ref, act_ref, *refs):
    got_ref, outs = act_ref, refs
    if extra:
        (extra_ref, *outs) = refs
    xkeep_ref, xsend_ref, ykeep_ref, ysend_ref = outs
    rows = keep_ref.shape[0]
    my_y, my_x = y_ref[0], x_ref[0]
    for kind, place, a_at, act_at, size, g_at, wide in plan:
        for k in range(2):
            y = k if kind == "x" else lax.rem(my_y + k, 2)
            left = keep_ref[:, pl.ds(pl.multiple_of(a_at + y * size, LANES), size)]
            right = act_ref[:rows, pl.ds(pl.multiple_of(act_at + y * size, LANES), size)]
            keep, send = (xkeep_ref, xsend_ref) if kind == "x" else (ykeep_ref, ysend_ref)
            block = 512 if wide % 512 == 0 else 384

            def columns(j, unused):
                at = pl.ds(pl.multiple_of(g_at + j * block, LANES), block)
                total = tn(left, own_ref[:rows, at]) + tn(right, got_ref[:rows, at])
                if kind == "x":
                    zs, each = keep.shape[1], keep.shape[2]
                    if extra:
                        total = total + extra_ref[k] * (j == wide // block - 1).astype(f32)
                    cols = pl.ds(pl.multiple_of(place + j * block, LANES), block)
                    total = total.reshape(zs, 2, each, block)
                    low, high = total[:, 0], total[:, 1]
                    keep[k, :, :, cols] = jnp.where(my_x == 0, low, high).astype(bf16)
                    send[k, :, :, cols] = jnp.where(my_x == 0, high, low).astype(bf16)
                else:
                    count = keep.shape[0]
                    each = size // count
                    cols = pl.ds(pl.multiple_of(j * block, LANES), block)
                    total = total.reshape(count, each, block).astype(bf16)
                    (send if k else keep)[:, place : place + each, cols] = total
                return unused

            lax.fori_loop(0, wide // block, columns, 0, unroll=True)


def fold_one_kernel(
    y_ref, x_ref, xkeep_ref, xgot_ref, ykeep_ref, ygot_ref,
    xkeep_out, xsend_out, ykeep_out, ysend_out,
):
    my_y, my_x = y_ref[0], x_ref[0]
    xkeep_out[...] = xkeep_ref[my_y].astype(f32) + xgot_ref[my_y].astype(f32)
    other = 1 - my_y
    xsend_out[...] = (xkeep_ref[other].astype(f32) + xgot_ref[other].astype(f32)).astype(bf16)
    for z in range(ykeep_out.shape[0]):
        at = 2 * z + my_x
        ykeep_out[z] = ykeep_ref[at].astype(f32) + ygot_ref[at].astype(f32)
        at = 2 * z + 1 - my_x
        ysend_out[z] = (ykeep_ref[at].astype(f32) + ygot_ref[at].astype(f32)).astype(bf16)


def laid(refs, width):
    at = 0
    for ref in refs:
        each = ref.shape[-2]
        for j in range(ref.shape[-1] // width):
            yield ref, at, j * width
            at += each


def fold_two_kernel(z_ref, xkeep_ref, xgot_ref, ykeep_ref, ygot_ref, keep_out, send_out):
    low = lax.rem(z_ref[0], 2)
    width = keep_out.shape[2]
    keeps = laid((xkeep_ref, ykeep_ref), width)
    gots = laid((xgot_ref, ygot_ref), width)
    for (keep, at, col), (got, *unused) in zip(keeps, gots):
        rows, cols = slice(at, at + keep.shape[-2]), slice(col, col + width)
        for high in range(keep_out.shape[0]):
            for out, z in ((keep_out, 2 * high + low), (send_out, 2 * high + 1 - low)):
                value = keep[z, :, cols] + got[z, :, cols].astype(f32)
                out[high, rows, :] = value.astype(out.dtype)


def fold_three_kernel(z_ref, keep_ref, got_ref, keep_out, send_out):
    high = lax.div(z_ref[0], 2)
    keep_out[...] = keep_ref[high] + got_ref[high].astype(f32)
    other = 1 - high
    send_out[...] = (keep_ref[other] + got_ref[other].astype(f32)).astype(bf16)


def summed(refs, rows):
    keep_ref, got_ref = refs
    return keep_ref[rows, :] + got_ref[rows, :].astype(f32)


def fold_four_kernel(keep_ref, got_ref, *outs):
    for out, at, col in laid(outs, keep_ref.shape[1]):
        rows = slice(at, at + out.shape[0])
        out[:, col : col + keep_ref.shape[1]] = summed((keep_ref, got_ref), rows)


def row_sums(value):
    ones = jnp.ones((8, value.shape[1]), bf16)
    return sum(nt(ones, part) for part in terms(value, 3))[:1]


def finish_post_kernel(
    keep_ref, sum_ref, one_ref, guw_ref, sow_ref, gffn_ref, gssm_ref,
    gu_ref, gate_ref, ao_ref, so_ref, dffn_ref, dssm_ref,
):
    both = (keep_ref, sum_ref)
    part, ups = one_ref.shape
    wide = keep_ref.shape[1]
    gu_ref[:, :ups] = one_ref[...]
    at = 0
    for out, start in ((gu_ref, ups), (gate_ref, 0)):
        for col in range(start, out.shape[1], wide):
            out[:, col : col + wide] = summed(both, slice(at, at + part))
            at += part
    for col in range(0, ao_ref.shape[1], wide):
        for out in (ao_ref, so_ref):
            out[:, col : col + wide] = summed(both, slice(at, at + out.shape[0]))
            at += out.shape[0]
    dffn_ref[...] = row_sums(guw_ref[...].astype(f32) * gu_ref[...]) / gffn_ref[...]
    dssm_ref[...] = row_sums(sow_ref[...].astype(f32) * so_ref[...]) / gssm_ref[...]


def finish_front_kernel(
    keep_ref, sum_ref, gate_ref, kvw_ref, qw_ref, iw_ref, gain_ref,
    kv_ref, q_ref, inner_ref, conv_ref, bias_ref, log_ref, step_ref, skip_ref, dgain_ref,
):
    both = (keep_ref, sum_ref)
    part, wide = kv_ref.shape[0], keep_ref.shape[1]
    count = A_COLS // wide
    blocks = [summed(both, slice(k * part, (k + 1) * part)) for k in range(count)]
    first = jnp.concatenate(blocks, axis=1)
    kv_ref[...] = first[:, :256]
    q_ref[...] = first[:, 256:768]
    inner_ref[:, :DS] = gate_ref[...]
    for k in range(DS // wide):
        rows = slice((count + k) * part, (count + k + 1) * part)
        inner_ref[:, DS + k * wide : DS + (k + 1) * wide] = summed(both, rows)
    last = first[:, 1024:]
    inner_ref[:, 2 * DS : 2 * DS + 2 * STATE] = first[:, 768:1024]
    inner_ref[:, DS + CONV_CH :] = last[:, :SSM_HEADS]
    turned_last = last.T
    own = bias_ref.shape[1]
    conv_ref[...] = turned_last[SSM_HEADS : SSM_HEADS + own, :CONV]
    bias_ref[...] = last[CONV : CONV + 1, SSM_HEADS : SSM_HEADS + own]
    for k, out in enumerate((log_ref, step_ref, skip_ref)):
        out[...] = last[CONV + 1 + k : CONV + 2 + k, SSM_HEADS : 2 * SSM_HEADS]
    total = row_sums(kvw_ref[...].astype(f32) * kv_ref[...])
    total = total + row_sums(qw_ref[...].astype(f32) * q_ref[...])
    total = total + row_sums(iw_ref[...].astype(f32) * inner_ref[...])
    dgain_ref[...] = total / gain_ref[...]


class PairReduction:
    def __init__(self, pieces, width):
        self.places = tuple(place_on(g).reshape(1).astype(jnp.int32) for g in ("y", "x", "z"))
        self.xkeep, xsend, self.ykeep, ysend = pieces
        self.width = width
        self.send(xsend, ysend, "x", "y")

    def send(self, xsend, ysend, first, second):
        self.sent = (xsend, ysend)
        self.gots = (
            swap(xsend, extents()[first][0]), swap(ysend, extents()[second][0])
        )

    def fold_one(self, *others):
        gots = after(self.gots, *others)
        x, y = self.xkeep.shape, self.ykeep.shape
        x, y = x[1:], (y[0] // 2, *y[1:])
        self.xkeep, xsend, self.ykeep, ysend = run(
            fold_one_kernel, "fold_one", [(x, f32), (x, bf16), (y, f32), (y, bf16)],
            (*self.places[:2], self.xkeep, gots[0], self.ykeep, gots[1]),
            scalars=2,
        )
        self.send(xsend, ysend, "y", "x")

    def fold_two(self, *others):
        gots = after(self.gots, *others)
        self.shapes = [self.xkeep.shape[1:], self.ykeep.shape[1:]]
        rows = sum(r * c // self.width for r, c in self.shapes)
        half = (self.xkeep.shape[0] // 2, rows, self.width)
        self.keep, self.sent = run(
            fold_two_kernel, "fold_two", [(half, f32), (half, bf16)],
            (self.places[2], self.xkeep, gots[0], self.ykeep, gots[1]),
            scalars=1,
        )
        self.gots = swap(self.sent, extents()["z"][0])

    def fold_three(self, *others):
        whole = self.keep.shape[1:]
        self.keep, self.sent = run(
            fold_three_kernel, "fold_three", [(whole, f32), (whole, bf16)],
            (self.places[2], self.keep, after(self.gots, *others)),
            scalars=1,
        )
        self.gots = swap(self.sent, 2 * extents()["z"][0])

    def fold_four(self, *others):
        return run(
            fold_four_kernel, "fold_four", [(shape, f32) for shape in self.shapes],
            (self.keep, after(self.gots, *others)),
        )


class PlainReduction:
    def __init__(self, pieces, rows):
        self.parts = [Reduction(pieces[0], rows[0], "x"), Reduction(pieces[1], rows[1], "y")]
        self.sent = [part.send() for part in self.parts]

    def fold_one(self, *others):
        for part in self.parts:
            part.receive(*others)
        self.sent = [part.send() for part in self.parts]

    fold_two = fold_one

    def fold_three(self, *others):
        pass

    def fold_four(self, *others):
        return [part.receive(*others) for part in self.parts]


def scan_back_kernel(
    dy_ref, x_ref, bc_ref, step_ref, cum_ref, cumt_ref, off_ref, dxw_ref, ds_ref,
    xw_ref, ce_ref, dyb_ref, dg_ref,
):
    rows = x_ref.shape[0]
    spread = head_spread()
    xw_ref[...] = (x_ref[...] * nn_left(step_ref[...], spread, 2)).astype(bf16)
    dyb_ref[...] = dy_ref[...].astype(bf16)
    ce_ref[...] = nn_left(cum_ref[...], spread, 3)
    keys, reads = bc_ref[:, :STATE].astype(bf16), bc_ref[:, STATE:].astype(bf16)
    early, late = iota((rows, rows), 0), iota((rows, rows), 1)
    keep = (early <= late) & (early >= late - off_ref[...])
    scores = jnp.where(keep, nt(keys, reads), 0.0)
    lane = iota((rows, LANES), 1)
    dg_ref[...] = jnp.zeros((rows, rows), f32)

    def pair(j, unused):
        cols = pl.ds(pl.multiple_of(j * LANES, LANES), LANES)
        wide = ce_ref[:, cols]
        xw, dy = xw_ref[:, cols], dyb_ref[:, cols]
        outs = []
        change = 0.0
        for k in range(2):
            first = wide[:, k * SSM_DIM : k * SSM_DIM + 1]
            second = cumt_ref[pl.ds(2 * j + k, 1), :]
            decay = jnp.exp(jnp.minimum(second - first, 0.0))
            outs.append(nn((decay * scores).astype(bf16), dy))
            mine = (lane < SSM_DIM) if k == 0 else (lane >= SSM_DIM)
            change = change + nt(xw * mine.astype(bf16), dy) * decay
        dg_ref[...] += change
        dxw_ref[:, cols] = jnp.where(lane < SSM_DIM, outs[0], outs[1])
        return unused

    lax.fori_loop(0, SSM_HEADS // 2, pair, 0)
    ds_ref[...] = jnp.where(keep, dg_ref[...], 0.0).astype(bf16)


def mixer_back_kernel(
    dy_ref, ycore_ref, x_ref, bc_ref, step_ref, cum_ref, z_ref, off_ref, entry_ref,
    down_ref, skip_ref, dec_ref, chan_ref, cw_ref, cb_ref, dxwl_ref, ds_ref,
    dext_ref, dz_ref, small_ref,
    dact_ref,
):
    rows = x_ref.shape[0]
    spread, gather = head_spread(), head_sum_matrix()
    off, cum = off_ref[...], cum_ref[...]
    step_wide = nn_left(step_ref[...], spread, 2)
    keys, reads = bc_ref[:, :STATE].astype(bf16), bc_ref[:, STATE:].astype(bf16)
    dscores = ds_ref[...]
    down = down_ref[...].astype(bf16)
    tail = nn_left(tail_of(cum, off), spread, 2)
    fade = nn_left(fade_of(cum, off), spread, 2)
    bd = nt(keys, down) * tail
    xw = (x_ref[...] * step_wide).astype(bf16).astype(f32)
    dxw = dxwl_ref[...] + bd
    dact_ref[:, DS : DS + STATE] = nn(dscores, reads) + nn((tail * xw).astype(bf16), down)
    dact_ref[:, DS + STATE :] = tn(dscores, keys) + nn(
        (fade * dy_ref[...]).astype(bf16), entry_ref[...].astype(bf16)
    )
    ones = jnp.ones((8, STATE), bf16)
    product = sum(nt(ones, part) for part in terms(down_ref[...] * entry_ref[...], 3))
    through = jnp.sum(xw * bd, axis=0, keepdims=True)
    direct = jnp.sum(dy_ref[...] * x_ref[...], axis=0, keepdims=True)
    row = iota((8, DS), 0)
    sums = jnp.where(row == 0, product, jnp.where(row == 1, through, direct))
    sums = nn_left(sums, gather, 3)
    through, kept = sums[1:2], sums[0:1] * carry_of(cum, off)
    last = (iota((rows, 1), 0) == rows - 1).astype(f32)
    dyb = dy_ref[...].astype(bf16).astype(f32)
    dcum = nn_left(dyb * ycore_ref[...] - xw * dxw, gather, 2) + last * (through + kept)
    tri = (iota((rows, rows), 0) <= iota((rows, rows), 1)).astype(f32).astype(bf16)
    dlog = nn_right(tri, dcum, 3)
    x = x_ref[...]
    step, dec = step_ref[...], dec_ref[...]
    dstep = nn_left(dxw * x, gather, 2) - dlog * dec
    dz = dstep * sigmoid(z_ref[...])
    dz_ref[...] = dz
    small_ref[...] = jnp.zeros(small_ref.shape, f32)
    small_ref[CONV + 1 : CONV + 2, :LANES] = jnp.sum(dlog * (-step * dec), axis=0, keepdims=True)
    small_ref[CONV + 1 : CONV + 2, LANES : 2 * LANES] = jnp.sum(dz, axis=0, keepdims=True)
    small_ref[CONV + 1 : CONV + 2, 2 * LANES : 3 * LANES] = sums[2:3]
    dact_ref[:, :DS] = dxw * step_wide + skip_ref[...] * dy_ref[...]
    for j in range(CONV_CH // 256):
        cols = slice(j * 256, (j + 1) * 256)
        taps = conv_taps(chan_ref, cols, off)
        mixed = cb_ref[:, cols]
        for i, tap in enumerate(taps):
            mixed = mixed + tap * cw_ref[i : i + 1, cols]
        sg = sigmoid(mixed)
        dmix = dact_ref[:, cols] * (sg * (1.0 + mixed * (1.0 - sg)))
        small_ref[CONV : CONV + 1, cols] = jnp.sum(dmix, axis=0, keepdims=True)
        total = 0.0
        for i, tap in enumerate(taps):
            back = CONV - 1 - i
            small_ref[i : i + 1, cols] = jnp.sum(dmix * tap, axis=0, keepdims=True)
            part = dmix * ((off >= back).astype(f32) * cw_ref[i : i + 1, cols])
            part = jnp.concatenate([jnp.zeros((RIM, 256), f32), part], axis=0)
            total = total + (pltpu.roll(part, rows + RIM - back, 0) if back else part)
        dext_ref[:, cols] = total


def back_grads_kernel(
    ys, core_ref, dq_ref, dkv_ref, dext_ref, dz_ref, cos_ref, sin_ref, normed_ref, nrim_ref,
    small_ref, ga_ref, keep_ref,
):
    core = core_ref[0]
    count, last = small_ref.shape[0], keep_ref.shape[0]
    ga_ref[last:, :] = jnp.zeros((ga_ref.shape[0] - last, ga_ref.shape[1]), bf16)
    ga_ref[last : last + count, :CONV_CH] = small_ref[...].astype(bf16)
    dkv = dkv_ref[0].astype(f32)
    for i in range(1, dkv_ref.shape[0]):
        dkv = dkv + dkv_ref[i].astype(f32)
    ga_ref[:RIM, :768] = jnp.zeros((RIM, 768), bf16)
    ga_ref[:RIM, 1024:A_COLS] = jnp.zeros((RIM, LANES), bf16)
    ga_ref[RIM:last, :LANES] = turned_back(dkv[:, :LANES], cos_ref[...], sin_ref[...]).astype(bf16)
    ga_ref[RIM:last, LANES:256] = dkv[:, LANES:].astype(bf16)
    ga_ref[RIM:last, 256:768] = dq_ref[...]
    ga_ref[:last, 768:1024] = dext_ref[:, DS:].astype(bf16)
    ga_ref[RIM:last, 1024:A_COLS] = dz_ref[...].astype(bf16)
    ga_ref[:last, A_COLS : A_COLS + DS] = dext_ref[:, :DS].astype(bf16)
    wide = normed_ref.shape[1] // ys
    at, to = 0, A_COLS + DS
    for y in range(ys):
        cols = slice(y * wide, (y + 1) * wide)
        for ref, rows in ((nrim_ref, slice(0, RIM)), (normed_ref, slice(RIM, last))):
            own, oth = halves(ref[:, cols], core)
            keep_ref[rows, at : at + wide // 2] = own
            ga_ref[rows, to + at : to + at + wide // 2] = oth
        at += wide // 2


def back_kernel(
    core_ref, gab_ref, wa_own, wa_oth, wb_own, wb_oth, tok_ref, dmid_ref, dng_ref, gain_ref,
    dtok_ref, drim_ref, dn_ref,
):
    core = core_ref[0]
    for y in range(wa_own.shape[0]):
        last = tok_ref.shape[0]
        ga, gb = gab_ref[:last, :A_COLS], gab_ref[:last, A_COLS : A_COLS + DS]
        own = nt(ga, wa_own[y]) + nt(gb, wb_own[y])
        oth = nt(ga, wa_oth[y]) + nt(gb, wb_oth[y])
        put(dn_ref, y, own, oth, core)

    def through_norm(dn, tok):
        tok = tok.astype(f32)
        rms = lax.rsqrt(jnp.mean(tok * tok, axis=1, keepdims=True) + EPS)
        unit = tok * rms
        dn = dn * gain_ref[...]
        return rms * (dn - unit * jnp.mean(dn * unit, axis=1, keepdims=True))

    drim_ref[...] = through_norm(dn_ref[:RIM, :], tok_ref[:RIM, :])
    dtok_ref[...] = dmid_ref[...] + through_norm(dn_ref[RIM:, :] + dng_ref[...], tok_ref[RIM:, :])


def gain_kernel(pairs, count, *refs):
    gains, refs = refs[:count], refs[count:]
    outs = refs[-count:]
    for k, out in enumerate(outs):
        total = 0.0
        for group, w, g in pairs:
            if group == k:
                total = total + jnp.sum(
                    refs[w][...].astype(f32) * refs[g][...], axis=1, keepdims=True
                )
        out[...] = total / gains[k][...].astype(f32)


def run(kernel, name, outs, args, scalars=0, scratch=(), us=3, left=0, sems=()):
    moved = sum(a.size * a.dtype.itemsize for a in args)
    shapes = [jax.ShapeDtypeStruct(shape, kind) for shape, kind in outs]
    moved += sum(s.size * s.dtype.itemsize for s in shapes)
    specs = [pl.BlockSpec(memory_space=pltpu.SMEM)] * scalars
    specs += [pl.BlockSpec(memory_space=pltpu.VMEM)] * (len(args) - scalars - left)
    specs += [pl.BlockSpec(memory_space=pl.ANY)] * left
    return pl.pallas_call(
        kernel,
        name=name,
        out_shape=shapes,
        in_specs=specs,
        out_specs=[pl.BlockSpec(memory_space=pltpu.VMEM)] * len(shapes),
        scratch_shapes=[pltpu.VMEM(shape, kind) for shape, kind in scratch]
        + [pltpu.SemaphoreType.DMA(shape) for shape in sems],
        compiler_params=pltpu.CompilerParams(vmem_limit_bytes=62 * 2**20),
        cost_estimate=pl.CostEstimate(
            flops=us * SCALE, bytes_accessed=moved, transcendentals=0
        ),
    )(*args)


def padded(vector, width):
    return jnp.pad(vector.astype(f32), (0, width - vector.shape[0]))[None, :]


def local(
    tokens, lengths, cotangent, mixer_gain, query_weight, keyval_weight, inner_weight, conv_weight,
    conv_bias, ssm_gain, attn_out_weight, ssm_out_weight, ffn_gain, gate_up_weight, down_weight,
    decay_log, step_bias, skip_gain,
):
    rows, width = tokens.shape
    seq_count, seq_rank = lax.axis_size(SEQ), lax.axis_index(SEQ)
    side = place_on("core").reshape(1)
    back = (rows * seq_count // 2) // rows
    part = query_weight.shape[0]
    heads_width, ff = HEADS * HEAD_DIM, gate_up_weight.shape[1] // 2
    a_rows, s_rows, f_rows = attn_out_weight.shape[0], ssm_out_weight.shape[0], down_weight.shape[0]
    ys = lax.axis_size("y")

    rim = shifted(tokens[rows - RIM :], 1)
    small = jnp.concatenate(
        [mixer_gain, conv_weight.reshape(-1), conv_bias, ssm_gain, ffn_gain]
    ).astype(f32)
    counts = [mixer_gain.size, conv_weight.size, conv_bias.size, ssm_gain.size, ffn_gain.size]
    slots = -(-small.size // LANES) * LANES
    small = gather_small(jnp.pad(small, (0, slots - small.size)))
    others = lax.axis_size(SEQ)
    aligned = ys == 2 and others == 8 and all(r % 16 == 0 for r in (part, a_rows, s_rows, f_rows))
    core_unit = extents()["core"][0]
    if aligned:
        packed, front = run(
            pack_kernel,
            "pack",
            [((6 * part + s_rows, width), bf16), ((part, A_COLS + DS), bf16)],
            (
                gate_up_weight, inner_weight, attn_out_weight, ssm_out_weight, keyval_weight,
                query_weight,
            ),
        )
    else:
        tail = jnp.pad(inner_weight[:, DS + CONV_CH :], ((0, 0), (0, LANES - SSM_HEADS)))
        front = jnp.concatenate(
            [
                keyval_weight, query_weight, inner_weight[:, 2 * DS : DS + CONV_CH], tail,
                inner_weight[:, DS : 2 * DS],
            ],
            1,
        )
        ao = jnp.concatenate([attn_out_weight[:, :512], attn_out_weight[:, 512:]], 0)
        packed = jnp.concatenate(
            [
                inner_weight[:, :width],
                jnp.concatenate([inner_weight[:, width:DS], ao], 1),
                ssm_out_weight,
            ]
            + [gate_up_weight[:, k * width : (k + 1) * width] for k in range(2 * ff // width)],
            0,
        )
    packed = lax.all_gather(packed, AXES, axis=0)
    packed = packed.reshape(ys, 2, others, *packed.shape[1:])
    front = shared(front, "z")
    front_one = Gathering(front[:, :, :A_COLS], "y")
    front_two = Gathering(front[:, :, A_COLS:], "x")
    down_slots = after(down_weight, front_one.full, front_two.full)[None]
    down_slots = jnp.broadcast_to(down_slots, (lax.axis_size("z"), *down_weight.shape))
    down_all = dealt(down_slots, "z")
    front_one.finish(down_slots)
    front_two.finish(down_slots)
    down_got = Gathering(after(down_all, front_one.full, front_two.full), "x")
    front_one.finish(down_got.full)
    front_two.finish(down_got.full)
    wa_own, wa_oth = front_one.sides(1)
    wb_own, wb_oth = front_two.sides(1)

    starts = [sum(counts[:i]) for i in range(len(counts))]
    gain_one, w_conv, b_conv, gain_ssm, gain_two = (
        small[:, s : s + c].reshape(-1) for s, c in zip(starts, counts)
    )
    w_conv = jnp.pad(w_conv.reshape(CONV_CH, CONV).T, ((0, 8 - CONV), (0, 0)))
    gain_one, b_conv, gain_ssm, gain_two = (
        v[None, :] for v in (gain_one, b_conv, gain_ssm, gain_two)
    )
    tokens_rim = jnp.concatenate([rim, tokens], 0)
    places = seq_rank * rows + jnp.arange(rows)
    begin = jnp.zeros_like(places)
    end = jnp.int32(0)
    for i in range(lengths.shape[1]):
        end = end + lengths[0, i]
        begin = jnp.where(end <= places, end, begin)
    offset = (places - begin).astype(jnp.int32)
    half = HEAD_DIM // 2
    freq = BASE ** (-jnp.arange(half).astype(f32) / half)
    angle = offset.astype(f32)[:, None] * freq[None, :]
    cos = jnp.tile(jnp.cos(angle), (1, 4))
    sin = jnp.sin(angle)
    sin = jnp.tile(jnp.concatenate([-sin, sin], 1), (1, 2))
    off = offset[:, None]
    step_bias_row, decay_row = padded(step_bias, LANES), padded(jnp.exp(decay_log), LANES)
    skip = jnp.repeat(skip_gain, SSM_DIM)[None, :]

    (q8, kv, normed, nrim, chan, x, bc, step, cum, cumt, z, state, carry) = run(
        front_kernel,
        "front",
        [
            ((HEADS, rows, LANES), bf16),
            ((rows, 256), bf16),
            ((rows, width), bf16),
            ((RIM, width), bf16),
            ((rows + RIM, CONV_CH), bf16),
            ((rows, DS), f32),
            ((rows, 2 * STATE), f32),
            ((rows, LANES), f32),
            ((rows, LANES), f32),
            ((LANES, rows), f32),
            ((rows, LANES), f32),
            ((DS, STATE), f32),
            ((1, LANES), f32),
        ],
        (
            side, tokens_rim, gain_one, wa_own, wa_oth, wb_own, wb_oth,
            cos, sin, off, w_conv, b_conv, step_bias_row, decay_row,
        ),
        scalars=1,
        scratch=[((rows + RIM, width), bf16), ((rows, DS), bf16)],
        us=8,
    )
    carrying = Carrying(state, carry, back, 1)
    sent_state = carrying.send()
    rank = seq_rank.reshape(1).astype(jnp.int32)
    kv_slots = jnp.broadcast_to(kv[None], (seq_count, *kv.shape))
    down_got.finish(sent_state, kv_slots)
    kv_all = dealt(kv_slots, SEQ)
    window = (back + 1) * rows
    y_local = run(
        scan_kernel, "scan", [((rows, DS), f32)],
        after((x, bc, step, cum, cumt, off), sent_state, kv_slots, down_got.full),
        scratch=[((rows, DS), bf16), ((rows, DS), f32)], us=8,
    )[0]
    entry = carrying.receive(y_local)
    if entry is None:
        sent_state = carrying.send()
    down_got.finish(y_local, sent_state)
    attended, lse = run(
        functools.partial(attend_kernel, back + 1),
        "attend",
        [((rows, heads_width), bf16), ((LANES, rows), f32)],
        after((rank, q8, kv_all, off), down_got.full),
        scalars=1,
        scratch=[
            ((window, LANES), bf16),
            ((window, LANES), bf16),
            ((rows, window), f32),
            ((HEADS, rows, LANES), f32),
        ],
        us=10,
    )
    while entry is None:
        entry = carrying.receive(attended)
        if entry is None:
            carrying.send()
    packed = after(packed, entry)
    down_sides = [
        f.reshape(ys, others, *f.shape[3:]) for f in (down_got.full, down_got.other)
    ]
    post_scratch, post_sems = [], []
    if aligned:
        parts, post_weights = (part, a_rows, s_rows, f_rows), (packed, *down_sides)
        rows_in_all = 6 * part + s_rows + f_rows
        post_scratch = [((2, ys, others, rows_in_all, width), bf16)]
        post_sems = [(4, 2)]
    else:
        parts = ()
        packed = [
            jnp.concatenate(
                [
                    lax.dynamic_index_in_dim(packed, place_on("core") ^ i, 1, False),
                    down_sides[i],
                ],
                2,
            )
            for i in range(2)
        ]
        gu_at = 2 * part + s_rows

        def taken(full, start, size, low, high):
            return full[:, :, start : start + size, low:high].reshape(ys, -1, high - low)

        def joined_columns(blocks):
            return [jnp.concatenate([taken(f, *block) for block in blocks], 2) for f in packed]

        post_weights = (
            *joined_columns([(0, part, 0, width), (part, part, 0, DS - width)]),
            *joined_columns([(part + k * a_rows, a_rows, 512, 1024) for k in range(2)]),
            *joined_columns([(2 * part, s_rows, 0, width)]),
            *joined_columns([(gu_at + 4 * part, f_rows, 0, width)]),
            *joined_columns([(gu_at + k * part, part, 0, width) for k in range(2 * ff // width)]),
        )
    half = (2 * width + ff + heads_width + DS) // 2
    sent = 2 * ff + 2 * width + DS
    output, dmid, datt, dssd, ycore, dentry, send, keep, dng = run(
        functools.partial(post_kernel, parts, ys),
        "post",
        [
            ((rows, width), bf16),
            ((rows, width), f32),
            ((rows, heads_width), bf16),
            ((rows, DS), f32),
            ((rows, DS), f32),
            ((DS, STATE), f32),
            ((rows, sent + half), bf16),
            ((rows, half), bf16),
            ((rows, width), f32),
        ],
        (
            side, tokens, cotangent, attended, y_local, x, bc, cum, off, entry, skip, normed,
            gain_ssm, gain_two, *post_weights,
        ),
        scalars=1,
        left=3 if aligned else 0,
        sems=post_sems,
        scratch=[
            ((rows, DS), f32),
            ((rows, DS), f32),
            ((rows, width), f32),
            ((rows, 2 * ff), f32),
            ((rows, width), f32),
            ((rows, DS), f32),
            ((rows, DS), bf16),
            ((rows, width), bf16),
            ((rows, ff), bf16),
            ((rows, DS), bf16),
            ((rows, ff), f32),
            ((rows, DS), f32),
            ((rows, DS), f32),
        ]
        + post_scratch,
        us=30,
    )
    got = swap(send, core_unit)
    carrying = Carrying(dentry, carry, back, -1)
    sent_state = carrying.send()
    off_row = offset[None, :]
    sizes = [width // 2, ff // 2, heads_width // 2, DS // 2, width // 2]
    ats = [sum(sizes[:i]) for i in range(5)]
    sizes = [size // ys for size in sizes]
    n2_at, hid_at, att_at, mix_at, norm_at = ats
    cot_at, dbr_at, dgate_at = 2 * ff, 2 * ff + width, 2 * ff + 2 * width
    places = tuple(place_on(g).reshape(1).astype(jnp.int32) for g in ("y", "x"))

    def weight_sums(name, x_parts, y_parts, keep, own, got, extra=()):
        plan, at, tall = [], 0, y_parts[0][4]
        for p in x_parts:
            plan.append(("x", at, *p))
            at += p[4]
        wide, at = at, 0
        for p in y_parts:
            plan.append(("y", at, *p))
            at += p[2] // others
        if aligned:
            xs = (ys, others // 2, x_parts[0][2] // others, wide)
            made = run(
                functools.partial(split_products_kernel, plan, len(extra)),
                name,
                [(xs, bf16), (xs, bf16), ((others, at, tall), bf16), ((others, at, tall), bf16)],
                (*places, keep, own, got, *extra),
                scalars=2,
                us=9,
            )
            return PairReduction(made, 512 if wide % 512 == 0 else 384)
        parts = x_parts + y_parts
        made = run(
            functools.partial(
                products_kernel, [(i, *p[:4]) for i, p in enumerate(parts)], len(extra)
            ),
            name,
            [((ys, p[2], p[4]), bf16) for p in parts],
            (keep, own, got, *extra),
            us=9,
        )
        heads = made[: len(x_parts)]
        tails = [m.reshape(ys, others, -1, tall) for m in made[len(x_parts) :]]
        rows_of = (x_parts[0][2] // others, at)
        return PlainReduction((jnp.concatenate(heads, 2), jnp.concatenate(tails, 2)), rows_of)

    dxw, dscores = run(
        scan_back_kernel,
        "scan_back",
        [((rows, DS), f32), ((rows, rows), bf16)],
        after((dssd, x, bc, step, cum, cumt, off_row), sent_state),
        scratch=[
            ((rows, DS), bf16),
            ((rows, DS), f32),
            ((rows, DS), bf16),
            ((rows, rows), f32),
        ],
        us=9,
    )

    downstream = carrying.receive(dxw)
    if downstream is None:
        sent_state = carrying.send()
    keep, send, got = after((keep, send, got), dxw, sent_state)
    red_one = weight_sums(
        "weights_one",
        [(n2_at, sent + n2_at, sizes[0], 0, ff)],
        [(hid_at, sent + hid_at, sizes[1], cot_at, width)],
        keep,
        send,
        got,
    )
    dq, dkv = run(
        functools.partial(attend_back_kernel, back + 1),
        "attend_back",
        [((rows, heads_width), bf16), ((seq_count, rows, 256), bf16)],
        after((rank, q8, kv_all, off_row, lse, datt, cos, sin), red_one.sent),
        scalars=1,
        scratch=[
            ((window, LANES), bf16),
            ((window, LANES), bf16),
            ((window, rows), f32),
            ((HEADS, rows, LANES), bf16),
            ((HEADS, rows, LANES), f32),
            ((window, 256), f32),
        ],
        us=14,
    )
    dkv_got = dealt(dkv, SEQ)
    keep, send, got = after((keep, send, got), red_one.sent, dq, dkv)
    red_two = weight_sums(
        "weights_two",
        [
            (n2_at, sent + n2_at, sizes[0], ff, ff),
            (norm_at, sent + norm_at, sizes[4], dgate_at, DS),
        ],
        [
            (att_at, sent + att_at, sizes[2], dbr_at, width),
            (mix_at, sent + mix_at, sizes[3], dbr_at, width),
        ],
        keep,
        send,
        got,
    )
    while downstream is None:
        downstream = carrying.receive(red_two.sent)
        if downstream is None:
            carrying.send()
    red_one.fold_one(red_two.sent, downstream)
    dext, dz, small = run(
        mixer_back_kernel,
        "mixer_back",
        [
            ((rows + RIM, CONV_CH), f32),
            ((rows, LANES), f32),
            ((8, CONV_CH), f32),
        ],
        after(
            (
                dssd, ycore, x, bc, step, cum, z, off, entry, downstream, skip, decay_row, chan,
                w_conv, b_conv, dxw, dscores,
            ),
            red_one.sent,
        ),
        scratch=[((rows, CONV_CH), f32)],
        us=13,
    )
    count = lax.axis_size(AXES)
    gab, norm_keep = run(
        functools.partial(back_grads_kernel, ys),
        "back_grads",
        [((rows + 2 * RIM, A_COLS + DS + width // 2), bf16), ((rows + RIM, width // 2), bf16)],
        (side, dq, dkv_got, dext, dz, cos, sin, normed, nrim, small),
        scalars=1,
    )
    gab_got = swap(gab, core_unit)
    small = small + gab_got[rows + RIM : rows + RIM + small.shape[0], :CONV_CH].astype(f32)
    free = LANES - SSM_HEADS
    convs = small[: CONV + 1].reshape(CONV + 1, count, -1).transpose(1, 0, 2)
    head_sums = small[CONV + 1, : 3 * LANES].reshape(3, LANES)[:, :SSM_HEADS]
    if aligned:
        head_sums = jnp.broadcast_to(head_sums[None], (count, 3, SSM_HEADS))
        per_device = jnp.concatenate(
            [
                jnp.pad(convs, ((0, 0), (0, 0), (0, free - convs.shape[2]))),
                jnp.pad(head_sums, ((0, 0), (0, 0), (0, free - SSM_HEADS))),
            ],
            1,
        )
        slots = CONV + 4
    else:
        head_sums = jnp.broadcast_to(head_sums.reshape(1, -1), (count, 3 * SSM_HEADS))
        per_device = jnp.concatenate([convs.reshape(count, -1), head_sums], 1)
        slots = per_device.shape[1]
        per_device = jnp.pad(per_device, ((0, 0), (0, part * free - slots)))
        per_device = per_device.reshape(count, part, free)
    per_device = lax.dynamic_index_in_dim(
        per_device.reshape(ys, 2, others, -1, free), place_on("core"), 1, False
    )
    aside = 384 if aligned else A_COLS % 512
    extra = jnp.pad(
        per_device, ((0, 0), (0, 0), (0, part - per_device.shape[2]), (aside - free, 0))
    ).reshape(ys, others * part, aside)
    grad_tokens, grad_rim = run(
        back_kernel,
        "back",
        [((rows, width), f32), ((RIM, width), f32)],
        (
            side, gab, wa_own, wa_oth, wb_own, wb_oth, tokens_rim, dmid, dng,
            gain_one,
        ),
        scalars=1,
        scratch=[((rows + RIM, width), f32)],
        us=7,
    )
    norm_keep, gab, gab_got, extra = after((norm_keep, gab, gab_got, extra), grad_tokens)
    red_three = weight_sums(
        "front_weights",
        [(0, A_COLS + DS, sizes[4], 0, A_COLS)],
        [(0, A_COLS + DS, sizes[4], A_COLS, DS)],
        norm_keep,
        gab,
        gab_got,
        (extra,),
    )
    red_two.fold_one(red_three.sent)
    red_one.fold_two(red_two.sent)
    red_three.fold_one(red_one.sent)
    red_one.fold_three(red_three.sent)
    red_two.fold_two(red_one.sent)
    red_three.fold_two(red_two.sent)
    red_two.fold_three(red_three.sent)
    rim_got = shifted(after(grad_rim, red_two.sent), -1)
    r_one, r_down = red_one.fold_four(red_two.sent)
    red_three.fold_three(r_one)
    if aligned:
        r_gu, r_gate, r_ao, r_so, g_ffn, g_ssm = run(
            finish_post_kernel,
            "finish_post",
            [
                ((part, 2 * ff), f32),
                ((part, DS), f32),
                ((a_rows, width), f32),
                ((s_rows, width), f32),
                ((1, part), f32),
                ((1, s_rows), f32),
            ],
            (
                red_two.keep, after(red_two.gots, red_three.sent), r_one, gate_up_weight, ssm_out_weight,
                ffn_gain.astype(f32)[None, :], ssm_gain.astype(f32)[None, :],
            ),
        )
        rim_got = after(rim_got, r_gu)
        grad_tokens = grad_tokens.at[rows - RIM :].add(rim_got)
        r_kv, r_q, g_inner, g_conv, g_bias, g_log, g_step, g_skip, g_mixer = run(
            finish_front_kernel,
            "finish_front",
            [
                ((part, 256), f32),
                ((part, heads_width), f32),
                ((part, inner_weight.shape[1]), f32),
                (conv_weight.shape, f32),
                ((1, conv_bias.size), f32),
                ((1, SSM_HEADS), f32),
                ((1, SSM_HEADS), f32),
                ((1, SSM_HEADS), f32),
                ((1, part), f32),
            ],
            (
                red_three.keep, after(red_three.gots, grad_tokens), r_gate, keyval_weight, query_weight,
                inner_weight, mixer_gain.astype(f32)[None, :],
            ),
        )
        g_bias, g_mixer, g_ssm, g_ffn = (v[0] for v in (g_bias, g_mixer, g_ssm, g_ffn))
        heads = [v[0] for v in (g_log, g_step, g_skip)]
    else:
        r_two, r_out = red_two.fold_four(red_three.sent)
        rim_got = after(rim_got, r_two)
        grad_tokens = grad_tokens.at[rows - RIM :].add(rim_got)
        r_e, r_f = red_three.fold_four(grad_tokens)
        r_gu = jnp.concatenate([r_one, r_two[:, :ff]], 1)
        small = r_e[:, A_COLS - free :].reshape(-1)[:slots]
        conv = small[: (CONV + 1) * conv_bias.size].reshape(CONV + 1, -1)
        g_conv, g_bias = conv[:CONV].T, conv[CONV]
        heads = small[(CONV + 1) * conv_bias.size :].reshape(3, SSM_HEADS)
        g_inner = jnp.concatenate([r_two[:, ff:], r_f, r_e[:, 768 : 1024 + SSM_HEADS]], 1)
        r_kv, r_q, r_ao, r_so = r_e[:, :256], r_e[:, 256:768], r_out[:a_rows], r_out[a_rows:]
        pairs = [(0, 0, 1), (0, 2, 3), (0, 4, 5), (1, 6, 7), (2, 8, 9)]
        gains = run(
            functools.partial(gain_kernel, pairs, 3),
            "gains",
            [((part, 1), f32), ((s_rows, 1), f32), ((part, 1), f32)],
            (
                mixer_gain[:, None], ssm_gain[:, None], ffn_gain[:, None],
                keyval_weight, r_kv, query_weight, r_q, inner_weight, g_inner,
                ssm_out_weight, r_so, gate_up_weight, r_gu,
            ),
        )
        g_mixer, g_ssm, g_ffn = (v[:, 0] for v in gains)
    return (
        output,
        grad_tokens,
        g_mixer,
        r_q,
        r_kv,
        g_inner,
        g_conv,
        g_bias,
        g_ssm,
        r_ao,
        r_so,
        g_ffn,
        r_gu,
        r_down,
        heads[0],
        heads[1],
        heads[2],
    )


def solution(mesh):
    across, along = mesh.shape["dp"], mesh.shape["seq"]
    mesh = jax.sharding.Mesh(mesh.devices.reshape(across // 2, 2, along // 2, 2), AXES)
    lead, flat, rep = P(AXES, None), P(AXES), P()
    return jax.shard_map(
        local,
        mesh=mesh,
        in_specs=(
            lead, P(AXES[:2], None), lead, flat, lead, lead, lead, lead, flat, flat, lead, lead, flat,
            lead, lead, rep, rep, rep,
        ),
        out_specs=(
            lead, lead, flat, lead, lead, lead, lead, flat, flat, lead, lead, flat, lead, lead,
            rep, rep, rep,
        ),
        check_vma=False,
    )
```

```python
import functools

import jax
import jax.numpy as jnp
from jax import lax
from jax.experimental import pallas as pl
from jax.experimental.pallas import tpu as pltpu
from jax.sharding import PartitionSpec as P

HEADS = 8
KV_HEADS = 2
HEAD_DIM = 64
SSM_HEADS = 24
SSM_DIM = 64
STATE = 128
CONV = 4
DS = 1536
CONV_CH = 1792
RIM = 16
LANES = 128
A_COLS = 2 * KV_HEADS * HEAD_DIM + HEADS * HEAD_DIM + 2 * STATE + LANES
EPS = 1e-6
BASE = 10000.0
NEG = -1e30
SCALE = 6_600_000_000
AXES = ("y", "core", "z", "x")
SEQ = AXES[2:]

f32 = jnp.float32
bf16 = jnp.bfloat16


def nn(a, b):
    return lax.dot_general(a, b, (((1,), (0,)), ((), ())), preferred_element_type=f32)


def tn(a, b):
    return lax.dot_general(a, b, (((0,), (0,)), ((), ())), preferred_element_type=f32)


def nt(a, b):
    return lax.dot_general(a, b, (((1,), (1,)), ((), ())), preferred_element_type=f32)


def terms(value, count):
    parts = []
    for unused in range(count):
        parts.append(value.astype(bf16))
        value = value - parts[-1].astype(f32)
    return parts


def nn_left(value, ones, count):
    return sum(nn(part, ones) for part in terms(value, count))


def nn_right(ones, value, count):
    return sum(nn(ones, part) for part in terms(value, count))


def iota(shape, dim):
    return lax.broadcasted_iota(jnp.int32, shape, dim)


def head_spread():
    row = iota((LANES, DS), 0)
    return (iota((LANES, DS), 1) // SSM_DIM == row).astype(f32).astype(bf16)


def head_sum_matrix():
    col = iota((DS, LANES), 1)
    return (iota((DS, LANES), 0) // SSM_DIM == col).astype(f32).astype(bf16)


def extents():
    along = lax.axis_size(SEQ)
    return {
        "x": (1, 2),
        "z": (2, along // 2),
        "core": (along, 2),
        "y": (2 * along, lax.axis_size("y")),
    }


def my_index():
    return lax.axis_index(AXES)


def place_on(group):
    unit, size = extents()[group]
    return (my_index() // unit) % size


def swap(array, mask):
    count = lax.axis_size(AXES)
    return lax.ppermute(array, AXES, [(i, i ^ mask) for i in range(count)])


def in_order(pieces, place):
    pieces = list(pieces)
    bit = 1
    while bit < len(pieces):
        flag = (place // bit) % 2 == 1
        pieces = [jnp.where(flag, pieces[j ^ bit], pieces[j]) for j in range(len(pieces))]
        bit *= 2
    return pieces


def collect(array, group, axis):
    unit, size = extents()[group]
    pieces = [array] + [swap(array, k * unit) for k in range(1, size)]
    return jnp.stack(in_order(pieces, place_on(group)), axis)


class Gathering:
    def __init__(self, full, first):
        self.full = full
        self.steps = [("y", 0), ("x", 2)] if first == "y" else [("x", 1), ("y", 0)]
        self.start()

    def start(self):
        unit, size = extents()[self.steps[0][0]]
        self.got = [swap(self.full, k * unit) for k in range(1, size)]

    def finish(self, *others):
        group, axis = self.steps.pop(0)
        pieces = [self.full] + list(after(self.got, *others))
        self.full = jnp.stack(in_order(pieces, place_on(group)), axis)
        if self.steps:
            self.start()
        else:
            self.other = swap(self.full, extents()["core"][0])

    def sides(self, kept):
        shape = (self.full.shape[0], -1, *self.full.shape[5 - kept :])
        return self.full.reshape(shape), self.other.reshape(shape)


def cut(total, group, axis):
    size = extents()[group][1]
    place = place_on(group)
    keep = lax.dynamic_index_in_dim(total, place, axis, False)
    parts = [lax.dynamic_index_in_dim(total, place ^ k, axis, False) for k in range(1, size)]
    return keep, [p.astype(bf16) for p in parts]


def crossed(parts, group):
    unit = extents()[group][0]
    return [swap(part, (k + 1) * unit) for k, part in enumerate(parts)]


def joined(keep, received):
    total = keep.astype(f32)
    for part in received:
        total = total + part.astype(f32)
    return total


class Reduction:
    def __init__(self, total, rows, first):
        table = extents()
        self.total = total.reshape(
            table["y"][1], table["z"][1], table["x"][1], rows, total.shape[-1]
        )
        order = [("x", 2), ("y", 0)] if first == "x" else [("y", 0), ("x", 1)]
        self.stages = order + [("z", 0)]

    def send(self):
        (group, axis), self.stages = self.stages[0], self.stages[1:]
        self.keep, self.parts = cut(self.total, group, axis)
        self.received = crossed(self.parts, group)
        return self.parts

    def receive(self, *others):
        self.received = after(self.received, *others)
        self.total = joined(self.keep, self.received)
        return self.total


def after(value, *others):
    return lax.optimization_barrier((value, others))[0]


def gather_small(vector):
    full = collect(collect(collect(vector, "z", 0), "x", 1), "core", 0)
    return collect(full, "y", 0).reshape(-1, vector.shape[-1])


def dealt(array, axes):
    return lax.all_to_all(array, axes, 0, 0, tiled=True)


def shared(array, axes):
    return dealt(jnp.broadcast_to(array[None], (lax.axis_size(axes), *array.shape)), axes)


def shifted(array, by):
    count = lax.axis_size(SEQ)
    pairs = [(i, i + by) for i in range(count) if 0 <= i + by < count]
    return lax.ppermute(array, SEQ, pairs)


def link(earlier, later):
    carry = later[1]
    wide = jnp.repeat(carry[0, :SSM_HEADS], SSM_DIM)[:, None]
    return (later[0] + wide * earlier[0], carry * earlier[1])


class Carrying:
    def __init__(self, state, carry, back, sign):
        self.pair, self.back, self.sign, self.by = (state, carry), back, sign, 0

    def send(self):
        packed = jnp.concatenate(
            [self.pair[0], jnp.pad(self.pair[1], ((0, RIM - 1), (0, 0)))], 0
        ).astype(bf16)
        steps = [self.by] if self.by else [1] + [2] * (self.back > 1)
        self.got = [shifted(packed, self.sign * by) for by in steps]
        return packed

    def receive(self, *others):
        pairs = []
        for got in after(self.got, *others):
            got = got.astype(f32)
            pairs.append((got[:DS], got[DS : DS + 1]))
        self.by = 2 * self.by if self.by else min(self.back, 2)
        if len(pairs) == 2:
            self.pair = link(pairs[1], pairs[0])
        else:
            self.pair = link(pairs[0], self.pair) if self.by > 2 else pairs[0]
        return self.pair[0] if self.by >= self.back else None


def halves(block, core):
    width = block.shape[1] // 2
    low, high = block[:, :width], block[:, width:]
    return jnp.where(core == 0, low, high), jnp.where(core == 0, high, low)


def put(ref, y, own, other, core):
    width = own.shape[1]
    base = y * 2 * width
    ref[:, base : base + width] = jnp.where(core == 0, own, other).astype(ref.dtype)
    ref[:, base + width : base + 2 * width] = jnp.where(core == 0, other, own).astype(ref.dtype)


def sides(ref, core, count):
    width = ref.shape[-1] // count
    return [halves(ref[:, y * width : (y + 1) * width], core) for y in range(count)]


def cross_half(value):
    lane = iota(value.shape, 1) % HEAD_DIM
    up = pltpu.roll(value, LANES - HEAD_DIM // 2, 1)
    down = pltpu.roll(value, HEAD_DIM // 2, 1)
    return jnp.where(lane < HEAD_DIM // 2, up, down)


def turned(value, cos, sin):
    return value * cos + cross_half(value) * sin


def turned_back(value, cos, sin):
    return value * cos - cross_half(value) * sin


def split_heads(pair, which, lane):
    flipped = pltpu.roll(pair, HEAD_DIM, 1)
    if which == 0:
        return jnp.where(lane < HEAD_DIM, pair, 0.0), jnp.where(lane < HEAD_DIM, flipped, 0.0)
    return jnp.where(lane >= HEAD_DIM, flipped, 0.0), jnp.where(lane >= HEAD_DIM, pair, 0.0)


def join_heads(even, odd, which, lane):
    if which == 0:
        return jnp.where(lane < HEAD_DIM, even, pltpu.roll(odd, HEAD_DIM, 1))
    return jnp.where(lane < HEAD_DIM, pltpu.roll(even, HEAD_DIM, 1), odd)


def conv_taps(chan_ref, cols, off):
    ext = chan_ref[:, cols].astype(f32)
    taps = []
    for i in range(CONV):
        back = CONV - 1 - i
        rows = pltpu.roll(ext, back, 0)[RIM:] if back else ext[RIM:]
        taps.append(rows * (off >= back).astype(f32))
    return taps


def sigmoid(v):
    return 1.0 / (1.0 + jnp.exp(-v))


def softplus(v):
    return jnp.maximum(v, 0.0) + jnp.log1p(jnp.exp(-jnp.abs(v)))


def tail_of(cum, off):
    rows = cum.shape[0]
    last_off = off[rows - 1 :, :]
    keep = iota((rows, 1), 0) >= rows - 1 - last_off
    return jnp.exp(cum[rows - 1 :, :] - cum) * keep.astype(f32)


def fade_of(cum, off):
    keep = off > iota((cum.shape[0], 1), 0)
    return jnp.exp(cum) * keep.astype(f32)


def carry_of(cum, off):
    rows = cum.shape[0]
    return jnp.exp(cum[rows - 1 :, :]) * (off[rows - 1 :, :] >= rows).astype(f32)


def pack_kernel(
    gu_ref, inner_ref, ao_ref, so_ref, kv_ref, q_ref, post_ref, front_ref
):
    part, width = gu_ref.shape[0], post_ref.shape[1]
    a_rows = ao_ref.shape[0]
    post_ref[:part, :] = inner_ref[:, :width]
    post_ref[part : 2 * part, : DS - width] = inner_ref[:, width:DS]
    for k in range(2):
        rows = slice(part + k * a_rows, part + (k + 1) * a_rows)
        post_ref[rows, DS - width :] = ao_ref[:, k * 512 : (k + 1) * 512]
    at = 2 * part
    post_ref[at : at + so_ref.shape[0], :] = so_ref[...]
    at += so_ref.shape[0]
    for k in range(gu_ref.shape[1] // width):
        post_ref[at : at + part, :] = gu_ref[:, k * width : (k + 1) * width]
        at += part
    front_ref[:, :256] = kv_ref[...]
    front_ref[:, 256:768] = q_ref[...]
    front_ref[:, 768:1024] = inner_ref[:, 2 * DS : DS + CONV_CH]
    front_ref[:, 1024:A_COLS] = jnp.zeros((part, LANES), bf16)
    front_ref[:, 1024 : 1024 + SSM_HEADS] = inner_ref[:, DS + CONV_CH :]
    front_ref[:, A_COLS:] = inner_ref[:, DS : 2 * DS]


def front_kernel(
    core_ref, tok_ref, gain_ref, wa_own, wa_oth, wb_own, wb_oth, cos_ref, sin_ref, off_ref,
    cw_ref, cb_ref, sb_ref, dec_ref,
    q8_ref, kv_ref, normed_ref, nrim_ref, chan_ref, x_ref, bc_ref, step_ref, cum_ref, cumt_ref, z_ref,
    state_ref, carry_ref,
    n_ref, xt_ref,
):
    core = core_ref[0]
    rows = cos_ref.shape[0]
    tok = tok_ref[...].astype(f32)
    rms = lax.rsqrt(jnp.mean(tok * tok, axis=1, keepdims=True) + EPS)
    n_ref[...] = (tok * rms * gain_ref[...]).astype(bf16)
    normed_ref[...] = n_ref[RIM:, :]
    nrim_ref[...] = n_ref[:RIM, :]
    count = wa_own.shape[0]
    blocks = sides(n_ref, core, count)

    def project(own_ref, oth_ref, cols):
        total = 0.0
        for y, (own, oth) in enumerate(blocks):
            total = total + nn(own, own_ref[y, :, cols]) + nn(oth, oth_ref[y, :, cols])
        return total

    lane = iota((rows, LANES), 1)
    cos, sin, off = cos_ref[...], sin_ref[...], off_ref[...]
    kv = project(wa_own, wa_oth, pl.ds(0, 256))[RIM:]
    kv_ref[:, :LANES] = turned(kv[:, :LANES], cos, sin).astype(bf16)
    kv_ref[:, LANES:] = kv[:, LANES:].astype(bf16)
    queries = project(wa_own, wa_oth, pl.ds(256, 512))[RIM:]
    for j in range(HEADS // 2):
        pair = turned(queries[:, j * LANES : (j + 1) * LANES], cos, sin)
        even, odd = split_heads(pair, j // 2, lane)
        q8_ref[2 * j] = even.astype(bf16)
        q8_ref[2 * j + 1] = odd.astype(bf16)
    rest = project(wa_own, wa_oth, pl.ds(768, 384))
    chan_ref[:, DS:] = rest[:, : 2 * STATE].astype(bf16)
    z = rest[RIM:, 2 * STATE :].astype(bf16).astype(f32) + sb_ref[...]
    for j in range(DS // 512):
        cols = slice(j * 512, (j + 1) * 512)
        chan_ref[:, cols] = project(wb_own, wb_oth, pl.ds(j * 512, 512)).astype(bf16)
    z_ref[...] = z
    step = softplus(z)
    step_ref[...] = step
    tri = (iota((rows, rows), 0) >= iota((rows, rows), 1)).astype(f32).astype(bf16)
    cum = nn_right(tri, -step * dec_ref[...], 3)
    cum_ref[...] = cum
    cumt_ref[...] = cum.T
    carry_ref[...] = carry_of(cum, off)
    weight = nn_left(step * tail_of(cum, off), head_spread(), 2)
    for j in range(CONV_CH // 256):
        cols = slice(j * 256, (j + 1) * 256)
        mixed = cb_ref[:, cols]
        for i, tap in enumerate(conv_taps(chan_ref, cols, off)):
            mixed = mixed + tap * cw_ref[i : i + 1, cols]
        active = mixed * sigmoid(mixed)
        if j < DS // 256:
            x_ref[:, cols] = active
            xt_ref[:, cols] = (active * weight[:, cols]).astype(bf16)
        else:
            bc_ref[...] = active
    state_ref[...] = tn(xt_ref[...], bc_ref[:, :STATE].astype(bf16))


def scan_masks(off, rows):
    t, s = iota((rows, rows), 0), iota((rows, rows), 1)
    return (s <= t) & (s >= t - off)


def scan_kernel(x_ref, bc_ref, step_ref, cum_ref, cumt_ref, off_ref, y_ref, xw_ref, ce_ref):
    rows = x_ref.shape[0]
    spread = head_spread()
    xw_ref[...] = (x_ref[...] * nn_left(step_ref[...], spread, 2)).astype(bf16)
    ce_ref[...] = nn_left(cum_ref[...], spread, 3)
    keys, reads = bc_ref[:, :STATE].astype(bf16), bc_ref[:, STATE:].astype(bf16)
    scores = jnp.where(scan_masks(off_ref[...], rows), nt(reads, keys), 0.0)
    lane = iota((rows, LANES), 1)

    def pair(j, unused):
        cols = pl.ds(pl.multiple_of(j * LANES, LANES), LANES)
        wide = ce_ref[:, cols]
        xw = xw_ref[:, cols]
        outs = []
        for k in range(2):
            late = wide[:, k * SSM_DIM : k * SSM_DIM + 1]
            early = cumt_ref[pl.ds(2 * j + k, 1), :]
            decay = jnp.exp(jnp.minimum(late - early, 0.0))
            outs.append(nn((decay * scores).astype(bf16), xw))
        y_ref[:, cols] = jnp.where(lane < SSM_DIM, outs[0], outs[1])
        return unused

    lax.fori_loop(0, SSM_HEADS // 2, pair, 0)


def attend_bias(off, rows, window):
    query = iota((rows, window), 0) + (window - rows)
    key = iota((rows, window), 1)
    return jnp.where((key <= query) & (key >= query - off), 0.0, NEG)


def window_of(count, rank, kv_ref, k_ref, v_ref):
    rows = kv_ref.shape[1]
    for i in range(count):
        piece = jnp.maximum(rank - (count - 1 - i), 0)
        k_ref[i * rows : (i + 1) * rows, :] = kv_ref[piece, :, :LANES]
        v_ref[i * rows : (i + 1) * rows, :] = kv_ref[piece, :, LANES:]


def attend_kernel(
    count, rank_ref, q8_ref, kv_ref, off_ref, att_ref, lse_ref, k_ref, v_ref, bias_ref, o_ref
):
    rows = off_ref.shape[0]
    window = count * rows
    window_of(count, rank_ref[0], kv_ref, k_ref, v_ref)
    bias_ref[...] = attend_bias(off_ref[...], rows, window)
    lane = iota((rows, LANES), 1)

    def head(h, lses):
        scores = nt(q8_ref[h], k_ref[...]) * HEAD_DIM**-0.5 + bias_ref[...]
        top = jnp.max(scores, axis=1, keepdims=True)
        probs = jnp.exp(scores - top)
        total = jnp.sum(probs, axis=1, keepdims=True)
        o_ref[h] = nn((probs * (1.0 / total)).astype(bf16), v_ref[...])
        return jnp.where(lane == h, top + jnp.log(total), lses)

    lse_ref[...] = lax.fori_loop(0, HEADS, head, jnp.zeros((rows, LANES), f32)).T
    for j in range(HEADS // 2):
        pair = join_heads(o_ref[2 * j], o_ref[2 * j + 1], j // 2, lane)
        att_ref[:, j * LANES : (j + 1) * LANES] = pair.astype(bf16)


def attend_back_kernel(
    count, rank_ref, q8_ref, kv_ref, off_ref, lse_ref, datt_ref, cos_ref, sin_ref,
    dq_ref, out_ref, k_ref, v_ref, bias_ref, do_ref, dq8_ref, dkv_ref,
):
    rows = off_ref.shape[1]
    window = count * rows
    rank = rank_ref[0]
    window_of(count, rank, kv_ref, k_ref, v_ref)
    query = iota((window, rows), 1) + (window - rows)
    key = iota((window, rows), 0)
    bias_ref[...] = jnp.where((key <= query) & (key >= query - off_ref[...]), 0.0, NEG)
    lane = iota((rows, LANES), 1)
    for j in range(HEADS // 2):
        pair = datt_ref[:, j * LANES : (j + 1) * LANES].astype(f32)
        even, odd = split_heads(pair, j // 2, lane)
        do_ref[2 * j] = even.astype(bf16)
        do_ref[2 * j + 1] = odd.astype(bf16)
    dkv_ref[...] = jnp.zeros(dkv_ref.shape, f32)

    def head(h, unused):
        query, grad = q8_ref[h], do_ref[h]
        scores = nt(k_ref[...], query) * HEAD_DIM**-0.5 + bias_ref[...]
        probs = jnp.exp(scores - lse_ref[pl.ds(h, 1), :])
        dprobs = nt(v_ref[...], grad)
        mean = jnp.sum(probs * dprobs, axis=0, keepdims=True)
        draw = (probs * (dprobs - mean) * HEAD_DIM**-0.5).astype(bf16)
        dkv_ref[:, :LANES] += nn(draw, query)
        dkv_ref[:, LANES:] += nn(probs.astype(bf16), grad)
        dq8_ref[h] = tn(draw, k_ref[...])
        return unused

    lax.fori_loop(0, HEADS, head, 0)
    out_ref[...] = jnp.zeros(out_ref.shape, bf16)
    for i in range(count):
        piece = rank - (count - 1 - i)

        @pl.when(piece >= 0)
        def unused():
            out_ref[piece] = dkv_ref[i * rows : (i + 1) * rows, :].astype(bf16)

    for j in range(HEADS // 2):
        pair = join_heads(dq8_ref[2 * j], dq8_ref[2 * j + 1], j // 2, lane)
        back = turned_back(pair, cos_ref[...], sin_ref[...])
        dq_ref[:, j * LANES : (j + 1) * LANES] = back.astype(bf16)


class PackedWeights:
    def __init__(self, most, downs, core, held, sems, parts):
        self.held = held
        part, a_part, s_part, f_part = self.parts = parts
        self.so_at = 2 * part
        self.gu_at = self.so_at + s_part
        self.down_at = self.gu_at + 4 * part
        places = [
            (0, self.so_at), (self.so_at, s_part), (self.gu_at, 4 * part), (self.down_at, f_part),
        ]
        self.copies = []
        for k, (at, size) in enumerate(places):
            pair = []
            for i in range(2):
                rows = pl.ds(at, size)
                source = most.at[:, lax.rem(core + i, 2), :, rows] if k < 3 else downs[i]
                target = held.at[i, :, :, rows]
                pair.append(pltpu.make_async_copy(source, target, sems.at[k, i]))
            self.copies.append(pair)
        for pair in self.copies:
            for copy in pair:
                copy.start()

    def wait(self, k):
        for copy in self.copies[k]:
            copy.wait()

    def block(self, i, y, start, size, col):
        rows, cols = pl.ds(pl.multiple_of(start, 16), size), pl.ds(pl.multiple_of(col, 512), 512)
        got = self.held[i, y, :, rows, cols]
        return got.reshape(got.shape[0] * size, 512)

    def gate(self, i, y, j):
        part = self.parts[0]
        return self.block(i, y, j // 2 * part, part, j % 2 * 512)

    def ao(self, i, y, j):
        part, a_part = self.parts[:2]
        return self.block(i, y, part + j * a_part, a_part, 512)

    def so(self, i, y, j):
        return self.block(i, y, self.so_at, self.parts[2], j * 512)

    def down(self, i, y, j):
        return self.block(i, y, self.down_at, self.parts[3], j * 512)

    def gu(self, i, y, j):
        part = self.parts[0]
        return self.block(i, y, self.gu_at + j // 2 * part, part, j % 2 * 512)


class PlainWeights:
    def __init__(self, refs):
        self.refs = refs

    def wait(self, k):
        pass

    def block(self, name, i, y, j):
        return self.refs[2 * name + i][y, :, pl.ds(pl.multiple_of(j * 512, 512), 512)]

    def gate(self, i, y, j):
        return self.block(0, i, y, j)

    def ao(self, i, y, j):
        return self.block(1, i, y, j)

    def so(self, i, y, j):
        return self.block(2, i, y, j)

    def down(self, i, y, j):
        return self.block(3, i, y, j)

    def gu(self, i, y, j):
        return self.refs[8 + i][y, :, pl.ds(pl.multiple_of(j * 512, 512), 512)]


def post_kernel(
    parts, ys, core_ref, tok_ref, cot_ref, att_ref, yl_ref, x_ref, bc_ref, cum_ref, off_ref,
    entry_ref, skip_ref, normed_ref, gssm_ref, gffn_ref, *refs,
):
    if parts:
        weights = PackedWeights(refs[0], refs[1:3], core_ref[0], refs[-2], refs[-1], parts)
        refs = refs[3:-2]
    else:
        weights, refs = PlainWeights(refs[:10]), refs[10:]
    pairs = [(i, y) for y in range(ys) for i in range(2)]

    def through(blocks, weight, j):
        return sum(nn(blocks[y][i], weight(i, y, j)) for i, y in pairs)

    def back_through(ref, grad, weight, count):
        for y in range(ys):
            both = []
            for i in range(2):
                both.append(
                    sum(nt(grad[:, j * 512 : j * 512 + 512], weight(i, y, j)) for j in range(count))
                )
            put(ref, y, both[0], both[1], core)

    (
        out_ref, dmid_ref, datt_ref, dssd_ref, ycore_ref, dentry_ref, send_ref, keep_ref, dng_ref,
        gi_ref, gd_ref, mid_ref, gu_ref, dn_ref, dmx_ref, fd_ref, n2_ref, hid_ref, mixed_ref, dh_ref, fade_ref, ent_ref,
    ) = refs
    core = core_ref[0]
    rows, width = tok_ref.shape
    heads_width = att_ref.shape[1]
    ff = hid_ref.shape[1]
    half = keep_ref.shape[1]
    cot_at, dbr_at, dgate_at, sel_at = 2 * ff, 2 * ff + width, 2 * ff + 2 * width, 2 * ff + 2 * width + DS
    reads = bc_ref[:, STATE:].astype(bf16)
    spread = head_spread()
    fade_ref[...] = nn_left(fade_of(cum_ref[...], off_ref[...]), spread, 2)
    ent_ref[...] = nt(reads, entry_ref[...].astype(bf16))
    none = jnp.zeros((rows, 1), f32)

    def at(j, first=0):
        return pl.ds(pl.multiple_of(first + j * 512, 512), 512)

    weights.wait(0)
    blocks = sides(normed_ref, core, ys)

    def gates(j, square):
        cols = at(j)
        gate = through(blocks, weights.gate, j).astype(bf16).astype(f32)
        gi_ref[:, cols] = gate
        ycore = yl_ref[:, cols] + fade_ref[:, cols] * ent_ref[:, cols]
        ycore_ref[:, cols] = ycore
        ssd = ycore + skip_ref[:, cols] * x_ref[:, cols]
        gated = ssd * gate * sigmoid(gate)
        gd_ref[:, cols] = gated
        return square + jnp.sum(gated * gated, axis=1, keepdims=True)

    square = lax.fori_loop(0, DS // 512, gates, none, unroll=True)
    rms_gate = lax.rsqrt(square / DS + EPS)
    mixed_ref[...] = (gd_ref[...] * rms_gate * gssm_ref[...]).astype(bf16)
    weights.wait(1)
    att_blocks, mix_blocks = sides(att_ref, core, ys), sides(mixed_ref, core, ys)

    def branches(j, square):
        branch = through(att_blocks, weights.ao, j) + through(mix_blocks, weights.so, j)
        middle = tok_ref[:, at(j)].astype(f32) + branch
        mid_ref[:, at(j)] = middle
        return square + jnp.sum(middle * middle, axis=1, keepdims=True)

    square = lax.fori_loop(0, width // 512, branches, none, unroll=True)
    rms = lax.rsqrt(square / width + EPS)
    n2_ref[...] = (mid_ref[...] * rms * gffn_ref[...]).astype(bf16)
    weights.wait(2)
    ups = sides(n2_ref, core, ys)

    def up(j, unused):
        gu_ref[:, at(j)] = through(ups, weights.gu, j)
        return unused

    lax.fori_loop(0, 2 * ff // 512, up, 0)

    def hide(j, unused):
        gate = gu_ref[:, at(j)]
        hid_ref[:, at(j)] = (gate * sigmoid(gate) * gu_ref[:, at(j, ff)]).astype(bf16)
        return unused

    lax.fori_loop(0, ff // 512, hide, 0)
    weights.wait(3)
    hids = sides(hid_ref, core, ys)

    def finals(j, unused):
        out_ref[:, at(j)] = (mid_ref[:, at(j)] + through(hids, weights.down, j)).astype(bf16)
        return unused

    lax.fori_loop(0, width // 512, finals, 0, unroll=True)
    cot = cot_ref[...]
    back_through(dh_ref, cot, weights.down, 2)

    def unhide(j, unused):
        gate, lift, dhid = gu_ref[:, at(j)], gu_ref[:, at(j, ff)], dh_ref[:, at(j)]
        sg = sigmoid(gate)
        dgate = dhid * lift * (sg * (1.0 + gate * (1.0 - sg)))
        send_ref[:, at(j)] = dgate.astype(bf16)
        send_ref[:, at(j, ff)] = (dhid * gate * sg).astype(bf16)
        return unused

    lax.fori_loop(0, ff // 512, unhide, 0)
    send_ref[:, cot_at:dbr_at] = cot
    wide = width // ys // 2

    def down(j, totals):
        grad = send_ref[:, pl.ds(pl.multiple_of(j * 512, 512), 512)]
        return [t + nt(grad, weights.gu(i, y, j)) for t, (i, y) in zip(totals, pairs)]

    zero = [jnp.zeros((rows, wide), f32)] * len(pairs)
    totals = lax.fori_loop(0, 2 * ff // 512, down, zero)
    for y in range(ys):
        put(dn_ref, y, totals[2 * y], totals[2 * y + 1], core)
    unit = mid_ref[...] * rms
    dn = dn_ref[...]
    dn = dn * gffn_ref[...]
    dmid = cot.astype(f32) + rms * (dn - unit * jnp.mean(dn * unit, axis=1, keepdims=True))
    dmid_ref[...] = dmid
    dbr = dmid.astype(bf16)
    send_ref[:, dbr_at:dgate_at] = dbr
    back_through(datt_ref, dbr, weights.ao, 2)
    back_through(dmx_ref, dbr, weights.so, 2)

    def means(j, mean):
        unit = gd_ref[:, at(j)] * rms_gate
        return mean + jnp.sum(dmx_ref[:, at(j)] * gssm_ref[:, at(j)] * unit, axis=1, keepdims=True)

    mean = lax.fori_loop(0, DS // 512, means, none) / DS

    def ungate(j, unused):
        cols = at(j)
        unit = gd_ref[:, cols] * rms_gate
        dgated = rms_gate * (dmx_ref[:, cols] * gssm_ref[:, cols] - unit * mean)
        gate = gi_ref[:, cols]
        sg = sigmoid(gate)
        ssd = ycore_ref[:, cols] + skip_ref[:, cols] * x_ref[:, cols]
        dssd = dgated * gate * sg
        dssd_ref[:, cols] = dssd
        dgate = (dgated * ssd * (sg * (1.0 + gate * (1.0 - sg)))).astype(bf16)
        send_ref[:, at(j, dgate_at)] = dgate
        fd_ref[:, cols] = (dssd * fade_ref[:, cols]).astype(bf16)
        return unused

    lax.fori_loop(0, DS // 512, ungate, 0)
    back_through(dng_ref, send_ref[:, dgate_at:sel_at], weights.gate, 3)
    dentry_ref[...] = tn(fd_ref[...], reads)
    to = 0
    for ref in (n2_ref, hid_ref, att_ref, mixed_ref, normed_ref):
        count = ys
        wide = ref.shape[1] // count
        for y in range(count):
            own, oth = halves(ref[:, y * wide : (y + 1) * wide], core)
            keep_ref[:, to : to + wide // 2] = own
            send_ref[:, sel_at + to : sel_at + to + wide // 2] = oth
            to += wide // 2


def products_kernel(plan, extra, keep_ref, own_ref, act_ref, *refs):
    got_ref, outs = act_ref, refs
    if extra:
        (extra_ref, *outs) = refs
    for which, a_at, act_at, size, g_at in plan:
        out = outs[which]
        for y in range(out.shape[0]):
            left = keep_ref[:, a_at + y * size : a_at + (y + 1) * size]
            right = act_ref[: left.shape[0], act_at + y * size : act_at + (y + 1) * size]
            for j in range(0, out.shape[-1], 512):
                stop = min(j + 512, out.shape[-1])
                total = tn(left, own_ref[: left.shape[0], g_at + j : g_at + stop])
                total = total + tn(right, got_ref[: left.shape[0], g_at + j : g_at + stop])
                if extra and which == 0 and stop == out.shape[-1]:
                    total = total + extra_ref[y]
                out[y, :, j:stop] = total.astype(bf16)


def split_products_kernel(plan, extra, y_ref, x_ref, keep_ref, own_ref, act_ref, *refs):
    got_ref, outs = act_ref, refs
    if extra:
        (extra_ref, *outs) = refs
    xkeep_ref, xsend_ref, ykeep_ref, ysend_ref = outs
    rows = keep_ref.shape[0]
    my_y, my_x = y_ref[0], x_ref[0]
    for kind, place, a_at, act_at, size, g_at, wide in plan:
        for k in range(2):
            y = k if kind == "x" else lax.rem(my_y + k, 2)
            left = keep_ref[:, pl.ds(pl.multiple_of(a_at + y * size, LANES), size)]
            right = act_ref[:rows, pl.ds(pl.multiple_of(act_at + y * size, LANES), size)]
            keep, send = (xkeep_ref, xsend_ref) if kind == "x" else (ykeep_ref, ysend_ref)
            block = 512 if wide % 512 == 0 else 384

            def columns(j, unused):
                at = pl.ds(pl.multiple_of(g_at + j * block, LANES), block)
                total = tn(left, own_ref[:rows, at]) + tn(right, got_ref[:rows, at])
                if kind == "x":
                    zs, each = keep.shape[1], keep.shape[2]
                    if extra:
                        total = total + extra_ref[k] * (j == wide // block - 1).astype(f32)
                    cols = pl.ds(pl.multiple_of(place + j * block, LANES), block)
                    total = total.reshape(zs, 2, each, block)
                    low, high = total[:, 0], total[:, 1]
                    keep[k, :, :, cols] = jnp.where(my_x == 0, low, high).astype(bf16)
                    send[k, :, :, cols] = jnp.where(my_x == 0, high, low).astype(bf16)
                else:
                    count = keep.shape[0]
                    each = size // count
                    cols = pl.ds(pl.multiple_of(j * block, LANES), block)
                    total = total.reshape(count, each, block).astype(bf16)
                    (send if k else keep)[:, place : place + each, cols] = total
                return unused

            lax.fori_loop(0, wide // block, columns, 0, unroll=True)


def fold_one_kernel(
    y_ref, x_ref, xkeep_ref, xgot_ref, ykeep_ref, ygot_ref,
    xkeep_out, xsend_out, ykeep_out, ysend_out,
):
    my_y, my_x = y_ref[0], x_ref[0]
    xkeep_out[...] = xkeep_ref[my_y].astype(f32) + xgot_ref[my_y].astype(f32)
    other = 1 - my_y
    xsend_out[...] = (xkeep_ref[other].astype(f32) + xgot_ref[other].astype(f32)).astype(bf16)
    for z in range(ykeep_out.shape[0]):
        at = 2 * z + my_x
        ykeep_out[z] = ykeep_ref[at].astype(f32) + ygot_ref[at].astype(f32)
        at = 2 * z + 1 - my_x
        ysend_out[z] = (ykeep_ref[at].astype(f32) + ygot_ref[at].astype(f32)).astype(bf16)


def laid(refs, width):
    at = 0
    for ref in refs:
        each = ref.shape[-2]
        for j in range(ref.shape[-1] // width):
            yield ref, at, j * width
            at += each


def fold_two_kernel(z_ref, xkeep_ref, xgot_ref, ykeep_ref, ygot_ref, keep_out, send_out):
    low = lax.rem(z_ref[0], 2)
    width = keep_out.shape[2]
    keeps = laid((xkeep_ref, ykeep_ref), width)
    gots = laid((xgot_ref, ygot_ref), width)
    for (keep, at, col), (got, *unused) in zip(keeps, gots):
        rows, cols = slice(at, at + keep.shape[-2]), slice(col, col + width)
        for high in range(keep_out.shape[0]):
            for out, z in ((keep_out, 2 * high + low), (send_out, 2 * high + 1 - low)):
                value = keep[z, :, cols] + got[z, :, cols].astype(f32)
                out[high, rows, :] = value.astype(out.dtype)


def fold_three_kernel(z_ref, keep_ref, got_ref, keep_out, send_out):
    high = lax.div(z_ref[0], 2)
    keep_out[...] = keep_ref[high] + got_ref[high].astype(f32)
    other = 1 - high
    send_out[...] = (keep_ref[other] + got_ref[other].astype(f32)).astype(bf16)


def summed(refs, rows):
    keep_ref, got_ref = refs
    return keep_ref[rows, :] + got_ref[rows, :].astype(f32)


def fold_four_kernel(keep_ref, got_ref, *outs):
    for out, at, col in laid(outs, keep_ref.shape[1]):
        rows = slice(at, at + out.shape[0])
        out[:, col : col + keep_ref.shape[1]] = summed((keep_ref, got_ref), rows)


def row_sums(value):
    ones = jnp.ones((8, value.shape[1]), bf16)
    return sum(nt(ones, part) for part in terms(value, 3))[:1]


def finish_post_kernel(
    keep_ref, sum_ref, one_ref, guw_ref, sow_ref, gffn_ref, gssm_ref,
    gu_ref, gate_ref, ao_ref, so_ref, dffn_ref, dssm_ref,
):
    both = (keep_ref, sum_ref)
    part, ups = one_ref.shape
    wide = keep_ref.shape[1]
    gu_ref[:, :ups] = one_ref[...]
    at = 0
    for out, start in ((gu_ref, ups), (gate_ref, 0)):
        for col in range(start, out.shape[1], wide):
            out[:, col : col + wide] = summed(both, slice(at, at + part))
            at += part
    for col in range(0, ao_ref.shape[1], wide):
        for out in (ao_ref, so_ref):
            out[:, col : col + wide] = summed(both, slice(at, at + out.shape[0]))
            at += out.shape[0]
    dffn_ref[...] = row_sums(guw_ref[...].astype(f32) * gu_ref[...]) / gffn_ref[...]
    dssm_ref[...] = row_sums(sow_ref[...].astype(f32) * so_ref[...]) / gssm_ref[...]


def finish_front_kernel(
    keep_ref, sum_ref, gate_ref, kvw_ref, qw_ref, iw_ref, gain_ref,
    kv_ref, q_ref, inner_ref, conv_ref, bias_ref, log_ref, step_ref, skip_ref, dgain_ref,
):
    both = (keep_ref, sum_ref)
    part, wide = kv_ref.shape[0], keep_ref.shape[1]
    count = A_COLS // wide
    blocks = [summed(both, slice(k * part, (k + 1) * part)) for k in range(count)]
    first = jnp.concatenate(blocks, axis=1)
    kv_ref[...] = first[:, :256]
    q_ref[...] = first[:, 256:768]
    inner_ref[:, :DS] = gate_ref[...]
    for k in range(DS // wide):
        rows = slice((count + k) * part, (count + k + 1) * part)
        inner_ref[:, DS + k * wide : DS + (k + 1) * wide] = summed(both, rows)
    last = first[:, 1024:]
    inner_ref[:, 2 * DS : 2 * DS + 2 * STATE] = first[:, 768:1024]
    inner_ref[:, DS + CONV_CH :] = last[:, :SSM_HEADS]
    turned_last = last.T
    own = bias_ref.shape[1]
    conv_ref[...] = turned_last[SSM_HEADS : SSM_HEADS + own, :CONV]
    bias_ref[...] = last[CONV : CONV + 1, SSM_HEADS : SSM_HEADS + own]
    for k, out in enumerate((log_ref, step_ref, skip_ref)):
        out[...] = last[CONV + 1 + k : CONV + 2 + k, SSM_HEADS : 2 * SSM_HEADS]
    total = row_sums(kvw_ref[...].astype(f32) * kv_ref[...])
    total = total + row_sums(qw_ref[...].astype(f32) * q_ref[...])
    total = total + row_sums(iw_ref[...].astype(f32) * inner_ref[...])
    dgain_ref[...] = total / gain_ref[...]


class PairReduction:
    def __init__(self, pieces, width):
        self.places = tuple(place_on(g).reshape(1).astype(jnp.int32) for g in ("y", "x", "z"))
        self.xkeep, xsend, self.ykeep, ysend = pieces
        self.width = width
        self.send(xsend, ysend, "x", "y")

    def send(self, xsend, ysend, first, second):
        self.sent = (xsend, ysend)
        self.gots = (
            swap(xsend, extents()[first][0]), swap(ysend, extents()[second][0])
        )

    def fold_one(self, *others):
        gots = after(self.gots, *others)
        x, y = self.xkeep.shape, self.ykeep.shape
        x, y = x[1:], (y[0] // 2, *y[1:])
        self.xkeep, xsend, self.ykeep, ysend = run(
            fold_one_kernel, "fold_one", [(x, f32), (x, bf16), (y, f32), (y, bf16)],
            (*self.places[:2], self.xkeep, gots[0], self.ykeep, gots[1]),
            scalars=2,
        )
        self.send(xsend, ysend, "y", "x")

    def fold_two(self, *others):
        gots = after(self.gots, *others)
        self.shapes = [self.xkeep.shape[1:], self.ykeep.shape[1:]]
        rows = sum(r * c // self.width for r, c in self.shapes)
        half = (self.xkeep.shape[0] // 2, rows, self.width)
        self.keep, self.sent = run(
            fold_two_kernel, "fold_two", [(half, f32), (half, bf16)],
            (self.places[2], self.xkeep, gots[0], self.ykeep, gots[1]),
            scalars=1,
        )
        self.gots = swap(self.sent, extents()["z"][0])

    def fold_three(self, *others):
        whole = self.keep.shape[1:]
        self.keep, self.sent = run(
            fold_three_kernel, "fold_three", [(whole, f32), (whole, bf16)],
            (self.places[2], self.keep, after(self.gots, *others)),
            scalars=1,
        )
        self.gots = swap(self.sent, 2 * extents()["z"][0])

    def fold_four(self, *others):
        return run(
            fold_four_kernel, "fold_four", [(shape, f32) for shape in self.shapes],
            (self.keep, after(self.gots, *others)),
        )


class PlainReduction:
    def __init__(self, pieces, rows):
        self.parts = [Reduction(pieces[0], rows[0], "x"), Reduction(pieces[1], rows[1], "y")]
        self.sent = [part.send() for part in self.parts]

    def fold_one(self, *others):
        for part in self.parts:
            part.receive(*others)
        self.sent = [part.send() for part in self.parts]

    fold_two = fold_one

    def fold_three(self, *others):
        pass

    def fold_four(self, *others):
        return [part.receive(*others) for part in self.parts]


def scan_back_kernel(
    dy_ref, x_ref, bc_ref, step_ref, cum_ref, cumt_ref, off_ref, dxw_ref, ds_ref,
    xw_ref, ce_ref, dyb_ref, dg_ref,
):
    rows = x_ref.shape[0]
    spread = head_spread()
    xw_ref[...] = (x_ref[...] * nn_left(step_ref[...], spread, 2)).astype(bf16)
    dyb_ref[...] = dy_ref[...].astype(bf16)
    ce_ref[...] = nn_left(cum_ref[...], spread, 3)
    keys, reads = bc_ref[:, :STATE].astype(bf16), bc_ref[:, STATE:].astype(bf16)
    early, late = iota((rows, rows), 0), iota((rows, rows), 1)
    keep = (early <= late) & (early >= late - off_ref[...])
    scores = jnp.where(keep, nt(keys, reads), 0.0)
    lane = iota((rows, LANES), 1)
    dg_ref[...] = jnp.zeros((rows, rows), f32)

    def pair(j, unused):
        cols = pl.ds(pl.multiple_of(j * LANES, LANES), LANES)
        wide = ce_ref[:, cols]
        xw, dy = xw_ref[:, cols], dyb_ref[:, cols]
        outs = []
        change = 0.0
        for k in range(2):
            first = wide[:, k * SSM_DIM : k * SSM_DIM + 1]
            second = cumt_ref[pl.ds(2 * j + k, 1), :]
            decay = jnp.exp(jnp.minimum(second - first, 0.0))
            outs.append(nn((decay * scores).astype(bf16), dy))
            mine = (lane < SSM_DIM) if k == 0 else (lane >= SSM_DIM)
            change = change + nt(xw * mine.astype(bf16), dy) * decay
        dg_ref[...] += change
        dxw_ref[:, cols] = jnp.where(lane < SSM_DIM, outs[0], outs[1])
        return unused

    lax.fori_loop(0, SSM_HEADS // 2, pair, 0)
    ds_ref[...] = jnp.where(keep, dg_ref[...], 0.0).astype(bf16)


def mixer_back_kernel(
    dy_ref, ycore_ref, x_ref, bc_ref, step_ref, cum_ref, z_ref, off_ref, entry_ref,
    down_ref, skip_ref, dec_ref, chan_ref, cw_ref, cb_ref, dxwl_ref, ds_ref,
    dext_ref, dz_ref, small_ref,
    dact_ref,
):
    rows = x_ref.shape[0]
    spread, gather = head_spread(), head_sum_matrix()
    off, cum = off_ref[...], cum_ref[...]
    step_wide = nn_left(step_ref[...], spread, 2)
    keys, reads = bc_ref[:, :STATE].astype(bf16), bc_ref[:, STATE:].astype(bf16)
    dscores = ds_ref[...]
    down = down_ref[...].astype(bf16)
    tail = nn_left(tail_of(cum, off), spread, 2)
    fade = nn_left(fade_of(cum, off), spread, 2)
    bd = nt(keys, down) * tail
    xw = (x_ref[...] * step_wide).astype(bf16).astype(f32)
    dxw = dxwl_ref[...] + bd
    dact_ref[:, DS : DS + STATE] = nn(dscores, reads) + nn((tail * xw).astype(bf16), down)
    dact_ref[:, DS + STATE :] = tn(dscores, keys) + nn(
        (fade * dy_ref[...]).astype(bf16), entry_ref[...].astype(bf16)
    )
    ones = jnp.ones((8, STATE), bf16)
    product = sum(nt(ones, part) for part in terms(down_ref[...] * entry_ref[...], 3))
    through = jnp.sum(xw * bd, axis=0, keepdims=True)
    direct = jnp.sum(dy_ref[...] * x_ref[...], axis=0, keepdims=True)
    row = iota((8, DS), 0)
    sums = jnp.where(row == 0, product, jnp.where(row == 1, through, direct))
    sums = nn_left(sums, gather, 3)
    through, kept = sums[1:2], sums[0:1] * carry_of(cum, off)
    last = (iota((rows, 1), 0) == rows - 1).astype(f32)
    dyb = dy_ref[...].astype(bf16).astype(f32)
    dcum = nn_left(dyb * ycore_ref[...] - xw * dxw, gather, 2) + last * (through + kept)
    tri = (iota((rows, rows), 0) <= iota((rows, rows), 1)).astype(f32).astype(bf16)
    dlog = nn_right(tri, dcum, 3)
    x = x_ref[...]
    step, dec = step_ref[...], dec_ref[...]
    dstep = nn_left(dxw * x, gather, 2) - dlog * dec
    dz = dstep * sigmoid(z_ref[...])
    dz_ref[...] = dz
    small_ref[...] = jnp.zeros(small_ref.shape, f32)
    small_ref[CONV + 1 : CONV + 2, :LANES] = jnp.sum(dlog * (-step * dec), axis=0, keepdims=True)
    small_ref[CONV + 1 : CONV + 2, LANES : 2 * LANES] = jnp.sum(dz, axis=0, keepdims=True)
    small_ref[CONV + 1 : CONV + 2, 2 * LANES : 3 * LANES] = sums[2:3]
    dact_ref[:, :DS] = dxw * step_wide + skip_ref[...] * dy_ref[...]
    for j in range(CONV_CH // 256):
        cols = slice(j * 256, (j + 1) * 256)
        taps = conv_taps(chan_ref, cols, off)
        mixed = cb_ref[:, cols]
        for i, tap in enumerate(taps):
            mixed = mixed + tap * cw_ref[i : i + 1, cols]
        sg = sigmoid(mixed)
        dmix = dact_ref[:, cols] * (sg * (1.0 + mixed * (1.0 - sg)))
        small_ref[CONV : CONV + 1, cols] = jnp.sum(dmix, axis=0, keepdims=True)
        total = 0.0
        for i, tap in enumerate(taps):
            back = CONV - 1 - i
            small_ref[i : i + 1, cols] = jnp.sum(dmix * tap, axis=0, keepdims=True)
            part = dmix * ((off >= back).astype(f32) * cw_ref[i : i + 1, cols])
            part = jnp.concatenate([jnp.zeros((RIM, 256), f32), part], axis=0)
            total = total + (pltpu.roll(part, rows + RIM - back, 0) if back else part)
        dext_ref[:, cols] = total


def back_grads_kernel(
    ys, core_ref, dq_ref, dkv_ref, dext_ref, dz_ref, cos_ref, sin_ref, normed_ref, nrim_ref,
    small_ref, ga_ref, keep_ref,
):
    core = core_ref[0]
    count, last = small_ref.shape[0], keep_ref.shape[0]
    ga_ref[last:, :] = jnp.zeros((ga_ref.shape[0] - last, ga_ref.shape[1]), bf16)
    ga_ref[last : last + count, :CONV_CH] = small_ref[...].astype(bf16)
    dkv = dkv_ref[0].astype(f32)
    for i in range(1, dkv_ref.shape[0]):
        dkv = dkv + dkv_ref[i].astype(f32)
    ga_ref[:RIM, :768] = jnp.zeros((RIM, 768), bf16)
    ga_ref[:RIM, 1024:A_COLS] = jnp.zeros((RIM, LANES), bf16)
    ga_ref[RIM:last, :LANES] = turned_back(dkv[:, :LANES], cos_ref[...], sin_ref[...]).astype(bf16)
    ga_ref[RIM:last, LANES:256] = dkv[:, LANES:].astype(bf16)
    ga_ref[RIM:last, 256:768] = dq_ref[...]
    ga_ref[:last, 768:1024] = dext_ref[:, DS:].astype(bf16)
    ga_ref[RIM:last, 1024:A_COLS] = dz_ref[...].astype(bf16)
    ga_ref[:last, A_COLS : A_COLS + DS] = dext_ref[:, :DS].astype(bf16)
    wide = normed_ref.shape[1] // ys
    at, to = 0, A_COLS + DS
    for y in range(ys):
        cols = slice(y * wide, (y + 1) * wide)
        for ref, rows in ((nrim_ref, slice(0, RIM)), (normed_ref, slice(RIM, last))):
            own, oth = halves(ref[:, cols], core)
            keep_ref[rows, at : at + wide // 2] = own
            ga_ref[rows, to + at : to + at + wide // 2] = oth
        at += wide // 2


def back_kernel(
    core_ref, gab_ref, wa_own, wa_oth, wb_own, wb_oth, tok_ref, dmid_ref, dng_ref, gain_ref,
    dtok_ref, drim_ref, dn_ref,
):
    core = core_ref[0]
    for y in range(wa_own.shape[0]):
        last = tok_ref.shape[0]
        ga, gb = gab_ref[:last, :A_COLS], gab_ref[:last, A_COLS : A_COLS + DS]
        own = nt(ga, wa_own[y]) + nt(gb, wb_own[y])
        oth = nt(ga, wa_oth[y]) + nt(gb, wb_oth[y])
        put(dn_ref, y, own, oth, core)

    def through_norm(dn, tok):
        tok = tok.astype(f32)
        rms = lax.rsqrt(jnp.mean(tok * tok, axis=1, keepdims=True) + EPS)
        unit = tok * rms
        dn = dn * gain_ref[...]
        return rms * (dn - unit * jnp.mean(dn * unit, axis=1, keepdims=True))

    drim_ref[...] = through_norm(dn_ref[:RIM, :], tok_ref[:RIM, :])
    dtok_ref[...] = dmid_ref[...] + through_norm(dn_ref[RIM:, :] + dng_ref[...], tok_ref[RIM:, :])


def gain_kernel(pairs, count, *refs):
    gains, refs = refs[:count], refs[count:]
    outs = refs[-count:]
    for k, out in enumerate(outs):
        total = 0.0
        for group, w, g in pairs:
            if group == k:
                total = total + jnp.sum(
                    refs[w][...].astype(f32) * refs[g][...], axis=1, keepdims=True
                )
        out[...] = total / gains[k][...].astype(f32)


def run(kernel, name, outs, args, scalars=0, scratch=(), us=3, left=0, sems=()):
    moved = sum(a.size * a.dtype.itemsize for a in args)
    shapes = [jax.ShapeDtypeStruct(shape, kind) for shape, kind in outs]
    moved += sum(s.size * s.dtype.itemsize for s in shapes)
    specs = [pl.BlockSpec(memory_space=pltpu.SMEM)] * scalars
    specs += [pl.BlockSpec(memory_space=pltpu.VMEM)] * (len(args) - scalars - left)
    specs += [pl.BlockSpec(memory_space=pl.ANY)] * left
    return pl.pallas_call(
        kernel,
        name=name,
        out_shape=shapes,
        in_specs=specs,
        out_specs=[pl.BlockSpec(memory_space=pltpu.VMEM)] * len(shapes),
        scratch_shapes=[pltpu.VMEM(shape, kind) for shape, kind in scratch]
        + [pltpu.SemaphoreType.DMA(shape) for shape in sems],
        compiler_params=pltpu.CompilerParams(vmem_limit_bytes=62 * 2**20),
        cost_estimate=pl.CostEstimate(
            flops=us * SCALE, bytes_accessed=moved, transcendentals=0
        ),
    )(*args)


def padded(vector, width):
    return jnp.pad(vector.astype(f32), (0, width - vector.shape[0]))[None, :]


def local(
    tokens, lengths, cotangent, mixer_gain, query_weight, keyval_weight, inner_weight, conv_weight,
    conv_bias, ssm_gain, attn_out_weight, ssm_out_weight, ffn_gain, gate_up_weight, down_weight,
    decay_log, step_bias, skip_gain,
):
    rows, width = tokens.shape
    seq_count, seq_rank = lax.axis_size(SEQ), lax.axis_index(SEQ)
    side = place_on("core").reshape(1)
    back = (rows * seq_count // 2) // rows
    part = query_weight.shape[0]
    heads_width, ff = HEADS * HEAD_DIM, gate_up_weight.shape[1] // 2
    a_rows, s_rows, f_rows = attn_out_weight.shape[0], ssm_out_weight.shape[0], down_weight.shape[0]
    ys = lax.axis_size("y")

    rim = shifted(tokens[rows - RIM :], 1)
    small = jnp.concatenate(
        [mixer_gain, conv_weight.reshape(-1), conv_bias, ssm_gain, ffn_gain]
    ).astype(f32)
    counts = [mixer_gain.size, conv_weight.size, conv_bias.size, ssm_gain.size, ffn_gain.size]
    slots = -(-small.size // LANES) * LANES
    small = gather_small(jnp.pad(small, (0, slots - small.size)))
    others = lax.axis_size(SEQ)
    aligned = ys == 2 and others == 8 and all(r % 16 == 0 for r in (part, a_rows, s_rows, f_rows))
    core_unit = extents()["core"][0]
    if aligned:
        packed, front = run(
            pack_kernel,
            "pack",
            [((6 * part + s_rows, width), bf16), ((part, A_COLS + DS), bf16)],
            (
                gate_up_weight, inner_weight, attn_out_weight, ssm_out_weight, keyval_weight,
                query_weight,
            ),
        )
    else:
        tail = jnp.pad(inner_weight[:, DS + CONV_CH :], ((0, 0), (0, LANES - SSM_HEADS)))
        front = jnp.concatenate(
            [
                keyval_weight, query_weight, inner_weight[:, 2 * DS : DS + CONV_CH], tail,
                inner_weight[:, DS : 2 * DS],
            ],
            1,
        )
        ao = jnp.concatenate([attn_out_weight[:, :512], attn_out_weight[:, 512:]], 0)
        packed = jnp.concatenate(
            [
                inner_weight[:, :width],
                jnp.concatenate([inner_weight[:, width:DS], ao], 1),
                ssm_out_weight,
            ]
            + [gate_up_weight[:, k * width : (k + 1) * width] for k in range(2 * ff // width)],
            0,
        )
    packed = lax.all_gather(packed, AXES, axis=0)
    packed = packed.reshape(ys, 2, others, *packed.shape[1:])
    front = shared(front, "z")
    front_one = Gathering(front[:, :, :A_COLS], "y")
    front_two = Gathering(front[:, :, A_COLS:], "x")
    down_slots = after(down_weight, front_one.full, front_two.full)[None]
    down_slots = jnp.broadcast_to(down_slots, (lax.axis_size("z"), *down_weight.shape))
    down_all = dealt(down_slots, "z")
    front_one.finish(down_slots)
    front_two.finish(down_slots)
    down_got = Gathering(after(down_all, front_one.full, front_two.full), "x")
    front_one.finish(down_got.full)
    front_two.finish(down_got.full)
    wa_own, wa_oth = front_one.sides(1)
    wb_own, wb_oth = front_two.sides(1)

    starts = [sum(counts[:i]) for i in range(len(counts))]
    gain_one, w_conv, b_conv, gain_ssm, gain_two = (
        small[:, s : s + c].reshape(-1) for s, c in zip(starts, counts)
    )
    w_conv = jnp.pad(w_conv.reshape(CONV_CH, CONV).T, ((0, 8 - CONV), (0, 0)))
    gain_one, b_conv, gain_ssm, gain_two = (
        v[None, :] for v in (gain_one, b_conv, gain_ssm, gain_two)
    )
    tokens_rim = jnp.concatenate([rim, tokens], 0)
    places = seq_rank * rows + jnp.arange(rows)
    begin = jnp.zeros_like(places)
    end = jnp.int32(0)
    for i in range(lengths.shape[1]):
        end = end + lengths[0, i]
        begin = jnp.where(end <= places, end, begin)
    offset = (places - begin).astype(jnp.int32)
    half = HEAD_DIM // 2
    freq = BASE ** (-jnp.arange(half).astype(f32) / half)
    angle = offset.astype(f32)[:, None] * freq[None, :]
    cos = jnp.tile(jnp.cos(angle), (1, 4))
    sin = jnp.sin(angle)
    sin = jnp.tile(jnp.concatenate([-sin, sin], 1), (1, 2))
    off = offset[:, None]
    step_bias_row, decay_row = padded(step_bias, LANES), padded(jnp.exp(decay_log), LANES)
    skip = jnp.repeat(skip_gain, SSM_DIM)[None, :]

    (q8, kv, normed, nrim, chan, x, bc, step, cum, cumt, z, state, carry) = run(
        front_kernel,
        "front",
        [
            ((HEADS, rows, LANES), bf16),
            ((rows, 256), bf16),
            ((rows, width), bf16),
            ((RIM, width), bf16),
            ((rows + RIM, CONV_CH), bf16),
            ((rows, DS), f32),
            ((rows, 2 * STATE), f32),
            ((rows, LANES), f32),
            ((rows, LANES), f32),
            ((LANES, rows), f32),
            ((rows, LANES), f32),
            ((DS, STATE), f32),
            ((1, LANES), f32),
        ],
        (
            side, tokens_rim, gain_one, wa_own, wa_oth, wb_own, wb_oth,
            cos, sin, off, w_conv, b_conv, step_bias_row, decay_row,
        ),
        scalars=1,
        scratch=[((rows + RIM, width), bf16), ((rows, DS), bf16)],
        us=8,
    )
    carrying = Carrying(state, carry, back, 1)
    sent_state = carrying.send()
    rank = seq_rank.reshape(1).astype(jnp.int32)
    kv_slots = jnp.broadcast_to(kv[None], (seq_count, *kv.shape))
    down_got.finish(sent_state, kv_slots)
    kv_all = dealt(kv_slots, SEQ)
    window = (back + 1) * rows
    y_local = run(
        scan_kernel, "scan", [((rows, DS), f32)],
        after((x, bc, step, cum, cumt, off), sent_state, kv_slots, down_got.full),
        scratch=[((rows, DS), bf16), ((rows, DS), f32)], us=8,
    )[0]
    entry = carrying.receive(y_local)
    if entry is None:
        sent_state = carrying.send()
    down_got.finish(y_local, sent_state)
    attended, lse = run(
        functools.partial(attend_kernel, back + 1),
        "attend",
        [((rows, heads_width), bf16), ((LANES, rows), f32)],
        after((rank, q8, kv_all, off), down_got.full),
        scalars=1,
        scratch=[
            ((window, LANES), bf16),
            ((window, LANES), bf16),
            ((rows, window), f32),
            ((HEADS, rows, LANES), f32),
        ],
        us=10,
    )
    while entry is None:
        entry = carrying.receive(attended)
        if entry is None:
            carrying.send()
    packed = after(packed, entry)
    down_sides = [
        f.reshape(ys, others, *f.shape[3:]) for f in (down_got.full, down_got.other)
    ]
    post_scratch, post_sems = [], []
    if aligned:
        parts, post_weights = (part, a_rows, s_rows, f_rows), (packed, *down_sides)
        rows_in_all = 6 * part + s_rows + f_rows
        post_scratch = [((2, ys, others, rows_in_all, width), bf16)]
        post_sems = [(4, 2)]
    else:
        parts = ()
        packed = [
            jnp.concatenate(
                [
                    lax.dynamic_index_in_dim(packed, place_on("core") ^ i, 1, False),
                    down_sides[i],
                ],
                2,
            )
            for i in range(2)
        ]
        gu_at = 2 * part + s_rows

        def taken(full, start, size, low, high):
            return full[:, :, start : start + size, low:high].reshape(ys, -1, high - low)

        def joined_columns(blocks):
            return [jnp.concatenate([taken(f, *block) for block in blocks], 2) for f in packed]

        post_weights = (
            *joined_columns([(0, part, 0, width), (part, part, 0, DS - width)]),
            *joined_columns([(part + k * a_rows, a_rows, 512, 1024) for k in range(2)]),
            *joined_columns([(2 * part, s_rows, 0, width)]),
            *joined_columns([(gu_at + 4 * part, f_rows, 0, width)]),
            *joined_columns([(gu_at + k * part, part, 0, width) for k in range(2 * ff // width)]),
        )
    half = (2 * width + ff + heads_width + DS) // 2
    sent = 2 * ff + 2 * width + DS
    output, dmid, datt, dssd, ycore, dentry, send, keep, dng = run(
        functools.partial(post_kernel, parts, ys),
        "post",
        [
            ((rows, width), bf16),
            ((rows, width), f32),
            ((rows, heads_width), bf16),
            ((rows, DS), f32),
            ((rows, DS), f32),
            ((DS, STATE), f32),
            ((rows, sent + half), bf16),
            ((rows, half), bf16),
            ((rows, width), f32),
        ],
        (
            side, tokens, cotangent, attended, y_local, x, bc, cum, off, entry, skip, normed,
            gain_ssm, gain_two, *post_weights,
        ),
        scalars=1,
        left=3 if aligned else 0,
        sems=post_sems,
        scratch=[
            ((rows, DS), f32),
            ((rows, DS), f32),
            ((rows, width), f32),
            ((rows, 2 * ff), f32),
            ((rows, width), f32),
            ((rows, DS), f32),
            ((rows, DS), bf16),
            ((rows, width), bf16),
            ((rows, ff), bf16),
            ((rows, DS), bf16),
            ((rows, ff), f32),
            ((rows, DS), f32),
            ((rows, DS), f32),
        ]
        + post_scratch,
        us=30,
    )
    got = swap(send, core_unit)
    carrying = Carrying(dentry, carry, back, -1)
    sent_state = carrying.send()
    off_row = offset[None, :]
    sizes = [width // 2, ff // 2, heads_width // 2, DS // 2, width // 2]
    ats = [sum(sizes[:i]) for i in range(5)]
    sizes = [size // ys for size in sizes]
    n2_at, hid_at, att_at, mix_at, norm_at = ats
    cot_at, dbr_at, dgate_at = 2 * ff, 2 * ff + width, 2 * ff + 2 * width
    places = tuple(place_on(g).reshape(1).astype(jnp.int32) for g in ("y", "x"))

    def weight_sums(name, x_parts, y_parts, keep, own, got, extra=()):
        plan, at, tall = [], 0, y_parts[0][4]
        for p in x_parts:
            plan.append(("x", at, *p))
            at += p[4]
        wide, at = at, 0
        for p in y_parts:
            plan.append(("y", at, *p))
            at += p[2] // others
        if aligned:
            xs = (ys, others // 2, x_parts[0][2] // others, wide)
            made = run(
                functools.partial(split_products_kernel, plan, len(extra)),
                name,
                [(xs, bf16), (xs, bf16), ((others, at, tall), bf16), ((others, at, tall), bf16)],
                (*places, keep, own, got, *extra),
                scalars=2,
                us=9,
            )
            return PairReduction(made, 512 if wide % 512 == 0 else 384)
        parts = x_parts + y_parts
        made = run(
            functools.partial(
                products_kernel, [(i, *p[:4]) for i, p in enumerate(parts)], len(extra)
            ),
            name,
            [((ys, p[2], p[4]), bf16) for p in parts],
            (keep, own, got, *extra),
            us=9,
        )
        heads = made[: len(x_parts)]
        tails = [m.reshape(ys, others, -1, tall) for m in made[len(x_parts) :]]
        rows_of = (x_parts[0][2] // others, at)
        return PlainReduction((jnp.concatenate(heads, 2), jnp.concatenate(tails, 2)), rows_of)

    dxw, dscores = run(
        scan_back_kernel,
        "scan_back",
        [((rows, DS), f32), ((rows, rows), bf16)],
        after((dssd, x, bc, step, cum, cumt, off_row), sent_state),
        scratch=[
            ((rows, DS), bf16),
            ((rows, DS), f32),
            ((rows, DS), bf16),
            ((rows, rows), f32),
        ],
        us=9,
    )

    downstream = carrying.receive(dxw)
    if downstream is None:
        sent_state = carrying.send()
    keep, send, got = after((keep, send, got), dxw, sent_state)
    red_one = weight_sums(
        "weights_one",
        [(n2_at, sent + n2_at, sizes[0], 0, ff)],
        [(hid_at, sent + hid_at, sizes[1], cot_at, width)],
        keep,
        send,
        got,
    )
    dq, dkv = run(
        functools.partial(attend_back_kernel, back + 1),
        "attend_back",
        [((rows, heads_width), bf16), ((seq_count, rows, 256), bf16)],
        after((rank, q8, kv_all, off_row, lse, datt, cos, sin), red_one.sent),
        scalars=1,
        scratch=[
            ((window, LANES), bf16),
            ((window, LANES), bf16),
            ((window, rows), f32),
            ((HEADS, rows, LANES), bf16),
            ((HEADS, rows, LANES), f32),
            ((window, 256), f32),
        ],
        us=14,
    )
    dkv_got = dealt(dkv, SEQ)
    keep, send, got = after((keep, send, got), red_one.sent, dq, dkv)
    red_two = weight_sums(
        "weights_two",
        [
            (n2_at, sent + n2_at, sizes[0], ff, ff),
            (norm_at, sent + norm_at, sizes[4], dgate_at, DS),
        ],
        [
            (att_at, sent + att_at, sizes[2], dbr_at, width),
            (mix_at, sent + mix_at, sizes[3], dbr_at, width),
        ],
        keep,
        send,
        got,
    )
    while downstream is None:
        downstream = carrying.receive(red_two.sent)
        if downstream is None:
            carrying.send()
    red_one.fold_one(red_two.sent, downstream)
    dext, dz, small = run(
        mixer_back_kernel,
        "mixer_back",
        [
            ((rows + RIM, CONV_CH), f32),
            ((rows, LANES), f32),
            ((8, CONV_CH), f32),
        ],
        after(
            (
                dssd, ycore, x, bc, step, cum, z, off, entry, downstream, skip, decay_row, chan,
                w_conv, b_conv, dxw, dscores,
            ),
            red_one.sent,
        ),
        scratch=[((rows, CONV_CH), f32)],
        us=13,
    )
    count = lax.axis_size(AXES)
    gab, norm_keep = run(
        functools.partial(back_grads_kernel, ys),
        "back_grads",
        [((rows + 2 * RIM, A_COLS + DS + width // 2), bf16), ((rows + RIM, width // 2), bf16)],
        (side, dq, dkv_got, dext, dz, cos, sin, normed, nrim, small),
        scalars=1,
    )
    gab_got = swap(gab, core_unit)
    small = small + gab_got[rows + RIM : rows + RIM + small.shape[0], :CONV_CH].astype(f32)
    free = LANES - SSM_HEADS
    convs = small[: CONV + 1].reshape(CONV + 1, count, -1).transpose(1, 0, 2)
    head_sums = small[CONV + 1, : 3 * LANES].reshape(3, LANES)[:, :SSM_HEADS]
    if aligned:
        head_sums = jnp.broadcast_to(head_sums[None], (count, 3, SSM_HEADS))
        per_device = jnp.concatenate(
            [
                jnp.pad(convs, ((0, 0), (0, 0), (0, free - convs.shape[2]))),
                jnp.pad(head_sums, ((0, 0), (0, 0), (0, free - SSM_HEADS))),
            ],
            1,
        )
        slots = CONV + 4
    else:
        head_sums = jnp.broadcast_to(head_sums.reshape(1, -1), (count, 3 * SSM_HEADS))
        per_device = jnp.concatenate([convs.reshape(count, -1), head_sums], 1)
        slots = per_device.shape[1]
        per_device = jnp.pad(per_device, ((0, 0), (0, part * free - slots)))
        per_device = per_device.reshape(count, part, free)
    per_device = lax.dynamic_index_in_dim(
        per_device.reshape(ys, 2, others, -1, free), place_on("core"), 1, False
    )
    aside = 384 if aligned else A_COLS % 512
    extra = jnp.pad(
        per_device, ((0, 0), (0, 0), (0, part - per_device.shape[2]), (aside - free, 0))
    ).reshape(ys, others * part, aside)
    grad_tokens, grad_rim = run(
        back_kernel,
        "back",
        [((rows, width), f32), ((RIM, width), f32)],
        (
            side, gab, wa_own, wa_oth, wb_own, wb_oth, tokens_rim, dmid, dng,
            gain_one,
        ),
        scalars=1,
        scratch=[((rows + RIM, width), f32)],
        us=7,
    )
    red_two.fold_one(grad_tokens)
    norm_keep, gab, gab_got, extra = after((norm_keep, gab, gab_got, extra), red_two.sent)
    red_three = weight_sums(
        "front_weights",
        [(0, A_COLS + DS, sizes[4], 0, A_COLS)],
        [(0, A_COLS + DS, sizes[4], A_COLS, DS)],
        norm_keep,
        gab,
        gab_got,
        (extra,),
    )
    red_one.fold_two(red_three.sent)
    red_two.fold_two(red_one.sent)
    red_one.fold_three(red_two.sent)
    red_three.fold_one(red_one.sent)
    red_two.fold_three(red_three.sent)
    red_three.fold_two(red_two.sent)
    rim_got = shifted(after(grad_rim, red_three.sent), -1)
    r_one, r_down = red_one.fold_four(red_three.sent)
    red_three.fold_three(r_one)
    if aligned:
        r_gu, r_gate, r_ao, r_so, g_ffn, g_ssm = run(
            finish_post_kernel,
            "finish_post",
            [
                ((part, 2 * ff), f32),
                ((part, DS), f32),
                ((a_rows, width), f32),
                ((s_rows, width), f32),
                ((1, part), f32),
                ((1, s_rows), f32),
            ],
            (
                red_two.keep, after(red_two.gots, red_three.sent), r_one, gate_up_weight, ssm_out_weight,
                ffn_gain.astype(f32)[None, :], ssm_gain.astype(f32)[None, :],
            ),
        )
        rim_got = after(rim_got, r_gu)
        grad_tokens = grad_tokens.at[rows - RIM :].add(rim_got)
        r_kv, r_q, g_inner, g_conv, g_bias, g_log, g_step, g_skip, g_mixer = run(
            finish_front_kernel,
            "finish_front",
            [
                ((part, 256), f32),
                ((part, heads_width), f32),
                ((part, inner_weight.shape[1]), f32),
                (conv_weight.shape, f32),
                ((1, conv_bias.size), f32),
                ((1, SSM_HEADS), f32),
                ((1, SSM_HEADS), f32),
                ((1, SSM_HEADS), f32),
                ((1, part), f32),
            ],
            (
                red_three.keep, after(red_three.gots, grad_tokens), r_gate, keyval_weight, query_weight,
                inner_weight, mixer_gain.astype(f32)[None, :],
            ),
        )
        g_bias, g_mixer, g_ssm, g_ffn = (v[0] for v in (g_bias, g_mixer, g_ssm, g_ffn))
        heads = [v[0] for v in (g_log, g_step, g_skip)]
    else:
        r_two, r_out = red_two.fold_four(red_three.sent)
        rim_got = after(rim_got, r_two)
        grad_tokens = grad_tokens.at[rows - RIM :].add(rim_got)
        r_e, r_f = red_three.fold_four(grad_tokens)
        r_gu = jnp.concatenate([r_one, r_two[:, :ff]], 1)
        small = r_e[:, A_COLS - free :].reshape(-1)[:slots]
        conv = small[: (CONV + 1) * conv_bias.size].reshape(CONV + 1, -1)
        g_conv, g_bias = conv[:CONV].T, conv[CONV]
        heads = small[(CONV + 1) * conv_bias.size :].reshape(3, SSM_HEADS)
        g_inner = jnp.concatenate([r_two[:, ff:], r_f, r_e[:, 768 : 1024 + SSM_HEADS]], 1)
        r_kv, r_q, r_ao, r_so = r_e[:, :256], r_e[:, 256:768], r_out[:a_rows], r_out[a_rows:]
        pairs = [(0, 0, 1), (0, 2, 3), (0, 4, 5), (1, 6, 7), (2, 8, 9)]
        gains = run(
            functools.partial(gain_kernel, pairs, 3),
            "gains",
            [((part, 1), f32), ((s_rows, 1), f32), ((part, 1), f32)],
            (
                mixer_gain[:, None], ssm_gain[:, None], ffn_gain[:, None],
                keyval_weight, r_kv, query_weight, r_q, inner_weight, g_inner,
                ssm_out_weight, r_so, gate_up_weight, r_gu,
            ),
        )
        g_mixer, g_ssm, g_ffn = (v[:, 0] for v in gains)
    return (
        output,
        grad_tokens,
        g_mixer,
        r_q,
        r_kv,
        g_inner,
        g_conv,
        g_bias,
        g_ssm,
        r_ao,
        r_so,
        g_ffn,
        r_gu,
        r_down,
        heads[0],
        heads[1],
        heads[2],
    )


def solution(mesh):
    across, along = mesh.shape["dp"], mesh.shape["seq"]
    mesh = jax.sharding.Mesh(mesh.devices.reshape(across // 2, 2, along // 2, 2), AXES)
    lead, flat, rep = P(AXES, None), P(AXES), P()
    return jax.shard_map(
        local,
        mesh=mesh,
        in_specs=(
            lead, P(AXES[:2], None), lead, flat, lead, lead, lead, lead, flat, flat, lead, lead, flat,
            lead, lead, rep, rep, rep,
        ),
        out_specs=(
            lead, lead, flat, lead, lead, lead, lead, flat, flat, lead, lead, flat, lead, lead,
            rep, rep, rep,
        ),
        check_vma=False,
    )
```

```python
import functools

import jax
import jax.numpy as jnp
from jax import lax
from jax.experimental import pallas as pl
from jax.experimental.pallas import tpu as pltpu
from jax.sharding import PartitionSpec as P

HEADS = 8
KV_HEADS = 2
HEAD_DIM = 64
SSM_HEADS = 24
SSM_DIM = 64
STATE = 128
CONV = 4
DS = 1536
CONV_CH = 1792
RIM = 16
LANES = 128
A_COLS = 2 * KV_HEADS * HEAD_DIM + HEADS * HEAD_DIM + 2 * STATE + LANES
EPS = 1e-6
BASE = 10000.0
NEG = -1e30
SCALE = 6_600_000_000
AXES = ("y", "core", "z", "x")
SEQ = AXES[2:]

f32 = jnp.float32
bf16 = jnp.bfloat16


def nn(a, b):
    return lax.dot_general(a, b, (((1,), (0,)), ((), ())), preferred_element_type=f32)


def tn(a, b):
    return lax.dot_general(a, b, (((0,), (0,)), ((), ())), preferred_element_type=f32)


def nt(a, b):
    return lax.dot_general(a, b, (((1,), (1,)), ((), ())), preferred_element_type=f32)


def terms(value, count):
    parts = []
    for unused in range(count):
        parts.append(value.astype(bf16))
        value = value - parts[-1].astype(f32)
    return parts


def nn_left(value, ones, count):
    return sum(nn(part, ones) for part in terms(value, count))


def nn_right(ones, value, count):
    return sum(nn(ones, part) for part in terms(value, count))


def iota(shape, dim):
    return lax.broadcasted_iota(jnp.int32, shape, dim)


def head_spread():
    row = iota((LANES, DS), 0)
    return (iota((LANES, DS), 1) // SSM_DIM == row).astype(f32).astype(bf16)


def head_sum_matrix():
    col = iota((DS, LANES), 1)
    return (iota((DS, LANES), 0) // SSM_DIM == col).astype(f32).astype(bf16)


def extents():
    along = lax.axis_size(SEQ)
    return {
        "x": (1, 2),
        "z": (2, along // 2),
        "core": (along, 2),
        "y": (2 * along, lax.axis_size("y")),
    }


def my_index():
    return lax.axis_index(AXES)


def place_on(group):
    unit, size = extents()[group]
    return (my_index() // unit) % size


def swap(array, mask):
    count = lax.axis_size(AXES)
    return lax.ppermute(array, AXES, [(i, i ^ mask) for i in range(count)])


def in_order(pieces, place):
    pieces = list(pieces)
    bit = 1
    while bit < len(pieces):
        flag = (place // bit) % 2 == 1
        pieces = [jnp.where(flag, pieces[j ^ bit], pieces[j]) for j in range(len(pieces))]
        bit *= 2
    return pieces


def collect(array, group, axis):
    unit, size = extents()[group]
    pieces = [array] + [swap(array, k * unit) for k in range(1, size)]
    return jnp.stack(in_order(pieces, place_on(group)), axis)


class Gathering:
    def __init__(self, full, first):
        self.full = full
        self.steps = [("y", 0), ("x", 2)] if first == "y" else [("x", 1), ("y", 0)]
        self.start()

    def start(self):
        unit, size = extents()[self.steps[0][0]]
        self.got = [swap(self.full, k * unit) for k in range(1, size)]

    def finish(self, *others):
        group, axis = self.steps.pop(0)
        pieces = [self.full] + list(after(self.got, *others))
        self.full = jnp.stack(in_order(pieces, place_on(group)), axis)
        if self.steps:
            self.start()
        else:
            self.other = swap(self.full, extents()["core"][0])

    def sides(self, kept):
        shape = (self.full.shape[0], -1, *self.full.shape[5 - kept :])
        return self.full.reshape(shape), self.other.reshape(shape)


def cut(total, group, axis):
    size = extents()[group][1]
    place = place_on(group)
    keep = lax.dynamic_index_in_dim(total, place, axis, False)
    parts = [lax.dynamic_index_in_dim(total, place ^ k, axis, False) for k in range(1, size)]
    return keep, [p.astype(bf16) for p in parts]


def crossed(parts, group):
    unit = extents()[group][0]
    return [swap(part, (k + 1) * unit) for k, part in enumerate(parts)]


def joined(keep, received):
    total = keep.astype(f32)
    for part in received:
        total = total + part.astype(f32)
    return total


class Reduction:
    def __init__(self, total, rows, first):
        table = extents()
        self.total = total.reshape(
            table["y"][1], table["z"][1], table["x"][1], rows, total.shape[-1]
        )
        order = [("x", 2), ("y", 0)] if first == "x" else [("y", 0), ("x", 1)]
        self.stages = order + [("z", 0)]

    def send(self):
        (group, axis), self.stages = self.stages[0], self.stages[1:]
        self.keep, self.parts = cut(self.total, group, axis)
        self.received = crossed(self.parts, group)
        return self.parts

    def receive(self, *others):
        self.received = after(self.received, *others)
        self.total = joined(self.keep, self.received)
        return self.total


def after(value, *others):
    return lax.optimization_barrier((value, others))[0]


def gather_small(vector):
    full = collect(collect(collect(vector, "z", 0), "x", 1), "core", 0)
    return collect(full, "y", 0).reshape(-1, vector.shape[-1])


def dealt(array, axes):
    return lax.all_to_all(array, axes, 0, 0, tiled=True)


def shared(array, axes):
    return dealt(jnp.broadcast_to(array[None], (lax.axis_size(axes), *array.shape)), axes)


def shifted(array, by):
    count = lax.axis_size(SEQ)
    pairs = [(i, i + by) for i in range(count) if 0 <= i + by < count]
    return lax.ppermute(array, SEQ, pairs)


def link(earlier, later):
    carry = later[1]
    wide = jnp.repeat(carry[0, :SSM_HEADS], SSM_DIM)[:, None]
    return (later[0] + wide * earlier[0], carry * earlier[1])


class Carrying:
    def __init__(self, state, carry, back, sign):
        self.pair, self.back, self.sign, self.by = (state, carry), back, sign, 0

    def send(self):
        packed = jnp.concatenate(
            [self.pair[0], jnp.pad(self.pair[1], ((0, RIM - 1), (0, 0)))], 0
        ).astype(bf16)
        steps = [self.by] if self.by else [1] + [2] * (self.back > 1)
        self.got = [shifted(packed, self.sign * by) for by in steps]
        return packed

    def receive(self, *others):
        pairs = []
        for got in after(self.got, *others):
            got = got.astype(f32)
            pairs.append((got[:DS], got[DS : DS + 1]))
        self.by = 2 * self.by if self.by else min(self.back, 2)
        if len(pairs) == 2:
            self.pair = link(pairs[1], pairs[0])
        else:
            self.pair = link(pairs[0], self.pair) if self.by > 2 else pairs[0]
        return self.pair[0] if self.by >= self.back else None


def halves(block, core):
    width = block.shape[1] // 2
    low, high = block[:, :width], block[:, width:]
    return jnp.where(core == 0, low, high), jnp.where(core == 0, high, low)


def put(ref, y, own, other, core):
    width = own.shape[1]
    base = y * 2 * width
    ref[:, base : base + width] = jnp.where(core == 0, own, other).astype(ref.dtype)
    ref[:, base + width : base + 2 * width] = jnp.where(core == 0, other, own).astype(ref.dtype)


def sides(ref, core, count):
    width = ref.shape[-1] // count
    return [halves(ref[:, y * width : (y + 1) * width], core) for y in range(count)]


def cross_half(value):
    lane = iota(value.shape, 1) % HEAD_DIM
    up = pltpu.roll(value, LANES - HEAD_DIM // 2, 1)
    down = pltpu.roll(value, HEAD_DIM // 2, 1)
    return jnp.where(lane < HEAD_DIM // 2, up, down)


def turned(value, cos, sin):
    return value * cos + cross_half(value) * sin


def turned_back(value, cos, sin):
    return value * cos - cross_half(value) * sin


def split_heads(pair, which, lane):
    flipped = pltpu.roll(pair, HEAD_DIM, 1)
    if which == 0:
        return jnp.where(lane < HEAD_DIM, pair, 0.0), jnp.where(lane < HEAD_DIM, flipped, 0.0)
    return jnp.where(lane >= HEAD_DIM, flipped, 0.0), jnp.where(lane >= HEAD_DIM, pair, 0.0)


def join_heads(even, odd, which, lane):
    if which == 0:
        return jnp.where(lane < HEAD_DIM, even, pltpu.roll(odd, HEAD_DIM, 1))
    return jnp.where(lane < HEAD_DIM, pltpu.roll(even, HEAD_DIM, 1), odd)


def conv_taps(chan_ref, cols, off):
    ext = chan_ref[:, cols].astype(f32)
    taps = []
    for i in range(CONV):
        back = CONV - 1 - i
        rows = pltpu.roll(ext, back, 0)[RIM:] if back else ext[RIM:]
        taps.append(rows * (off >= back).astype(f32))
    return taps


def sigmoid(v):
    return 1.0 / (1.0 + jnp.exp(-v))


def softplus(v):
    return jnp.maximum(v, 0.0) + jnp.log1p(jnp.exp(-jnp.abs(v)))


def tail_of(cum, off):
    rows = cum.shape[0]
    last_off = off[rows - 1 :, :]
    keep = iota((rows, 1), 0) >= rows - 1 - last_off
    return jnp.exp(cum[rows - 1 :, :] - cum) * keep.astype(f32)


def fade_of(cum, off):
    keep = off > iota((cum.shape[0], 1), 0)
    return jnp.exp(cum) * keep.astype(f32)


def carry_of(cum, off):
    rows = cum.shape[0]
    return jnp.exp(cum[rows - 1 :, :]) * (off[rows - 1 :, :] >= rows).astype(f32)


def pack_kernel(
    gu_ref, inner_ref, ao_ref, so_ref, kv_ref, q_ref, post_ref, front_ref
):
    part, width = gu_ref.shape[0], post_ref.shape[1]
    a_rows = ao_ref.shape[0]
    post_ref[:part, :] = inner_ref[:, :width]
    post_ref[part : 2 * part, : DS - width] = inner_ref[:, width:DS]
    for k in range(2):
        rows = slice(part + k * a_rows, part + (k + 1) * a_rows)
        post_ref[rows, DS - width :] = ao_ref[:, k * 512 : (k + 1) * 512]
    at = 2 * part
    post_ref[at : at + so_ref.shape[0], :] = so_ref[...]
    at += so_ref.shape[0]
    for k in range(gu_ref.shape[1] // width):
        post_ref[at : at + part, :] = gu_ref[:, k * width : (k + 1) * width]
        at += part
    front_ref[:, :256] = kv_ref[...]
    front_ref[:, 256:768] = q_ref[...]
    front_ref[:, 768:1024] = inner_ref[:, 2 * DS : DS + CONV_CH]
    front_ref[:, 1024:A_COLS] = jnp.zeros((part, LANES), bf16)
    front_ref[:, 1024 : 1024 + SSM_HEADS] = inner_ref[:, DS + CONV_CH :]
    front_ref[:, A_COLS:] = inner_ref[:, DS : 2 * DS]


def front_kernel(
    core_ref, tok_ref, gain_ref, wa_own, wa_oth, wb_own, wb_oth, cos_ref, sin_ref, off_ref,
    cw_ref, cb_ref, sb_ref, dec_ref,
    q8_ref, kv_ref, normed_ref, nrim_ref, chan_ref, x_ref, bc_ref, step_ref, cum_ref, cumt_ref, z_ref,
    state_ref, carry_ref,
    n_ref, xt_ref,
):
    core = core_ref[0]
    rows = cos_ref.shape[0]
    tok = tok_ref[...].astype(f32)
    rms = lax.rsqrt(jnp.mean(tok * tok, axis=1, keepdims=True) + EPS)
    n_ref[...] = (tok * rms * gain_ref[...]).astype(bf16)
    normed_ref[...] = n_ref[RIM:, :]
    nrim_ref[...] = n_ref[:RIM, :]
    count = wa_own.shape[0]
    blocks = sides(n_ref, core, count)

    def project(own_ref, oth_ref, cols):
        total = 0.0
        for y, (own, oth) in enumerate(blocks):
            total = total + nn(own, own_ref[y, :, cols]) + nn(oth, oth_ref[y, :, cols])
        return total

    lane = iota((rows, LANES), 1)
    cos, sin, off = cos_ref[...], sin_ref[...], off_ref[...]
    kv = project(wa_own, wa_oth, pl.ds(0, 256))[RIM:]
    kv_ref[:, :LANES] = turned(kv[:, :LANES], cos, sin).astype(bf16)
    kv_ref[:, LANES:] = kv[:, LANES:].astype(bf16)
    queries = project(wa_own, wa_oth, pl.ds(256, 512))[RIM:]
    for j in range(HEADS // 2):
        pair = turned(queries[:, j * LANES : (j + 1) * LANES], cos, sin)
        even, odd = split_heads(pair, j // 2, lane)
        q8_ref[2 * j] = even.astype(bf16)
        q8_ref[2 * j + 1] = odd.astype(bf16)
    rest = project(wa_own, wa_oth, pl.ds(768, 384))
    chan_ref[:, DS:] = rest[:, : 2 * STATE].astype(bf16)
    z = rest[RIM:, 2 * STATE :].astype(bf16).astype(f32) + sb_ref[...]
    for j in range(DS // 512):
        cols = slice(j * 512, (j + 1) * 512)
        chan_ref[:, cols] = project(wb_own, wb_oth, pl.ds(j * 512, 512)).astype(bf16)
    z_ref[...] = z
    step = softplus(z)
    step_ref[...] = step
    tri = (iota((rows, rows), 0) >= iota((rows, rows), 1)).astype(f32).astype(bf16)
    cum = nn_right(tri, -step * dec_ref[...], 3)
    cum_ref[...] = cum
    cumt_ref[...] = cum.T
    carry_ref[...] = carry_of(cum, off)
    weight = nn_left(step * tail_of(cum, off), head_spread(), 2)
    for j in range(CONV_CH // 256):
        cols = slice(j * 256, (j + 1) * 256)
        mixed = cb_ref[:, cols]
        for i, tap in enumerate(conv_taps(chan_ref, cols, off)):
            mixed = mixed + tap * cw_ref[i : i + 1, cols]
        active = mixed * sigmoid(mixed)
        if j < DS // 256:
            x_ref[:, cols] = active
            xt_ref[:, cols] = (active * weight[:, cols]).astype(bf16)
        else:
            bc_ref[...] = active
    state_ref[...] = tn(xt_ref[...], bc_ref[:, :STATE].astype(bf16))


def scan_masks(off, rows):
    t, s = iota((rows, rows), 0), iota((rows, rows), 1)
    return (s <= t) & (s >= t - off)


def scan_kernel(x_ref, bc_ref, step_ref, cum_ref, cumt_ref, off_ref, y_ref, xw_ref, ce_ref):
    rows = x_ref.shape[0]
    spread = head_spread()
    xw_ref[...] = (x_ref[...] * nn_left(step_ref[...], spread, 2)).astype(bf16)
    ce_ref[...] = nn_left(cum_ref[...], spread, 3)
    keys, reads = bc_ref[:, :STATE].astype(bf16), bc_ref[:, STATE:].astype(bf16)
    scores = jnp.where(scan_masks(off_ref[...], rows), nt(reads, keys), 0.0)
    lane = iota((rows, LANES), 1)

    def pair(j, unused):
        cols = pl.ds(pl.multiple_of(j * LANES, LANES), LANES)
        wide = ce_ref[:, cols]
        xw = xw_ref[:, cols]
        outs = []
        for k in range(2):
            late = wide[:, k * SSM_DIM : k * SSM_DIM + 1]
            early = cumt_ref[pl.ds(2 * j + k, 1), :]
            decay = jnp.exp(jnp.minimum(late - early, 0.0))
            outs.append(nn((decay * scores).astype(bf16), xw))
        y_ref[:, cols] = jnp.where(lane < SSM_DIM, outs[0], outs[1])
        return unused

    lax.fori_loop(0, SSM_HEADS // 2, pair, 0)


def attend_bias(off, rows, window):
    query = iota((rows, window), 0) + (window - rows)
    key = iota((rows, window), 1)
    return jnp.where((key <= query) & (key >= query - off), 0.0, NEG)


def window_of(count, rank, kv_ref, k_ref, v_ref):
    rows = kv_ref.shape[1]
    for i in range(count):
        piece = jnp.maximum(rank - (count - 1 - i), 0)
        k_ref[i * rows : (i + 1) * rows, :] = kv_ref[piece, :, :LANES]
        v_ref[i * rows : (i + 1) * rows, :] = kv_ref[piece, :, LANES:]


def attend_kernel(
    count, rank_ref, q8_ref, kv_ref, off_ref, att_ref, lse_ref, k_ref, v_ref, bias_ref, o_ref
):
    rows = off_ref.shape[0]
    window = count * rows
    window_of(count, rank_ref[0], kv_ref, k_ref, v_ref)
    bias_ref[...] = attend_bias(off_ref[...], rows, window)
    lane = iota((rows, LANES), 1)

    def head(h, lses):
        scores = nt(q8_ref[h], k_ref[...]) * HEAD_DIM**-0.5 + bias_ref[...]
        top = jnp.max(scores, axis=1, keepdims=True)
        probs = jnp.exp(scores - top)
        total = jnp.sum(probs, axis=1, keepdims=True)
        o_ref[h] = nn((probs * (1.0 / total)).astype(bf16), v_ref[...])
        return jnp.where(lane == h, top + jnp.log(total), lses)

    lse_ref[...] = lax.fori_loop(0, HEADS, head, jnp.zeros((rows, LANES), f32)).T
    for j in range(HEADS // 2):
        pair = join_heads(o_ref[2 * j], o_ref[2 * j + 1], j // 2, lane)
        att_ref[:, j * LANES : (j + 1) * LANES] = pair.astype(bf16)


def attend_back_kernel(
    count, rank_ref, q8_ref, kv_ref, off_ref, lse_ref, datt_ref, cos_ref, sin_ref,
    dq_ref, out_ref, k_ref, v_ref, bias_ref, do_ref, dq8_ref, dkv_ref,
):
    rows = off_ref.shape[1]
    window = count * rows
    rank = rank_ref[0]
    window_of(count, rank, kv_ref, k_ref, v_ref)
    query = iota((window, rows), 1) + (window - rows)
    key = iota((window, rows), 0)
    bias_ref[...] = jnp.where((key <= query) & (key >= query - off_ref[...]), 0.0, NEG)
    lane = iota((rows, LANES), 1)
    for j in range(HEADS // 2):
        pair = datt_ref[:, j * LANES : (j + 1) * LANES].astype(f32)
        even, odd = split_heads(pair, j // 2, lane)
        do_ref[2 * j] = even.astype(bf16)
        do_ref[2 * j + 1] = odd.astype(bf16)
    dkv_ref[...] = jnp.zeros(dkv_ref.shape, f32)

    def head(h, unused):
        query, grad = q8_ref[h], do_ref[h]
        scores = nt(k_ref[...], query) * HEAD_DIM**-0.5 + bias_ref[...]
        probs = jnp.exp(scores - lse_ref[pl.ds(h, 1), :])
        dprobs = nt(v_ref[...], grad)
        mean = jnp.sum(probs * dprobs, axis=0, keepdims=True)
        draw = (probs * (dprobs - mean) * HEAD_DIM**-0.5).astype(bf16)
        dkv_ref[:, :LANES] += nn(draw, query)
        dkv_ref[:, LANES:] += nn(probs.astype(bf16), grad)
        dq8_ref[h] = tn(draw, k_ref[...])
        return unused

    lax.fori_loop(0, HEADS, head, 0)
    out_ref[...] = jnp.zeros(out_ref.shape, bf16)
    for i in range(count):
        piece = rank - (count - 1 - i)

        @pl.when(piece >= 0)
        def unused():
            out_ref[piece] = dkv_ref[i * rows : (i + 1) * rows, :].astype(bf16)

    for j in range(HEADS // 2):
        pair = join_heads(dq8_ref[2 * j], dq8_ref[2 * j + 1], j // 2, lane)
        back = turned_back(pair, cos_ref[...], sin_ref[...])
        dq_ref[:, j * LANES : (j + 1) * LANES] = back.astype(bf16)


class PackedWeights:
    def __init__(self, most, downs, core, held, sems, parts):
        self.held = held
        part, a_part, s_part, f_part = self.parts = parts
        self.so_at = 2 * part
        self.gu_at = self.so_at + s_part
        self.down_at = self.gu_at + 4 * part
        places = [
            (0, self.so_at), (self.so_at, s_part), (self.gu_at, 4 * part), (self.down_at, f_part),
        ]
        self.copies = []
        for k, (at, size) in enumerate(places):
            pair = []
            for i in range(2):
                rows = pl.ds(at, size)
                source = most.at[:, lax.rem(core + i, 2), :, rows] if k < 3 else downs[i]
                target = held.at[i, :, :, rows]
                pair.append(pltpu.make_async_copy(source, target, sems.at[k, i]))
            self.copies.append(pair)
        for pair in self.copies:
            for copy in pair:
                copy.start()

    def wait(self, k):
        for copy in self.copies[k]:
            copy.wait()

    def block(self, i, y, start, size, col):
        rows, cols = pl.ds(pl.multiple_of(start, 16), size), pl.ds(pl.multiple_of(col, 512), 512)
        got = self.held[i, y, :, rows, cols]
        return got.reshape(got.shape[0] * size, 512)

    def gate(self, i, y, j):
        part = self.parts[0]
        return self.block(i, y, j // 2 * part, part, j % 2 * 512)

    def ao(self, i, y, j):
        part, a_part = self.parts[:2]
        return self.block(i, y, part + j * a_part, a_part, 512)

    def so(self, i, y, j):
        return self.block(i, y, self.so_at, self.parts[2], j * 512)

    def down(self, i, y, j):
        return self.block(i, y, self.down_at, self.parts[3], j * 512)

    def gu(self, i, y, j):
        part = self.parts[0]
        return self.block(i, y, self.gu_at + j // 2 * part, part, j % 2 * 512)


class PlainWeights:
    def __init__(self, refs):
        self.refs = refs

    def wait(self, k):
        pass

    def block(self, name, i, y, j):
        return self.refs[2 * name + i][y, :, pl.ds(pl.multiple_of(j * 512, 512), 512)]

    def gate(self, i, y, j):
        return self.block(0, i, y, j)

    def ao(self, i, y, j):
        return self.block(1, i, y, j)

    def so(self, i, y, j):
        return self.block(2, i, y, j)

    def down(self, i, y, j):
        return self.block(3, i, y, j)

    def gu(self, i, y, j):
        return self.refs[8 + i][y, :, pl.ds(pl.multiple_of(j * 512, 512), 512)]


def post_kernel(
    parts, ys, core_ref, tok_ref, cot_ref, att_ref, yl_ref, x_ref, bc_ref, cum_ref, off_ref,
    entry_ref, skip_ref, normed_ref, gssm_ref, gffn_ref, *refs,
):
    if parts:
        weights = PackedWeights(refs[0], refs[1:3], core_ref[0], refs[-2], refs[-1], parts)
        refs = refs[3:-2]
    else:
        weights, refs = PlainWeights(refs[:10]), refs[10:]
    pairs = [(i, y) for y in range(ys) for i in range(2)]

    def through(blocks, weight, j):
        return sum(nn(blocks[y][i], weight(i, y, j)) for i, y in pairs)

    def back_through(ref, grad, weight, count):
        for y in range(ys):
            both = []
            for i in range(2):
                both.append(
                    sum(nt(grad[:, j * 512 : j * 512 + 512], weight(i, y, j)) for j in range(count))
                )
            put(ref, y, both[0], both[1], core)

    (
        out_ref, dmid_ref, datt_ref, dssd_ref, ycore_ref, dentry_ref, send_ref, keep_ref, dng_ref,
        gi_ref, gd_ref, mid_ref, gu_ref, dn_ref, dmx_ref, fd_ref, n2_ref, hid_ref, mixed_ref, dh_ref, fade_ref, ent_ref,
    ) = refs
    core = core_ref[0]
    rows, width = tok_ref.shape
    heads_width = att_ref.shape[1]
    ff = hid_ref.shape[1]
    half = keep_ref.shape[1]
    cot_at, dbr_at, dgate_at, sel_at = 2 * ff, 2 * ff + width, 2 * ff + 2 * width, 2 * ff + 2 * width + DS
    reads = bc_ref[:, STATE:].astype(bf16)
    spread = head_spread()
    fade_ref[...] = nn_left(fade_of(cum_ref[...], off_ref[...]), spread, 2)
    ent_ref[...] = nt(reads, entry_ref[...].astype(bf16))
    none = jnp.zeros((rows, 1), f32)

    def at(j, first=0):
        return pl.ds(pl.multiple_of(first + j * 512, 512), 512)

    weights.wait(0)
    blocks = sides(normed_ref, core, ys)

    def gates(j, square):
        cols = at(j)
        gate = through(blocks, weights.gate, j).astype(bf16).astype(f32)
        gi_ref[:, cols] = gate
        ycore = yl_ref[:, cols] + fade_ref[:, cols] * ent_ref[:, cols]
        ycore_ref[:, cols] = ycore
        ssd = ycore + skip_ref[:, cols] * x_ref[:, cols]
        gated = ssd * gate * sigmoid(gate)
        gd_ref[:, cols] = gated
        return square + jnp.sum(gated * gated, axis=1, keepdims=True)

    square = lax.fori_loop(0, DS // 512, gates, none, unroll=True)
    rms_gate = lax.rsqrt(square / DS + EPS)
    mixed_ref[...] = (gd_ref[...] * rms_gate * gssm_ref[...]).astype(bf16)
    weights.wait(1)
    att_blocks, mix_blocks = sides(att_ref, core, ys), sides(mixed_ref, core, ys)

    def branches(j, square):
        branch = through(att_blocks, weights.ao, j) + through(mix_blocks, weights.so, j)
        middle = tok_ref[:, at(j)].astype(f32) + branch
        mid_ref[:, at(j)] = middle
        return square + jnp.sum(middle * middle, axis=1, keepdims=True)

    square = lax.fori_loop(0, width // 512, branches, none, unroll=True)
    rms = lax.rsqrt(square / width + EPS)
    n2_ref[...] = (mid_ref[...] * rms * gffn_ref[...]).astype(bf16)
    weights.wait(2)
    ups = sides(n2_ref, core, ys)

    def up(j, unused):
        gu_ref[:, at(j)] = through(ups, weights.gu, j)
        return unused

    lax.fori_loop(0, 2 * ff // 512, up, 0, unroll=True)

    def hide(j, unused):
        gate = gu_ref[:, at(j)]
        hid_ref[:, at(j)] = (gate * sigmoid(gate) * gu_ref[:, at(j, ff)]).astype(bf16)
        return unused

    lax.fori_loop(0, ff // 512, hide, 0)
    weights.wait(3)
    hids = sides(hid_ref, core, ys)

    def finals(j, unused):
        out_ref[:, at(j)] = (mid_ref[:, at(j)] + through(hids, weights.down, j)).astype(bf16)
        return unused

    lax.fori_loop(0, width // 512, finals, 0, unroll=True)
    cot = cot_ref[...]
    back_through(dh_ref, cot, weights.down, 2)

    def unhide(j, unused):
        gate, lift, dhid = gu_ref[:, at(j)], gu_ref[:, at(j, ff)], dh_ref[:, at(j)]
        sg = sigmoid(gate)
        dgate = dhid * lift * (sg * (1.0 + gate * (1.0 - sg)))
        send_ref[:, at(j)] = dgate.astype(bf16)
        send_ref[:, at(j, ff)] = (dhid * gate * sg).astype(bf16)
        return unused

    lax.fori_loop(0, ff // 512, unhide, 0)
    send_ref[:, cot_at:dbr_at] = cot
    wide = width // ys // 2

    def down(j, totals):
        grad = send_ref[:, pl.ds(pl.multiple_of(j * 512, 512), 512)]
        return [t + nt(grad, weights.gu(i, y, j)) for t, (i, y) in zip(totals, pairs)]

    zero = [jnp.zeros((rows, wide), f32)] * len(pairs)
    totals = lax.fori_loop(0, 2 * ff // 512, down, zero, unroll=True)
    for y in range(ys):
        put(dn_ref, y, totals[2 * y], totals[2 * y + 1], core)
    unit = mid_ref[...] * rms
    dn = dn_ref[...]
    dn = dn * gffn_ref[...]
    dmid = cot.astype(f32) + rms * (dn - unit * jnp.mean(dn * unit, axis=1, keepdims=True))
    dmid_ref[...] = dmid
    dbr = dmid.astype(bf16)
    send_ref[:, dbr_at:dgate_at] = dbr
    back_through(datt_ref, dbr, weights.ao, 2)
    back_through(dmx_ref, dbr, weights.so, 2)

    def means(j, mean):
        unit = gd_ref[:, at(j)] * rms_gate
        return mean + jnp.sum(dmx_ref[:, at(j)] * gssm_ref[:, at(j)] * unit, axis=1, keepdims=True)

    mean = lax.fori_loop(0, DS // 512, means, none) / DS

    def ungate(j, unused):
        cols = at(j)
        unit = gd_ref[:, cols] * rms_gate
        dgated = rms_gate * (dmx_ref[:, cols] * gssm_ref[:, cols] - unit * mean)
        gate = gi_ref[:, cols]
        sg = sigmoid(gate)
        ssd = ycore_ref[:, cols] + skip_ref[:, cols] * x_ref[:, cols]
        dssd = dgated * gate * sg
        dssd_ref[:, cols] = dssd
        dgate = (dgated * ssd * (sg * (1.0 + gate * (1.0 - sg)))).astype(bf16)
        send_ref[:, at(j, dgate_at)] = dgate
        fd_ref[:, cols] = (dssd * fade_ref[:, cols]).astype(bf16)
        return unused

    lax.fori_loop(0, DS // 512, ungate, 0)
    back_through(dng_ref, send_ref[:, dgate_at:sel_at], weights.gate, 3)
    dentry_ref[...] = tn(fd_ref[...], reads)
    to = 0
    for ref in (n2_ref, hid_ref, att_ref, mixed_ref, normed_ref):
        count = ys
        wide = ref.shape[1] // count
        for y in range(count):
            own, oth = halves(ref[:, y * wide : (y + 1) * wide], core)
            keep_ref[:, to : to + wide // 2] = own
            send_ref[:, sel_at + to : sel_at + to + wide // 2] = oth
            to += wide // 2


def products_kernel(plan, extra, keep_ref, own_ref, act_ref, *refs):
    got_ref, outs = act_ref, refs
    if extra:
        (extra_ref, *outs) = refs
    for which, a_at, act_at, size, g_at in plan:
        out = outs[which]
        for y in range(out.shape[0]):
            left = keep_ref[:, a_at + y * size : a_at + (y + 1) * size]
            right = act_ref[: left.shape[0], act_at + y * size : act_at + (y + 1) * size]
            for j in range(0, out.shape[-1], 512):
                stop = min(j + 512, out.shape[-1])
                total = tn(left, own_ref[: left.shape[0], g_at + j : g_at + stop])
                total = total + tn(right, got_ref[: left.shape[0], g_at + j : g_at + stop])
                if extra and which == 0 and stop == out.shape[-1]:
                    total = total + extra_ref[y]
                out[y, :, j:stop] = total.astype(bf16)


def split_products_kernel(plan, extra, y_ref, x_ref, keep_ref, own_ref, act_ref, *refs):
    got_ref, outs = act_ref, refs
    if extra:
        (extra_ref, *outs) = refs
    xkeep_ref, xsend_ref, ykeep_ref, ysend_ref = outs
    rows = keep_ref.shape[0]
    my_y, my_x = y_ref[0], x_ref[0]
    for kind, place, a_at, act_at, size, g_at, wide in plan:
        for k in range(2):
            y = k if kind == "x" else lax.rem(my_y + k, 2)
            left = keep_ref[:, pl.ds(pl.multiple_of(a_at + y * size, LANES), size)]
            right = act_ref[:rows, pl.ds(pl.multiple_of(act_at + y * size, LANES), size)]
            keep, send = (xkeep_ref, xsend_ref) if kind == "x" else (ykeep_ref, ysend_ref)
            block = 512 if wide % 512 == 0 else 384

            def columns(j, unused):
                at = pl.ds(pl.multiple_of(g_at + j * block, LANES), block)
                total = tn(left, own_ref[:rows, at]) + tn(right, got_ref[:rows, at])
                if kind == "x":
                    zs, each = keep.shape[1], keep.shape[2]
                    if extra:
                        total = total + extra_ref[k] * (j == wide // block - 1).astype(f32)
                    cols = pl.ds(pl.multiple_of(place + j * block, LANES), block)
                    total = total.reshape(zs, 2, each, block)
                    low, high = total[:, 0], total[:, 1]
                    keep[k, :, :, cols] = jnp.where(my_x == 0, low, high).astype(bf16)
                    send[k, :, :, cols] = jnp.where(my_x == 0, high, low).astype(bf16)
                else:
                    count = keep.shape[0]
                    each = size // count
                    cols = pl.ds(pl.multiple_of(j * block, LANES), block)
                    total = total.reshape(count, each, block).astype(bf16)
                    (send if k else keep)[:, place : place + each, cols] = total
                return unused

            lax.fori_loop(0, wide // block, columns, 0, unroll=True)


def fold_one_kernel(
    y_ref, x_ref, xkeep_ref, xgot_ref, ykeep_ref, ygot_ref,
    xkeep_out, xsend_out, ykeep_out, ysend_out,
):
    my_y, my_x = y_ref[0], x_ref[0]
    xkeep_out[...] = xkeep_ref[my_y].astype(f32) + xgot_ref[my_y].astype(f32)
    other = 1 - my_y
    xsend_out[...] = (xkeep_ref[other].astype(f32) + xgot_ref[other].astype(f32)).astype(bf16)
    for z in range(ykeep_out.shape[0]):
        at = 2 * z + my_x
        ykeep_out[z] = ykeep_ref[at].astype(f32) + ygot_ref[at].astype(f32)
        at = 2 * z + 1 - my_x
        ysend_out[z] = (ykeep_ref[at].astype(f32) + ygot_ref[at].astype(f32)).astype(bf16)


def laid(refs, width):
    at = 0
    for ref in refs:
        each = ref.shape[-2]
        for j in range(ref.shape[-1] // width):
            yield ref, at, j * width
            at += each


def fold_two_kernel(z_ref, xkeep_ref, xgot_ref, ykeep_ref, ygot_ref, keep_out, send_out):
    low = lax.rem(z_ref[0], 2)
    width = keep_out.shape[2]
    keeps = laid((xkeep_ref, ykeep_ref), width)
    gots = laid((xgot_ref, ygot_ref), width)
    for (keep, at, col), (got, *unused) in zip(keeps, gots):
        rows, cols = slice(at, at + keep.shape[-2]), slice(col, col + width)
        for high in range(keep_out.shape[0]):
            for out, z in ((keep_out, 2 * high + low), (send_out, 2 * high + 1 - low)):
                value = keep[z, :, cols] + got[z, :, cols].astype(f32)
                out[high, rows, :] = value.astype(out.dtype)


def fold_three_kernel(z_ref, keep_ref, got_ref, keep_out, send_out):
    high = lax.div(z_ref[0], 2)
    keep_out[...] = keep_ref[high] + got_ref[high].astype(f32)
    other = 1 - high
    send_out[...] = (keep_ref[other] + got_ref[other].astype(f32)).astype(bf16)


def summed(refs, rows):
    keep_ref, got_ref = refs
    return keep_ref[rows, :] + got_ref[rows, :].astype(f32)


def fold_four_kernel(keep_ref, got_ref, *outs):
    for out, at, col in laid(outs, keep_ref.shape[1]):
        rows = slice(at, at + out.shape[0])
        out[:, col : col + keep_ref.shape[1]] = summed((keep_ref, got_ref), rows)


def row_sums(value):
    ones = jnp.ones((8, value.shape[1]), bf16)
    return sum(nt(ones, part) for part in terms(value, 3))[:1]


def finish_post_kernel(
    keep_ref, sum_ref, one_ref, guw_ref, sow_ref, gffn_ref, gssm_ref,
    gu_ref, gate_ref, ao_ref, so_ref, dffn_ref, dssm_ref,
):
    both = (keep_ref, sum_ref)
    part, ups = one_ref.shape
    wide = keep_ref.shape[1]
    gu_ref[:, :ups] = one_ref[...]
    at = 0
    for out, start in ((gu_ref, ups), (gate_ref, 0)):
        for col in range(start, out.shape[1], wide):
            out[:, col : col + wide] = summed(both, slice(at, at + part))
            at += part
    for col in range(0, ao_ref.shape[1], wide):
        for out in (ao_ref, so_ref):
            out[:, col : col + wide] = summed(both, slice(at, at + out.shape[0]))
            at += out.shape[0]
    dffn_ref[...] = row_sums(guw_ref[...].astype(f32) * gu_ref[...]) / gffn_ref[...]
    dssm_ref[...] = row_sums(sow_ref[...].astype(f32) * so_ref[...]) / gssm_ref[...]


def finish_front_kernel(
    keep_ref, sum_ref, gate_ref, kvw_ref, qw_ref, iw_ref, gain_ref,
    kv_ref, q_ref, inner_ref, conv_ref, bias_ref, log_ref, step_ref, skip_ref, dgain_ref,
):
    both = (keep_ref, sum_ref)
    part, wide = kv_ref.shape[0], keep_ref.shape[1]
    count = A_COLS // wide
    blocks = [summed(both, slice(k * part, (k + 1) * part)) for k in range(count)]
    first = jnp.concatenate(blocks, axis=1)
    kv_ref[...] = first[:, :256]
    q_ref[...] = first[:, 256:768]
    inner_ref[:, :DS] = gate_ref[...]
    for k in range(DS // wide):
        rows = slice((count + k) * part, (count + k + 1) * part)
        inner_ref[:, DS + k * wide : DS + (k + 1) * wide] = summed(both, rows)
    last = first[:, 1024:]
    inner_ref[:, 2 * DS : 2 * DS + 2 * STATE] = first[:, 768:1024]
    inner_ref[:, DS + CONV_CH :] = last[:, :SSM_HEADS]
    turned_last = last.T
    own = bias_ref.shape[1]
    conv_ref[...] = turned_last[SSM_HEADS : SSM_HEADS + own, :CONV]
    bias_ref[...] = last[CONV : CONV + 1, SSM_HEADS : SSM_HEADS + own]
    for k, out in enumerate((log_ref, step_ref, skip_ref)):
        out[...] = last[CONV + 1 + k : CONV + 2 + k, SSM_HEADS : 2 * SSM_HEADS]
    total = row_sums(kvw_ref[...].astype(f32) * kv_ref[...])
    total = total + row_sums(qw_ref[...].astype(f32) * q_ref[...])
    total = total + row_sums(iw_ref[...].astype(f32) * inner_ref[...])
    dgain_ref[...] = total / gain_ref[...]


class PairReduction:
    def __init__(self, pieces, width):
        self.places = tuple(place_on(g).reshape(1).astype(jnp.int32) for g in ("y", "x", "z"))
        self.xkeep, xsend, self.ykeep, ysend = pieces
        self.width = width
        self.send(xsend, ysend, "x", "y")

    def send(self, xsend, ysend, first, second):
        self.sent = (xsend, ysend)
        self.gots = (
            swap(xsend, extents()[first][0]), swap(ysend, extents()[second][0])
        )

    def fold_one(self, *others):
        gots = after(self.gots, *others)
        x, y = self.xkeep.shape, self.ykeep.shape
        x, y = x[1:], (y[0] // 2, *y[1:])
        self.xkeep, xsend, self.ykeep, ysend = run(
            fold_one_kernel, "fold_one", [(x, f32), (x, bf16), (y, f32), (y, bf16)],
            (*self.places[:2], self.xkeep, gots[0], self.ykeep, gots[1]),
            scalars=2,
        )
        self.send(xsend, ysend, "y", "x")

    def fold_two(self, *others):
        gots = after(self.gots, *others)
        self.shapes = [self.xkeep.shape[1:], self.ykeep.shape[1:]]
        rows = sum(r * c // self.width for r, c in self.shapes)
        half = (self.xkeep.shape[0] // 2, rows, self.width)
        self.keep, self.sent = run(
            fold_two_kernel, "fold_two", [(half, f32), (half, bf16)],
            (self.places[2], self.xkeep, gots[0], self.ykeep, gots[1]),
            scalars=1,
        )
        self.gots = swap(self.sent, extents()["z"][0])

    def fold_three(self, *others):
        whole = self.keep.shape[1:]
        self.keep, self.sent = run(
            fold_three_kernel, "fold_three", [(whole, f32), (whole, bf16)],
            (self.places[2], self.keep, after(self.gots, *others)),
            scalars=1,
        )
        self.gots = swap(self.sent, 2 * extents()["z"][0])

    def fold_four(self, *others):
        return run(
            fold_four_kernel, "fold_four", [(shape, f32) for shape in self.shapes],
            (self.keep, after(self.gots, *others)),
        )


class PlainReduction:
    def __init__(self, pieces, rows):
        self.parts = [Reduction(pieces[0], rows[0], "x"), Reduction(pieces[1], rows[1], "y")]
        self.sent = [part.send() for part in self.parts]

    def fold_one(self, *others):
        for part in self.parts:
            part.receive(*others)
        self.sent = [part.send() for part in self.parts]

    fold_two = fold_one

    def fold_three(self, *others):
        pass

    def fold_four(self, *others):
        return [part.receive(*others) for part in self.parts]


def scan_back_kernel(
    dy_ref, x_ref, bc_ref, step_ref, cum_ref, cumt_ref, off_ref, dxw_ref, ds_ref,
    xw_ref, ce_ref, dyb_ref, dg_ref,
):
    rows = x_ref.shape[0]
    spread = head_spread()
    xw_ref[...] = (x_ref[...] * nn_left(step_ref[...], spread, 2)).astype(bf16)
    dyb_ref[...] = dy_ref[...].astype(bf16)
    ce_ref[...] = nn_left(cum_ref[...], spread, 3)
    keys, reads = bc_ref[:, :STATE].astype(bf16), bc_ref[:, STATE:].astype(bf16)
    early, late = iota((rows, rows), 0), iota((rows, rows), 1)
    keep = (early <= late) & (early >= late - off_ref[...])
    scores = jnp.where(keep, nt(keys, reads), 0.0)
    lane = iota((rows, LANES), 1)
    dg_ref[...] = jnp.zeros((rows, rows), f32)

    def pair(j, unused):
        cols = pl.ds(pl.multiple_of(j * LANES, LANES), LANES)
        wide = ce_ref[:, cols]
        xw, dy = xw_ref[:, cols], dyb_ref[:, cols]
        outs = []
        change = 0.0
        for k in range(2):
            first = wide[:, k * SSM_DIM : k * SSM_DIM + 1]
            second = cumt_ref[pl.ds(2 * j + k, 1), :]
            decay = jnp.exp(jnp.minimum(second - first, 0.0))
            outs.append(nn((decay * scores).astype(bf16), dy))
            mine = (lane < SSM_DIM) if k == 0 else (lane >= SSM_DIM)
            change = change + nt(xw * mine.astype(bf16), dy) * decay
        dg_ref[...] += change
        dxw_ref[:, cols] = jnp.where(lane < SSM_DIM, outs[0], outs[1])
        return unused

    lax.fori_loop(0, SSM_HEADS // 2, pair, 0)
    ds_ref[...] = jnp.where(keep, dg_ref[...], 0.0).astype(bf16)


def mixer_back_kernel(
    dy_ref, ycore_ref, x_ref, bc_ref, step_ref, cum_ref, z_ref, off_ref, entry_ref,
    down_ref, skip_ref, dec_ref, chan_ref, cw_ref, cb_ref, dxwl_ref, ds_ref,
    dext_ref, dz_ref, small_ref,
    dact_ref,
):
    rows = x_ref.shape[0]
    spread, gather = head_spread(), head_sum_matrix()
    off, cum = off_ref[...], cum_ref[...]
    step_wide = nn_left(step_ref[...], spread, 2)
    keys, reads = bc_ref[:, :STATE].astype(bf16), bc_ref[:, STATE:].astype(bf16)
    dscores = ds_ref[...]
    down = down_ref[...].astype(bf16)
    tail = nn_left(tail_of(cum, off), spread, 2)
    fade = nn_left(fade_of(cum, off), spread, 2)
    bd = nt(keys, down) * tail
    xw = (x_ref[...] * step_wide).astype(bf16).astype(f32)
    dxw = dxwl_ref[...] + bd
    dact_ref[:, DS : DS + STATE] = nn(dscores, reads) + nn((tail * xw).astype(bf16), down)
    dact_ref[:, DS + STATE :] = tn(dscores, keys) + nn(
        (fade * dy_ref[...]).astype(bf16), entry_ref[...].astype(bf16)
    )
    ones = jnp.ones((8, STATE), bf16)
    product = sum(nt(ones, part) for part in terms(down_ref[...] * entry_ref[...], 3))
    through = jnp.sum(xw * bd, axis=0, keepdims=True)
    direct = jnp.sum(dy_ref[...] * x_ref[...], axis=0, keepdims=True)
    row = iota((8, DS), 0)
    sums = jnp.where(row == 0, product, jnp.where(row == 1, through, direct))
    sums = nn_left(sums, gather, 3)
    through, kept = sums[1:2], sums[0:1] * carry_of(cum, off)
    last = (iota((rows, 1), 0) == rows - 1).astype(f32)
    dyb = dy_ref[...].astype(bf16).astype(f32)
    dcum = nn_left(dyb * ycore_ref[...] - xw * dxw, gather, 2) + last * (through + kept)
    tri = (iota((rows, rows), 0) <= iota((rows, rows), 1)).astype(f32).astype(bf16)
    dlog = nn_right(tri, dcum, 3)
    x = x_ref[...]
    step, dec = step_ref[...], dec_ref[...]
    dstep = nn_left(dxw * x, gather, 2) - dlog * dec
    dz = dstep * sigmoid(z_ref[...])
    dz_ref[...] = dz
    small_ref[...] = jnp.zeros(small_ref.shape, f32)
    small_ref[CONV + 1 : CONV + 2, :LANES] = jnp.sum(dlog * (-step * dec), axis=0, keepdims=True)
    small_ref[CONV + 1 : CONV + 2, LANES : 2 * LANES] = jnp.sum(dz, axis=0, keepdims=True)
    small_ref[CONV + 1 : CONV + 2, 2 * LANES : 3 * LANES] = sums[2:3]
    dact_ref[:, :DS] = dxw * step_wide + skip_ref[...] * dy_ref[...]
    for j in range(CONV_CH // 256):
        cols = slice(j * 256, (j + 1) * 256)
        taps = conv_taps(chan_ref, cols, off)
        mixed = cb_ref[:, cols]
        for i, tap in enumerate(taps):
            mixed = mixed + tap * cw_ref[i : i + 1, cols]
        sg = sigmoid(mixed)
        dmix = dact_ref[:, cols] * (sg * (1.0 + mixed * (1.0 - sg)))
        small_ref[CONV : CONV + 1, cols] = jnp.sum(dmix, axis=0, keepdims=True)
        total = 0.0
        for i, tap in enumerate(taps):
            back = CONV - 1 - i
            small_ref[i : i + 1, cols] = jnp.sum(dmix * tap, axis=0, keepdims=True)
            part = dmix * ((off >= back).astype(f32) * cw_ref[i : i + 1, cols])
            part = jnp.concatenate([jnp.zeros((RIM, 256), f32), part], axis=0)
            total = total + (pltpu.roll(part, rows + RIM - back, 0) if back else part)
        dext_ref[:, cols] = total


def back_grads_kernel(
    ys, core_ref, dq_ref, dkv_ref, dext_ref, dz_ref, cos_ref, sin_ref, normed_ref, nrim_ref,
    small_ref, ga_ref, keep_ref,
):
    core = core_ref[0]
    count, last = small_ref.shape[0], keep_ref.shape[0]
    ga_ref[last:, :] = jnp.zeros((ga_ref.shape[0] - last, ga_ref.shape[1]), bf16)
    ga_ref[last : last + count, :CONV_CH] = small_ref[...].astype(bf16)
    dkv = dkv_ref[0].astype(f32)
    for i in range(1, dkv_ref.shape[0]):
        dkv = dkv + dkv_ref[i].astype(f32)
    ga_ref[:RIM, :768] = jnp.zeros((RIM, 768), bf16)
    ga_ref[:RIM, 1024:A_COLS] = jnp.zeros((RIM, LANES), bf16)
    ga_ref[RIM:last, :LANES] = turned_back(dkv[:, :LANES], cos_ref[...], sin_ref[...]).astype(bf16)
    ga_ref[RIM:last, LANES:256] = dkv[:, LANES:].astype(bf16)
    ga_ref[RIM:last, 256:768] = dq_ref[...]
    ga_ref[:last, 768:1024] = dext_ref[:, DS:].astype(bf16)
    ga_ref[RIM:last, 1024:A_COLS] = dz_ref[...].astype(bf16)
    ga_ref[:last, A_COLS : A_COLS + DS] = dext_ref[:, :DS].astype(bf16)
    wide = normed_ref.shape[1] // ys
    at, to = 0, A_COLS + DS
    for y in range(ys):
        cols = slice(y * wide, (y + 1) * wide)
        for ref, rows in ((nrim_ref, slice(0, RIM)), (normed_ref, slice(RIM, last))):
            own, oth = halves(ref[:, cols], core)
            keep_ref[rows, at : at + wide // 2] = own
            ga_ref[rows, to + at : to + at + wide // 2] = oth
        at += wide // 2


def back_kernel(
    core_ref, gab_ref, wa_own, wa_oth, wb_own, wb_oth, tok_ref, dmid_ref, dng_ref, gain_ref,
    dtok_ref, drim_ref, dn_ref,
):
    core = core_ref[0]
    for y in range(wa_own.shape[0]):
        last = tok_ref.shape[0]
        ga, gb = gab_ref[:last, :A_COLS], gab_ref[:last, A_COLS : A_COLS + DS]
        own = nt(ga, wa_own[y]) + nt(gb, wb_own[y])
        oth = nt(ga, wa_oth[y]) + nt(gb, wb_oth[y])
        put(dn_ref, y, own, oth, core)

    def through_norm(dn, tok):
        tok = tok.astype(f32)
        rms = lax.rsqrt(jnp.mean(tok * tok, axis=1, keepdims=True) + EPS)
        unit = tok * rms
        dn = dn * gain_ref[...]
        return rms * (dn - unit * jnp.mean(dn * unit, axis=1, keepdims=True))

    drim_ref[...] = through_norm(dn_ref[:RIM, :], tok_ref[:RIM, :])
    dtok_ref[...] = dmid_ref[...] + through_norm(dn_ref[RIM:, :] + dng_ref[...], tok_ref[RIM:, :])


def gain_kernel(pairs, count, *refs):
    gains, refs = refs[:count], refs[count:]
    outs = refs[-count:]
    for k, out in enumerate(outs):
        total = 0.0
        for group, w, g in pairs:
            if group == k:
                total = total + jnp.sum(
                    refs[w][...].astype(f32) * refs[g][...], axis=1, keepdims=True
                )
        out[...] = total / gains[k][...].astype(f32)


def run(kernel, name, outs, args, scalars=0, scratch=(), us=3, left=0, sems=()):
    moved = sum(a.size * a.dtype.itemsize for a in args)
    shapes = [jax.ShapeDtypeStruct(shape, kind) for shape, kind in outs]
    moved += sum(s.size * s.dtype.itemsize for s in shapes)
    specs = [pl.BlockSpec(memory_space=pltpu.SMEM)] * scalars
    specs += [pl.BlockSpec(memory_space=pltpu.VMEM)] * (len(args) - scalars - left)
    specs += [pl.BlockSpec(memory_space=pl.ANY)] * left
    return pl.pallas_call(
        kernel,
        name=name,
        out_shape=shapes,
        in_specs=specs,
        out_specs=[pl.BlockSpec(memory_space=pltpu.VMEM)] * len(shapes),
        scratch_shapes=[pltpu.VMEM(shape, kind) for shape, kind in scratch]
        + [pltpu.SemaphoreType.DMA(shape) for shape in sems],
        compiler_params=pltpu.CompilerParams(vmem_limit_bytes=62 * 2**20),
        cost_estimate=pl.CostEstimate(
            flops=us * SCALE, bytes_accessed=moved, transcendentals=0
        ),
    )(*args)


def padded(vector, width):
    return jnp.pad(vector.astype(f32), (0, width - vector.shape[0]))[None, :]


def local(
    tokens, lengths, cotangent, mixer_gain, query_weight, keyval_weight, inner_weight, conv_weight,
    conv_bias, ssm_gain, attn_out_weight, ssm_out_weight, ffn_gain, gate_up_weight, down_weight,
    decay_log, step_bias, skip_gain,
):
    rows, width = tokens.shape
    seq_count, seq_rank = lax.axis_size(SEQ), lax.axis_index(SEQ)
    side = place_on("core").reshape(1)
    back = (rows * seq_count // 2) // rows
    part = query_weight.shape[0]
    heads_width, ff = HEADS * HEAD_DIM, gate_up_weight.shape[1] // 2
    a_rows, s_rows, f_rows = attn_out_weight.shape[0], ssm_out_weight.shape[0], down_weight.shape[0]
    ys = lax.axis_size("y")

    rim = shifted(tokens[rows - RIM :], 1)
    small = jnp.concatenate(
        [mixer_gain, conv_weight.reshape(-1), conv_bias, ssm_gain, ffn_gain]
    ).astype(f32)
    counts = [mixer_gain.size, conv_weight.size, conv_bias.size, ssm_gain.size, ffn_gain.size]
    slots = -(-small.size // LANES) * LANES
    small = gather_small(jnp.pad(small, (0, slots - small.size)))
    others = lax.axis_size(SEQ)
    aligned = ys == 2 and others == 8 and all(r % 16 == 0 for r in (part, a_rows, s_rows, f_rows))
    core_unit = extents()["core"][0]
    if aligned:
        packed, front = run(
            pack_kernel,
            "pack",
            [((6 * part + s_rows, width), bf16), ((part, A_COLS + DS), bf16)],
            (
                gate_up_weight, inner_weight, attn_out_weight, ssm_out_weight, keyval_weight,
                query_weight,
            ),
        )
    else:
        tail = jnp.pad(inner_weight[:, DS + CONV_CH :], ((0, 0), (0, LANES - SSM_HEADS)))
        front = jnp.concatenate(
            [
                keyval_weight, query_weight, inner_weight[:, 2 * DS : DS + CONV_CH], tail,
                inner_weight[:, DS : 2 * DS],
            ],
            1,
        )
        ao = jnp.concatenate([attn_out_weight[:, :512], attn_out_weight[:, 512:]], 0)
        packed = jnp.concatenate(
            [
                inner_weight[:, :width],
                jnp.concatenate([inner_weight[:, width:DS], ao], 1),
                ssm_out_weight,
            ]
            + [gate_up_weight[:, k * width : (k + 1) * width] for k in range(2 * ff // width)],
            0,
        )
    packed = lax.all_gather(packed, AXES, axis=0)
    packed = packed.reshape(ys, 2, others, *packed.shape[1:])
    front = shared(front, "z")
    front_one = Gathering(front[:, :, :A_COLS], "y")
    front_two = Gathering(front[:, :, A_COLS:], "x")
    down_slots = after(down_weight, front_one.full, front_two.full)[None]
    down_slots = jnp.broadcast_to(down_slots, (lax.axis_size("z"), *down_weight.shape))
    down_all = dealt(down_slots, "z")
    front_one.finish(down_slots)
    front_two.finish(down_slots)
    down_got = Gathering(after(down_all, front_one.full, front_two.full), "x")
    front_one.finish(down_got.full)
    front_two.finish(down_got.full)
    wa_own, wa_oth = front_one.sides(1)
    wb_own, wb_oth = front_two.sides(1)

    starts = [sum(counts[:i]) for i in range(len(counts))]
    gain_one, w_conv, b_conv, gain_ssm, gain_two = (
        small[:, s : s + c].reshape(-1) for s, c in zip(starts, counts)
    )
    w_conv = jnp.pad(w_conv.reshape(CONV_CH, CONV).T, ((0, 8 - CONV), (0, 0)))
    gain_one, b_conv, gain_ssm, gain_two = (
        v[None, :] for v in (gain_one, b_conv, gain_ssm, gain_two)
    )
    tokens_rim = jnp.concatenate([rim, tokens], 0)
    places = seq_rank * rows + jnp.arange(rows)
    begin = jnp.zeros_like(places)
    end = jnp.int32(0)
    for i in range(lengths.shape[1]):
        end = end + lengths[0, i]
        begin = jnp.where(end <= places, end, begin)
    offset = (places - begin).astype(jnp.int32)
    half = HEAD_DIM // 2
    freq = BASE ** (-jnp.arange(half).astype(f32) / half)
    angle = offset.astype(f32)[:, None] * freq[None, :]
    cos = jnp.tile(jnp.cos(angle), (1, 4))
    sin = jnp.sin(angle)
    sin = jnp.tile(jnp.concatenate([-sin, sin], 1), (1, 2))
    off = offset[:, None]
    step_bias_row, decay_row = padded(step_bias, LANES), padded(jnp.exp(decay_log), LANES)
    skip = jnp.repeat(skip_gain, SSM_DIM)[None, :]

    (q8, kv, normed, nrim, chan, x, bc, step, cum, cumt, z, state, carry) = run(
        front_kernel,
        "front",
        [
            ((HEADS, rows, LANES), bf16),
            ((rows, 256), bf16),
            ((rows, width), bf16),
            ((RIM, width), bf16),
            ((rows + RIM, CONV_CH), bf16),
            ((rows, DS), f32),
            ((rows, 2 * STATE), f32),
            ((rows, LANES), f32),
            ((rows, LANES), f32),
            ((LANES, rows), f32),
            ((rows, LANES), f32),
            ((DS, STATE), f32),
            ((1, LANES), f32),
        ],
        (
            side, tokens_rim, gain_one, wa_own, wa_oth, wb_own, wb_oth,
            cos, sin, off, w_conv, b_conv, step_bias_row, decay_row,
        ),
        scalars=1,
        scratch=[((rows + RIM, width), bf16), ((rows, DS), bf16)],
        us=8,
    )
    carrying = Carrying(state, carry, back, 1)
    sent_state = carrying.send()
    rank = seq_rank.reshape(1).astype(jnp.int32)
    kv_slots = jnp.broadcast_to(kv[None], (seq_count, *kv.shape))
    down_got.finish(sent_state, kv_slots)
    kv_all = dealt(kv_slots, SEQ)
    window = (back + 1) * rows
    y_local = run(
        scan_kernel, "scan", [((rows, DS), f32)],
        after((x, bc, step, cum, cumt, off), sent_state, kv_slots, down_got.full),
        scratch=[((rows, DS), bf16), ((rows, DS), f32)], us=8,
    )[0]
    entry = carrying.receive(y_local)
    if entry is None:
        sent_state = carrying.send()
    down_got.finish(y_local, sent_state)
    attended, lse = run(
        functools.partial(attend_kernel, back + 1),
        "attend",
        [((rows, heads_width), bf16), ((LANES, rows), f32)],
        after((rank, q8, kv_all, off), down_got.full),
        scalars=1,
        scratch=[
            ((window, LANES), bf16),
            ((window, LANES), bf16),
            ((rows, window), f32),
            ((HEADS, rows, LANES), f32),
        ],
        us=10,
    )
    while entry is None:
        entry = carrying.receive(attended)
        if entry is None:
            carrying.send()
    packed = after(packed, entry)
    down_sides = [
        f.reshape(ys, others, *f.shape[3:]) for f in (down_got.full, down_got.other)
    ]
    post_scratch, post_sems = [], []
    if aligned:
        parts, post_weights = (part, a_rows, s_rows, f_rows), (packed, *down_sides)
        rows_in_all = 6 * part + s_rows + f_rows
        post_scratch = [((2, ys, others, rows_in_all, width), bf16)]
        post_sems = [(4, 2)]
    else:
        parts = ()
        packed = [
            jnp.concatenate(
                [
                    lax.dynamic_index_in_dim(packed, place_on("core") ^ i, 1, False),
                    down_sides[i],
                ],
                2,
            )
            for i in range(2)
        ]
        gu_at = 2 * part + s_rows

        def taken(full, start, size, low, high):
            return full[:, :, start : start + size, low:high].reshape(ys, -1, high - low)

        def joined_columns(blocks):
            return [jnp.concatenate([taken(f, *block) for block in blocks], 2) for f in packed]

        post_weights = (
            *joined_columns([(0, part, 0, width), (part, part, 0, DS - width)]),
            *joined_columns([(part + k * a_rows, a_rows, 512, 1024) for k in range(2)]),
            *joined_columns([(2 * part, s_rows, 0, width)]),
            *joined_columns([(gu_at + 4 * part, f_rows, 0, width)]),
            *joined_columns([(gu_at + k * part, part, 0, width) for k in range(2 * ff // width)]),
        )
    half = (2 * width + ff + heads_width + DS) // 2
    sent = 2 * ff + 2 * width + DS
    output, dmid, datt, dssd, ycore, dentry, send, keep, dng = run(
        functools.partial(post_kernel, parts, ys),
        "post",
        [
            ((rows, width), bf16),
            ((rows, width), f32),
            ((rows, heads_width), bf16),
            ((rows, DS), f32),
            ((rows, DS), f32),
            ((DS, STATE), f32),
            ((rows, sent + half), bf16),
            ((rows, half), bf16),
            ((rows, width), f32),
        ],
        (
            side, tokens, cotangent, attended, y_local, x, bc, cum, off, entry, skip, normed,
            gain_ssm, gain_two, *post_weights,
        ),
        scalars=1,
        left=3 if aligned else 0,
        sems=post_sems,
        scratch=[
            ((rows, DS), f32),
            ((rows, DS), f32),
            ((rows, width), f32),
            ((rows, 2 * ff), f32),
            ((rows, width), f32),
            ((rows, DS), f32),
            ((rows, DS), bf16),
            ((rows, width), bf16),
            ((rows, ff), bf16),
            ((rows, DS), bf16),
            ((rows, ff), f32),
            ((rows, DS), f32),
            ((rows, DS), f32),
        ]
        + post_scratch,
        us=30,
    )
    got = swap(send, core_unit)
    carrying = Carrying(dentry, carry, back, -1)
    sent_state = carrying.send()
    off_row = offset[None, :]
    sizes = [width // 2, ff // 2, heads_width // 2, DS // 2, width // 2]
    ats = [sum(sizes[:i]) for i in range(5)]
    sizes = [size // ys for size in sizes]
    n2_at, hid_at, att_at, mix_at, norm_at = ats
    cot_at, dbr_at, dgate_at = 2 * ff, 2 * ff + width, 2 * ff + 2 * width
    places = tuple(place_on(g).reshape(1).astype(jnp.int32) for g in ("y", "x"))

    def weight_sums(name, x_parts, y_parts, keep, own, got, extra=()):
        plan, at, tall = [], 0, y_parts[0][4]
        for p in x_parts:
            plan.append(("x", at, *p))
            at += p[4]
        wide, at = at, 0
        for p in y_parts:
            plan.append(("y", at, *p))
            at += p[2] // others
        if aligned:
            xs = (ys, others // 2, x_parts[0][2] // others, wide)
            made = run(
                functools.partial(split_products_kernel, plan, len(extra)),
                name,
                [(xs, bf16), (xs, bf16), ((others, at, tall), bf16), ((others, at, tall), bf16)],
                (*places, keep, own, got, *extra),
                scalars=2,
                us=9,
            )
            return PairReduction(made, 512 if wide % 512 == 0 else 384)
        parts = x_parts + y_parts
        made = run(
            functools.partial(
                products_kernel, [(i, *p[:4]) for i, p in enumerate(parts)], len(extra)
            ),
            name,
            [((ys, p[2], p[4]), bf16) for p in parts],
            (keep, own, got, *extra),
            us=9,
        )
        heads = made[: len(x_parts)]
        tails = [m.reshape(ys, others, -1, tall) for m in made[len(x_parts) :]]
        rows_of = (x_parts[0][2] // others, at)
        return PlainReduction((jnp.concatenate(heads, 2), jnp.concatenate(tails, 2)), rows_of)

    dxw, dscores = run(
        scan_back_kernel,
        "scan_back",
        [((rows, DS), f32), ((rows, rows), bf16)],
        after((dssd, x, bc, step, cum, cumt, off_row), sent_state),
        scratch=[
            ((rows, DS), bf16),
            ((rows, DS), f32),
            ((rows, DS), bf16),
            ((rows, rows), f32),
        ],
        us=9,
    )

    downstream = carrying.receive(dxw)
    if downstream is None:
        sent_state = carrying.send()
    keep, send, got = after((keep, send, got), dxw, sent_state)
    red_one = weight_sums(
        "weights_one",
        [(n2_at, sent + n2_at, sizes[0], 0, ff)],
        [(hid_at, sent + hid_at, sizes[1], cot_at, width)],
        keep,
        send,
        got,
    )
    dq, dkv = run(
        functools.partial(attend_back_kernel, back + 1),
        "attend_back",
        [((rows, heads_width), bf16), ((seq_count, rows, 256), bf16)],
        after((rank, q8, kv_all, off_row, lse, datt, cos, sin), red_one.sent),
        scalars=1,
        scratch=[
            ((window, LANES), bf16),
            ((window, LANES), bf16),
            ((window, rows), f32),
            ((HEADS, rows, LANES), bf16),
            ((HEADS, rows, LANES), f32),
            ((window, 256), f32),
        ],
        us=14,
    )
    dkv_got = dealt(dkv, SEQ)
    keep, send, got = after((keep, send, got), red_one.sent, dq, dkv)
    red_two = weight_sums(
        "weights_two",
        [
            (n2_at, sent + n2_at, sizes[0], ff, ff),
            (norm_at, sent + norm_at, sizes[4], dgate_at, DS),
        ],
        [
            (att_at, sent + att_at, sizes[2], dbr_at, width),
            (mix_at, sent + mix_at, sizes[3], dbr_at, width),
        ],
        keep,
        send,
        got,
    )
    while downstream is None:
        downstream = carrying.receive(red_two.sent)
        if downstream is None:
            carrying.send()
    red_one.fold_one(red_two.sent, downstream)
    dext, dz, small = run(
        mixer_back_kernel,
        "mixer_back",
        [
            ((rows + RIM, CONV_CH), f32),
            ((rows, LANES), f32),
            ((8, CONV_CH), f32),
        ],
        after(
            (
                dssd, ycore, x, bc, step, cum, z, off, entry, downstream, skip, decay_row, chan,
                w_conv, b_conv, dxw, dscores,
            ),
            red_one.sent,
        ),
        scratch=[((rows, CONV_CH), f32)],
        us=13,
    )
    count = lax.axis_size(AXES)
    gab, norm_keep = run(
        functools.partial(back_grads_kernel, ys),
        "back_grads",
        [((rows + 2 * RIM, A_COLS + DS + width // 2), bf16), ((rows + RIM, width // 2), bf16)],
        (side, dq, dkv_got, dext, dz, cos, sin, normed, nrim, small),
        scalars=1,
    )
    gab_got = swap(gab, core_unit)
    small = small + gab_got[rows + RIM : rows + RIM + small.shape[0], :CONV_CH].astype(f32)
    free = LANES - SSM_HEADS
    convs = small[: CONV + 1].reshape(CONV + 1, count, -1).transpose(1, 0, 2)
    head_sums = small[CONV + 1, : 3 * LANES].reshape(3, LANES)[:, :SSM_HEADS]
    if aligned:
        head_sums = jnp.broadcast_to(head_sums[None], (count, 3, SSM_HEADS))
        per_device = jnp.concatenate(
            [
                jnp.pad(convs, ((0, 0), (0, 0), (0, free - convs.shape[2]))),
                jnp.pad(head_sums, ((0, 0), (0, 0), (0, free - SSM_HEADS))),
            ],
            1,
        )
        slots = CONV + 4
    else:
        head_sums = jnp.broadcast_to(head_sums.reshape(1, -1), (count, 3 * SSM_HEADS))
        per_device = jnp.concatenate([convs.reshape(count, -1), head_sums], 1)
        slots = per_device.shape[1]
        per_device = jnp.pad(per_device, ((0, 0), (0, part * free - slots)))
        per_device = per_device.reshape(count, part, free)
    per_device = lax.dynamic_index_in_dim(
        per_device.reshape(ys, 2, others, -1, free), place_on("core"), 1, False
    )
    aside = 384 if aligned else A_COLS % 512
    extra = jnp.pad(
        per_device, ((0, 0), (0, 0), (0, part - per_device.shape[2]), (aside - free, 0))
    ).reshape(ys, others * part, aside)
    grad_tokens, grad_rim = run(
        back_kernel,
        "back",
        [((rows, width), f32), ((RIM, width), f32)],
        (
            side, gab, wa_own, wa_oth, wb_own, wb_oth, tokens_rim, dmid, dng,
            gain_one,
        ),
        scalars=1,
        scratch=[((rows + RIM, width), f32)],
        us=7,
    )
    red_two.fold_one(grad_tokens)
    norm_keep, gab, gab_got, extra = after((norm_keep, gab, gab_got, extra), red_two.sent)
    red_three = weight_sums(
        "front_weights",
        [(0, A_COLS + DS, sizes[4], 0, A_COLS)],
        [(0, A_COLS + DS, sizes[4], A_COLS, DS)],
        norm_keep,
        gab,
        gab_got,
        (extra,),
    )
    red_one.fold_two(red_three.sent)
    red_two.fold_two(red_one.sent)
    red_one.fold_three(red_two.sent)
    red_three.fold_one(red_one.sent)
    red_two.fold_three(red_three.sent)
    red_three.fold_two(red_two.sent)
    rim_got = shifted(after(grad_rim, red_three.sent), -1)
    r_one, r_down = red_one.fold_four(red_three.sent)
    red_three.fold_three(r_one)
    if aligned:
        r_gu, r_gate, r_ao, r_so, g_ffn, g_ssm = run(
            finish_post_kernel,
            "finish_post",
            [
                ((part, 2 * ff), f32),
                ((part, DS), f32),
                ((a_rows, width), f32),
                ((s_rows, width), f32),
                ((1, part), f32),
                ((1, s_rows), f32),
            ],
            (
                red_two.keep, after(red_two.gots, red_three.sent), r_one, gate_up_weight, ssm_out_weight,
                ffn_gain.astype(f32)[None, :], ssm_gain.astype(f32)[None, :],
            ),
        )
        rim_got = after(rim_got, r_gu)
        grad_tokens = grad_tokens.at[rows - RIM :].add(rim_got)
        r_kv, r_q, g_inner, g_conv, g_bias, g_log, g_step, g_skip, g_mixer = run(
            finish_front_kernel,
            "finish_front",
            [
                ((part, 256), f32),
                ((part, heads_width), f32),
                ((part, inner_weight.shape[1]), f32),
                (conv_weight.shape, f32),
                ((1, conv_bias.size), f32),
                ((1, SSM_HEADS), f32),
                ((1, SSM_HEADS), f32),
                ((1, SSM_HEADS), f32),
                ((1, part), f32),
            ],
            (
                red_three.keep, after(red_three.gots, grad_tokens), r_gate, keyval_weight, query_weight,
                inner_weight, mixer_gain.astype(f32)[None, :],
            ),
        )
        g_bias, g_mixer, g_ssm, g_ffn = (v[0] for v in (g_bias, g_mixer, g_ssm, g_ffn))
        heads = [v[0] for v in (g_log, g_step, g_skip)]
    else:
        r_two, r_out = red_two.fold_four(red_three.sent)
        rim_got = after(rim_got, r_two)
        grad_tokens = grad_tokens.at[rows - RIM :].add(rim_got)
        r_e, r_f = red_three.fold_four(grad_tokens)
        r_gu = jnp.concatenate([r_one, r_two[:, :ff]], 1)
        small = r_e[:, A_COLS - free :].reshape(-1)[:slots]
        conv = small[: (CONV + 1) * conv_bias.size].reshape(CONV + 1, -1)
        g_conv, g_bias = conv[:CONV].T, conv[CONV]
        heads = small[(CONV + 1) * conv_bias.size :].reshape(3, SSM_HEADS)
        g_inner = jnp.concatenate([r_two[:, ff:], r_f, r_e[:, 768 : 1024 + SSM_HEADS]], 1)
        r_kv, r_q, r_ao, r_so = r_e[:, :256], r_e[:, 256:768], r_out[:a_rows], r_out[a_rows:]
        pairs = [(0, 0, 1), (0, 2, 3), (0, 4, 5), (1, 6, 7), (2, 8, 9)]
        gains = run(
            functools.partial(gain_kernel, pairs, 3),
            "gains",
            [((part, 1), f32), ((s_rows, 1), f32), ((part, 1), f32)],
            (
                mixer_gain[:, None], ssm_gain[:, None], ffn_gain[:, None],
                keyval_weight, r_kv, query_weight, r_q, inner_weight, g_inner,
                ssm_out_weight, r_so, gate_up_weight, r_gu,
            ),
        )
        g_mixer, g_ssm, g_ffn = (v[:, 0] for v in gains)
    return (
        output,
        grad_tokens,
        g_mixer,
        r_q,
        r_kv,
        g_inner,
        g_conv,
        g_bias,
        g_ssm,
        r_ao,
        r_so,
        g_ffn,
        r_gu,
        r_down,
        heads[0],
        heads[1],
        heads[2],
    )


def solution(mesh):
    across, along = mesh.shape["dp"], mesh.shape["seq"]
    mesh = jax.sharding.Mesh(mesh.devices.reshape(across // 2, 2, along // 2, 2), AXES)
    lead, flat, rep = P(AXES, None), P(AXES), P()
    return jax.shard_map(
        local,
        mesh=mesh,
        in_specs=(
            lead, P(AXES[:2], None), lead, flat, lead, lead, lead, lead, flat, flat, lead, lead, flat,
            lead, lead, rep, rep, rep,
        ),
        out_specs=(
            lead, lead, flat, lead, lead, lead, lead, flat, flat, lead, lead, flat, lead, lead,
            rep, rep, rep,
        ),
        check_vma=False,
    )
```
